32 devices in a mesh: fsdp: 2 (over x), ctx: 4 (over z), tp: 4 (over y, core).
Axes of the slice: x: 2, y: 2, z: 4, core: 2. Of those that a mesh axis runs over, the one named last changes fastest.
Arguments:
- layer_input: bfloat16 [2048, 8, 1536], P(('ctx', 'tp'), 'fsdp'), may hold values from -6 to 6
- lengths: int32 [8], P('fsdp'), may hold values from 512 to 2048, as said below
- attn_gain: bfloat16 [1536], P(('fsdp', 'ctx')), may hold values from 0.5 to 1.5
- w_query: bfloat16 [1536, 1536], P(('fsdp', 'ctx'), 'tp'), may hold values from -0.15625 to 0.15625
- w_key: bfloat16 [1536, 1536], P(('fsdp', 'ctx'), 'tp'), may hold values from -0.15625 to 0.15625
- w_value: bfloat16 [1536, 1536], P(('fsdp', 'ctx'), 'tp'), may hold values from -0.15625 to 0.15625
- w_forget: bfloat16 [1536, 24], P(('fsdp', 'ctx'), 'tp'), may hold values from -0.15625 to 0.15625
- forget_bias: bfloat16 [24], P('tp'), may hold values from 2 to 9
- w_gate_out: bfloat16 [1536, 1536], P(('fsdp', 'ctx'), 'tp'), may hold values from -0.15625 to 0.15625
- w_out: bfloat16 [1536, 1536], P(('fsdp', 'ctx'), 'tp'), may hold values from -0.625 to 0.625
- mlp_gain: bfloat16 [1536], P(('fsdp', 'ctx')), may hold values from 0.5 to 1.5
- w_gate: bfloat16 [1536, 4096], P(('fsdp', 'ctx'), 'tp'), may hold values from -0.15625 to 0.15625
- w_up: bfloat16 [1536, 4096], P(('fsdp', 'ctx'), 'tp'), may hold values from -0.15625 to 0.15625
- w_down: bfloat16 [1536, 4096], P(('fsdp', 'ctx'), 'tp'), may hold values from -0.09375 to 0.09375
- cotangent: bfloat16 [2048, 8, 1536], P(('ctx', 'tp'), 'fsdp'), may hold values from -6 to 6
Outputs:
- output: bfloat16 [2048, 8, 1536], P(('ctx', 'tp'), 'fsdp')
- input_grad: bfloat16 [2048, 8, 1536], P(('ctx', 'tp'), 'fsdp')
- attn_gain_grad: float32 [1536], P(('fsdp', 'ctx'))
- w_query_grad: float32 [1536, 1536], P(('fsdp', 'ctx'), 'tp')
- w_key_grad: float32 [1536, 1536], P(('fsdp', 'ctx'), 'tp')
- w_value_grad: float32 [1536, 1536], P(('fsdp', 'ctx'), 'tp')
- w_forget_grad: float32 [1536, 24], P(('fsdp', 'ctx'), 'tp')
- forget_bias_grad: float32 [24], P('tp')
- w_gate_out_grad: float32 [1536, 1536], P(('fsdp', 'ctx'), 'tp')
- w_out_grad: float32 [1536, 1536], P(('fsdp', 'ctx'), 'tp')
- mlp_gain_grad: float32 [1536], P(('fsdp', 'ctx'))
- w_gate_grad: float32 [1536, 4096], P(('fsdp', 'ctx'), 'tp')
- w_up_grad: float32 [1536, 4096], P(('fsdp', 'ctx'), 'tp')
- w_down_grad: float32 [1536, 4096], P(('fsdp', 'ctx'), 'tp')
The draws below stay inside these ranges and needn't reach their ends.
Inputs may be any that keep to these rules, and one draw needn't show every extreme that they name: Slots l < lengths[b] of sequence b are valid; in every draw one sequence has 2048 valid slots and one has 512.
All inputs are finite; a program needn't handle non-finite values.
Results may differ from the reference program's by a relative error of at most 0.017.
Values may be sent and summed in bfloat16 or wider, within the bound.
A program may use at most 256 MiB of HBM per device.

```python
import math
import jax
import jax.numpy as jnp
from jax import lax

D = 1536
H = 24
HD = 64
FF = 4096
L = 2048
MIN_LEN = 512
QB = 512
B = 8


def draw_lengths(key, part):
    base = jax.random.randint(jax.random.fold_in(key, 11), (B,), MIN_LEN, L + 1)
    order = jax.random.permutation(jax.random.fold_in(key, 12), B)
    base = base.at[order[0]].set(L)
    base = base.at[order[1]].set(MIN_LEN)
    return base.astype(jnp.int32)


def with_spikes(values, own_key, source, target, parts, factor):
    def block_of(position):
        return (jnp.arange(values.shape[position]) // (values.shape[position] // parts)).reshape((-1,) + (1,) * (values.ndim - 1 - position))

    one_side = jax.random.permutation(own_key, parts)[block_of(target)]
    other_side = (block_of(target) + parts // 2) % parts
    return jnp.where((block_of(source) == one_side) | (block_of(source) == other_side), factor * values, values)


def block_scale(rng, extent, pieces, smallest, top_value):
    level = 1.0
    for axis_at, parts in pieces:
        draws = jax.random.uniform(jax.random.fold_in(jax.random.fold_in(rng, 6), axis_at), (parts,), jnp.float32, smallest / len(pieces), top_value / len(pieces))
        level = level * jnp.repeat(jnp.exp(draws), extent[axis_at] // parts).reshape((-1,) + (1,) * (len(extent) - 1 - axis_at))
    return level


def gaussian(key, dims, spread, bound, split=(), held_as=jnp.bfloat16):
    loudness = block_scale(key, dims, split, -0.22, 0.18) if split else 1.0
    values = jax.random.normal(key, dims, jnp.float32) * spread * loudness
    return jnp.minimum(jnp.maximum(values, -bound), bound).astype(held_as)


def bell_draw_with(rng, shape, spread, bound, pieces, heavy, kind=jnp.bfloat16):
    entries = spread * jax.random.normal(rng, shape, jnp.float32)
    if pieces:
        entries = entries * block_scale(rng, shape, pieces, -0.22, 0.18)
    return jnp.clip(with_spikes(entries, jax.random.fold_in(rng, 3), *heavy), -bound, bound).astype(kind)


def setup_inputs(seed: int = 0) -> dict:
    key_of = jax.random.split(jax.random.key(seed), 16)
    layer_input = gaussian(key_of[0], (L, B, D), 1.0, 6.0, ((0, 16), (1, 2)))
    lengths = draw_lengths(jax.random.fold_in(key_of[15], 71), 0)
    attn_gain = jnp.clip(1.0 + 0.1 * jax.random.normal(key_of[2], (D,), jnp.float32), 0.5, 1.5).astype(jnp.bfloat16)
    w_query = gaussian(key_of[3], (D, H * HD), D ** -0.5, 0.15625, ((0, 8), (1, 4)))
    w_key = gaussian(key_of[4], (D, H * HD), D ** -0.5, 0.15625, ((0, 8), (1, 4)))
    w_value = gaussian(key_of[5], (D, H * HD), D ** -0.5, 0.15625, ((0, 8), (1, 4)))
    w_forget = gaussian(key_of[6], (D, H), D ** -0.5, 0.15625, ((0, 8), (1, 4)))
    forget_bias = jnp.clip(2.0 + 7.0 * jax.random.uniform(key_of[7], (H,), jnp.float32) ** block_scale(key_of[7], (H,), ((0, 4),), -0.2, 0.2), 2.0, 9.0).astype(jnp.bfloat16)
    w_gate_out = gaussian(key_of[8], (D, H * HD), D ** -0.5, 0.15625, ((0, 8), (1, 4)))
    w_out = gaussian(key_of[9], (D, H * HD), (H * HD // 16) ** -0.5, 0.625, ((0, 8), (1, 4)))
    mlp_gain = jnp.clip(1.0 + 0.1 * jax.random.normal(key_of[10], (D,), jnp.float32), 0.5, 1.5).astype(jnp.bfloat16)
    w_gate = gaussian(key_of[11], (D, FF), D ** -0.5, 0.15625, ((0, 8), (1, 4)))
    w_up = gaussian(key_of[12], (D, FF), D ** -0.5, 0.15625, ((0, 8), (1, 4)))
    w_down = gaussian(key_of[13], (D, FF), FF ** -0.5, 0.09375, ((0, 8), (1, 4)))
    cotangent = bell_draw_with(key_of[14], (L, B, D), 1.0, 6.0, ((0, 16), (1, 2)), (0, 2, 16, 2.0))
    return {"layer_input": layer_input, "lengths": lengths, "attn_gain": attn_gain, "w_query": w_query, "w_key": w_key, "w_value": w_value, "w_forget": w_forget, "forget_bias": forget_bias, "w_gate_out": w_gate_out, "w_out": w_out, "mlp_gain": mlp_gain, "w_gate": w_gate, "w_up": w_up, "w_down": w_down, "cotangent": cotangent}


epsilon = 1e-06
highest = lax.Precision.HIGHEST
masked_score = -1e+30

@jax.custom_vjp
def low(v):
    return lax.optimization_barrier(v.astype(jnp.bfloat16)).astype(jnp.float32)

@jax.custom_vjp
def low_back(v):
    return v

def low_keep(v):
    return (low(v), None)

def low_pass(kept, grad):
    return (grad,)

def back_keep(v):
    return (v, None)

def back_low(kept, grad):
    return (low(grad),)
low.defvjp(low_keep, low_pass)
low_back.defvjp(back_keep, back_low)

def row_norm(values, gain_vec):
    inverse = lax.rsqrt(lax.optimization_barrier(jnp.mean(values * values, axis=-1, keepdims=True)) + epsilon)
    return values * inverse * gain_vec

def attend_item(query_rows, key_rows, value_rows, forget_rows, length):
    decay_sum = jnp.cumsum(forget_rows)
    key_pos = jnp.arange(L, dtype=jnp.int32)
    score_scale = HD ** (-0.5)

    def one_block(block_index):
        row_start = block_index * QB
        query_block = lax.dynamic_slice_in_dim(query_rows, row_start, QB, 0)
        decay_here = lax.dynamic_slice_in_dim(decay_sum, row_start, QB, 0)
        query_pos = row_start + jnp.arange(QB, dtype=jnp.int32)
        scores = jnp.dot(query_block, key_rows.T, precision=highest) * score_scale
        scores = low_back(scores + decay_here[:, None] - decay_sum[None, :])
        allowed = (key_pos[None, :] <= query_pos[:, None]) & (key_pos[None, :] < length)
        scores = jnp.where(allowed, scores, masked_score)
        row_top = lax.optimization_barrier(jnp.max(scores, axis=1, keepdims=True))
        weight = jnp.exp(scores - row_top)
        prob_rows = weight / lax.optimization_barrier(jnp.sum(weight, axis=1, keepdims=True))
        return jnp.dot(low(prob_rows), value_rows, precision=highest)
    blocks = lax.map(jax.checkpoint(one_block), jnp.arange(L // QB, dtype=jnp.int32))
    return blocks.reshape(L, HD)

def layer_forward(hidden_in, valid_rows, group_len, attn_gain, w_query, w_key, w_value, w_forget, forget_bias, w_gate_out, w_out, mlp_gain, w_gate, w_up, w_down):
    group_size = hidden_in.shape[1]
    normed = low(row_norm(hidden_in, attn_gain))

    def project(weight):
        return jnp.einsum('lgd,dc->lgc', normed, weight, precision=highest)
    query_all = low_back(low(project(w_query)))
    key_all = low_back(low(project(w_key)))
    value_all = low_back(low(project(w_value)))
    forget_logit = low_back(project(w_forget) + forget_bias)
    log_forget = low_back(low(valid_rows[:, :, None] * jax.nn.log_sigmoid(forget_logit)))

    def by_head(rows):
        return rows.reshape(L, group_size, H, HD).transpose(1, 2, 0, 3)
    attend = jax.vmap(jax.vmap(attend_item, in_axes=(0, 0, 0, 0, None)), in_axes=(0, 0, 0, 0, 0))
    attended = attend(by_head(query_all), by_head(key_all), by_head(value_all), log_forget.transpose(1, 2, 0), group_len)
    attended = low_back(low(attended.transpose(2, 0, 1, 3).reshape(L, group_size, H * HD)))
    out_gate = jax.nn.sigmoid(low_back(project(w_gate_out)))
    mixed_out = low(attended * out_gate)
    attn_branch = low_back(jnp.einsum('lgc,dc->lgd', mixed_out, w_out, precision=highest))
    hidden_state = hidden_in + attn_branch
    normed_mlp = low(row_norm(hidden_state, mlp_gain))
    gate_preactivation = low_back(jnp.einsum('lgd,df->lgf', normed_mlp, w_gate, precision=highest))
    up_projection = low_back(jnp.einsum('lgd,df->lgf', normed_mlp, w_up, precision=highest))
    inner_activation = low(jax.nn.silu(gate_preactivation) * up_projection)
    feedforward_branch = low_back(jnp.einsum('lgf,df->lgd', inner_activation, w_down, precision=highest))
    return valid_rows[:, :, None] * (hidden_state + feedforward_branch)

def reference(layer_input, lengths, attn_gain, w_query, w_key, w_value, w_forget, forget_bias, w_gate_out, w_out, mlp_gain, w_gate, w_up, w_down, cotangent):
    params = tuple((tensor.astype(jnp.float32) for tensor in (attn_gain, w_query, w_key, w_value, w_forget, forget_bias, w_gate_out, w_out, mlp_gain, w_gate, w_up, w_down)))
    group_size = math.gcd(B, max(1, 4096 // L))
    slot_pos = jnp.arange(L, dtype=jnp.int32)

    def one_group(totals, group_index):
        first_seq = group_index * group_size
        hidden_in = lax.dynamic_slice_in_dim(layer_input, first_seq, group_size, 1).astype(jnp.float32)
        group_len = lax.dynamic_slice_in_dim(lengths, first_seq, group_size, 0)
        grad_in = lax.dynamic_slice_in_dim(cotangent, first_seq, group_size, 1).astype(jnp.float32)
        valid_rows = (slot_pos[:, None] < group_len[None, :]).astype(jnp.float32)

        def apply_layer(hidden_values, *weights):
            return layer_forward(hidden_values, valid_rows, group_len, *weights)
        result, pullback = jax.vjp(apply_layer, hidden_in, *params)
        gradients = pullback(grad_in)
        totals = tuple((total_now + grad_now for total_now, grad_now in zip(totals, gradients[1:])))
        return (totals, (result.astype(jnp.bfloat16), gradients[0].astype(jnp.bfloat16)))
    start_totals = tuple((jnp.zeros_like(tensor) for tensor in params))
    totals, (outputs, input_grads) = lax.scan(one_group, start_totals, jnp.arange(B // group_size, dtype=jnp.int32))

    def to_layout(stacked):
        return stacked.transpose(1, 0, 2, 3).reshape(L, B, D)
    return (to_layout(outputs), to_layout(input_grads), totals[0], totals[1], totals[2], totals[3], totals[4], totals[5], totals[6], totals[7], totals[8], totals[9], totals[10], totals[11])
```

```python
import functools

import jax
import jax.numpy as jnp
from jax import lax
from jax.experimental import pallas as pl
from jax.experimental.pallas import tpu as pltpu
from jax.sharding import PartitionSpec as P

F32 = jnp.float32
BF16 = jnp.bfloat16
LANES = 128
epsilon = 1e-06
masked_score = -1e30
NT = (((1,), (1,)), ((), ()))
NN = (((1,), (0,)), ((), ()))
TN = (((0,), (0,)), ((), ()))


def dot(left, right, dims):
    return lax.dot_general(left, right, dims, preferred_element_type=F32)


def of_head(block, head, head_size, ones_at=None):
    lane = lax.broadcasted_iota(jnp.int32, block.shape, 1)
    out = jnp.where(lane // head_size == head, block, jnp.zeros_like(block))
    if ones_at is not None:
        out = jnp.where(lane == ones_at, jnp.ones_like(block), out)
    return out


def spare_lane(head, head_size):
    return ((head + 1) % 2) * head_size


def attend_forward(len_ref, qkv_ref, decay_ref, out_ref, exact_ref, lse_ref, *, heads, head_size):
    count, _, block, width = qkv_ref.shape
    scale = head_size**-0.5
    live = pl.cdiv(len_ref[0], block)
    out_ref[...] = jnp.zeros_like(out_ref)
    exact_ref[...] = jnp.zeros_like(exact_ref)
    lse_ref[...] = jnp.zeros_like(lse_ref)
    row = lax.broadcasted_iota(jnp.int32, (block, block), 0)
    column = lax.broadcasted_iota(jnp.int32, (block, block), 1)
    causal = column <= row

    def query_block(i, _):
        query = qkv_ref[i, 0]
        lanes = pl.ds(pl.multiple_of(i * block, block), block)
        result = jnp.zeros((block, width), F32)
        for head in range(heads):
            query_head = of_head(query, head, head_size)

            def step(j, carry, masked):
                top, total, acc = carry
                keys = pl.ds(pl.multiple_of(j * block, block), block)
                score = dot(query_head, qkv_ref[j, 1], NT) * scale
                score = score - decay_ref[head : head + 1, keys]
                if masked:
                    score = jnp.where(causal, score, masked_score)
                new_top = jnp.maximum(top, jnp.max(score, axis=1, keepdims=True))
                prob = jnp.exp(score - new_top)
                shrink = jnp.exp(top - new_top)
                total = total * shrink + jnp.sum(prob, axis=1, keepdims=True)
                acc = acc * shrink + dot(prob.astype(BF16), qkv_ref[j, 2], NN)
                return new_top, total, acc

            carry = (
                jnp.full((block, 1), masked_score, F32),
                jnp.zeros((block, 1), F32),
                jnp.zeros((block, width), F32),
            )
            carry = lax.fori_loop(0, i, lambda j, c: step(j, c, False), carry)
            top, total, acc = step(i, carry, True)
            lane = lax.broadcasted_iota(jnp.int32, acc.shape, 1)
            result = jnp.where(lane // head_size == head, acc / total, result)
            stat = jnp.broadcast_to(top + jnp.log(total), (block, LANES)).T
            lse_ref[head : head + 1, lanes] = stat[0:1]
        exact_ref[i] = result
        out_ref[i] = result.astype(BF16)
        return 0

    lax.fori_loop(0, live, query_block, 0)


def attend_backward(
    len_ref,
    qkv_ref,
    grad_ref,
    exact_ref,
    lse_ref,
    decay_ref,
    dqkv_ref,
    row_ref,
    column_ref,
    dq_acc,
    delta,
    *,
    heads,
    head_size,
):
    count, _, block, width = qkv_ref.shape
    scale = head_size**-0.5
    live = pl.cdiv(len_ref[0], block)
    for ref in (dqkv_ref, row_ref, column_ref, dq_acc):
        ref[...] = jnp.zeros_like(ref)
    row = lax.broadcasted_iota(jnp.int32, (block, block), 0)
    column = lax.broadcasted_iota(jnp.int32, (block, block), 1)
    causal = row <= column

    def prepare(i, _):
        lanes = pl.ds(pl.multiple_of(i * block, block), block)
        product = grad_ref[i].astype(F32) * exact_ref[i]
        lane = lax.broadcasted_iota(jnp.int32, product.shape, 1)
        for head in range(heads):
            part = jnp.where(lane // head_size == head, product, 0.0)
            part = jnp.sum(part, axis=1, keepdims=True)
            delta[head : head + 1, lanes] = jnp.broadcast_to(part, (block, LANES)).T[0:1]
        return 0

    lax.fori_loop(0, live, prepare, 0)

    def key_block(j, _):
        keys = pl.ds(pl.multiple_of(j * block, block), block)
        key = qkv_ref[j, 1]
        value = qkv_ref[j, 2]
        value_total = jnp.zeros((block, width), F32)
        key_total = jnp.zeros((block, width), F32)
        for head in range(heads):
            spare = spare_lane(head, head_size)
            key_ones = of_head(key, head, head_size, spare)
            decay = jnp.broadcast_to(decay_ref[head : head + 1, keys], (LANES, block)).T[:, 0:1]

            def step(i, carry, masked):
                value_acc, key_acc = carry
                lanes = pl.ds(pl.multiple_of(i * block, block), block)
                query = qkv_ref[i, 0]
                grad = of_head(grad_ref[i], head, head_size)
                score = dot(key, of_head(query, head, head_size), NT) * scale
                score = score - decay - lse_ref[head : head + 1, lanes]
                if masked:
                    score = jnp.where(causal, score, masked_score)
                prob = jnp.exp(score)
                grad_prob = dot(value, grad, NT)
                grad_score = prob * (grad_prob - delta[head : head + 1, lanes])
                grad_score = grad_score.astype(BF16)
                value_acc = value_acc + dot(prob.astype(BF16), grad, NN)
                query_ones = of_head(query, head, head_size, spare)
                key_acc = key_acc + dot(grad_score, query_ones, NN)
                dq_acc[head, i] += dot(grad_score, key_ones, TN)
                return value_acc, key_acc

            zero = jnp.zeros((block, width), F32)
            carry = step(j, (zero, zero), True)
            carry = lax.fori_loop(j + 1, live, lambda i, c: step(i, c, False), carry)
            value_acc, key_acc = carry
            value_total = value_total + value_acc
            lane = lax.broadcasted_iota(jnp.int32, key_acc.shape, 1)
            key_total = jnp.where(lane // head_size == head, key_acc, key_total)
            column_ref[head : head + 1, keys] = key_acc.T[spare : spare + 1]
        dqkv_ref[j, 1] = (key_total * scale).astype(BF16)
        dqkv_ref[j, 2] = value_total.astype(BF16)
        return 0

    lax.fori_loop(0, live, key_block, 0)

    def finish(i, _):
        lanes = pl.ds(pl.multiple_of(i * block, block), block)
        total = jnp.zeros((block, width), F32)
        for head in range(heads):
            spare = spare_lane(head, head_size)
            part = dq_acc[head, i]
            lane = lax.broadcasted_iota(jnp.int32, part.shape, 1)
            total = jnp.where(lane // head_size == head, part, total)
            row_ref[head : head + 1, lanes] = part.T[spare : spare + 1]
        dqkv_ref[i, 0] = (total * scale).astype(BF16)
        return 0

    lax.fori_loop(0, live, finish, 0)


def attend_specs(count):
    smem = pl.BlockSpec(memory_space=pltpu.SMEM)
    return [smem] + [pl.BlockSpec(memory_space=pltpu.VMEM)] * count


def attend_cost(qkv, decay, products):
    count, _, block, width = qkv.shape
    heads = decay.shape[0]
    pairs = heads * (count * block) ** 2 // 3
    return pl.CostEstimate(
        flops=2 * products * pairs * 256, bytes_accessed=2 * qkv.size * 2, transcendentals=pairs
    )


def attend(length, qkv, decay, head_size):
    count, _, block, width = qkv.shape
    return pl.pallas_call(
        functools.partial(attend_forward, heads=decay.shape[0], head_size=head_size),
        out_shape=[
            jax.ShapeDtypeStruct((count, block, width), BF16),
            jax.ShapeDtypeStruct((count, block, width), F32),
            jax.ShapeDtypeStruct(decay.shape, F32),
        ],
        in_specs=attend_specs(2),
        out_specs=attend_specs(3)[1:],
        compiler_params=pltpu.CompilerParams(vmem_limit_bytes=40 << 20),
        cost_estimate=attend_cost(qkv, decay, 2),
        name="attend_forward",
    )(length, qkv, decay)


def attend_grad(length, qkv, grad, exact, lse, decay, head_size):
    count, _, block, width = qkv.shape
    heads = decay.shape[0]
    return pl.pallas_call(
        functools.partial(attend_backward, heads=heads, head_size=head_size),
        out_shape=[
            jax.ShapeDtypeStruct(qkv.shape, BF16),
            jax.ShapeDtypeStruct(decay.shape, F32),
            jax.ShapeDtypeStruct(decay.shape, F32),
        ],
        in_specs=attend_specs(5),
        out_specs=attend_specs(3)[1:],
        scratch_shapes=[
            pltpu.VMEM((heads, count, block, width), F32),
            pltpu.VMEM((8, count * block), F32),
        ],
        compiler_params=pltpu.CompilerParams(vmem_limit_bytes=40 << 20),
        cost_estimate=attend_cost(qkv, decay, 5),
        name="attend_backward",
    )(length, qkv, grad, exact, lse, decay)


MESH = pl.DeviceIdType.MESH
CHUNKS = 4


def tp_places():
    me = lax.axis_index("tp")
    sibling = me + 1 - 2 * lax.rem(me, 2)
    across = lax.rem(me + 2, 4)
    diagonal = lax.rem(sibling + 2, 4)
    return me, sibling, across, diagonal


def greet(peers):
    barrier = pltpu.get_barrier_semaphore()
    for peer in peers:
        pl.semaphore_signal(barrier, inc=1, device_id={"tp": peer}, device_id_type=MESH)
    pl.semaphore_wait(barrier, len(peers))


def sending(source, target, send_sem, recv_sem, peer):
    return pltpu.make_async_remote_copy(
        src_ref=source,
        dst_ref=target,
        send_sem=send_sem,
        recv_sem=recv_sem,
        device_id={"tp": peer},
        device_id_type=MESH,
    )


def pick(step, chunks, places):
    me, sibling, across, diagonal = places
    late = step - 2 * chunks
    far = jnp.where(lax.rem(late, 2) == 0, across, diagonal)
    slot = jnp.where(step < chunks, me, jnp.where(step < 2 * chunks, sibling, far))
    chunk = jnp.where(step < 2 * chunks, lax.rem(step, chunks), late // 2)
    return slot, chunk


def gather_loop(table, sems, compute):
    near_send, near_recv, far_send, far_recv, pass_send, pass_recv = sems
    me, sibling, across, diagonal = places = tp_places()
    rows = table.shape[1] // CHUNKS

    def part(slot, chunk):
        return table.at[slot, pl.ds(pl.multiple_of(chunk * rows, rows), rows)]

    def far(chunk):
        return sending(
            part(me, chunk), part(me, chunk), far_send.at[chunk], far_recv.at[chunk], across
        )

    def far_arrival(chunk):
        spot = part(across, chunk)
        return sending(spot, spot, far_send.at[chunk], far_recv.at[chunk], across)

    def passing(chunk):
        spot = part(across, chunk)
        return sending(spot, spot, pass_send.at[chunk], pass_recv.at[chunk], sibling)

    def pass_arrival(chunk):
        spot = part(diagonal, chunk)
        return sending(spot, spot, pass_send.at[chunk], pass_recv.at[chunk], sibling)

    for chunk in range(CHUNKS):
        far(chunk).start()
    near = sending(table.at[me], table.at[me], near_send, near_recv, sibling)
    near.start()

    def body(step, _):
        slot, chunk = pick(step, CHUNKS, places)
        late = step - 2 * CHUNKS

        @pl.when(step == CHUNKS)
        def _():
            spot = table.at[sibling]
            sending(spot, spot, near_send, near_recv, sibling).wait_recv()

        @pl.when((late >= 0) & (lax.rem(late, 2) == 0))
        def _():
            far_arrival(chunk).wait_recv()
            passing(chunk).start()

        @pl.when((late >= 0) & (lax.rem(late, 2) == 1))
        def _():
            pass_arrival(chunk).wait_recv()

        compute(slot, chunk)
        return 0

    lax.fori_loop(0, 4 * CHUNKS, body, 0)
    near.wait_send()
    for chunk in range(CHUNKS):
        far(chunk).wait_send()
        passing(chunk).wait_send()


GATHER_SEMS = [pltpu.SemaphoreType.DMA] * 2 + [pltpu.SemaphoreType.DMA((CHUNKS,))] * 4


def scatter_loop(buffers, sems, partial, finish):
    near_out, near_in, far_out, far_in = buffers
    near_send, near_recv, far_send, far_recv = sems
    me, sibling, across, diagonal = tp_places()
    rows = far_out.shape[0] // CHUNKS

    def span(chunk):
        return pl.ds(pl.multiple_of(chunk * rows, rows), rows)

    def near(half, chunk):
        return sending(
            near_out.at[half, span(chunk)],
            near_in.at[half, span(chunk)],
            near_send.at[half, chunk],
            near_recv.at[half, chunk],
            sibling,
        )

    def far(chunk):
        return sending(
            far_out.at[span(chunk)],
            far_in.at[span(chunk)],
            far_send.at[chunk],
            far_recv.at[chunk],
            across,
        )

    def body(step, _):
        phase, chunk = step // CHUNKS, lax.rem(step, CHUNKS)
        slot = jnp.where(
            phase == 0, diagonal, jnp.where(phase == 1, across, jnp.where(phase == 2, sibling, me))
        )
        value = partial(slot, chunk)
        spot = span(chunk)

        @pl.when(lax.rem(phase, 2) == 0)
        def _():
            half = phase // 2
            near_out[half, spot] = value.astype(BF16)
            near(half, chunk).start()

        @pl.when(phase == 1)
        def _():
            near(0, chunk).wait_recv()
            far_out[spot] = (value + near_in[0, spot].astype(F32)).astype(BF16)
            far(chunk).start()

        @pl.when(phase == 3)
        def _():
            near(1, chunk).wait_recv()
            far(chunk).wait_recv()
            finish(chunk, value + near_in[1, spot].astype(F32) + far_in[spot].astype(F32))

        return 0

    lax.fori_loop(0, 4 * CHUNKS, body, 0)
    for chunk in range(CHUNKS):
        near(0, chunk).wait_send()
        near(1, chunk).wait_send()
        far(chunk).wait_send()


SCATTER_SEMS = [pltpu.SemaphoreType.DMA((2, CHUNKS))] * 2 + [pltpu.SemaphoreType.DMA((CHUNKS,))] * 2


def scatter_buffers(rows, width):
    return [
        pltpu.VMEM((2, rows, width), BF16),
        pltpu.VMEM((2, rows, width), BF16),
        pltpu.VMEM((rows, width), BF16),
        pltpu.VMEM((rows, width), BF16),
    ]


def gather_two_kernel(first_ref, second_ref, first_all, second_all, near_send, near_recv, far_send, far_recv, pass_send, pass_recv, own_sem):
    me, sibling, across, diagonal = tp_places()
    greet((sibling, across))
    pairs = ((first_ref, first_all), (second_ref, second_all))
    rows = first_ref.shape[0] // CHUNKS
    started = []
    for n, (source, table) in enumerate(pairs):
        own = pltpu.make_async_copy(source, table.at[me], own_sem.at[n])
        own.start()
        started.append(own)
    fars, nears, passes = [], [], []
    for n, (source, table) in enumerate(pairs):
        for chunk in range(CHUNKS):
            spot = pl.ds(chunk * rows, rows)
            copy = sending(source.at[spot], table.at[me, spot], far_send.at[n, chunk], far_recv.at[n, chunk], across)
            copy.start()
            fars.append(copy)
        near = sending(source, table.at[me], near_send.at[n], near_recv.at[n], sibling)
        near.start()
        nears.append(near)
    for n, (source, table) in enumerate(pairs):
        for chunk in range(CHUNKS):
            spot = pl.ds(chunk * rows, rows)
            fars[n * CHUNKS + chunk].wait_recv()
            copy = sending(table.at[across, spot], table.at[across, spot], pass_send.at[n, chunk], pass_recv.at[n, chunk], sibling)
            copy.start()
            passes.append(copy)
    for copy in passes + nears:
        copy.wait()
    for copy in fars:
        copy.wait_send()
    for copy in started:
        copy.wait()


def gather_two(first, second, ident):
    rows, width = first.shape
    many = pltpu.SemaphoreType.DMA((2, CHUNKS))
    return pl.pallas_call(
        gather_two_kernel,
        out_shape=[jax.ShapeDtypeStruct((4, rows, width), BF16)] * 2,
        in_specs=[pl.BlockSpec(memory_space=pl.ANY)] * 2,
        out_specs=[pl.BlockSpec(memory_space=pl.ANY)] * 2,
        scratch_shapes=[pltpu.SemaphoreType.DMA((2,))] * 2 + [many] * 4 + [pltpu.SemaphoreType.DMA((2,))],
        compiler_params=pltpu.CompilerParams(collective_id=ident, has_side_effects=True),
        name="gather_rows",
    )(first, second)


def whole(shape, column=None):
    zeros = (0,) * (len(shape) - 1)
    return pl.BlockSpec(shape, lambda i: zeros + (column or 0,), pipeline_mode=pl.Buffered(1))


def remote_params(ident, megabytes):
    return pltpu.CompilerParams(
        collective_id=ident, has_side_effects=True, vmem_limit_bytes=megabytes << 20, dimension_semantics=("arbitrary",)
    )


def project_kernel(layout, x_ref, gain_ref, w_ref, normed_ref, forget_ref, *item_refs):
    seq_count, groups, width, places = layout
    x = x_ref[0].astype(F32)
    normed = (x * lax.rsqrt(jnp.mean(x * x, axis=1, keepdims=True) + epsilon) * gain_ref[...]).astype(BF16)
    normed_ref[0] = normed
    inner = groups * width
    rows = x.shape[0] // seq_count
    count = len(item_refs)
    for kind in range(3):
        value = dot(normed, w_ref[:, kind * inner : (kind + 1) * inner], NN).astype(BF16)
        for slot, (s, g) in enumerate(places):
            piece = value[s * rows : (s + 1) * rows, g * width : (g + 1) * width]
            item_refs[slot % count][slot // count, kind] = piece
    forget_ref[0] = dot(normed, w_ref[:, 3 * inner :], NN)


def project(x_all, gain, full_one, layout, item_count, ctx_size):
    seq_count, groups, width, places = layout
    tp_size, rows, model_width = x_all.shape
    local = rows // seq_count
    item = jax.ShapeDtypeStruct((ctx_size, 3, tp_size * local, width), BF16)
    columns = full_one.shape[1]
    block = pl.BlockSpec((1, rows, model_width), lambda t: (t, 0, 0))
    return pl.pallas_call(
        functools.partial(project_kernel, layout),
        grid=(tp_size,),
        out_shape=[
            jax.ShapeDtypeStruct(x_all.shape, BF16),
            jax.ShapeDtypeStruct((tp_size, rows, LANES), F32),
        ]
        + [item] * item_count,
        in_specs=[
            block,
            pl.BlockSpec((1, model_width), lambda t: (0, 0)),
            pl.BlockSpec((model_width, columns), lambda t: (0, 0), pipeline_mode=pl.Buffered(1)),
        ],
        out_specs=[block, pl.BlockSpec((1, rows, LANES), lambda t: (t, 0, 0))]
        + [pl.BlockSpec((ctx_size, 3, local, width), lambda t: (0, 0, t, 0))] * item_count,
        compiler_params=pltpu.CompilerParams(vmem_limit_bytes=48 << 20, dimension_semantics=("arbitrary",)),
        cost_estimate=pl.CostEstimate(
            flops=2 * x_all.size * columns, bytes_accessed=4 * x_all.size, transcendentals=0
        ),
        name="project",
    )(x_all, gain, full_one)


def out_kernel(layout, count, x_ref, gate_ref, w_ref, gain_ref, *refs):
    seq_count, groups, width, places = layout
    items, (hidden_ref, normed_ref, attended_ref, mixed_ref) = refs[:count], refs[count : count + 4]
    buffers, sems = refs[count + 4 : count + 8], refs[count + 8 :]
    me, sibling, across, diagonal = tp_places()
    greet((sibling, across))
    tp_size, rows, _ = gate_ref.shape
    local = rows // seq_count

    def mix(t, _):
        here = pl.ds(pl.multiple_of(t * local, local), local)
        for slot, (s, g) in enumerate(places[: seq_count * groups]):
            there = (t, pl.ds(s * local, local), pl.ds(g * width, width))
            value = items[slot % count][slot // count, here]
            attended_ref[there] = value
            mixed_ref[there] = (value.astype(F32) * gate_ref[there]).astype(BF16)
        return 0

    lax.fori_loop(0, tp_size, mix, 0)
    size = rows // CHUNKS

    def span(chunk):
        return pl.ds(pl.multiple_of(chunk * size, size), size)

    def partial(slot, chunk):
        return dot(mixed_ref[slot, span(chunk)], w_ref[...], NT)

    def finish(chunk, total):
        hidden = x_ref[span(chunk)].astype(F32) + total
        hidden_ref[span(chunk)] = hidden
        inverse = lax.rsqrt(jnp.mean(hidden * hidden, axis=1, keepdims=True) + epsilon)
        normed_ref[span(chunk)] = (hidden * inverse * gain_ref[...]).astype(BF16)

    scatter_loop(buffers, sems, partial, finish)


def out_project(x, gate, full_two, column, gain, items, layout, ident):
    seq_count, groups, width, places = layout
    rows, model_width = x.shape
    inner = groups * width
    tp_size = gate.shape[0]
    return pl.pallas_call(
        functools.partial(out_kernel, layout, len(items)),
        grid=(1,),
        out_shape=[
            jax.ShapeDtypeStruct(x.shape, F32),
            jax.ShapeDtypeStruct(x.shape, BF16),
            jax.ShapeDtypeStruct(gate.shape, BF16),
            jax.ShapeDtypeStruct(gate.shape, BF16),
        ],
        in_specs=[
            whole(x.shape),
            whole(gate.shape),
            whole((model_width, inner), column),
            whole(gain.shape),
        ]
        + [whole(item.shape) for item in items],
        out_specs=[whole(x.shape), whole(x.shape), whole(gate.shape), whole(gate.shape)],
        scratch_shapes=scatter_buffers(rows, model_width) + SCATTER_SEMS,
        compiler_params=remote_params(ident, 48),
        cost_estimate=pl.CostEstimate(
            flops=2 * gate.size * model_width, bytes_accessed=100 << 20, transcendentals=0
        ),
        name="out_project",
    )(x, gate, full_two, gain, *items)


def mlp_kernel(normed_ref, grad_ref, gate_w, up_w, down_w, all_ref, inner_ref, pair_ref, table, own_sem, *sems):
    me, sibling, across, diagonal = tp_places()
    greet((sibling, across))
    table[me] = normed_ref[...]
    rows, hidden = table.shape[1] // CHUNKS, gate_w.shape[1]
    tile = min(hidden, 512)

    def compute(slot, chunk):
        spot = pl.ds(pl.multiple_of(chunk * rows, rows), rows)
        normed, grad = table[slot, spot], grad_ref[slot, spot]
        for start in range(0, hidden, tile):
            columns = pl.ds(start, tile)
            gate = dot(normed, gate_w[:, columns], NN)
            up = dot(normed, up_w[:, columns], NN)
            back = dot(grad, down_w[:, columns], NN)
            sig = 1.0 / (1.0 + jnp.exp(-gate))
            silu = gate * sig
            inner_ref[slot, spot, columns] = (silu * up).astype(BF16)
            pair_ref[slot, spot, columns] = (back * up * sig * (1.0 + gate * (1.0 - sig))).astype(BF16)
            pair_ref[slot, spot, pl.ds(hidden + start, tile)] = (back * silu).astype(BF16)

    gather_loop(table, sems, compute)
    copy = pltpu.make_async_copy(table, all_ref, own_sem)
    copy.start()
    copy.wait()


def mlp(normed, grad_all, full_two, hidden, ident):
    tp_size, rows, model_width = grad_all.shape
    total = tp_size * rows
    return pl.pallas_call(
        mlp_kernel,
        grid=(1,),
        out_shape=[
            jax.ShapeDtypeStruct(grad_all.shape, BF16),
            jax.ShapeDtypeStruct((tp_size, rows, hidden), BF16),
            jax.ShapeDtypeStruct((tp_size, rows, 2 * hidden), BF16),
        ],
        in_specs=[whole(normed.shape), whole(grad_all.shape)]
        + [whole((model_width, hidden), column) for column in range(3)],
        out_specs=[
            pl.BlockSpec(memory_space=pl.ANY),
            whole((tp_size, rows, hidden)),
            whole((tp_size, rows, 2 * hidden)),
        ],
        scratch_shapes=[pltpu.VMEM(grad_all.shape, BF16), pltpu.SemaphoreType.DMA] + GATHER_SEMS,
        compiler_params=remote_params(ident, 56),
        cost_estimate=pl.CostEstimate(
            flops=6 * total * model_width * hidden, bytes_accessed=100 << 20, transcendentals=total * hidden
        ),
        name="mlp",
    )(normed, grad_all, full_two, full_two, full_two)


def mlp_back_kernel(pair_ref, w_ref, hidden_ref, grad_ref, gain_ref, out_ref, branch_ref, part_ref, *refs):
    buffers, sems = refs[:4], refs[4:]
    me, sibling, across, diagonal = tp_places()
    greet((sibling, across))
    part_ref[...] = jnp.zeros_like(part_ref)
    size = hidden_ref.shape[0] // CHUNKS

    def span(chunk):
        return pl.ds(pl.multiple_of(chunk * size, size), size)

    def partial(slot, chunk):
        return dot(pair_ref[slot, span(chunk)], w_ref[...], NT)

    def finish(chunk, total):
        hidden = hidden_ref[span(chunk)]
        inverse = lax.rsqrt(jnp.mean(hidden * hidden, axis=1, keepdims=True) + epsilon)
        unit = hidden * inverse
        part_ref[...] += jnp.sum(total * unit, axis=0, keepdims=True)
        scaled = total * gain_ref[...]
        middle = jnp.mean(scaled * unit, axis=1, keepdims=True)
        grad = grad_ref[span(chunk)].astype(F32) + inverse * (scaled - unit * middle)
        out_ref[span(chunk)] = grad
        branch_ref[span(chunk)] = grad.astype(BF16)

    scatter_loop(buffers, sems, partial, finish)


def mlp_back(pair, full_two, hidden_state, grad_out, gain, ident):
    tp_size, rows, wide = pair.shape
    model_width = hidden_state.shape[1]
    return pl.pallas_call(
        mlp_back_kernel,
        grid=(1,),
        out_shape=[
            jax.ShapeDtypeStruct(hidden_state.shape, F32),
            jax.ShapeDtypeStruct(hidden_state.shape, BF16),
            jax.ShapeDtypeStruct(gain.shape, F32),
        ],
        in_specs=[
            whole(pair.shape),
            whole((model_width, wide), 0),
            whole(hidden_state.shape),
            whole(grad_out.shape),
            whole(gain.shape),
        ],
        out_specs=[whole(hidden_state.shape), whole(hidden_state.shape), whole(gain.shape)],
        scratch_shapes=scatter_buffers(rows, model_width) + SCATTER_SEMS,
        compiler_params=remote_params(ident, 56),
        cost_estimate=pl.CostEstimate(
            flops=2 * pair.size * model_width, bytes_accessed=100 << 20, transcendentals=0
        ),
        name="mlp_back",
    )(pair, full_two, hidden_state, grad_out, gain)


def out_back_kernel(layout, count, branch_ref, w_ref, gate_ref, attended_ref, *refs):
    seq_count, groups, width, places = layout
    all_ref, logit_ref, items = refs[0], refs[1], refs[2 : 2 + count]
    table, grads, own_sem = refs[2 + count : 5 + count]
    sems = refs[5 + count :]
    me, sibling, across, diagonal = tp_places()
    greet((sibling, across))
    table[me] = branch_ref[...]
    tp_size, rows, _ = gate_ref.shape
    local, size = rows // seq_count, rows // CHUNKS

    def compute(slot, chunk):
        spot = pl.ds(pl.multiple_of(chunk * size, size), size)
        mixed = dot(table[slot, spot], w_ref[...], NN)
        gate = gate_ref[slot, spot]
        scaled = mixed * gate
        grads[slot, spot] = scaled.astype(BF16)
        attended = attended_ref[slot, spot].astype(F32)
        logit_ref[slot, spot] = (scaled * attended * (1.0 - gate)).astype(BF16)

    gather_loop(table, sems, compute)
    copy = pltpu.make_async_copy(table, all_ref, own_sem)
    copy.start()

    def deal(t, _):
        here = pl.ds(pl.multiple_of(t * local, local), local)
        for slot, (s, g) in enumerate(places):
            items[slot % count][slot // count, here] = grads[t, pl.ds(s * local, local), pl.ds(g * width, width)]
        return 0

    lax.fori_loop(0, tp_size, deal, 0)
    copy.wait()


def out_back(branch, full_two, column, gate, attended, layout, item_count, ctx_size, ident):
    seq_count, groups, width, places = layout
    rows, model_width = branch.shape
    tp_size, _, inner = gate.shape
    item = (ctx_size, tp_size * rows // seq_count, width)
    table = (tp_size, rows, model_width)
    return pl.pallas_call(
        functools.partial(out_back_kernel, layout, item_count),
        grid=(1,),
        out_shape=[jax.ShapeDtypeStruct(table, BF16), jax.ShapeDtypeStruct(gate.shape, BF16)]
        + [jax.ShapeDtypeStruct(item, BF16)] * item_count,
        in_specs=[
            whole(branch.shape),
            whole((model_width, inner), column),
            whole(gate.shape),
            whole(attended.shape),
        ],
        out_specs=[pl.BlockSpec(memory_space=pl.ANY), whole(gate.shape)] + [whole(item)] * item_count,
        scratch_shapes=[pltpu.VMEM(table, BF16), pltpu.VMEM(gate.shape, BF16), pltpu.SemaphoreType.DMA]
        + GATHER_SEMS,
        compiler_params=remote_params(ident, 48),
        cost_estimate=pl.CostEstimate(
            flops=2 * gate.size * model_width, bytes_accessed=100 << 20, transcendentals=0
        ),
        name="out_back",
    )(branch, full_two, gate, attended)


def assemble_kernel(layout, count, *refs):
    seq_count, groups, width, places = layout
    items, out_ref = refs[:count], refs[count]
    local = items[0].shape[2]
    inner = groups * width
    for slot, (s, g) in enumerate(places[: seq_count * groups]):
        for kind in range(3):
            columns = pl.ds(kind * inner + g * width, width)
            out_ref[0, pl.ds(s * local, local), columns] = items[slot % count][slot // count, kind]


def assemble(items, layout, tp_size):
    seq_count, groups, width, places = layout
    ctx_size, kinds, ctx_rows, _ = items[0].shape
    local = ctx_rows // tp_size
    shape = (tp_size, seq_count * local, kinds * groups * width)
    return pl.pallas_call(
        functools.partial(assemble_kernel, layout, len(items)),
        grid=(tp_size,),
        out_shape=jax.ShapeDtypeStruct(shape, BF16),
        in_specs=[pl.BlockSpec((ctx_size, kinds, local, width), lambda t: (0, 0, t, 0))] * len(items),
        out_specs=pl.BlockSpec((1,) + shape[1:], lambda t: (t, 0, 0)),
        compiler_params=pltpu.CompilerParams(vmem_limit_bytes=32 << 20, dimension_semantics=("arbitrary",)),
        cost_estimate=pl.CostEstimate(flops=0, bytes_accessed=16 << 20, transcendentals=0),
        name="assemble",
    )(*items)


def input_kernel(qkv_ref, logit_ref, forget_ref, qkv_w, forget_w, gate_w, x_ref, grad_ref, gain_ref, out_ref, part_ref, *refs):
    buffers, sems = refs[:4], refs[4:]
    me, sibling, across, diagonal = tp_places()
    greet((sibling, across))
    part_ref[...] = jnp.zeros_like(part_ref)
    size = x_ref.shape[0] // CHUNKS

    def span(chunk):
        return pl.ds(pl.multiple_of(chunk * size, size), size)

    def partial(slot, chunk):
        value = dot(qkv_ref[slot, span(chunk)], qkv_w[...], NT)
        value = value + dot(logit_ref[slot, span(chunk)], gate_w[...], NT)
        return value + dot(forget_ref[slot, span(chunk)], forget_w[...], NT)

    def finish(chunk, total):
        x = x_ref[span(chunk)].astype(F32)
        inverse = lax.rsqrt(jnp.mean(x * x, axis=1, keepdims=True) + epsilon)
        unit = x * inverse
        part_ref[...] += jnp.sum(total * unit, axis=0, keepdims=True)
        scaled = total * gain_ref[...]
        middle = jnp.mean(scaled * unit, axis=1, keepdims=True)
        out_ref[span(chunk)] = (grad_ref[span(chunk)] + inverse * (scaled - unit * middle)).astype(BF16)

    scatter_loop(buffers, sems, partial, finish)


def input_back(grad_qkv, grad_logit, grad_forget, full_one, full_two, column, x, grad_hidden, gain, ident):
    rows, model_width = x.shape
    wide, inner = grad_qkv.shape[2], grad_logit.shape[2]
    return pl.pallas_call(
        input_kernel,
        grid=(1,),
        out_shape=[jax.ShapeDtypeStruct(x.shape, BF16), jax.ShapeDtypeStruct(gain.shape, F32)],
        in_specs=[
            whole(grad_qkv.shape),
            whole(grad_logit.shape),
            whole(grad_forget.shape),
            whole((model_width, wide), 0),
            whole((model_width, LANES), wide // LANES),
            whole((model_width, inner), column),
            whole(x.shape),
            whole(x.shape),
            whole(gain.shape),
        ],
        out_specs=[whole(x.shape), whole(gain.shape)],
        scratch_shapes=scatter_buffers(rows, model_width) + SCATTER_SEMS,
        compiler_params=remote_params(ident, 56),
        cost_estimate=pl.CostEstimate(
            flops=8 * rows * model_width * (wide + inner + LANES), bytes_accessed=100 << 20, transcendentals=0
        ),
        name="input_back",
    )(grad_qkv, grad_logit, grad_forget, full_one, full_one, full_two, x, grad_hidden, gain)


def running_sum(values):
    length = values.shape[-1]
    cut = values.reshape(values.shape[:-1] + (length // LANES, LANES))
    lower = jnp.tril(jnp.ones((LANES, LANES), F32))
    inside = jnp.einsum("...bk,jk->...bj", cut, lower, precision=lax.Precision.HIGHEST)
    ahead = jnp.tril(jnp.ones((length // LANES, length // LANES), F32), -1)
    before = jnp.sum(jnp.sum(cut, axis=-1)[..., None, :] * ahead, axis=-1)
    return (inside + before[..., None]).reshape(values.shape)


def row_norm(values):
    inverse = lax.rsqrt(jnp.mean(values * values, axis=-1, keepdims=True) + epsilon)
    return (values * inverse, inverse)


def norm_back(grad_normed, unit_rows, inverse, gain_vec):
    scaled = grad_normed * gain_vec
    inner_mean = jnp.mean(scaled * unit_rows, axis=-1, keepdims=True)
    return inverse * (scaled - unit_rows * inner_mean)


def spread_rows(row_values):
    return lax.all_gather(row_values, "tp", axis=0, tiled=True)


def summed_rows(partial):
    total = lax.psum_scatter(partial.astype(BF16), "tp", scatter_dimension=0, tiled=True)
    return total.astype(F32)


def per_device(
    layer_input,
    lengths,
    attn_gain,
    w_query,
    w_key,
    w_value,
    w_forget,
    forget_bias,
    w_gate_out,
    w_out,
    mlp_gain,
    w_gate,
    w_up,
    w_down,
    cotangent,
):
    local_rows, seq_count, model_width = layer_input.shape
    head_count = forget_bias.shape[0]
    inner_width = w_query.shape[1]
    hidden = w_gate.shape[1]
    head_size = inner_width // head_count
    tp_size = lax.axis_size("tp")
    ctx_size = lax.axis_size("ctx")
    shard_count = lax.axis_size("fsdp") * ctx_size
    ctx_rows = local_rows * tp_size
    seq_len = ctx_rows * ctx_size
    all_rows = seq_count * ctx_rows
    ctx_index = lax.axis_index("ctx")
    tp_index = lax.axis_index("tp")
    shard_index = lax.axis_index("fsdp") * ctx_size + ctx_index

    pair = LANES // head_size
    groups = head_count // pair
    width = pair * head_size
    item_count = pl.cdiv(seq_count * groups, ctx_size)
    used = seq_count * groups

    def place(slot):
        slot = slot % used
        return (slot // groups + slot % groups) % seq_count, slot % groups

    places = tuple(place(slot) for slot in range(ctx_size * item_count))
    layout = (seq_count, groups, width, places)

    weights = ("fsdp", "ctx")
    packed_one = jnp.concatenate(
        [
            w_query,
            w_key,
            w_value,
            w_forget,
            attn_gain[:, None],
            mlp_gain[:, None],
            jnp.zeros((attn_gain.shape[0], LANES - head_count - 2), BF16),
        ],
        axis=1,
    )
    packed_two = jnp.concatenate([w_gate, w_up, w_down, w_out, w_gate_out], axis=1)
    full_one = lax.all_gather(packed_one, weights, axis=0, tiled=True)
    full_two = lax.all_gather(packed_two, weights, axis=0, tiled=True)
    edge = 3 * inner_width
    gains = full_one[:, edge + head_count : edge + head_count + 2].astype(F32).T
    gain_one, gain_two = gains[0:1], gains[1:2]
    down_w = full_two[:, 2 * hidden : 3 * hidden]
    out_column = 3 * hidden // inner_width
    gate_out_w = full_two[:, 3 * hidden + inner_width :]

    def by_sequence(rows):
        return rows.transpose(1, 0, 2).reshape(seq_count * local_rows, model_width)

    def by_position(rows):
        return rows.reshape(seq_count, local_rows, model_width).transpose(1, 0, 2)

    local_pos = (ctx_index * tp_size + tp_index) * local_rows + jnp.arange(
        local_rows, dtype=jnp.int32
    )
    valid_rows = (local_pos[None, :] < lengths[:, None]).astype(F32)
    valid_rows = valid_rows.reshape(seq_count * local_rows, 1)
    ctx_pos = ctx_index * ctx_rows + jnp.arange(ctx_rows, dtype=jnp.int32)
    ctx_pos = ctx_pos.reshape(tp_size, 1, local_rows)
    ctx_valid = (ctx_pos < lengths[None, :, None]).astype(F32)

    input_rows = by_sequence(layer_input)
    grad_out = (valid_rows * by_sequence(cotangent).astype(F32)).astype(BF16)
    input_all, grad_all = gather_two(input_rows, grad_out, 1)
    normed_one, forget_rows, *items = project(
        input_all, gain_one, full_one, layout, item_count, ctx_size
    )
    normed_flat = normed_one.reshape(all_rows, model_width)
    forget_logit = forget_rows.reshape(all_rows, LANES)[:, :head_count].T
    forget_logit = forget_logit + forget_bias.astype(F32)[:, None]
    forget_logit = forget_logit.reshape(head_count, tp_size, seq_count, local_rows)
    log_forget = (ctx_valid[None] * jax.nn.log_sigmoid(forget_logit)).astype(BF16)

    def forget_items(rows):
        cut = rows.reshape(groups, pair, tp_size, seq_count, local_rows)
        picked = jnp.stack([cut[g, :, :, s] for s, g in places])
        return picked.reshape(ctx_size, item_count, pair, ctx_rows)

    def exchange(items):
        return lax.all_to_all(items, "ctx", split_axis=0, concat_axis=0, tiled=True)

    decay_in = exchange(forget_items(log_forget)).transpose(1, 2, 0, 3)
    decay_sum = running_sum(decay_in.reshape(item_count, pair, seq_len).astype(F32))
    seq_ids = jnp.arange(seq_count, dtype=jnp.int32)
    saved, attended_items = [], []
    for m in range(item_count):
        qkv = exchange(items[m])
        slot = ctx_index * item_count + m
        own_seq, _ = place(slot)
        own_seq = jnp.where(slot < used, own_seq, seq_count)
        item_len = jnp.sum(jnp.where(seq_ids == own_seq, lengths, 0)).reshape(1)
        out, exact, lse = attend(item_len, qkv, decay_sum[m], head_size)
        saved.append((item_len, qkv, exact, lse))
        attended_items.append(exchange(out))
    gate_logit = dot(normed_flat, gate_out_w, NN)
    out_gate = jax.nn.sigmoid(gate_logit).reshape(tp_size, -1, inner_width)
    hidden_state, normed_two, attended, mixed = out_project(
        input_rows, out_gate, full_two, out_column, gain_two, attended_items, layout, 2
    )
    normed_two_all, inner_act, grad_pair = mlp(normed_two, grad_all, full_two, hidden, 3)
    normed_two_flat = normed_two_all.reshape(all_rows, model_width)
    inner_flat = inner_act.reshape(all_rows, hidden)
    grad_pair_flat = grad_pair.reshape(all_rows, 2 * hidden)
    grad_flat = grad_all.reshape(all_rows, model_width)
    grad_hidden, branch, mlp_gain_part = mlp_back(
        grad_pair, full_two, hidden_state, grad_out, gain_two, 4
    )
    feedforward = summed_rows(dot(inner_flat, down_w, NT))
    output = (valid_rows * (hidden_state + feedforward)).astype(BF16)

    def owned_sum(part):
        total = lax.psum_scatter(part, weights, scatter_dimension=0, tiled=True)
        return total.astype(F32)

    gate_up_sum = owned_sum(dot(normed_two_flat, grad_pair_flat, TN).astype(BF16))
    branch_all, grad_gate_logit, *grads = out_back(
        branch, full_two, out_column, out_gate, attended, layout, item_count, ctx_size, 5
    )
    branch_flat = branch_all.reshape(all_rows, model_width)
    logit_flat = grad_gate_logit.reshape(all_rows, inner_width)

    grad_items, decay_grads = [], []
    for m in range(item_count):
        item_len, qkv, exact, lse = saved[m]
        dqkv, row_sum, column_sum = attend_grad(
            item_len, qkv, exchange(grads[m]), exact, lse, decay_sum[m], head_size
        )
        grad_items.append(exchange(dqkv))
        decay_grads.append(row_sum - column_sum)
    down_out_part = jnp.concatenate(
        [
            dot(grad_flat, inner_flat, TN).astype(BF16),
            dot(branch_flat, mixed.reshape(all_rows, inner_width), TN).astype(BF16),
            dot(normed_flat, logit_flat, TN).astype(BF16),
        ],
        axis=1,
    )
    down_out_sum = owned_sum(down_out_part)

    decay_grad = jnp.stack(decay_grads)
    forget_grad = jnp.flip(running_sum(jnp.flip(decay_grad, -1)), -1).astype(BF16)
    forget_grad = forget_grad.reshape(item_count, pair, ctx_size, ctx_rows).transpose(2, 0, 1, 3)
    forget_back = exchange(forget_grad).reshape(
        ctx_size * item_count, pair, tp_size, local_rows
    )
    slots = {place(slot): slot for slot in range(used)}
    forget_back = jnp.stack(
        [
            jnp.stack([forget_back[slots[s, g]] for s in range(seq_count)], axis=2)
            for g in range(groups)
        ]
    ).reshape(head_count, tp_size, seq_count, local_rows)
    grad_forget_logit = forget_back.astype(F32) * ctx_valid[None] * jax.nn.sigmoid(-forget_logit)
    grad_forget_logit = grad_forget_logit.astype(BF16).reshape(head_count, all_rows)
    bias_part = jnp.sum(grad_forget_logit.astype(F32), axis=1)
    grad_forget_rows = jnp.pad(grad_forget_logit, ((0, LANES - head_count), (0, 0))).T
    grad_qkv = assemble(grad_items, layout, tp_size)
    grad_qkvf = jnp.concatenate([grad_qkv.reshape(all_rows, edge), grad_forget_rows], axis=1)
    qkv_sum = owned_sum(dot(normed_flat, grad_qkvf, TN).astype(BF16))
    input_grad, attn_gain_part = input_back(
        grad_qkv,
        grad_gate_logit,
        grad_forget_rows.reshape(tp_size, -1, LANES),
        full_one,
        full_two,
        out_column + 1,
        input_rows,
        grad_hidden,
        gain_one,
        6,
    )
    attn_gain_part = attn_gain_part[0]
    mlp_gain_part = mlp_gain_part[0]

    bias_full = lax.dynamic_update_slice(
        jnp.zeros((head_count * tp_size,), F32), bias_part, (tp_index * head_count,)
    )
    gain_one_sum, gain_two_sum, bias_sum = lax.psum(
        (attn_gain_part, mlp_gain_part, bias_full), ("fsdp", "ctx", "tp")
    )
    shard_rows = model_width // shard_count
    attn_gain_grad = lax.dynamic_slice_in_dim(gain_one_sum, shard_index * shard_rows, shard_rows, 0)
    mlp_gain_grad = lax.dynamic_slice_in_dim(gain_two_sum, shard_index * shard_rows, shard_rows, 0)
    forget_bias_grad = lax.dynamic_slice_in_dim(bias_sum, tp_index * head_count, head_count, 0)
    wide = inner_width
    return (
        by_position(output),
        by_position(input_grad),
        attn_gain_grad,
        qkv_sum[:, :wide],
        qkv_sum[:, wide : 2 * wide],
        qkv_sum[:, 2 * wide : 3 * wide],
        qkv_sum[:, 3 * wide : 3 * wide + head_count],
        forget_bias_grad,
        down_out_sum[:, hidden + wide :],
        down_out_sum[:, hidden : hidden + wide],
        mlp_gain_grad,
        gate_up_sum[:, :hidden],
        gate_up_sum[:, hidden:],
        down_out_sum[:, :hidden],
    )


def solution(mesh):
    rows = P(("ctx", "tp"), "fsdp", None)
    matrix = P(("fsdp", "ctx"), "tp")
    vector = P(("fsdp", "ctx"))
    return jax.shard_map(
        per_device,
        mesh=mesh,
        in_specs=(
            rows,
            P("fsdp"),
            vector,
            matrix,
            matrix,
            matrix,
            matrix,
            P("tp"),
            matrix,
            matrix,
            vector,
            matrix,
            matrix,
            matrix,
            rows,
        ),
        out_specs=(
            rows,
            rows,
            vector,
            matrix,
            matrix,
            matrix,
            matrix,
            P("tp"),
            matrix,
            matrix,
            vector,
            matrix,
            matrix,
            matrix,
        ),
        check_vma=False,
    )
```

```python
import functools

import jax
import jax.numpy as jnp
from jax import lax
from jax.experimental import pallas as pl
from jax.experimental.pallas import tpu as pltpu
from jax.sharding import PartitionSpec as P

F32 = jnp.float32
BF16 = jnp.bfloat16
LANES = 128
MESH = pl.DeviceIdType.MESH
epsilon = 1e-06
masked_score = -1e30
NT = (((1,), (1,)), ((), ()))
NN = (((1,), (0,)), ((), ()))
TN = (((0,), (0,)), ((), ()))


def dot(left, right, dims):
    return lax.dot_general(left, right, dims, preferred_element_type=F32)


def of_head(block, head, head_size, ones_at=None):
    lane = lax.broadcasted_iota(jnp.int32, block.shape, 1)
    out = jnp.where(lane // head_size == head, block, jnp.zeros_like(block))
    if ones_at is not None:
        out = jnp.where(lane == ones_at, jnp.ones_like(block), out)
    return out


def spare_lane(head, head_size):
    return ((head + 1) % 2) * head_size


def attend_item(qkv, decay, out, exact, lse, heads, head_size):
    count, _, block, width = qkv.shape
    scale = head_size**-0.5
    row = lax.broadcasted_iota(jnp.int32, (block, block), 0)
    column = lax.broadcasted_iota(jnp.int32, (block, block), 1)
    causal = column <= row

    def query_block(i, _):
        query = qkv[i, 0]
        lanes = pl.ds(pl.multiple_of(i * block, block), block)
        result = jnp.zeros((block, width), F32)
        for head in range(heads):
            query_head = of_head(query, head, head_size)

            def step(j, carry, masked):
                top, total, acc = carry
                keys = pl.ds(pl.multiple_of(j * block, block), block)
                score = dot(query_head, qkv[j, 1], NT) * scale
                score = score - decay[head : head + 1, keys]
                if masked:
                    score = jnp.where(causal, score, masked_score)
                new_top = jnp.maximum(top, jnp.max(score, axis=1, keepdims=True))
                prob = jnp.exp(score - new_top)
                shrink = jnp.exp(top - new_top)
                total = total * shrink + jnp.sum(prob, axis=1, keepdims=True)
                acc = acc * shrink + dot(prob.astype(BF16), qkv[j, 2], NN)
                return new_top, total, acc

            carry = (
                jnp.full((block, 1), masked_score, F32),
                jnp.zeros((block, 1), F32),
                jnp.zeros((block, width), F32),
            )
            carry = lax.fori_loop(0, i, lambda j, c: step(j, c, False), carry)
            top, total, acc = step(i, carry, True)
            lane = lax.broadcasted_iota(jnp.int32, acc.shape, 1)
            result = jnp.where(lane // head_size == head, acc / total, result)
            stat = jnp.broadcast_to(top + jnp.log(total), (block, LANES)).T
            lse[head : head + 1, lanes] = stat[0:1]
        exact[i] = result
        out[i] = result.astype(BF16)
        return 0

    lax.fori_loop(0, count, query_block, 0)


def attend_item_back(qkv, grads, exact, lse, decay, dqkv, change, dq_acc, delta, heads, head_size):
    count, _, block, width = qkv.shape
    scale = head_size**-0.5
    row = lax.broadcasted_iota(jnp.int32, (block, block), 0)
    column = lax.broadcasted_iota(jnp.int32, (block, block), 1)
    causal = row <= column
    dq_acc[...] = jnp.zeros_like(dq_acc)
    change[...] = jnp.zeros_like(change)

    def prepare(i, _):
        lanes = pl.ds(pl.multiple_of(i * block, block), block)
        product = grads[i].astype(F32) * exact[i]
        lane = lax.broadcasted_iota(jnp.int32, product.shape, 1)
        for head in range(heads):
            part = jnp.where(lane // head_size == head, product, 0.0)
            part = jnp.sum(part, axis=1, keepdims=True)
            delta[head : head + 1, lanes] = jnp.broadcast_to(part, (block, LANES)).T[0:1]
        return 0

    lax.fori_loop(0, count, prepare, 0)

    def key_block(j, _):
        keys = pl.ds(pl.multiple_of(j * block, block), block)
        key = qkv[j, 1]
        value = qkv[j, 2]
        value_total = jnp.zeros((block, width), F32)
        key_total = jnp.zeros((block, width), F32)
        for head in range(heads):
            spare = spare_lane(head, head_size)
            key_ones = of_head(key, head, head_size, spare)
            fall = jnp.broadcast_to(decay[head : head + 1, keys], (LANES, block)).T[:, 0:1]

            def step(i, carry, masked):
                value_acc, key_acc = carry
                lanes = pl.ds(pl.multiple_of(i * block, block), block)
                query = qkv[i, 0]
                grad = of_head(grads[i], head, head_size)
                score = dot(key, of_head(query, head, head_size), NT) * scale
                score = score - fall - lse[head : head + 1, lanes]
                if masked:
                    score = jnp.where(causal, score, masked_score)
                prob = jnp.exp(score)
                grad_prob = dot(value, grad, NT)
                grad_score = prob * (grad_prob - delta[head : head + 1, lanes])
                grad_score = grad_score.astype(BF16)
                value_acc = value_acc + dot(prob.astype(BF16), grad, NN)
                query_ones = of_head(query, head, head_size, spare)
                key_acc = key_acc + dot(grad_score, query_ones, NN)
                dq_acc[head, i] += dot(grad_score, key_ones, TN)
                return value_acc, key_acc

            zero = jnp.zeros((block, width), F32)
            carry = step(j, (zero, zero), True)
            carry = lax.fori_loop(j + 1, count, lambda i, c: step(i, c, False), carry)
            value_acc, key_acc = carry
            value_total = value_total + value_acc
            lane = lax.broadcasted_iota(jnp.int32, key_acc.shape, 1)
            key_total = jnp.where(lane // head_size == head, key_acc, key_total)
            change[head : head + 1, keys] -= key_acc.T[spare : spare + 1]
        dqkv[j, 1] = (key_total * scale).astype(BF16)
        dqkv[j, 2] = value_total.astype(BF16)
        return 0

    lax.fori_loop(0, count, key_block, 0)

    def finish(i, _):
        lanes = pl.ds(pl.multiple_of(i * block, block), block)
        total = jnp.zeros((block, width), F32)
        for head in range(heads):
            spare = spare_lane(head, head_size)
            part = dq_acc[head, i]
            lane = lax.broadcasted_iota(jnp.int32, part.shape, 1)
            total = jnp.where(lane // head_size == head, part, total)
            change[head : head + 1, lanes] += part.T[spare : spare + 1]
        dqkv[i, 0] = (total * scale).astype(BF16)
        return 0

    lax.fori_loop(0, count, finish, 0)


def triangle(upward):
    row = lax.broadcasted_iota(jnp.int32, (LANES, LANES), 0)
    column = lax.broadcasted_iota(jnp.int32, (LANES, LANES), 1)
    keep = (row <= column) if upward else (row >= column)
    return jnp.where(keep, 1.0, 0.0).astype(BF16)


def exact_product(values, matrix):
    high = values.astype(BF16)
    rest = values - high.astype(F32)
    middle = rest.astype(BF16)
    low = (rest - middle.astype(F32)).astype(BF16)
    return dot(high, matrix, NN) + dot(middle, matrix, NN) + dot(low, matrix, NN)


def ctx_sending(source, target, send_sem, recv_sem, peer):
    return pltpu.make_async_remote_copy(
        src_ref=source,
        dst_ref=target,
        send_sem=send_sem,
        recv_sem=recv_sem,
        device_id={"ctx": peer},
        device_id_type=MESH,
    )


def ctx_greet(size):
    me = lax.axis_index("ctx")
    barrier = pltpu.get_barrier_semaphore()
    for step in range(1, size):
        peer = lax.rem(me + step, size)
        pl.semaphore_signal(barrier, inc=1, device_id={"ctx": peer}, device_id_type=MESH)
    pl.semaphore_wait(barrier, size - 1)
    return me


class Exchange:
    def __init__(self, me, size, source, target, sems):
        self.me, self.size, self.source, self.target = me, size, source, target
        self.send_sem, self.recv_sem, self.own_sem = sems

    def own(self, item):
        return pltpu.make_async_copy(
            self.source.at[item, self.me], self.target.at[item, self.me], self.own_sem.at[item]
        )

    def copy(self, item, step):
        peer = lax.rem(self.me + step, self.size)
        return ctx_sending(
            self.source.at[item, peer],
            self.target.at[item, self.me],
            self.send_sem.at[item, step],
            self.recv_sem.at[item, step],
            peer,
        )

    def start(self, item):
        self.own(item).start()
        for step in range(1, self.size):
            self.copy(item, step).start()

    def arrive(self, item):
        self.own(item).wait()
        for step in range(1, self.size):
            self.copy(item, step).wait_recv()

    def drain(self, item):
        for step in range(1, self.size):
            self.copy(item, step).wait_send()


def exchange_sems(items, size):
    return [
        pltpu.SemaphoreType.DMA((items, size)),
        pltpu.SemaphoreType.DMA((items, size)),
        pltpu.SemaphoreType.DMA((items,)),
    ]


def context_kernel(
    heads, head_size, items_ref, forget_ref, back_ref, qkv_ref, exact_ref, lse_ref, decay_ref, *refs
):
    qkv, forget, out, save_sem = refs[:4]
    sems = refs[4:]
    count, size, _, block, width = items_ref.shape
    me = ctx_greet(size)
    forgets = Exchange(me, size, forget_ref, forget, sems[0:3])
    inputs = Exchange(me, size, items_ref, qkv, sems[3:6])
    results = Exchange(me, size, out, back_ref, sems[6:9])

    @pl.loop(0, count)
    def _(item):
        forgets.start(item)

    inputs.start(0)

    @pl.loop(0, count)
    def _(item):
        forgets.arrive(item)

    @pl.loop(0, count)
    def _(item):
        upper = triangle(True)
        before = jnp.zeros((8, 1), F32)
        for start in range(0, size * block, LANES):
            part = forget[item, start // block, :, pl.ds(start % block, LANES)]
            total = before + dot(part.astype(BF16), upper, NN)
            decay_ref[item, :, pl.ds(start, LANES)] = total
            before = total[:, LANES - 1 :]

    lse_ref[...] = jnp.zeros_like(lse_ref)

    @pl.loop(0, count)
    def _(item):
        @pl.when(item + 1 < count)
        def _():
            inputs.start(item + 1)

        inputs.arrive(item)
        saving = pltpu.make_async_copy(qkv.at[item], qkv_ref.at[item], save_sem)
        saving.start()
        attend_item(
            qkv.at[item], decay_ref.at[item], out.at[item], exact_ref.at[item], lse_ref.at[item], heads, head_size
        )
        results.start(item)
        saving.wait()

    @pl.loop(0, count)
    def _(item):
        forgets.drain(item)
        inputs.drain(item)
        results.arrive(item)
        results.drain(item)


def full_block(shape):
    return pl.BlockSpec(shape, lambda i: (0,) * len(shape), pipeline_mode=pl.Buffered(1))


def attend_cost(items, heads, products):
    count, size, _, block, width = items.shape
    pairs = count * heads * (size * block) ** 2 // 2
    return pl.CostEstimate(
        flops=2 * products * pairs * 256, bytes_accessed=100 << 20, transcendentals=pairs
    )


def context(items, forget, head_size, ident):
    count, size, _, block, width = items.shape
    heads = width // head_size
    place = pl.BlockSpec(memory_space=pl.ANY)
    exact, stat = (count, size, block, width), (count, 8, size * block)
    return pl.pallas_call(
        functools.partial(context_kernel, heads, head_size),
        grid=(1,),
        out_shape=[
            jax.ShapeDtypeStruct(exact, BF16),
            jax.ShapeDtypeStruct(items.shape, BF16),
            jax.ShapeDtypeStruct(exact, F32),
            jax.ShapeDtypeStruct(stat, F32),
            jax.ShapeDtypeStruct(stat, F32),
        ],
        in_specs=[place, place],
        out_specs=[place, place, full_block(exact), full_block(stat), full_block(stat)],
        scratch_shapes=[
            pltpu.VMEM(items.shape, BF16),
            pltpu.VMEM(forget.shape, F32),
            pltpu.VMEM(exact, BF16),
            pltpu.SemaphoreType.DMA,
        ]
        + exchange_sems(count, size) * 3,
        compiler_params=remote_params(ident, 48),
        cost_estimate=attend_cost(items, heads, 2),
        name="context",
    )(items, forget)


def context_back_kernel(
    heads, head_size, items_ref, qkv_ref, exact_ref, lse_ref, decay_ref, back_ref, forget_ref, *refs
):
    grads, dqkv, change, slope, dq_acc, delta = refs[:6]
    sems = refs[6:]
    count, size, block, width = items_ref.shape
    me = ctx_greet(size)
    inputs = Exchange(me, size, items_ref, grads, sems[0:3])
    results = Exchange(me, size, dqkv, back_ref, sems[3:6])
    forgets = Exchange(me, size, slope, forget_ref, sems[6:9])

    @pl.loop(0, count)
    def _(item):
        inputs.start(item)

    @pl.loop(0, count)
    def _(item):
        inputs.arrive(item)
        attend_item_back(
            qkv_ref.at[item],
            grads.at[item],
            exact_ref.at[item],
            lse_ref.at[item],
            decay_ref.at[item],
            dqkv.at[item],
            change,
            dq_acc,
            delta,
            heads,
            head_size,
        )
        results.start(item)
        lower = triangle(False)
        after = jnp.zeros((8, 1), F32)
        for start in reversed(range(0, size * block, LANES)):
            total = after + exact_product(change[:, pl.ds(start, LANES)], lower)
            slope[item, start // block, :, pl.ds(start % block, LANES)] = total
            after = total[:, 0:1]
        forgets.start(item)

    @pl.loop(0, count)
    def _(item):
        inputs.drain(item)
        results.arrive(item)
        results.drain(item)
        forgets.arrive(item)
        forgets.drain(item)


def context_back(grads, qkv, exact, lse, decay, head_size, ident):
    count, size, _, block, width = qkv.shape
    heads = width // head_size
    place = pl.BlockSpec(memory_space=pl.ANY)
    forget = (count, size, 8, block)
    return pl.pallas_call(
        functools.partial(context_back_kernel, heads, head_size),
        grid=(1,),
        out_shape=[
            jax.ShapeDtypeStruct(qkv.shape, BF16),
            jax.ShapeDtypeStruct(forget, F32),
        ],
        in_specs=[
            place,
            full_block(qkv.shape),
            full_block(exact.shape),
            full_block(lse.shape),
            full_block(decay.shape),
        ],
        out_specs=[place, place],
        scratch_shapes=[
            pltpu.VMEM(grads.shape, BF16),
            pltpu.VMEM(qkv.shape, BF16),
            pltpu.VMEM((8, size * block), F32),
            pltpu.VMEM(forget, F32),
            pltpu.VMEM((heads, size, block, width), F32),
            pltpu.VMEM((8, size * block), F32),
        ]
        + exchange_sems(count, size) * 3,
        compiler_params=remote_params(ident, 56),
        cost_estimate=attend_cost(qkv, heads, 5),
        name="context_back",
    )(grads, qkv, exact, lse, decay)


CHUNKS = 4


def tp_places():
    me = lax.axis_index("tp")
    sibling = me + 1 - 2 * lax.rem(me, 2)
    across = lax.rem(me + 2, 4)
    diagonal = lax.rem(sibling + 2, 4)
    return me, sibling, across, diagonal


def greet(peers):
    barrier = pltpu.get_barrier_semaphore()
    for peer in peers:
        pl.semaphore_signal(barrier, inc=1, device_id={"tp": peer}, device_id_type=MESH)
    pl.semaphore_wait(barrier, len(peers))


def sending(source, target, send_sem, recv_sem, peer):
    return pltpu.make_async_remote_copy(
        src_ref=source,
        dst_ref=target,
        send_sem=send_sem,
        recv_sem=recv_sem,
        device_id={"tp": peer},
        device_id_type=MESH,
    )


def pick(step, chunks, places):
    me, sibling, across, diagonal = places
    late = step - 2 * chunks
    far = jnp.where(lax.rem(late, 2) == 0, across, diagonal)
    slot = jnp.where(step < chunks, me, jnp.where(step < 2 * chunks, sibling, far))
    chunk = jnp.where(step < 2 * chunks, lax.rem(step, chunks), late // 2)
    return slot, chunk


def gather_loop(table, sems, compute, own=None, relative=False):
    near_send, near_recv, far_send, far_recv, pass_send, pass_recv = sems
    me, sibling, across, diagonal = tp_places()
    places = (0, 1, 2, 3) if relative else (me, sibling, across, diagonal)
    mine, near_by, far_off, corner = places
    near_spot, far_spot, pass_spot = (1, 2, 3) if relative else (me, me, across)
    rows = table.shape[1] // CHUNKS

    def part(slot, chunk):
        return table.at[slot, pl.ds(pl.multiple_of(chunk * rows, rows), rows)]

    def far(chunk):
        source = part(mine, chunk)
        if own is not None:
            source = own.at[pl.ds(pl.multiple_of(chunk * rows, rows), rows)]
        return sending(source, part(far_spot, chunk), far_send.at[chunk], far_recv.at[chunk], across)

    def far_arrival(chunk):
        spot = part(far_off, chunk)
        return sending(spot, spot, far_send.at[chunk], far_recv.at[chunk], across)

    def passing(chunk):
        return sending(
            part(far_off, chunk), part(pass_spot, chunk), pass_send.at[chunk], pass_recv.at[chunk], sibling
        )

    def pass_arrival(chunk):
        spot = part(corner, chunk)
        return sending(spot, spot, pass_send.at[chunk], pass_recv.at[chunk], sibling)

    for chunk in range(CHUNKS):
        far(chunk).start()
    own = table.at[mine] if own is None else own
    near = sending(own, table.at[near_spot], near_send, near_recv, sibling)
    near.start()

    def body(step, _):
        slot, chunk = pick(step, CHUNKS, places)
        late = step - 2 * CHUNKS

        @pl.when(step == CHUNKS)
        def _():
            spot = table.at[near_by]
            sending(spot, spot, near_send, near_recv, sibling).wait_recv()

        @pl.when((late >= 0) & (lax.rem(late, 2) == 0))
        def _():
            far_arrival(chunk).wait_recv()
            passing(chunk).start()

        @pl.when((late >= 0) & (lax.rem(late, 2) == 1))
        def _():
            pass_arrival(chunk).wait_recv()

        compute(slot, chunk)
        return 0

    lax.fori_loop(0, 4 * CHUNKS, body, 0)
    near.wait_send()
    for chunk in range(CHUNKS):
        far(chunk).wait_send()
        passing(chunk).wait_send()


GATHER_SEMS = [pltpu.SemaphoreType.DMA] * 2 + [pltpu.SemaphoreType.DMA((CHUNKS,))] * 4


def scatter_loop(buffers, sems, partial, finish, relative=False):
    near_out, near_in, far_out, far_in = buffers
    near_send, near_recv, far_send, far_recv = sems
    me, sibling, across, diagonal = tp_places()
    mine, near_by, far_off, corner = (0, 1, 2, 3) if relative else (me, sibling, across, diagonal)
    rows = far_out.shape[0] // CHUNKS

    def span(chunk):
        return pl.ds(pl.multiple_of(chunk * rows, rows), rows)

    def near(half, chunk):
        return sending(
            near_out.at[half, span(chunk)],
            near_in.at[half, span(chunk)],
            near_send.at[half, chunk],
            near_recv.at[half, chunk],
            sibling,
        )

    def far(chunk):
        return sending(
            far_out.at[span(chunk)],
            far_in.at[span(chunk)],
            far_send.at[chunk],
            far_recv.at[chunk],
            across,
        )

    def body(step, _):
        phase, chunk = step // CHUNKS, lax.rem(step, CHUNKS)
        slot = jnp.where(
            phase == 0, corner, jnp.where(phase == 1, far_off, jnp.where(phase == 2, near_by, mine))
        )
        value = partial(slot, chunk)
        spot = span(chunk)

        @pl.when(lax.rem(phase, 2) == 0)
        def _():
            half = phase // 2
            near_out[half, spot] = value.astype(BF16)
            near(half, chunk).start()

        @pl.when(phase == 1)
        def _():
            near(0, chunk).wait_recv()
            far_out[spot] = (value + near_in[0, spot].astype(F32)).astype(BF16)
            far(chunk).start()

        @pl.when(phase == 3)
        def _():
            near(1, chunk).wait_recv()
            far(chunk).wait_recv()
            finish(chunk, value + near_in[1, spot].astype(F32) + far_in[spot].astype(F32))

        return 0

    lax.fori_loop(0, 4 * CHUNKS, body, 0)
    for chunk in range(CHUNKS):
        near(0, chunk).wait_send()
        near(1, chunk).wait_send()
        far(chunk).wait_send()


SCATTER_SEMS = [pltpu.SemaphoreType.DMA((2, CHUNKS))] * 2 + [pltpu.SemaphoreType.DMA((CHUNKS,))] * 2


def scatter_buffers(rows, width):
    return [
        pltpu.VMEM((2, rows, width), BF16),
        pltpu.VMEM((2, rows, width), BF16),
        pltpu.VMEM((rows, width), BF16),
        pltpu.VMEM((rows, width), BF16),
    ]


def gather_rows_kernel(rows_ref, all_ref, own_sem, *sems):
    me, sibling, across, diagonal = tp_places()
    greet((sibling, across))
    own = pltpu.make_async_copy(rows_ref, all_ref.at[me], own_sem)
    own.start()
    gather_loop(all_ref, sems, lambda slot, chunk: None, rows_ref)
    own.wait()


def gather_rows(rows, ident):
    return pl.pallas_call(
        gather_rows_kernel,
        out_shape=jax.ShapeDtypeStruct((4,) + rows.shape, BF16),
        in_specs=[pl.BlockSpec(memory_space=pl.ANY)],
        out_specs=pl.BlockSpec(memory_space=pl.ANY),
        scratch_shapes=[pltpu.SemaphoreType.DMA] + GATHER_SEMS,
        compiler_params=pltpu.CompilerParams(collective_id=ident, has_side_effects=True),
        name="gather_rows",
    )(rows)


def whole(shape, column=None):
    zeros = (0,) * (len(shape) - 1)
    return pl.BlockSpec(shape, lambda i: zeros + (column or 0,), pipeline_mode=pl.Buffered(1))


def remote_params(ident, megabytes):
    return pltpu.CompilerParams(
        collective_id=ident, has_side_effects=True, vmem_limit_bytes=megabytes << 20, dimension_semantics=("arbitrary",)
    )


def project_kernel(layout, x_ref, gain_ref, w_ref, normed_ref, forget_ref, items_ref):
    seq_count, groups, width, places = layout
    x = x_ref[0].astype(F32)
    normed = (x * lax.rsqrt(jnp.mean(x * x, axis=1, keepdims=True) + epsilon) * gain_ref[...]).astype(BF16)
    normed_ref[0] = normed
    inner = groups * width
    rows = x.shape[0] // seq_count
    count = items_ref.shape[0]
    for kind in range(3):
        value = dot(normed, w_ref[:, kind * inner : (kind + 1) * inner], NN).astype(BF16)
        for slot, (s, g) in enumerate(places):
            piece = value[s * rows : (s + 1) * rows, g * width : (g + 1) * width]
            items_ref[slot % count, slot // count, kind] = piece
    forget_ref[0] = dot(normed, w_ref[:, 3 * inner :], NN)


def project(x_all, gain, full_one, layout, item_count, ctx_size):
    seq_count, groups, width, places = layout
    tp_size, rows, model_width = x_all.shape
    local = rows // seq_count
    item = jax.ShapeDtypeStruct((item_count, ctx_size, 3, tp_size * local, width), BF16)
    columns = full_one.shape[1]
    block = pl.BlockSpec((1, rows, model_width), lambda t: (t, 0, 0))
    return pl.pallas_call(
        functools.partial(project_kernel, layout),
        grid=(tp_size,),
        out_shape=[
            jax.ShapeDtypeStruct(x_all.shape, BF16),
            jax.ShapeDtypeStruct((tp_size, rows, LANES), F32),
            item,
        ],
        in_specs=[
            block,
            pl.BlockSpec((1, model_width), lambda t: (0, 0)),
            pl.BlockSpec((model_width, columns), lambda t: (0, 0), pipeline_mode=pl.Buffered(1)),
        ],
        out_specs=[
            block,
            pl.BlockSpec((1, rows, LANES), lambda t: (t, 0, 0)),
            pl.BlockSpec((item_count, ctx_size, 3, local, width), lambda t: (0, 0, 0, t, 0)),
        ],
        compiler_params=pltpu.CompilerParams(vmem_limit_bytes=48 << 20, dimension_semantics=("arbitrary",)),
        cost_estimate=pl.CostEstimate(
            flops=2 * x_all.size * columns, bytes_accessed=4 * x_all.size, transcendentals=0
        ),
        name="project",
    )(x_all, gain, full_one)


def out_kernel(layout, x_ref, gate_ref, w_ref, gain_ref, items, *refs):
    seq_count, groups, width, places = layout
    hidden_ref, normed_ref, attended_ref, mixed_ref = refs[:4]
    buffers, sems = refs[4:8], refs[8:]
    count = items.shape[0]
    me, sibling, across, diagonal = tp_places()
    greet((sibling, across))
    tp_size, rows, _ = gate_ref.shape
    local = rows // seq_count

    def mix(t, _):
        here = pl.ds(pl.multiple_of(t * local, local), local)
        for slot, (s, g) in enumerate(places[: seq_count * groups]):
            there = (t, pl.ds(s * local, local), pl.ds(g * width, width))
            value = items[slot % count, slot // count, here]
            attended_ref[there] = value
            mixed_ref[there] = (value.astype(F32) * gate_ref[there]).astype(BF16)
        return 0

    lax.fori_loop(0, tp_size, mix, 0)
    size = rows // CHUNKS

    def span(chunk):
        return pl.ds(pl.multiple_of(chunk * size, size), size)

    def partial(slot, chunk):
        return dot(mixed_ref[slot, span(chunk)], w_ref[...], NT)

    def finish(chunk, total):
        hidden = x_ref[span(chunk)].astype(F32) + total
        hidden_ref[span(chunk)] = hidden
        inverse = lax.rsqrt(jnp.mean(hidden * hidden, axis=1, keepdims=True) + epsilon)
        normed_ref[span(chunk)] = (hidden * inverse * gain_ref[...]).astype(BF16)

    scatter_loop(buffers, sems, partial, finish)


def out_project(x, gate, full_two, column, gain, items, layout, ident):
    seq_count, groups, width, places = layout
    rows, model_width = x.shape
    inner = groups * width
    tp_size = gate.shape[0]
    return pl.pallas_call(
        functools.partial(out_kernel, layout),
        grid=(1,),
        out_shape=[
            jax.ShapeDtypeStruct(x.shape, F32),
            jax.ShapeDtypeStruct(x.shape, BF16),
            jax.ShapeDtypeStruct(gate.shape, BF16),
            jax.ShapeDtypeStruct(gate.shape, BF16),
        ],
        in_specs=[
            whole(x.shape),
            whole(gate.shape),
            whole((model_width, inner), column),
            whole(gain.shape),
            whole(items.shape),
        ],
        out_specs=[whole(x.shape), whole(x.shape), whole(gate.shape), whole(gate.shape)],
        scratch_shapes=scatter_buffers(rows, model_width) + SCATTER_SEMS,
        compiler_params=remote_params(ident, 48),
        cost_estimate=pl.CostEstimate(
            flops=2 * gate.size * model_width, bytes_accessed=100 << 20, transcendentals=0
        ),
        name="out_project",
    )(x, gate, full_two, gain, items)


def mlp_kernel(normed_ref, grad_ref, gate_w, up_w, down_w, all_ref, inner_ref, pair_ref, table, own_sem, *sems):
    me, sibling, across, diagonal = tp_places()
    greet((sibling, across))
    table[0] = normed_ref[...]
    rows, hidden = table.shape[1] // CHUNKS, gate_w.shape[1]
    tile = min(hidden, 512)

    def compute(slot, chunk):
        spot = pl.ds(pl.multiple_of(chunk * rows, rows), rows)
        normed, grad = table[slot, spot], grad_ref[slot, spot]
        for start in range(0, hidden, tile):
            columns = pl.ds(start, tile)
            gate = dot(normed, gate_w[:, columns], NN)
            up = dot(normed, up_w[:, columns], NN)
            back = dot(grad, down_w[:, columns], NN)
            sig = 1.0 / (1.0 + jnp.exp(-gate))
            silu = gate * sig
            inner_ref[slot, spot, columns] = (silu * up).astype(BF16)
            pair_ref[slot, spot, columns] = (back * up * sig * (1.0 + gate * (1.0 - sig))).astype(BF16)
            pair_ref[slot, spot, pl.ds(hidden + start, tile)] = (back * silu).astype(BF16)

    gather_loop(table, sems, compute, relative=True)
    copy = pltpu.make_async_copy(table, all_ref, own_sem)
    copy.start()
    copy.wait()


def mlp(normed, grad_all, full_two, hidden, ident):
    tp_size, rows, model_width = grad_all.shape
    total = tp_size * rows
    return pl.pallas_call(
        mlp_kernel,
        grid=(1,),
        out_shape=[
            jax.ShapeDtypeStruct(grad_all.shape, BF16),
            jax.ShapeDtypeStruct((tp_size, rows, hidden), BF16),
            jax.ShapeDtypeStruct((tp_size, rows, 2 * hidden), BF16),
        ],
        in_specs=[whole(normed.shape), whole(grad_all.shape)]
        + [whole((model_width, hidden), column) for column in range(3)],
        out_specs=[
            pl.BlockSpec(memory_space=pl.ANY),
            whole((tp_size, rows, hidden)),
            whole((tp_size, rows, 2 * hidden)),
        ],
        scratch_shapes=[pltpu.VMEM(grad_all.shape, BF16), pltpu.SemaphoreType.DMA] + GATHER_SEMS,
        compiler_params=remote_params(ident, 56),
        cost_estimate=pl.CostEstimate(
            flops=6 * total * model_width * hidden, bytes_accessed=100 << 20, transcendentals=total * hidden
        ),
        name="mlp",
    )(normed, grad_all, full_two, full_two, full_two)


def mlp_back_kernel(pair_ref, w_ref, hidden_ref, grad_ref, gain_ref, out_ref, branch_ref, part_ref, *refs):
    buffers, sems = refs[:4], refs[4:]
    me, sibling, across, diagonal = tp_places()
    greet((sibling, across))
    part_ref[...] = jnp.zeros_like(part_ref)
    size = hidden_ref.shape[0] // CHUNKS

    def span(chunk):
        return pl.ds(pl.multiple_of(chunk * size, size), size)

    def partial(slot, chunk):
        return dot(pair_ref[slot, span(chunk)], w_ref[...], NT)

    def finish(chunk, total):
        hidden = hidden_ref[span(chunk)]
        inverse = lax.rsqrt(jnp.mean(hidden * hidden, axis=1, keepdims=True) + epsilon)
        unit = hidden * inverse
        part_ref[...] += jnp.sum(total * unit, axis=0, keepdims=True)
        scaled = total * gain_ref[...]
        middle = jnp.mean(scaled * unit, axis=1, keepdims=True)
        grad = grad_ref[span(chunk)].astype(F32) + inverse * (scaled - unit * middle)
        out_ref[span(chunk)] = grad
        branch_ref[span(chunk)] = grad.astype(BF16)

    scatter_loop(buffers, sems, partial, finish, relative=True)


def mlp_back(pair, full_two, hidden_state, grad_out, gain, ident):
    tp_size, rows, wide = pair.shape
    model_width = hidden_state.shape[1]
    return pl.pallas_call(
        mlp_back_kernel,
        grid=(1,),
        out_shape=[
            jax.ShapeDtypeStruct(hidden_state.shape, F32),
            jax.ShapeDtypeStruct(hidden_state.shape, BF16),
            jax.ShapeDtypeStruct(gain.shape, F32),
        ],
        in_specs=[
            whole(pair.shape),
            whole((model_width, wide), 0),
            whole(hidden_state.shape),
            whole(grad_out.shape),
            whole(gain.shape),
        ],
        out_specs=[whole(hidden_state.shape), whole(hidden_state.shape), whole(gain.shape)],
        scratch_shapes=scatter_buffers(rows, model_width) + SCATTER_SEMS,
        compiler_params=remote_params(ident, 56),
        cost_estimate=pl.CostEstimate(
            flops=2 * pair.size * model_width, bytes_accessed=100 << 20, transcendentals=0
        ),
        name="mlp_back",
    )(pair, full_two, hidden_state, grad_out, gain)


def out_back_kernel(layout, branch_ref, w_ref, gate_ref, attended_ref, *refs):
    seq_count, groups, width, places = layout
    all_ref, logit_ref, items, table, grads, own_sem = refs[:6]
    sems = refs[6:]
    count = items.shape[0]
    me, sibling, across, diagonal = tp_places()
    greet((sibling, across))
    table[me] = branch_ref[...]
    tp_size, rows, _ = gate_ref.shape
    local, size = rows // seq_count, rows // CHUNKS

    def compute(slot, chunk):
        spot = pl.ds(pl.multiple_of(chunk * size, size), size)
        mixed = dot(table[slot, spot], w_ref[...], NN)
        gate = gate_ref[slot, spot]
        scaled = mixed * gate
        grads[slot, spot] = scaled.astype(BF16)
        attended = attended_ref[slot, spot].astype(F32)
        logit_ref[slot, spot] = (scaled * attended * (1.0 - gate)).astype(BF16)

    gather_loop(table, sems, compute)
    copy = pltpu.make_async_copy(table, all_ref, own_sem)
    copy.start()

    def deal(t, _):
        here = pl.ds(pl.multiple_of(t * local, local), local)
        for slot, (s, g) in enumerate(places):
            piece = grads[t, pl.ds(s * local, local), pl.ds(g * width, width)]
            items[slot % count, slot // count, here] = piece
        return 0

    lax.fori_loop(0, tp_size, deal, 0)
    copy.wait()


def out_back(branch, full_two, column, gate, attended, layout, item_count, ctx_size, ident):
    seq_count, groups, width, places = layout
    rows, model_width = branch.shape
    tp_size, _, inner = gate.shape
    item = (item_count, ctx_size, tp_size * rows // seq_count, width)
    table = (tp_size, rows, model_width)
    return pl.pallas_call(
        functools.partial(out_back_kernel, layout),
        grid=(1,),
        out_shape=[
            jax.ShapeDtypeStruct(table, BF16),
            jax.ShapeDtypeStruct(gate.shape, BF16),
            jax.ShapeDtypeStruct(item, BF16),
        ],
        in_specs=[
            whole(branch.shape),
            whole((model_width, inner), column),
            whole(gate.shape),
            whole(attended.shape),
        ],
        out_specs=[pl.BlockSpec(memory_space=pl.ANY), whole(gate.shape), whole(item)],
        scratch_shapes=[pltpu.VMEM(table, BF16), pltpu.VMEM(gate.shape, BF16), pltpu.SemaphoreType.DMA]
        + GATHER_SEMS,
        compiler_params=remote_params(ident, 48),
        cost_estimate=pl.CostEstimate(
            flops=2 * gate.size * model_width, bytes_accessed=100 << 20, transcendentals=0
        ),
        name="out_back",
    )(branch, full_two, gate, attended)


def assemble_kernel(layout, items, out_ref):
    seq_count, groups, width, places = layout
    count, local = items.shape[0], items.shape[3]
    inner = groups * width
    for slot, (s, g) in enumerate(places[: seq_count * groups]):
        for kind in range(3):
            columns = pl.ds(kind * inner + g * width, width)
            out_ref[0, pl.ds(s * local, local), columns] = items[slot % count, slot // count, kind]


def assemble(items, layout, tp_size):
    seq_count, groups, width, places = layout
    count, ctx_size, kinds, ctx_rows, _ = items.shape
    local = ctx_rows // tp_size
    shape = (tp_size, seq_count * local, kinds * groups * width)
    return pl.pallas_call(
        functools.partial(assemble_kernel, layout),
        grid=(tp_size,),
        out_shape=jax.ShapeDtypeStruct(shape, BF16),
        in_specs=[pl.BlockSpec((count, ctx_size, kinds, local, width), lambda t: (0, 0, 0, t, 0))],
        out_specs=pl.BlockSpec((1,) + shape[1:], lambda t: (t, 0, 0)),
        compiler_params=pltpu.CompilerParams(vmem_limit_bytes=32 << 20, dimension_semantics=("arbitrary",)),
        cost_estimate=pl.CostEstimate(flops=0, bytes_accessed=16 << 20, transcendentals=0),
        name="assemble",
    )(items)


def input_kernel(qkv_ref, logit_ref, forget_ref, qkv_w, forget_w, gate_w, x_ref, grad_ref, gain_ref, out_ref, part_ref, *refs):
    buffers, sems = refs[:4], refs[4:]
    me, sibling, across, diagonal = tp_places()
    greet((sibling, across))
    part_ref[...] = jnp.zeros_like(part_ref)
    size = x_ref.shape[0] // CHUNKS

    def span(chunk):
        return pl.ds(pl.multiple_of(chunk * size, size), size)

    def partial(slot, chunk):
        value = dot(qkv_ref[slot, span(chunk)], qkv_w[...], NT)
        value = value + dot(logit_ref[slot, span(chunk)], gate_w[...], NT)
        return value + dot(forget_ref[slot, span(chunk)], forget_w[...], NT)

    def finish(chunk, total):
        x = x_ref[span(chunk)].astype(F32)
        inverse = lax.rsqrt(jnp.mean(x * x, axis=1, keepdims=True) + epsilon)
        unit = x * inverse
        part_ref[...] += jnp.sum(total * unit, axis=0, keepdims=True)
        scaled = total * gain_ref[...]
        middle = jnp.mean(scaled * unit, axis=1, keepdims=True)
        out_ref[span(chunk)] = (grad_ref[span(chunk)] + inverse * (scaled - unit * middle)).astype(BF16)

    scatter_loop(buffers, sems, partial, finish)


def input_back(grad_qkv, grad_logit, grad_forget, full_one, full_two, column, x, grad_hidden, gain, ident):
    rows, model_width = x.shape
    wide, inner = grad_qkv.shape[2], grad_logit.shape[2]
    return pl.pallas_call(
        input_kernel,
        grid=(1,),
        out_shape=[jax.ShapeDtypeStruct(x.shape, BF16), jax.ShapeDtypeStruct(gain.shape, F32)],
        in_specs=[
            whole(grad_qkv.shape),
            whole(grad_logit.shape),
            whole(grad_forget.shape),
            whole((model_width, wide), 0),
            whole((model_width, LANES), wide // LANES),
            whole((model_width, inner), column),
            whole(x.shape),
            whole(x.shape),
            whole(gain.shape),
        ],
        out_specs=[whole(x.shape), whole(gain.shape)],
        scratch_shapes=scatter_buffers(rows, model_width) + SCATTER_SEMS,
        compiler_params=remote_params(ident, 56),
        cost_estimate=pl.CostEstimate(
            flops=8 * rows * model_width * (wide + inner + LANES), bytes_accessed=100 << 20, transcendentals=0
        ),
        name="input_back",
    )(grad_qkv, grad_logit, grad_forget, full_one, full_one, full_two, x, grad_hidden, gain)


def to_sibling(values):
    return lax.ppermute(values, "tp", [(i, i + 1 - 2 * (i % 2)) for i in range(4)])


def to_across(values):
    return lax.ppermute(values, "tp", [(i, (i + 2) % 4) for i in range(4)])


def relative_rows(rows):
    far = to_across(rows)
    return jnp.stack([rows, to_sibling(rows), far, to_sibling(far)])


def summed_rows(partial):
    own, near, far, corner = (partial[n] for n in range(4))
    corner = to_sibling(corner.astype(BF16)).astype(F32)
    near = to_sibling(near.astype(BF16)).astype(F32)
    far = to_across((far + corner).astype(BF16)).astype(F32)
    return own + near + far


def per_device(
    layer_input,
    lengths,
    attn_gain,
    w_query,
    w_key,
    w_value,
    w_forget,
    forget_bias,
    w_gate_out,
    w_out,
    mlp_gain,
    w_gate,
    w_up,
    w_down,
    cotangent,
):
    local_rows, seq_count, model_width = layer_input.shape
    head_count = forget_bias.shape[0]
    inner_width = w_query.shape[1]
    hidden = w_gate.shape[1]
    head_size = inner_width // head_count
    tp_size = lax.axis_size("tp")
    ctx_size = lax.axis_size("ctx")
    shard_count = lax.axis_size("fsdp") * ctx_size
    ctx_rows = local_rows * tp_size
    seq_len = ctx_rows * ctx_size
    all_rows = seq_count * ctx_rows
    ctx_index = lax.axis_index("ctx")
    tp_index = lax.axis_index("tp")
    shard_index = lax.axis_index("fsdp") * ctx_size + ctx_index

    pair = LANES // head_size
    groups = head_count // pair
    width = pair * head_size
    item_count = pl.cdiv(seq_count * groups, ctx_size)
    used = seq_count * groups

    def place(slot):
        slot = slot % used
        return (slot // groups + slot % groups) % seq_count, slot % groups

    places = tuple(place(slot) for slot in range(ctx_size * item_count))
    layout = (seq_count, groups, width, places)

    weights = ("fsdp", "ctx")
    packed_one = jnp.concatenate(
        [
            w_query,
            w_key,
            w_value,
            w_forget,
            attn_gain[:, None],
            mlp_gain[:, None],
            jnp.zeros((attn_gain.shape[0], LANES - head_count - 2), BF16),
        ],
        axis=1,
    )
    packed_two = jnp.concatenate([w_gate, w_up, w_down, w_out, w_gate_out], axis=1)
    full_one = lax.all_gather(packed_one, weights, axis=0, tiled=True)
    full_two = lax.all_gather(packed_two, weights, axis=0, tiled=True)
    edge = 3 * inner_width
    gains = full_one[:, edge + head_count : edge + head_count + 2].astype(F32).T
    gain_one, gain_two = gains[0:1], gains[1:2]
    down_w = full_two[:, 2 * hidden : 3 * hidden]
    out_column = 3 * hidden // inner_width
    gate_out_w = full_two[:, 3 * hidden + inner_width :]

    def by_sequence(rows):
        return rows.transpose(1, 0, 2).reshape(seq_count * local_rows, model_width)

    def by_position(rows):
        return rows.reshape(seq_count, local_rows, model_width).transpose(1, 0, 2)

    local_pos = (ctx_index * tp_size + tp_index) * local_rows + jnp.arange(
        local_rows, dtype=jnp.int32
    )
    valid_rows = (local_pos[None, :] < lengths[:, None]).astype(F32)
    valid_rows = valid_rows.reshape(seq_count * local_rows, 1)
    ctx_pos = ctx_index * ctx_rows + jnp.arange(ctx_rows, dtype=jnp.int32)
    ctx_pos = ctx_pos.reshape(tp_size, 1, local_rows)
    ctx_valid = (ctx_pos < lengths[None, :, None]).astype(F32)

    input_rows = by_sequence(layer_input)
    grad_out = (valid_rows * by_sequence(cotangent).astype(F32)).astype(BF16)
    input_all = gather_rows(input_rows, 1)
    normed_one, forget_rows, items = project(
        input_all, gain_one, full_one, layout, item_count, ctx_size
    )
    normed_flat = normed_one.reshape(all_rows, model_width)
    forget_logit = forget_rows.reshape(all_rows, LANES)[:, :head_count].T
    forget_logit = forget_logit + forget_bias.astype(F32)[:, None]
    forget_logit = forget_logit.reshape(head_count, tp_size, seq_count, local_rows)
    log_forget = (ctx_valid[None] * jax.nn.log_sigmoid(forget_logit)).astype(BF16)

    cut = log_forget.astype(F32).reshape(groups, pair, tp_size, seq_count, local_rows)
    picked = jnp.stack([cut[g, :, :, s] for s, g in places])
    picked = picked.reshape(ctx_size, item_count, pair, ctx_rows).transpose(1, 0, 2, 3)
    picked = jnp.pad(picked, ((0, 0), (0, 0), (0, 8 - pair), (0, 0)))
    attended_items, qkv, exact, lse, decay = context(items, picked, head_size, 7)
    gate_logit = dot(normed_flat, gate_out_w, NN)
    out_gate = jax.nn.sigmoid(gate_logit).reshape(tp_size, -1, inner_width)
    grad_all = relative_rows(grad_out)
    hidden_state, normed_two, attended, mixed = out_project(
        input_rows, out_gate, full_two, out_column, gain_two, attended_items, layout, 2
    )
    normed_two_all, inner_act, grad_pair = mlp(normed_two, grad_all, full_two, hidden, 3)
    normed_two_flat = normed_two_all.reshape(all_rows, model_width)
    inner_flat = inner_act.reshape(all_rows, hidden)
    grad_pair_flat = grad_pair.reshape(all_rows, 2 * hidden)
    grad_flat = grad_all.reshape(all_rows, model_width)

    def owned_sum(part):
        total = lax.psum_scatter(part, weights, scatter_dimension=0, tiled=True)
        return total.astype(F32)

    mlp_part = jnp.concatenate(
        [
            dot(normed_two_flat, grad_pair_flat, TN).astype(BF16),
            dot(grad_flat, inner_flat, TN).astype(BF16),
        ],
        axis=1,
    )
    mlp_part, grad_pair = lax.optimization_barrier((mlp_part, grad_pair))
    mlp_sum = owned_sum(mlp_part)
    grad_hidden, branch, mlp_gain_part = mlp_back(
        grad_pair, full_two, hidden_state, grad_out, gain_two, 4
    )
    feedforward = summed_rows(dot(inner_flat, down_w, NT).reshape(tp_size, -1, model_width))
    output = (valid_rows * (hidden_state + feedforward)).astype(BF16)

    branch_all, grad_gate_logit, grads = out_back(
        branch, full_two, out_column, out_gate, attended, layout, item_count, ctx_size, 5
    )
    branch_flat = branch_all.reshape(all_rows, model_width)
    logit_flat = grad_gate_logit.reshape(all_rows, inner_width)

    grad_items, forget_items = context_back(grads, qkv, exact, lse, decay, head_size, 8)
    out_part = jnp.concatenate(
        [
            dot(branch_flat, mixed.reshape(all_rows, inner_width), TN).astype(BF16),
            dot(normed_flat, logit_flat, TN).astype(BF16),
        ],
        axis=1,
    )
    out_sum = owned_sum(out_part)

    forget_back = forget_items[:, :, :pair].astype(BF16).transpose(1, 0, 2, 3)
    forget_back = forget_back.reshape(ctx_size * item_count, pair, tp_size, local_rows)
    slots = {place(slot): slot for slot in range(used)}
    forget_back = jnp.stack(
        [
            jnp.stack([forget_back[slots[s, g]] for s in range(seq_count)], axis=2)
            for g in range(groups)
        ]
    ).reshape(head_count, tp_size, seq_count, local_rows)
    grad_forget_logit = forget_back.astype(F32) * ctx_valid[None] * jax.nn.sigmoid(-forget_logit)
    grad_forget_logit = grad_forget_logit.astype(BF16).reshape(head_count, all_rows)
    bias_part = jnp.sum(grad_forget_logit.astype(F32), axis=1)
    grad_forget_rows = jnp.pad(grad_forget_logit, ((0, LANES - head_count), (0, 0))).T
    grad_qkv = assemble(grad_items, layout, tp_size)
    grad_qkvf = jnp.concatenate([grad_qkv.reshape(all_rows, edge), grad_forget_rows], axis=1)
    qkv_sum = owned_sum(dot(normed_flat, grad_qkvf, TN).astype(BF16))
    input_grad, attn_gain_part = input_back(
        grad_qkv,
        grad_gate_logit,
        grad_forget_rows.reshape(tp_size, -1, LANES),
        full_one,
        full_two,
        out_column + 1,
        input_rows,
        grad_hidden,
        gain_one,
        6,
    )
    attn_gain_part = attn_gain_part[0]
    mlp_gain_part = mlp_gain_part[0]

    bias_full = lax.dynamic_update_slice(
        jnp.zeros((head_count * tp_size,), F32), bias_part, (tp_index * head_count,)
    )
    gain_one_sum, gain_two_sum, bias_sum = lax.psum(
        (attn_gain_part, mlp_gain_part, bias_full), ("fsdp", "ctx", "tp")
    )
    shard_rows = model_width // shard_count
    attn_gain_grad = lax.dynamic_slice_in_dim(gain_one_sum, shard_index * shard_rows, shard_rows, 0)
    mlp_gain_grad = lax.dynamic_slice_in_dim(gain_two_sum, shard_index * shard_rows, shard_rows, 0)
    forget_bias_grad = lax.dynamic_slice_in_dim(bias_sum, tp_index * head_count, head_count, 0)
    wide = inner_width
    return (
        by_position(output),
        by_position(input_grad),
        attn_gain_grad,
        qkv_sum[:, :wide],
        qkv_sum[:, wide : 2 * wide],
        qkv_sum[:, 2 * wide : 3 * wide],
        qkv_sum[:, 3 * wide : 3 * wide + head_count],
        forget_bias_grad,
        out_sum[:, wide:],
        out_sum[:, :wide],
        mlp_gain_grad,
        mlp_sum[:, :hidden],
        mlp_sum[:, hidden : 2 * hidden],
        mlp_sum[:, 2 * hidden :],
    )


def solution(mesh):
    rows = P(("ctx", "tp"), "fsdp", None)
    matrix = P(("fsdp", "ctx"), "tp")
    vector = P(("fsdp", "ctx"))
    return jax.shard_map(
        per_device,
        mesh=mesh,
        in_specs=(
            rows,
            P("fsdp"),
            vector,
            matrix,
            matrix,
            matrix,
            matrix,
            P("tp"),
            matrix,
            matrix,
            vector,
            matrix,
            matrix,
            matrix,
            rows,
        ),
        out_specs=(
            rows,
            rows,
            vector,
            matrix,
            matrix,
            matrix,
            matrix,
            P("tp"),
            matrix,
            matrix,
            vector,
            matrix,
            matrix,
            matrix,
        ),
        check_vma=False,
    )
```

```python
import functools

import jax
import jax.numpy as jnp
from jax import lax
from jax.experimental import pallas as pl
from jax.experimental.pallas import tpu as pltpu
from jax.sharding import PartitionSpec as P

F32 = jnp.float32
BF16 = jnp.bfloat16
LANES = 128
MESH = pl.DeviceIdType.MESH
epsilon = 1e-06
masked_score = -1e30
NT = (((1,), (1,)), ((), ()))
NN = (((1,), (0,)), ((), ()))
TN = (((0,), (0,)), ((), ()))


def dot(left, right, dims):
    return lax.dot_general(left, right, dims, preferred_element_type=F32)


def of_head(block, head, head_size, ones_at=None):
    lane = lax.broadcasted_iota(jnp.int32, block.shape, 1)
    out = jnp.where(lane // head_size == head, block, jnp.zeros_like(block))
    if ones_at is not None:
        out = jnp.where(lane == ones_at, jnp.ones_like(block), out)
    return out


def spare_lane(head, head_size):
    return ((head + 1) % 2) * head_size


def attend_item(qkv, decay, out, exact, lse, heads, head_size):
    count, _, block, width = qkv.shape
    scale = head_size**-0.5
    row = lax.broadcasted_iota(jnp.int32, (block, block), 0)
    column = lax.broadcasted_iota(jnp.int32, (block, block), 1)
    causal = column <= row

    def query_block(i, _):
        query = qkv[i, 0]
        lanes = pl.ds(pl.multiple_of(i * block, block), block)
        result = jnp.zeros((block, width), F32)
        for head in range(heads):
            query_head = of_head(query, head, head_size)

            def step(j, carry, masked):
                top, total, acc = carry
                keys = pl.ds(pl.multiple_of(j * block, block), block)
                score = dot(query_head, qkv[j, 1], NT) * scale
                score = score - decay[head : head + 1, keys]
                if masked:
                    score = jnp.where(causal, score, masked_score)
                new_top = jnp.maximum(top, jnp.max(score, axis=1, keepdims=True))
                prob = jnp.exp(score - new_top)
                shrink = jnp.exp(top - new_top)
                total = total * shrink + jnp.sum(prob, axis=1, keepdims=True)
                acc = acc * shrink + dot(prob.astype(BF16), qkv[j, 2], NN)
                return new_top, total, acc

            carry = (
                jnp.full((block, 1), masked_score, F32),
                jnp.zeros((block, 1), F32),
                jnp.zeros((block, width), F32),
            )
            carry = lax.fori_loop(0, i, lambda j, c: step(j, c, False), carry)
            top, total, acc = step(i, carry, True)
            lane = lax.broadcasted_iota(jnp.int32, acc.shape, 1)
            result = jnp.where(lane // head_size == head, acc / total, result)
            stat = jnp.broadcast_to(top + jnp.log(total), (block, LANES)).T
            lse[head : head + 1, lanes] = stat[0:1]
        exact[i] = result
        out[i] = result.astype(BF16)
        return 0

    lax.fori_loop(0, count, query_block, 0)


def attend_item_back(qkv, grads, exact, lse, decay, dqkv, change, dq_acc, delta, heads, head_size):
    count, _, block, width = qkv.shape
    scale = head_size**-0.5
    row = lax.broadcasted_iota(jnp.int32, (block, block), 0)
    column = lax.broadcasted_iota(jnp.int32, (block, block), 1)
    causal = row <= column
    dq_acc[...] = jnp.zeros_like(dq_acc)
    change[...] = jnp.zeros_like(change)

    def prepare(i, _):
        lanes = pl.ds(pl.multiple_of(i * block, block), block)
        product = grads[i].astype(F32) * exact[i]
        lane = lax.broadcasted_iota(jnp.int32, product.shape, 1)
        for head in range(heads):
            part = jnp.where(lane // head_size == head, product, 0.0)
            part = jnp.sum(part, axis=1, keepdims=True)
            delta[head : head + 1, lanes] = jnp.broadcast_to(part, (block, LANES)).T[0:1]
        return 0

    lax.fori_loop(0, count, prepare, 0)

    def key_block(j, _):
        keys = pl.ds(pl.multiple_of(j * block, block), block)
        key = qkv[j, 1]
        value = qkv[j, 2]
        value_total = jnp.zeros((block, width), F32)
        key_total = jnp.zeros((block, width), F32)
        for head in range(heads):
            spare = spare_lane(head, head_size)
            key_ones = of_head(key, head, head_size, spare)
            fall = jnp.broadcast_to(decay[head : head + 1, keys], (LANES, block)).T[:, 0:1]

            def step(i, carry, masked):
                value_acc, key_acc = carry
                lanes = pl.ds(pl.multiple_of(i * block, block), block)
                query = qkv[i, 0]
                grad = of_head(grads[i], head, head_size)
                score = dot(key, of_head(query, head, head_size), NT) * scale
                score = score - fall - lse[head : head + 1, lanes]
                if masked:
                    score = jnp.where(causal, score, masked_score)
                prob = jnp.exp(score)
                grad_prob = dot(value, grad, NT)
                grad_score = prob * (grad_prob - delta[head : head + 1, lanes])
                grad_score = grad_score.astype(BF16)
                value_acc = value_acc + dot(prob.astype(BF16), grad, NN)
                query_ones = of_head(query, head, head_size, spare)
                key_acc = key_acc + dot(grad_score, query_ones, NN)
                dq_acc[head, i] += dot(grad_score, key_ones, TN)
                return value_acc, key_acc

            zero = jnp.zeros((block, width), F32)
            carry = step(j, (zero, zero), True)
            carry = lax.fori_loop(j + 1, count, lambda i, c: step(i, c, False), carry)
            value_acc, key_acc = carry
            value_total = value_total + value_acc
            lane = lax.broadcasted_iota(jnp.int32, key_acc.shape, 1)
            key_total = jnp.where(lane // head_size == head, key_acc, key_total)
            change[head : head + 1, keys] -= key_acc.T[spare : spare + 1]
        dqkv[j, 1] = (key_total * scale).astype(BF16)
        dqkv[j, 2] = value_total.astype(BF16)
        return 0

    lax.fori_loop(0, count, key_block, 0)

    def finish(i, _):
        lanes = pl.ds(pl.multiple_of(i * block, block), block)
        total = jnp.zeros((block, width), F32)
        for head in range(heads):
            spare = spare_lane(head, head_size)
            part = dq_acc[head, i]
            lane = lax.broadcasted_iota(jnp.int32, part.shape, 1)
            total = jnp.where(lane // head_size == head, part, total)
            change[head : head + 1, lanes] += part.T[spare : spare + 1]
        dqkv[i, 0] = (total * scale).astype(BF16)
        return 0

    lax.fori_loop(0, count, finish, 0)


def triangle(upward):
    row = lax.broadcasted_iota(jnp.int32, (LANES, LANES), 0)
    column = lax.broadcasted_iota(jnp.int32, (LANES, LANES), 1)
    keep = (row <= column) if upward else (row >= column)
    return jnp.where(keep, 1.0, 0.0).astype(BF16)


def exact_product(values, matrix):
    high = values.astype(BF16)
    rest = values - high.astype(F32)
    middle = rest.astype(BF16)
    low = (rest - middle.astype(F32)).astype(BF16)
    return dot(high, matrix, NN) + dot(middle, matrix, NN) + dot(low, matrix, NN)


def ctx_sending(source, target, send_sem, recv_sem, peer):
    return pltpu.make_async_remote_copy(
        src_ref=source,
        dst_ref=target,
        send_sem=send_sem,
        recv_sem=recv_sem,
        device_id={"ctx": peer},
        device_id_type=MESH,
    )


def ctx_greet(size):
    me = lax.axis_index("ctx")
    barrier = pltpu.get_barrier_semaphore()
    for step in range(1, size):
        peer = lax.rem(me + step, size)
        pl.semaphore_signal(barrier, inc=1, device_id={"ctx": peer}, device_id_type=MESH)
    pl.semaphore_wait(barrier, size - 1)
    return me


class Exchange:
    def __init__(self, me, size, source, target, sems):
        self.me, self.size, self.source, self.target = me, size, source, target
        self.send_sem, self.recv_sem, self.own_sem = sems

    def own(self, item):
        return pltpu.make_async_copy(
            self.source.at[item, self.me], self.target.at[item, self.me], self.own_sem.at[item]
        )

    def copy(self, item, step):
        peer = lax.rem(self.me + step, self.size)
        return ctx_sending(
            self.source.at[item, peer],
            self.target.at[item, self.me],
            self.send_sem.at[item, step],
            self.recv_sem.at[item, step],
            peer,
        )

    def start(self, item):
        self.own(item).start()
        for step in range(1, self.size):
            self.copy(item, step).start()

    def arrive(self, item):
        self.own(item).wait()
        for step in range(1, self.size):
            self.copy(item, step).wait_recv()

    def drain(self, item):
        for step in range(1, self.size):
            self.copy(item, step).wait_send()


def exchange_sems(items, size):
    return [
        pltpu.SemaphoreType.DMA((items, size)),
        pltpu.SemaphoreType.DMA((items, size)),
        pltpu.SemaphoreType.DMA((items,)),
    ]


def context_kernel(
    heads, head_size, items_ref, forget_ref, back_ref, qkv_ref, exact_ref, lse_ref, decay_ref, *refs
):
    qkv, forget, out, save_sem = refs[:4]
    sems = refs[4:]
    count, size, _, block, width = items_ref.shape
    me = ctx_greet(size)
    forgets = Exchange(me, size, forget_ref, forget, sems[0:3])
    inputs = Exchange(me, size, items_ref, qkv, sems[3:6])
    results = Exchange(me, size, out, back_ref, sems[6:9])

    @pl.loop(0, count)
    def _(item):
        forgets.start(item)

    inputs.start(0)

    @pl.loop(0, count)
    def _(item):
        forgets.arrive(item)

    @pl.loop(0, count)
    def _(item):
        upper = triangle(True)
        before = jnp.zeros((8, 1), F32)
        for start in range(0, size * block, LANES):
            part = forget[item, start // block, :, pl.ds(start % block, LANES)]
            total = before + dot(part.astype(BF16), upper, NN)
            decay_ref[item, :, pl.ds(start, LANES)] = total
            before = total[:, LANES - 1 :]

    lse_ref[...] = jnp.zeros_like(lse_ref)

    @pl.loop(0, count)
    def _(item):
        @pl.when(item + 1 < count)
        def _():
            inputs.start(item + 1)

        inputs.arrive(item)
        saving = pltpu.make_async_copy(qkv.at[item], qkv_ref.at[item], save_sem)
        saving.start()
        attend_item(
            qkv.at[item], decay_ref.at[item], out.at[item], exact_ref.at[item], lse_ref.at[item], heads, head_size
        )
        results.start(item)
        saving.wait()

    @pl.loop(0, count)
    def _(item):
        forgets.drain(item)
        inputs.drain(item)
        results.arrive(item)
        results.drain(item)


def full_block(shape):
    return pl.BlockSpec(shape, lambda i: (0,) * len(shape), pipeline_mode=pl.Buffered(1))


def attend_cost(items, heads, products):
    count, size, _, block, width = items.shape
    pairs = count * heads * (size * block) ** 2 // 2
    return pl.CostEstimate(
        flops=2 * products * pairs * 256, bytes_accessed=100 << 20, transcendentals=pairs
    )


def context(items, forget, head_size, ident):
    count, size, _, block, width = items.shape
    heads = width // head_size
    place = pl.BlockSpec(memory_space=pl.ANY)
    exact, stat = (count, size, block, width), (count, 8, size * block)
    return pl.pallas_call(
        functools.partial(context_kernel, heads, head_size),
        grid=(1,),
        out_shape=[
            jax.ShapeDtypeStruct(exact, BF16),
            jax.ShapeDtypeStruct(items.shape, BF16),
            jax.ShapeDtypeStruct(exact, F32),
            jax.ShapeDtypeStruct(stat, F32),
            jax.ShapeDtypeStruct(stat, F32),
        ],
        in_specs=[place, place],
        out_specs=[place, place, full_block(exact), full_block(stat), full_block(stat)],
        scratch_shapes=[
            pltpu.VMEM(items.shape, BF16),
            pltpu.VMEM(forget.shape, F32),
            pltpu.VMEM(exact, BF16),
            pltpu.SemaphoreType.DMA,
        ]
        + exchange_sems(count, size) * 3,
        compiler_params=remote_params(ident, 48),
        cost_estimate=attend_cost(items, heads, 2),
        name="context",
    )(items, forget)


def context_back_kernel(
    heads, head_size, items_ref, qkv_ref, exact_ref, lse_ref, decay_ref, back_ref, forget_ref, *refs
):
    grads, dqkv, change, slope, dq_acc, delta = refs[:6]
    sems = refs[6:]
    count, size, block, width = items_ref.shape
    me = ctx_greet(size)
    inputs = Exchange(me, size, items_ref, grads, sems[0:3])
    results = Exchange(me, size, dqkv, back_ref, sems[3:6])
    forgets = Exchange(me, size, slope, forget_ref, sems[6:9])

    @pl.loop(0, count)
    def _(item):
        inputs.start(item)

    @pl.loop(0, count)
    def _(item):
        inputs.arrive(item)
        attend_item_back(
            qkv_ref.at[item],
            grads.at[item],
            exact_ref.at[item],
            lse_ref.at[item],
            decay_ref.at[item],
            dqkv.at[item],
            change,
            dq_acc,
            delta,
            heads,
            head_size,
        )
        results.start(item)
        lower = triangle(False)
        after = jnp.zeros((8, 1), F32)
        for start in reversed(range(0, size * block, LANES)):
            total = after + exact_product(change[:, pl.ds(start, LANES)], lower)
            slope[item, start // block, :, pl.ds(start % block, LANES)] = total
            after = total[:, 0:1]
        forgets.start(item)

    @pl.loop(0, count)
    def _(item):
        inputs.drain(item)
        results.arrive(item)
        results.drain(item)
        forgets.arrive(item)
        forgets.drain(item)


def context_back(grads, qkv, exact, lse, decay, head_size, ident):
    count, size, _, block, width = qkv.shape
    heads = width // head_size
    place = pl.BlockSpec(memory_space=pl.ANY)
    forget = (count, size, 8, block)
    return pl.pallas_call(
        functools.partial(context_back_kernel, heads, head_size),
        grid=(1,),
        out_shape=[
            jax.ShapeDtypeStruct(qkv.shape, BF16),
            jax.ShapeDtypeStruct(forget, F32),
        ],
        in_specs=[
            place,
            full_block(qkv.shape),
            full_block(exact.shape),
            full_block(lse.shape),
            full_block(decay.shape),
        ],
        out_specs=[place, place],
        scratch_shapes=[
            pltpu.VMEM(grads.shape, BF16),
            pltpu.VMEM(qkv.shape, BF16),
            pltpu.VMEM((8, size * block), F32),
            pltpu.VMEM(forget, F32),
            pltpu.VMEM((heads, size, block, width), F32),
            pltpu.VMEM((8, size * block), F32),
        ]
        + exchange_sems(count, size) * 3,
        compiler_params=remote_params(ident, 56),
        cost_estimate=attend_cost(qkv, heads, 5),
        name="context_back",
    )(grads, qkv, exact, lse, decay)


CHUNKS = 4


def tp_places():
    me = lax.axis_index("tp")
    sibling = me + 1 - 2 * lax.rem(me, 2)
    across = lax.rem(me + 2, 4)
    diagonal = lax.rem(sibling + 2, 4)
    return me, sibling, across, diagonal


def greet(peers):
    barrier = pltpu.get_barrier_semaphore()
    for peer in peers:
        pl.semaphore_signal(barrier, inc=1, device_id={"tp": peer}, device_id_type=MESH)
    pl.semaphore_wait(barrier, len(peers))


def sending(source, target, send_sem, recv_sem, peer):
    return pltpu.make_async_remote_copy(
        src_ref=source,
        dst_ref=target,
        send_sem=send_sem,
        recv_sem=recv_sem,
        device_id={"tp": peer},
        device_id_type=MESH,
    )


def pick(step, chunks, places):
    me, sibling, across, diagonal = places
    late = step - 2 * chunks
    far = jnp.where(lax.rem(late, 2) == 0, across, diagonal)
    slot = jnp.where(step < chunks, me, jnp.where(step < 2 * chunks, sibling, far))
    chunk = jnp.where(step < 2 * chunks, lax.rem(step, chunks), late // 2)
    return slot, chunk


def gather_loop(table, sems, compute, own=None, relative=False):
    near_send, near_recv, far_send, far_recv, pass_send, pass_recv = sems
    me, sibling, across, diagonal = tp_places()
    places = (0, 1, 2, 3) if relative else (me, sibling, across, diagonal)
    mine, near_by, far_off, corner = places
    near_spot, far_spot, pass_spot = (1, 2, 3) if relative else (me, me, across)
    rows = table.shape[1] // CHUNKS

    def part(slot, chunk):
        return table.at[slot, pl.ds(pl.multiple_of(chunk * rows, rows), rows)]

    def far(chunk):
        source = part(mine, chunk)
        if own is not None:
            source = own.at[pl.ds(pl.multiple_of(chunk * rows, rows), rows)]
        return sending(source, part(far_spot, chunk), far_send.at[chunk], far_recv.at[chunk], across)

    def far_arrival(chunk):
        spot = part(far_off, chunk)
        return sending(spot, spot, far_send.at[chunk], far_recv.at[chunk], across)

    def passing(chunk):
        return sending(
            part(far_off, chunk), part(pass_spot, chunk), pass_send.at[chunk], pass_recv.at[chunk], sibling
        )

    def pass_arrival(chunk):
        spot = part(corner, chunk)
        return sending(spot, spot, pass_send.at[chunk], pass_recv.at[chunk], sibling)

    for chunk in range(CHUNKS):
        far(chunk).start()
    own = table.at[mine] if own is None else own
    near = sending(own, table.at[near_spot], near_send, near_recv, sibling)
    near.start()

    def body(step, _):
        slot, chunk = pick(step, CHUNKS, places)
        late = step - 2 * CHUNKS

        @pl.when(step == CHUNKS)
        def _():
            spot = table.at[near_by]
            sending(spot, spot, near_send, near_recv, sibling).wait_recv()

        @pl.when((late >= 0) & (lax.rem(late, 2) == 0))
        def _():
            far_arrival(chunk).wait_recv()
            passing(chunk).start()

        @pl.when((late >= 0) & (lax.rem(late, 2) == 1))
        def _():
            pass_arrival(chunk).wait_recv()

        compute(slot, chunk)
        return 0

    lax.fori_loop(0, 4 * CHUNKS, body, 0)
    near.wait_send()
    for chunk in range(CHUNKS):
        far(chunk).wait_send()
        passing(chunk).wait_send()


GATHER_SEMS = [pltpu.SemaphoreType.DMA] * 2 + [pltpu.SemaphoreType.DMA((CHUNKS,))] * 4


def scatter_loop(buffers, sems, partial, finish, relative=False, between=None):
    near_out, near_in, far_out, far_in = buffers
    near_send, near_recv, far_send, far_recv = sems
    me, sibling, across, diagonal = tp_places()
    mine, near_by, far_off, corner = (0, 1, 2, 3) if relative else (me, sibling, across, diagonal)
    rows = far_out.shape[0] // CHUNKS

    def span(chunk):
        return pl.ds(pl.multiple_of(chunk * rows, rows), rows)

    def near(half, chunk):
        return sending(
            near_out.at[half, span(chunk)],
            near_in.at[half, span(chunk)],
            near_send.at[half, chunk],
            near_recv.at[half, chunk],
            sibling,
        )

    def far(chunk):
        return sending(
            far_out.at[span(chunk)],
            far_in.at[span(chunk)],
            far_send.at[chunk],
            far_recv.at[chunk],
            across,
        )

    def body(step, _):
        phase, chunk = step // CHUNKS, lax.rem(step, CHUNKS)
        slot = jnp.where(
            phase == 0, corner, jnp.where(phase == 1, far_off, jnp.where(phase == 2, near_by, mine))
        )
        value = partial(slot, chunk)
        spot = span(chunk)

        @pl.when(lax.rem(phase, 2) == 0)
        def _():
            half = phase // 2
            near_out[half, spot] = value.astype(BF16)
            near(half, chunk).start()

        @pl.when(phase == 1)
        def _():
            near(0, chunk).wait_recv()
            far_out[spot] = (value + near_in[0, spot].astype(F32)).astype(BF16)
            far(chunk).start()

        @pl.when(phase == 3)
        def _():
            near(1, chunk).wait_recv()
            far(chunk).wait_recv()
            finish(chunk, value + near_in[1, spot].astype(F32) + far_in[spot].astype(F32))

        return 0

    if between is None:
        lax.fori_loop(0, 4 * CHUNKS, body, 0)
    else:
        lax.fori_loop(0, 3 * CHUNKS, body, 0)
        for chunk in range(CHUNKS):
            between(chunk)
            lax.fori_loop(3 * CHUNKS + chunk, 3 * CHUNKS + chunk + 1, body, 0)
    for chunk in range(CHUNKS):
        near(0, chunk).wait_send()
        near(1, chunk).wait_send()
        far(chunk).wait_send()


SCATTER_SEMS = [pltpu.SemaphoreType.DMA((2, CHUNKS))] * 2 + [pltpu.SemaphoreType.DMA((CHUNKS,))] * 2


def scatter_buffers(rows, width):
    return [
        pltpu.VMEM((2, rows, width), BF16),
        pltpu.VMEM((2, rows, width), BF16),
        pltpu.VMEM((rows, width), BF16),
        pltpu.VMEM((rows, width), BF16),
    ]


def group_peers():
    f_size, c_size = lax.axis_size("fsdp"), lax.axis_size("ctx")
    f, c = lax.axis_index("fsdp"), lax.axis_index("ctx")
    return [
        {"fsdp": lax.rem(f + i, f_size), "ctx": lax.rem(c + j, c_size)}
        for i in range(f_size)
        for j in range(c_size)
        if i or j
    ]


def greet_all(peers):
    barrier = pltpu.get_barrier_semaphore()
    for peer in peers:
        pl.semaphore_signal(barrier, inc=1, device_id=peer, device_id_type=MESH)
    pl.semaphore_wait(barrier, len(peers))


def moving(source, target, send_sem, recv_sem, peer):
    return pltpu.make_async_remote_copy(
        src_ref=source,
        dst_ref=target,
        send_sem=send_sem,
        recv_sem=recv_sem,
        device_id=peer,
        device_id_type=MESH,
    )


class WeightGather:
    def __init__(self, shard, full, sems):
        self.shard, self.full = shard, full
        self.f_size, self.c_size = lax.axis_size("fsdp"), lax.axis_size("ctx")
        self.f, self.c = lax.axis_index("fsdp"), lax.axis_index("ctx")
        self.sems = sems

    def spot(self, c, f=None):
        rows = self.shard.shape[0]
        block = (self.f if f is None else f) * self.c_size + c
        return self.full.at[pl.ds(pl.multiple_of(block * rows, rows), rows)]

    def along(self, c, hop, side, source=None):
        source = self.spot(c) if source is None else source
        peer = {"ctx": self.c + (1 if side else -1)}
        return moving(
            source, self.spot(c), self.sems[0].at[side, hop], self.sems[1].at[side, hop], peer
        )

    def over(self, c, step, source=None):
        source = self.spot(c) if source is None else source
        peer = {"fsdp": lax.rem(self.f + step, self.f_size)}
        return moving(
            source, self.spot(c), self.sems[2].at[step, c], self.sems[3].at[step, c], peer
        )

    def over_arrival(self, c, step):
        spot = self.spot(c, lax.rem(self.f + self.f_size - step, self.f_size))
        peer = {"fsdp": lax.rem(self.f + step, self.f_size)}
        return moving(spot, spot, self.sems[2].at[step, c], self.sems[3].at[step, c], peer)

    def can(self, side):
        return self.c + 1 < self.c_size if side else self.c > 0

    def holds(self, hop, side):
        return self.c - hop >= 0 if side else self.c + hop < self.c_size

    def begin(self):
        pltpu.make_async_copy(self.shard, self.spot(self.c), self.sems[4]).start()
        for side in (1, 0):

            @pl.when(self.can(side))
            def _(side=side):
                self.along(self.c, 1, side, self.shard).start()

        for step in range(1, self.f_size):
            self.over(self.c, step, self.shard).start()

    def advance(self, hop):
        for side in (1, 0):

            @pl.when(self.holds(hop, side))
            def _(side=side):
                c = self.c - hop if side else self.c + hop
                self.along(c, hop, side).wait_recv()

                @pl.when(self.can(side))
                def _():
                    self.along(c, hop + 1, side).start()

                for step in range(1, self.f_size):
                    self.over(c, step).start()

    def end(self):
        pltpu.make_async_copy(self.shard, self.spot(self.c), self.sems[4]).wait()
        for step in range(1, self.f_size):
            for c in range(self.c_size):
                self.over_arrival(c, step).wait_recv()
                self.over(c, step).wait_send()
        for side in (1, 0):

            @pl.when(self.can(side))
            def _(side=side):
                self.along(self.c, 1, side, self.shard).wait_send()

            for hop in range(1, self.c_size):

                @pl.when(self.holds(hop, side) & self.can(side))
                def _(side=side, hop=hop):
                    c = self.c - hop if side else self.c + hop
                    self.along(c, hop + 1, side).wait_send()


def weight_sems(f_size, c_size):
    dma = pltpu.SemaphoreType.DMA
    return [dma((2, c_size + 1))] * 2 + [dma((f_size, c_size))] * 2 + [dma]


def startup_kernel(rows_ref, shard_ref, all_ref, full_ref, own_sem, *sems):
    me, sibling, across, diagonal = tp_places()
    greet_all([{"tp": sibling}, {"tp": across}] + group_peers())
    near_send, near_recv, far_send, far_recv, pass_send, pass_recv = sems[:6]
    gather = WeightGather(shard_ref, full_ref, sems[6:])
    size = rows_ref.shape[0] // CHUNKS
    own = pltpu.make_async_copy(rows_ref, all_ref.at[me], own_sem)
    own.start()

    def span(chunk):
        return pl.ds(chunk * size, size)

    def far(chunk):
        return sending(
            rows_ref.at[span(chunk)],
            all_ref.at[me, span(chunk)],
            far_send.at[chunk],
            far_recv.at[chunk],
            across,
        )

    def passing(chunk):
        spot = all_ref.at[across, span(chunk)]
        return sending(spot, spot, pass_send.at[chunk], pass_recv.at[chunk], sibling)

    for chunk in range(CHUNKS):
        far(chunk).start()
    gather.begin()
    near = sending(rows_ref, all_ref.at[me], near_send, near_recv, sibling)
    near.start()
    for turn in range(max(CHUNKS, gather.c_size - 1)):
        if turn < CHUNKS:
            far(turn).wait_recv()
            passing(turn).start()
        if turn + 1 < gather.c_size:
            gather.advance(turn + 1)
    near.wait()
    for chunk in range(CHUNKS):
        far(chunk).wait_send()
        passing(chunk).wait()
    own.wait()
    gather.end()


def startup(rows, shard, f_size, c_size, ident):
    place = pl.BlockSpec(memory_space=pl.ANY)
    full = (shard.shape[0] * f_size * c_size, shard.shape[1])
    return pl.pallas_call(
        startup_kernel,
        out_shape=[
            jax.ShapeDtypeStruct((4,) + rows.shape, BF16),
            jax.ShapeDtypeStruct(full, BF16),
        ],
        in_specs=[place, place],
        out_specs=[place, place],
        scratch_shapes=[pltpu.SemaphoreType.DMA] + GATHER_SEMS + weight_sems(f_size, c_size),
        compiler_params=pltpu.CompilerParams(collective_id=ident, has_side_effects=True),
        name="startup",
    )(rows, shard)


def whole(shape, column=None):
    zeros = (0,) * (len(shape) - 1)
    return pl.BlockSpec(shape, lambda i: zeros + (column or 0,), pipeline_mode=pl.Buffered(1))


def remote_params(ident, megabytes):
    return pltpu.CompilerParams(
        collective_id=ident, has_side_effects=True, vmem_limit_bytes=megabytes << 20, dimension_semantics=("arbitrary",)
    )


def project_kernel(layout, x_ref, gain_ref, w_ref, normed_ref, forget_ref, items_ref):
    seq_count, groups, width, places = layout
    x = x_ref[0].astype(F32)
    normed = (x * lax.rsqrt(jnp.mean(x * x, axis=1, keepdims=True) + epsilon) * gain_ref[...]).astype(BF16)
    normed_ref[0] = normed
    inner = groups * width
    rows = x.shape[0] // seq_count
    count = items_ref.shape[0]
    for kind in range(3):
        value = dot(normed, w_ref[:, kind * inner : (kind + 1) * inner], NN).astype(BF16)
        for slot, (s, g) in enumerate(places):
            piece = value[s * rows : (s + 1) * rows, g * width : (g + 1) * width]
            items_ref[slot % count, slot // count, kind] = piece
    forget_ref[0] = dot(normed, w_ref[:, 3 * inner :], NN)


def project(x_all, gain, full_one, layout, item_count, ctx_size):
    seq_count, groups, width, places = layout
    tp_size, rows, model_width = x_all.shape
    local = rows // seq_count
    item = jax.ShapeDtypeStruct((item_count, ctx_size, 3, tp_size * local, width), BF16)
    columns = full_one.shape[1]
    block = pl.BlockSpec((1, rows, model_width), lambda t: (t, 0, 0))
    return pl.pallas_call(
        functools.partial(project_kernel, layout),
        grid=(tp_size,),
        out_shape=[
            jax.ShapeDtypeStruct(x_all.shape, BF16),
            jax.ShapeDtypeStruct((tp_size, rows, LANES), F32),
            item,
        ],
        in_specs=[
            block,
            pl.BlockSpec((1, model_width), lambda t: (0, 0)),
            pl.BlockSpec((model_width, columns), lambda t: (0, 0), pipeline_mode=pl.Buffered(1)),
        ],
        out_specs=[
            block,
            pl.BlockSpec((1, rows, LANES), lambda t: (t, 0, 0)),
            pl.BlockSpec((item_count, ctx_size, 3, local, width), lambda t: (0, 0, 0, t, 0)),
        ],
        compiler_params=pltpu.CompilerParams(vmem_limit_bytes=48 << 20, dimension_semantics=("arbitrary",)),
        cost_estimate=pl.CostEstimate(
            flops=2 * x_all.size * columns, bytes_accessed=4 * x_all.size, transcendentals=0
        ),
        name="project",
    )(x_all, gain, full_one)


def out_kernel(layout, x_ref, gate_ref, w_ref, gain_ref, items, *refs):
    seq_count, groups, width, places = layout
    hidden_ref, normed_ref, attended_ref, mixed_ref = refs[:4]
    buffers, sems = refs[4:8], refs[8:]
    count = items.shape[0]
    me, sibling, across, diagonal = tp_places()
    greet((sibling, across))
    tp_size, rows, _ = gate_ref.shape
    local = rows // seq_count

    def mix(t, _):
        here = pl.ds(pl.multiple_of(t * local, local), local)
        for slot, (s, g) in enumerate(places[: seq_count * groups]):
            there = (t, pl.ds(s * local, local), pl.ds(g * width, width))
            value = items[slot % count, slot // count, here]
            attended_ref[there] = value
            mixed_ref[there] = (value.astype(F32) * gate_ref[there]).astype(BF16)
        return 0

    lax.fori_loop(0, tp_size, mix, 0)
    size = rows // CHUNKS

    def span(chunk):
        return pl.ds(pl.multiple_of(chunk * size, size), size)

    def partial(slot, chunk):
        return dot(mixed_ref[slot, span(chunk)], w_ref[...], NT)

    def finish(chunk, total):
        hidden = x_ref[span(chunk)].astype(F32) + total
        hidden_ref[span(chunk)] = hidden
        inverse = lax.rsqrt(jnp.mean(hidden * hidden, axis=1, keepdims=True) + epsilon)
        normed_ref[span(chunk)] = (hidden * inverse * gain_ref[...]).astype(BF16)

    scatter_loop(buffers, sems, partial, finish)


def out_project(x, gate, full_two, column, gain, items, layout, ident):
    seq_count, groups, width, places = layout
    rows, model_width = x.shape
    inner = groups * width
    tp_size = gate.shape[0]
    return pl.pallas_call(
        functools.partial(out_kernel, layout),
        grid=(1,),
        out_shape=[
            jax.ShapeDtypeStruct(x.shape, F32),
            jax.ShapeDtypeStruct(x.shape, BF16),
            jax.ShapeDtypeStruct(gate.shape, BF16),
            jax.ShapeDtypeStruct(gate.shape, BF16),
        ],
        in_specs=[
            whole(x.shape),
            whole(gate.shape),
            whole((model_width, inner), column),
            whole(gain.shape),
            whole(items.shape),
        ],
        out_specs=[whole(x.shape), whole(x.shape), whole(gate.shape), whole(gate.shape)],
        scratch_shapes=scatter_buffers(rows, model_width) + SCATTER_SEMS,
        compiler_params=remote_params(ident, 48),
        cost_estimate=pl.CostEstimate(
            flops=2 * gate.size * model_width, bytes_accessed=100 << 20, transcendentals=0
        ),
        name="out_project",
    )(x, gate, full_two, gain, items)


def mlp_kernel(normed_ref, grad_ref, gate_w, up_w, down_w, all_ref, inner_ref, pair_ref, table, own_sem, *sems):
    me, sibling, across, diagonal = tp_places()
    greet((sibling, across))
    table[0] = normed_ref[...]
    rows, hidden = table.shape[1] // CHUNKS, gate_w.shape[1]
    tile = min(hidden, 512)

    def compute(slot, chunk):
        spot = pl.ds(pl.multiple_of(chunk * rows, rows), rows)
        normed, grad = table[slot, spot], grad_ref[slot, spot]
        for start in range(0, hidden, tile):
            columns = pl.ds(start, tile)
            gate = dot(normed, gate_w[:, columns], NN)
            up = dot(normed, up_w[:, columns], NN)
            back = dot(grad, down_w[:, columns], NN)
            sig = 1.0 / (1.0 + jnp.exp(-gate))
            silu = gate * sig
            inner_ref[slot, spot, columns] = (silu * up).astype(BF16)
            pair_ref[slot, spot, columns] = (back * up * sig * (1.0 + gate * (1.0 - sig))).astype(BF16)
            pair_ref[slot, spot, pl.ds(hidden + start, tile)] = (back * silu).astype(BF16)

    gather_loop(table, sems, compute, relative=True)
    copy = pltpu.make_async_copy(table, all_ref, own_sem)
    copy.start()
    copy.wait()


def mlp(normed, grad_all, full_two, hidden, ident):
    tp_size, rows, model_width = grad_all.shape
    total = tp_size * rows
    return pl.pallas_call(
        mlp_kernel,
        grid=(1,),
        out_shape=[
            jax.ShapeDtypeStruct(grad_all.shape, BF16),
            jax.ShapeDtypeStruct((tp_size, rows, hidden), BF16),
            jax.ShapeDtypeStruct((tp_size, rows, 2 * hidden), BF16),
        ],
        in_specs=[whole(normed.shape), whole(grad_all.shape)]
        + [whole((model_width, hidden), column) for column in range(3)],
        out_specs=[
            pl.BlockSpec(memory_space=pl.ANY),
            whole((tp_size, rows, hidden)),
            whole((tp_size, rows, 2 * hidden)),
        ],
        scratch_shapes=[pltpu.VMEM(grad_all.shape, BF16), pltpu.SemaphoreType.DMA] + GATHER_SEMS,
        compiler_params=remote_params(ident, 56),
        cost_estimate=pl.CostEstimate(
            flops=6 * total * model_width * hidden, bytes_accessed=100 << 20, transcendentals=total * hidden
        ),
        name="mlp",
    )(normed, grad_all, full_two, full_two, full_two)


def mlp_back_kernel(pair_ref, w_ref, hidden_ref, grad_ref, gain_ref, out_ref, branch_ref, part_ref, *refs):
    buffers, sems = refs[:4], refs[4:]
    me, sibling, across, diagonal = tp_places()
    greet((sibling, across))
    part_ref[...] = jnp.zeros_like(part_ref)
    size = hidden_ref.shape[0] // CHUNKS

    def span(chunk):
        return pl.ds(pl.multiple_of(chunk * size, size), size)

    def partial(slot, chunk):
        return dot(pair_ref[slot, span(chunk)], w_ref[...], NT)

    def finish(chunk, total):
        hidden = hidden_ref[span(chunk)]
        inverse = lax.rsqrt(jnp.mean(hidden * hidden, axis=1, keepdims=True) + epsilon)
        unit = hidden * inverse
        part_ref[...] += jnp.sum(total * unit, axis=0, keepdims=True)
        scaled = total * gain_ref[...]
        middle = jnp.mean(scaled * unit, axis=1, keepdims=True)
        grad = grad_ref[span(chunk)].astype(F32) + inverse * (scaled - unit * middle)
        out_ref[span(chunk)] = grad
        branch_ref[span(chunk)] = grad.astype(BF16)

    scatter_loop(buffers, sems, partial, finish, relative=True)


def mlp_back(pair, full_two, hidden_state, grad_out, gain, ident):
    tp_size, rows, wide = pair.shape
    model_width = hidden_state.shape[1]
    return pl.pallas_call(
        mlp_back_kernel,
        grid=(1,),
        out_shape=[
            jax.ShapeDtypeStruct(hidden_state.shape, F32),
            jax.ShapeDtypeStruct(hidden_state.shape, BF16),
            jax.ShapeDtypeStruct(gain.shape, F32),
        ],
        in_specs=[
            whole(pair.shape),
            whole((model_width, wide), 0),
            whole(hidden_state.shape),
            whole(grad_out.shape),
            whole(gain.shape),
        ],
        out_specs=[whole(hidden_state.shape), whole(hidden_state.shape), whole(gain.shape)],
        scratch_shapes=scatter_buffers(rows, model_width) + SCATTER_SEMS,
        compiler_params=remote_params(ident, 56),
        cost_estimate=pl.CostEstimate(
            flops=2 * pair.size * model_width, bytes_accessed=100 << 20, transcendentals=0
        ),
        name="mlp_back",
    )(pair, full_two, hidden_state, grad_out, gain)


def out_back_kernel(layout, branch_ref, w_ref, gate_ref, attended_ref, *refs):
    seq_count, groups, width, places = layout
    all_ref, logit_ref, items, table, grads, own_sem = refs[:6]
    sems = refs[6:]
    count = items.shape[0]
    me, sibling, across, diagonal = tp_places()
    greet((sibling, across))
    table[me] = branch_ref[...]
    tp_size, rows, _ = gate_ref.shape
    local, size = rows // seq_count, rows // CHUNKS

    def compute(slot, chunk):
        spot = pl.ds(pl.multiple_of(chunk * size, size), size)
        mixed = dot(table[slot, spot], w_ref[...], NN)
        gate = gate_ref[slot, spot]
        scaled = mixed * gate
        grads[slot, spot] = scaled.astype(BF16)
        attended = attended_ref[slot, spot].astype(F32)
        logit_ref[slot, spot] = (scaled * attended * (1.0 - gate)).astype(BF16)

    gather_loop(table, sems, compute)
    copy = pltpu.make_async_copy(table, all_ref, own_sem)
    copy.start()

    def deal(t, _):
        here = pl.ds(pl.multiple_of(t * local, local), local)
        for slot, (s, g) in enumerate(places):
            piece = grads[t, pl.ds(s * local, local), pl.ds(g * width, width)]
            items[slot % count, slot // count, here] = piece
        return 0

    lax.fori_loop(0, tp_size, deal, 0)
    copy.wait()


def out_back(branch, full_two, column, gate, attended, layout, item_count, ctx_size, ident):
    seq_count, groups, width, places = layout
    rows, model_width = branch.shape
    tp_size, _, inner = gate.shape
    item = (item_count, ctx_size, tp_size * rows // seq_count, width)
    table = (tp_size, rows, model_width)
    return pl.pallas_call(
        functools.partial(out_back_kernel, layout),
        grid=(1,),
        out_shape=[
            jax.ShapeDtypeStruct(table, BF16),
            jax.ShapeDtypeStruct(gate.shape, BF16),
            jax.ShapeDtypeStruct(item, BF16),
        ],
        in_specs=[
            whole(branch.shape),
            whole((model_width, inner), column),
            whole(gate.shape),
            whole(attended.shape),
        ],
        out_specs=[pl.BlockSpec(memory_space=pl.ANY), whole(gate.shape), whole(item)],
        scratch_shapes=[pltpu.VMEM(table, BF16), pltpu.VMEM(gate.shape, BF16), pltpu.SemaphoreType.DMA]
        + GATHER_SEMS,
        compiler_params=remote_params(ident, 48),
        cost_estimate=pl.CostEstimate(
            flops=2 * gate.size * model_width, bytes_accessed=100 << 20, transcendentals=0
        ),
        name="out_back",
    )(branch, full_two, gate, attended)


def assemble_kernel(layout, items, out_ref):
    seq_count, groups, width, places = layout
    count, local = items.shape[0], items.shape[3]
    inner = groups * width
    for slot, (s, g) in enumerate(places[: seq_count * groups]):
        for kind in range(3):
            columns = pl.ds(kind * inner + g * width, width)
            out_ref[0, pl.ds(s * local, local), columns] = items[slot % count, slot // count, kind]


def assemble(items, layout, tp_size):
    seq_count, groups, width, places = layout
    count, ctx_size, kinds, ctx_rows, _ = items.shape
    local = ctx_rows // tp_size
    shape = (tp_size, seq_count * local, kinds * groups * width)
    return pl.pallas_call(
        functools.partial(assemble_kernel, layout),
        grid=(tp_size,),
        out_shape=jax.ShapeDtypeStruct(shape, BF16),
        in_specs=[pl.BlockSpec((count, ctx_size, kinds, local, width), lambda t: (0, 0, 0, t, 0))],
        out_specs=pl.BlockSpec((1,) + shape[1:], lambda t: (t, 0, 0)),
        compiler_params=pltpu.CompilerParams(vmem_limit_bytes=32 << 20, dimension_semantics=("arbitrary",)),
        cost_estimate=pl.CostEstimate(flops=0, bytes_accessed=16 << 20, transcendentals=0),
        name="assemble",
    )(items)


class WeightSum:
    def __init__(self, part, out, buffers, sems):
        self.part, self.out = part, out
        self.over_in, self.total, self.along_out, self.along_in = buffers
        self.over_send, self.over_recv, self.along_send, self.along_recv = sems
        self.f_size, self.c_size = lax.axis_size("fsdp"), lax.axis_size("ctx")
        self.f, self.c = lax.axis_index("fsdp"), lax.axis_index("ctx")
        self.rows = out.shape[0]
        ends = [(self.c_size - 1 - i // 2) if i % 2 == 0 else i // 2 for i in range(self.c_size)]
        self.order = ends

    def block(self, f, c):
        index = f * self.c_size + c
        return pl.ds(pl.multiple_of(index * self.rows, self.rows), self.rows)

    def over(self, c, step):
        f = lax.rem(self.f + step, self.f_size)
        return moving(
            self.part.at[self.block(f, c)],
            self.over_in.at[step, c],
            self.over_send.at[step, c],
            self.over_recv.at[step, c],
            {"fsdp": f},
        )

    def along(self, c, side):
        peer = {"ctx": self.c + (1 if side else -1)}
        return moving(
            self.along_out.at[side, c],
            self.along_in.at[side, c],
            self.along_send.at[side, c],
            self.along_recv.at[side, c],
            peer,
        )

    def begin(self):
        for c in self.order:
            for step in range(1, self.f_size):
                self.over(c, step).start()

    def receive(self, c):
        value = self.part[self.block(self.f, c)].astype(F32)
        for step in range(1, self.f_size):
            self.over(c, step).wait_recv()
            value = value + self.over_in[step, c].astype(F32)
        self.total[c] = value
        for side, end in ((1, 0), (0, self.c_size - 1)):

            @pl.when((self.c == end) & (self.c != c))
            def _(side=side):
                self.along_out[side, c] = value.astype(BF16)
                self.along(c, side).start()

    def advance(self, c):
        for side in (1, 0):
            comes = (self.c > 0) & (self.c <= c) if side else (self.c >= c) & (self.c < self.c_size - 1)

            @pl.when(comes)
            def _(side=side):
                self.along(c, side).wait_recv()
                value = self.total[c] + self.along_in[side, c].astype(F32)

                @pl.when(self.c == c)
                def _():
                    self.total[c] = value

                @pl.when(self.c != c)
                def _():
                    self.along_out[side, c] = value.astype(BF16)
                    self.along(c, side).start()

    def end(self):
        self.out[...] = self.total[self.c]
        for c in range(self.c_size):
            for step in range(1, self.f_size):
                self.over(c, step).wait_send()
            for side in (1, 0):

                @pl.when(self.c < c if side else self.c > c)
                def _(side=side):
                    self.along(c, side).wait_send()


def last_kernel(
    qkv_ref,
    logit_ref,
    forget_ref,
    qkv_w,
    forget_w,
    gate_w,
    x_ref,
    grad_ref,
    gain_ref,
    part_ref,
    extra_ref,
    out_ref,
    sum_ref,
    vector_ref,
    *refs,
):
    buffers, weight_buffers = refs[:4], refs[4:8]
    mine, near_in, group_in = refs[8:11]
    sems, weight_sum_sems, vector_sems = refs[11:15], refs[15:19], refs[19:]
    me, sibling, across, diagonal = tp_places()
    others = group_peers()
    greet_all([{"tp": sibling}, {"tp": across}, {"tp": diagonal}] + others)
    weights = WeightSum(part_ref, sum_ref, weight_buffers, weight_sum_sems)
    weights.begin()
    mine[...] = extra_ref[...]
    size = x_ref.shape[0] // CHUNKS

    def span(chunk):
        return pl.ds(pl.multiple_of(chunk * size, size), size)

    def partial(slot, chunk):
        value = dot(qkv_ref[slot, span(chunk)], qkv_w[...], NT)
        value = value + dot(logit_ref[slot, span(chunk)], gate_w[...], NT)
        return value + dot(forget_ref[slot, span(chunk)], forget_w[...], NT)

    def finish(chunk, total):
        x = x_ref[span(chunk)].astype(F32)
        inverse = lax.rsqrt(jnp.mean(x * x, axis=1, keepdims=True) + epsilon)
        unit = x * inverse
        mine[0:1] += jnp.sum(total * unit, axis=0, keepdims=True)
        scaled = total * gain_ref[...]
        middle = jnp.mean(scaled * unit, axis=1, keepdims=True)
        out_ref[span(chunk)] = (grad_ref[span(chunk)] + inverse * (scaled - unit * middle)).astype(BF16)

    order = weights.order
    tasks = []
    for turn, c in enumerate(order):
        tasks.append((weights.receive, c))
        if turn:
            tasks.append((weights.advance, order[turn - 1]))
    tasks.append((weights.advance, order[-1]))
    share = -(-len(tasks) // CHUNKS)

    def between(chunk):
        for task, c in tasks[chunk * share : (chunk + 1) * share]:
            task(c)

    scatter_loop(buffers, sems, partial, finish, between=between)
    near_send, near_recv, group_send, group_recv = vector_sems
    copies = []
    for n, peer in enumerate((sibling, across, diagonal)):
        copies.append(sending(mine, near_in.at[n], near_send.at[n], near_recv.at[n], peer))
        copies[-1].start()
    for copy in copies:
        copy.wait()
    vector_ref[...] = mine[...] + near_in[0] + near_in[1] + near_in[2]
    mine[...] = vector_ref[...]
    copies = []
    for n, peer in enumerate(others):
        copies.append(moving(mine, group_in.at[n], group_send.at[n], group_recv.at[n], peer))
        copies[-1].start()
    for n, copy in enumerate(copies):
        copy.wait()
        vector_ref[...] += group_in[n]
    weights.end()


def last(grad_qkv, grad_logit, grad_forget, full_one, full_two, column, x, grad_hidden, gain, part, extra, f_size, c_size, ident):
    rows, model_width = x.shape
    wide, inner = grad_qkv.shape[2], grad_logit.shape[2]
    shard, columns = part.shape[0] // (f_size * c_size), part.shape[1]
    dma = pltpu.SemaphoreType.DMA
    return pl.pallas_call(
        last_kernel,
        grid=(1,),
        out_shape=[
            jax.ShapeDtypeStruct(x.shape, BF16),
            jax.ShapeDtypeStruct((shard, columns), F32),
            jax.ShapeDtypeStruct(extra.shape, F32),
        ],
        in_specs=[
            whole(grad_qkv.shape),
            whole(grad_logit.shape),
            whole(grad_forget.shape),
            whole((model_width, wide), 0),
            whole((model_width, LANES), wide // LANES),
            whole((model_width, inner), column),
            whole(x.shape),
            whole(x.shape),
            whole(gain.shape),
            whole(part.shape),
            whole(extra.shape),
        ],
        out_specs=[whole(x.shape), whole((shard, columns)), whole(extra.shape)],
        scratch_shapes=scatter_buffers(rows, model_width)
        + [
            pltpu.VMEM((f_size, c_size, shard, columns), BF16),
            pltpu.VMEM((c_size, shard, columns), F32),
            pltpu.VMEM((2, c_size, shard, columns), BF16),
            pltpu.VMEM((2, c_size, shard, columns), BF16),
            pltpu.VMEM(extra.shape, F32),
            pltpu.VMEM((3,) + extra.shape, F32),
            pltpu.VMEM((f_size * c_size - 1,) + extra.shape, F32),
        ]
        + SCATTER_SEMS
        + [dma((f_size, c_size))] * 2
        + [dma((2, c_size))] * 2
        + [dma((3,))] * 2
        + [dma((f_size * c_size - 1,))] * 2,
        compiler_params=remote_params(ident, 60),
        cost_estimate=pl.CostEstimate(
            flops=8 * rows * model_width * (wide + inner + LANES), bytes_accessed=100 << 20, transcendentals=0
        ),
        name="last",
    )(grad_qkv, grad_logit, grad_forget, full_one, full_one, full_two, x, grad_hidden, gain, part, extra)


def to_sibling(values):
    return lax.ppermute(values, "tp", [(i, i + 1 - 2 * (i % 2)) for i in range(4)])


def to_across(values):
    return lax.ppermute(values, "tp", [(i, (i + 2) % 4) for i in range(4)])


def relative_rows(rows):
    far = to_across(rows)
    return jnp.stack([rows, to_sibling(rows), far, to_sibling(far)])


def summed_rows(partial):
    own, near, far, corner = (partial[n] for n in range(4))
    corner = to_sibling(corner.astype(BF16)).astype(F32)
    near = to_sibling(near.astype(BF16)).astype(F32)
    far = to_across((far + corner).astype(BF16)).astype(F32)
    return own + near + far


def per_device(
    layer_input,
    lengths,
    attn_gain,
    w_query,
    w_key,
    w_value,
    w_forget,
    forget_bias,
    w_gate_out,
    w_out,
    mlp_gain,
    w_gate,
    w_up,
    w_down,
    cotangent,
):
    local_rows, seq_count, model_width = layer_input.shape
    head_count = forget_bias.shape[0]
    inner_width = w_query.shape[1]
    hidden = w_gate.shape[1]
    head_size = inner_width // head_count
    tp_size = lax.axis_size("tp")
    ctx_size = lax.axis_size("ctx")
    shard_count = lax.axis_size("fsdp") * ctx_size
    ctx_rows = local_rows * tp_size
    seq_len = ctx_rows * ctx_size
    all_rows = seq_count * ctx_rows
    ctx_index = lax.axis_index("ctx")
    tp_index = lax.axis_index("tp")
    shard_index = lax.axis_index("fsdp") * ctx_size + ctx_index

    pair = LANES // head_size
    groups = head_count // pair
    width = pair * head_size
    item_count = pl.cdiv(seq_count * groups, ctx_size)
    used = seq_count * groups

    def place(slot):
        slot = slot % used
        return (slot // groups + slot % groups) % seq_count, slot % groups

    places = tuple(place(slot) for slot in range(ctx_size * item_count))
    layout = (seq_count, groups, width, places)

    weights = ("fsdp", "ctx")
    packed_one = jnp.concatenate(
        [
            w_query,
            w_key,
            w_value,
            w_forget,
            attn_gain[:, None],
            mlp_gain[:, None],
            jnp.zeros((attn_gain.shape[0], LANES - head_count - 2), BF16),
        ],
        axis=1,
    )
    packed_two = jnp.concatenate([w_gate, w_up, w_down, w_out, w_gate_out], axis=1)
    full_two = lax.all_gather(packed_two, weights, axis=0, tiled=True)
    edge = 3 * inner_width
    input_rows = layer_input.transpose(1, 0, 2).reshape(seq_count * local_rows, model_width)
    input_all, full_one = startup(input_rows, packed_one, lax.axis_size("fsdp"), ctx_size, 1)
    gains = full_one[:, edge + head_count : edge + head_count + 2].astype(F32).T
    gain_one, gain_two = gains[0:1], gains[1:2]
    down_w = full_two[:, 2 * hidden : 3 * hidden]
    out_column = 3 * hidden // inner_width
    gate_out_w = full_two[:, 3 * hidden + inner_width :]

    def by_sequence(rows):
        return rows.transpose(1, 0, 2).reshape(seq_count * local_rows, model_width)

    def by_position(rows):
        return rows.reshape(seq_count, local_rows, model_width).transpose(1, 0, 2)

    local_pos = (ctx_index * tp_size + tp_index) * local_rows + jnp.arange(
        local_rows, dtype=jnp.int32
    )
    valid_rows = (local_pos[None, :] < lengths[:, None]).astype(F32)
    valid_rows = valid_rows.reshape(seq_count * local_rows, 1)
    ctx_pos = ctx_index * ctx_rows + jnp.arange(ctx_rows, dtype=jnp.int32)
    ctx_pos = ctx_pos.reshape(tp_size, 1, local_rows)
    ctx_valid = (ctx_pos < lengths[None, :, None]).astype(F32)

    grad_out = (valid_rows * by_sequence(cotangent).astype(F32)).astype(BF16)
    normed_one, forget_rows, items = project(
        input_all, gain_one, full_one, layout, item_count, ctx_size
    )
    normed_flat = normed_one.reshape(all_rows, model_width)
    forget_logit = forget_rows.reshape(all_rows, LANES)[:, :head_count].T
    forget_logit = forget_logit + forget_bias.astype(F32)[:, None]
    forget_logit = forget_logit.reshape(head_count, tp_size, seq_count, local_rows)
    log_forget = (ctx_valid[None] * jax.nn.log_sigmoid(forget_logit)).astype(BF16)

    cut = log_forget.astype(F32).reshape(groups, pair, tp_size, seq_count, local_rows)
    picked = jnp.stack([cut[g, :, :, s] for s, g in places])
    picked = picked.reshape(ctx_size, item_count, pair, ctx_rows).transpose(1, 0, 2, 3)
    picked = jnp.pad(picked, ((0, 0), (0, 0), (0, 8 - pair), (0, 0)))
    attended_items, qkv, exact, lse, decay = context(items, picked, head_size, 7)
    gate_logit = dot(normed_flat, gate_out_w, NN)
    out_gate = jax.nn.sigmoid(gate_logit).reshape(tp_size, -1, inner_width)
    grad_all = relative_rows(grad_out)
    hidden_state, normed_two, attended, mixed = out_project(
        input_rows, out_gate, full_two, out_column, gain_two, attended_items, layout, 2
    )
    normed_two_all, inner_act, grad_pair = mlp(normed_two, grad_all, full_two, hidden, 3)
    normed_two_flat = normed_two_all.reshape(all_rows, model_width)
    inner_flat = inner_act.reshape(all_rows, hidden)
    grad_pair_flat = grad_pair.reshape(all_rows, 2 * hidden)
    grad_flat = grad_all.reshape(all_rows, model_width)

    def owned_sum(part):
        total = lax.psum_scatter(part, weights, scatter_dimension=0, tiled=True)
        return total.astype(F32)

    mlp_part = jnp.concatenate(
        [
            dot(normed_two_flat, grad_pair_flat, TN).astype(BF16),
            dot(grad_flat, inner_flat, TN).astype(BF16),
        ],
        axis=1,
    )
    mlp_part, grad_pair = lax.optimization_barrier((mlp_part, grad_pair))
    mlp_sum = owned_sum(mlp_part)
    grad_hidden, branch, mlp_gain_part = mlp_back(
        grad_pair, full_two, hidden_state, grad_out, gain_two, 4
    )
    feedforward = summed_rows(dot(inner_flat, down_w, NT).reshape(tp_size, -1, model_width))
    output = (valid_rows * (hidden_state + feedforward)).astype(BF16)

    branch_all, grad_gate_logit, grads = out_back(
        branch, full_two, out_column, out_gate, attended, layout, item_count, ctx_size, 5
    )
    branch_flat = branch_all.reshape(all_rows, model_width)
    logit_flat = grad_gate_logit.reshape(all_rows, inner_width)

    grad_items, forget_items = context_back(grads, qkv, exact, lse, decay, head_size, 8)
    out_part = jnp.concatenate(
        [
            dot(branch_flat, mixed.reshape(all_rows, inner_width), TN).astype(BF16),
            dot(normed_flat, logit_flat, TN).astype(BF16),
        ],
        axis=1,
    )
    out_sum = owned_sum(out_part)

    forget_back = forget_items[:, :, :pair].astype(BF16).transpose(1, 0, 2, 3)
    forget_back = forget_back.reshape(ctx_size * item_count, pair, tp_size, local_rows)
    slots = {place(slot): slot for slot in range(used)}
    forget_back = jnp.stack(
        [
            jnp.stack([forget_back[slots[s, g]] for s in range(seq_count)], axis=2)
            for g in range(groups)
        ]
    ).reshape(head_count, tp_size, seq_count, local_rows)
    grad_forget_logit = forget_back.astype(F32) * ctx_valid[None] * jax.nn.sigmoid(-forget_logit)
    grad_forget_logit = grad_forget_logit.astype(BF16).reshape(head_count, all_rows)
    bias_part = jnp.sum(grad_forget_logit.astype(F32), axis=1)
    grad_forget_rows = jnp.pad(grad_forget_logit, ((0, LANES - head_count), (0, 0))).T
    grad_qkv = assemble(grad_items, layout, tp_size)
    grad_qkvf = jnp.concatenate([grad_qkv.reshape(all_rows, edge), grad_forget_rows], axis=1)
    bias_full = lax.dynamic_update_slice(
        jnp.zeros((1, model_width), F32), bias_part[None], (0, tp_index * head_count)
    )
    extra = jnp.concatenate(
        [jnp.zeros_like(bias_full), mlp_gain_part, bias_full, jnp.zeros((5, model_width), F32)]
    )
    input_grad, qkv_sum, vectors = last(
        grad_qkv,
        grad_gate_logit,
        grad_forget_rows.reshape(tp_size, -1, LANES),
        full_one,
        full_two,
        out_column + 1,
        input_rows,
        grad_hidden,
        gain_one,
        dot(normed_flat, grad_qkvf, TN).astype(BF16),
        extra,
        lax.axis_size("fsdp"),
        ctx_size,
        6,
    )
    gain_one_sum, gain_two_sum, bias_sum = vectors[0], vectors[1], vectors[2]
    shard_rows = model_width // shard_count
    attn_gain_grad = lax.dynamic_slice_in_dim(gain_one_sum, shard_index * shard_rows, shard_rows, 0)
    mlp_gain_grad = lax.dynamic_slice_in_dim(gain_two_sum, shard_index * shard_rows, shard_rows, 0)
    forget_bias_grad = lax.dynamic_slice_in_dim(bias_sum, tp_index * head_count, head_count, 0)
    wide = inner_width
    return (
        by_position(output),
        by_position(input_grad),
        attn_gain_grad,
        qkv_sum[:, :wide],
        qkv_sum[:, wide : 2 * wide],
        qkv_sum[:, 2 * wide : 3 * wide],
        qkv_sum[:, 3 * wide : 3 * wide + head_count],
        forget_bias_grad,
        out_sum[:, wide:],
        out_sum[:, :wide],
        mlp_gain_grad,
        mlp_sum[:, :hidden],
        mlp_sum[:, hidden : 2 * hidden],
        mlp_sum[:, 2 * hidden :],
    )


def solution(mesh):
    rows = P(("ctx", "tp"), "fsdp", None)
    matrix = P(("fsdp", "ctx"), "tp")
    vector = P(("fsdp", "ctx"))
    return jax.shard_map(
        per_device,
        mesh=mesh,
        in_specs=(
            rows,
            P("fsdp"),
            vector,
            matrix,
            matrix,
            matrix,
            matrix,
            P("tp"),
            matrix,
            matrix,
            vector,
            matrix,
            matrix,
            matrix,
            rows,
        ),
        out_specs=(
            rows,
            rows,
            vector,
            matrix,
            matrix,
            matrix,
            matrix,
            P("tp"),
            matrix,
            matrix,
            vector,
            matrix,
            matrix,
            matrix,
        ),
        check_vma=False,
    )
```

```python
import functools

import jax
import jax.numpy as jnp
from jax import lax
from jax.experimental import pallas as pl
from jax.experimental.pallas import tpu as pltpu
from jax.sharding import PartitionSpec as P

F32 = jnp.float32
BF16 = jnp.bfloat16
LANES = 128
MESH = pl.DeviceIdType.MESH
epsilon = 1e-06
masked_score = -1e30
NT = (((1,), (1,)), ((), ()))
NN = (((1,), (0,)), ((), ()))
TN = (((0,), (0,)), ((), ()))


def dot(left, right, dims):
    return lax.dot_general(left, right, dims, preferred_element_type=F32)


def of_head(block, head, head_size, ones_at=None):
    lane = lax.broadcasted_iota(jnp.int32, block.shape, 1)
    out = jnp.where(lane // head_size == head, block, jnp.zeros_like(block))
    if ones_at is not None:
        out = jnp.where(lane == ones_at, jnp.ones_like(block), out)
    return out


def spare_lane(head, head_size):
    return ((head + 1) % 2) * head_size


def attend_item(qkv, decay, out, exact, lse, heads, head_size):
    count, _, block, width = qkv.shape
    scale = head_size**-0.5
    row = lax.broadcasted_iota(jnp.int32, (block, block), 0)
    column = lax.broadcasted_iota(jnp.int32, (block, block), 1)
    causal = column <= row

    def query_block(i, _):
        query = qkv[i, 0]
        lanes = pl.ds(pl.multiple_of(i * block, block), block)
        result = jnp.zeros((block, width), F32)
        for head in range(heads):
            query_head = of_head(query, head, head_size)

            def step(j, carry, masked):
                top, total, acc = carry
                keys = pl.ds(pl.multiple_of(j * block, block), block)
                score = dot(query_head, qkv[j, 1], NT) * scale
                score = score - decay[head : head + 1, keys]
                if masked:
                    score = jnp.where(causal, score, masked_score)
                new_top = jnp.maximum(top, jnp.max(score, axis=1, keepdims=True))
                prob = jnp.exp(score - new_top)
                shrink = jnp.exp(top - new_top)
                total = total * shrink + jnp.sum(prob, axis=1, keepdims=True)
                acc = acc * shrink + dot(prob.astype(BF16), qkv[j, 2], NN)
                return new_top, total, acc

            carry = (
                jnp.full((block, 1), masked_score, F32),
                jnp.zeros((block, 1), F32),
                jnp.zeros((block, width), F32),
            )
            carry = lax.fori_loop(0, i, lambda j, c: step(j, c, False), carry)
            top, total, acc = step(i, carry, True)
            lane = lax.broadcasted_iota(jnp.int32, acc.shape, 1)
            result = jnp.where(lane // head_size == head, acc / total, result)
            stat = jnp.broadcast_to(top + jnp.log(total), (block, LANES)).T
            lse[head : head + 1, lanes] = stat[0:1]
        exact[i] = result
        out[i] = result.astype(BF16)
        return 0

    lax.fori_loop(0, count, query_block, 0)


def attend_item_back(qkv, grads, exact, lse, decay, dqkv, change, dq_acc, delta, heads, head_size):
    count, _, block, width = qkv.shape
    scale = head_size**-0.5
    row = lax.broadcasted_iota(jnp.int32, (block, block), 0)
    column = lax.broadcasted_iota(jnp.int32, (block, block), 1)
    causal = row <= column
    dq_acc[...] = jnp.zeros_like(dq_acc)
    change[...] = jnp.zeros_like(change)

    def prepare(i, _):
        lanes = pl.ds(pl.multiple_of(i * block, block), block)
        product = grads[i].astype(F32) * exact[i]
        lane = lax.broadcasted_iota(jnp.int32, product.shape, 1)
        for head in range(heads):
            part = jnp.where(lane // head_size == head, product, 0.0)
            part = jnp.sum(part, axis=1, keepdims=True)
            delta[head : head + 1, lanes] = jnp.broadcast_to(part, (block, LANES)).T[0:1]
        return 0

    lax.fori_loop(0, count, prepare, 0)

    def key_block(j, _):
        keys = pl.ds(pl.multiple_of(j * block, block), block)
        key = qkv[j, 1]
        value = qkv[j, 2]
        value_total = jnp.zeros((block, width), F32)
        key_total = jnp.zeros((block, width), F32)
        for head in range(heads):
            spare = spare_lane(head, head_size)
            key_ones = of_head(key, head, head_size, spare)
            fall = jnp.broadcast_to(decay[head : head + 1, keys], (LANES, block)).T[:, 0:1]

            def step(i, carry, masked):
                value_acc, key_acc = carry
                lanes = pl.ds(pl.multiple_of(i * block, block), block)
                query = qkv[i, 0]
                grad = of_head(grads[i], head, head_size)
                score = dot(key, of_head(query, head, head_size), NT) * scale
                score = score - fall - lse[head : head + 1, lanes]
                if masked:
                    score = jnp.where(causal, score, masked_score)
                prob = jnp.exp(score)
                grad_prob = dot(value, grad, NT)
                grad_score = prob * (grad_prob - delta[head : head + 1, lanes])
                grad_score = grad_score.astype(BF16)
                value_acc = value_acc + dot(prob.astype(BF16), grad, NN)
                query_ones = of_head(query, head, head_size, spare)
                key_acc = key_acc + dot(grad_score, query_ones, NN)
                dq_acc[head, i] += dot(grad_score, key_ones, TN)
                return value_acc, key_acc

            zero = jnp.zeros((block, width), F32)
            carry = step(j, (zero, zero), True)
            carry = lax.fori_loop(j + 1, count, lambda i, c: step(i, c, False), carry)
            value_acc, key_acc = carry
            value_total = value_total + value_acc
            lane = lax.broadcasted_iota(jnp.int32, key_acc.shape, 1)
            key_total = jnp.where(lane // head_size == head, key_acc, key_total)
            change[head : head + 1, keys] -= key_acc.T[spare : spare + 1]
        dqkv[j, 1] = (key_total * scale).astype(BF16)
        dqkv[j, 2] = value_total.astype(BF16)
        return 0

    lax.fori_loop(0, count, key_block, 0)

    def finish(i, _):
        lanes = pl.ds(pl.multiple_of(i * block, block), block)
        total = jnp.zeros((block, width), F32)
        for head in range(heads):
            spare = spare_lane(head, head_size)
            part = dq_acc[head, i]
            lane = lax.broadcasted_iota(jnp.int32, part.shape, 1)
            total = jnp.where(lane // head_size == head, part, total)
            change[head : head + 1, lanes] += part.T[spare : spare + 1]
        dqkv[i, 0] = (total * scale).astype(BF16)
        return 0

    lax.fori_loop(0, count, finish, 0)


def triangle(upward):
    row = lax.broadcasted_iota(jnp.int32, (LANES, LANES), 0)
    column = lax.broadcasted_iota(jnp.int32, (LANES, LANES), 1)
    keep = (row <= column) if upward else (row >= column)
    return jnp.where(keep, 1.0, 0.0).astype(BF16)


def exact_product(values, matrix):
    high = values.astype(BF16)
    rest = values - high.astype(F32)
    middle = rest.astype(BF16)
    low = (rest - middle.astype(F32)).astype(BF16)
    return dot(high, matrix, NN) + dot(middle, matrix, NN) + dot(low, matrix, NN)


def ctx_sending(source, target, send_sem, recv_sem, peer):
    return pltpu.make_async_remote_copy(
        src_ref=source,
        dst_ref=target,
        send_sem=send_sem,
        recv_sem=recv_sem,
        device_id={"ctx": peer},
        device_id_type=MESH,
    )


def ctx_greet(size):
    me = lax.axis_index("ctx")
    barrier = pltpu.get_barrier_semaphore()
    for step in range(1, size):
        peer = lax.rem(me + step, size)
        pl.semaphore_signal(barrier, inc=1, device_id={"ctx": peer}, device_id_type=MESH)
    pl.semaphore_wait(barrier, size - 1)
    return me


class Exchange:
    def __init__(self, me, size, source, target, sems):
        self.me, self.size, self.source, self.target = me, size, source, target
        self.send_sem, self.recv_sem, self.own_sem = sems

    def own(self, item):
        return pltpu.make_async_copy(
            self.source.at[item, self.me], self.target.at[item, self.me], self.own_sem.at[item]
        )

    def copy(self, item, step):
        peer = lax.rem(self.me + step, self.size)
        return ctx_sending(
            self.source.at[item, peer],
            self.target.at[item, self.me],
            self.send_sem.at[item, step],
            self.recv_sem.at[item, step],
            peer,
        )

    def start(self, item):
        self.own(item).start()
        for step in range(1, self.size):
            self.copy(item, step).start()

    def arrive(self, item):
        self.own(item).wait()
        for step in range(1, self.size):
            self.copy(item, step).wait_recv()

    def drain(self, item):
        for step in range(1, self.size):
            self.copy(item, step).wait_send()


def exchange_sems(items, size):
    return [
        pltpu.SemaphoreType.DMA((items, size)),
        pltpu.SemaphoreType.DMA((items, size)),
        pltpu.SemaphoreType.DMA((items,)),
    ]


def context_kernel(
    heads,
    head_size,
    items_ref,
    forget_ref,
    shard_ref,
    back_ref,
    qkv_ref,
    full_ref,
    exact_ref,
    lse_ref,
    decay_ref,
    *refs,
):
    qkv, forget, out, save_sem = refs[:4]
    sems = refs[4:]
    count, size, _, block, width = items_ref.shape
    greet_all(group_peers())
    me = lax.axis_index("ctx")
    gather = WeightGather(shard_ref, full_ref, sems[9:])
    forgets = Exchange(me, size, forget_ref, forget, sems[0:3])
    inputs = Exchange(me, size, items_ref, qkv, sems[3:6])
    results = Exchange(me, size, out, back_ref, sems[6:9])

    @pl.loop(0, count)
    def _(item):
        forgets.start(item)

    inputs.start(0)
    gather.begin()

    @pl.loop(0, count)
    def _(item):
        forgets.arrive(item)

    @pl.loop(0, count)
    def _(item):
        upper = triangle(True)
        before = jnp.zeros((8, 1), F32)
        for start in range(0, size * block, LANES):
            part = forget[item, start // block, :, pl.ds(start % block, LANES)]
            total = before + dot(part.astype(BF16), upper, NN)
            decay_ref[item, :, pl.ds(start, LANES)] = total
            before = total[:, LANES - 1 :]

    lse_ref[...] = jnp.zeros_like(lse_ref)

    @pl.loop(0, count)
    def _(item):
        @pl.when(item + 1 < count)
        def _():
            inputs.start(item + 1)

        inputs.arrive(item)
        saving = pltpu.make_async_copy(qkv.at[item], qkv_ref.at[item], save_sem)
        saving.start()
        attend_item(
            qkv.at[item], decay_ref.at[item], out.at[item], exact_ref.at[item], lse_ref.at[item], heads, head_size
        )
        results.start(item)
        saving.wait()
        for hop in range(1, min(size, count + 1)):

            @pl.when(item == hop - 1)
            def _(hop=hop):
                gather.advance(hop)

    for hop in range(count + 1, size):
        gather.advance(hop)

    @pl.loop(0, count)
    def _(item):
        forgets.drain(item)
        inputs.drain(item)
        results.arrive(item)
        results.drain(item)

    gather.end()


def full_block(shape):
    return pl.BlockSpec(shape, lambda i: (0,) * len(shape), pipeline_mode=pl.Buffered(1))


def attend_cost(items, heads, products):
    count, size, _, block, width = items.shape
    pairs = count * heads * (size * block) ** 2 // 2
    return pl.CostEstimate(
        flops=2 * products * pairs * 256, bytes_accessed=100 << 20, transcendentals=pairs
    )


def context(items, forget, shard, f_size, head_size, ident):
    count, size, _, block, width = items.shape
    heads = width // head_size
    place = pl.BlockSpec(memory_space=pl.ANY)
    exact, stat = (count, size, block, width), (count, 8, size * block)
    return pl.pallas_call(
        functools.partial(context_kernel, heads, head_size),
        grid=(1,),
        out_shape=[
            jax.ShapeDtypeStruct(exact, BF16),
            jax.ShapeDtypeStruct(items.shape, BF16),
            jax.ShapeDtypeStruct((shard.shape[0] * f_size * size, shard.shape[1]), BF16),
            jax.ShapeDtypeStruct(exact, F32),
            jax.ShapeDtypeStruct(stat, F32),
            jax.ShapeDtypeStruct(stat, F32),
        ],
        in_specs=[place, place, place],
        out_specs=[place, place, place, full_block(exact), full_block(stat), full_block(stat)],
        scratch_shapes=[
            pltpu.VMEM(items.shape, BF16),
            pltpu.VMEM(forget.shape, F32),
            pltpu.VMEM(exact, BF16),
            pltpu.SemaphoreType.DMA,
        ]
        + exchange_sems(count, size) * 3
        + weight_sems(f_size, size),
        compiler_params=remote_params(ident, 48),
        cost_estimate=attend_cost(items, heads, 2),
        name="context",
    )(items, forget, shard)


def context_back_kernel(
    heads,
    head_size,
    items_ref,
    qkv_ref,
    exact_ref,
    lse_ref,
    decay_ref,
    part_ref,
    back_ref,
    forget_ref,
    sum_ref,
    *refs,
):
    grads, dqkv, change, slope, dq_acc, delta = refs[:6]
    sems = refs[6:15]
    count, size, block, width = items_ref.shape
    greet_all(group_peers())
    me = lax.axis_index("ctx")
    weights = WeightSum(part_ref, 0, sum_ref, refs[15:])
    inputs = Exchange(me, size, items_ref, grads, sems[0:3])
    results = Exchange(me, size, dqkv, back_ref, sems[3:6])
    forgets = Exchange(me, size, slope, forget_ref, sems[6:9])

    @pl.loop(0, count)
    def _(item):
        inputs.start(item)

    weights.begin()

    @pl.loop(0, count)
    def _(item):
        inputs.arrive(item)
        attend_item_back(
            qkv_ref.at[item],
            grads.at[item],
            exact_ref.at[item],
            lse_ref.at[item],
            decay_ref.at[item],
            dqkv.at[item],
            change,
            dq_acc,
            delta,
            heads,
            head_size,
        )
        results.start(item)
        lower = triangle(False)
        after = jnp.zeros((8, 1), F32)
        for start in reversed(range(0, size * block, LANES)):
            total = after + exact_product(change[:, pl.ds(start, LANES)], lower)
            slope[item, start // block, :, pl.ds(start % block, LANES)] = total
            after = total[:, 0:1]
        forgets.start(item)

        @pl.when(item == count - 2)
        def _():
            for c in weights.order:
                weights.receive(c)

    for c in weights.order:
        weights.advance(c)

    @pl.loop(0, count)
    def _(item):
        inputs.drain(item)
        results.arrive(item)
        results.drain(item)
        forgets.arrive(item)
        forgets.drain(item)

    weights.end()


def context_back(grads, qkv, exact, lse, decay, part, f_size, head_size, ident):
    count, size, _, block, width = qkv.shape
    heads = width // head_size
    place = pl.BlockSpec(memory_space=pl.ANY)
    forget = (count, size, 8, block)
    total = (part.shape[0] // (f_size * size), part.shape[1])
    return pl.pallas_call(
        functools.partial(context_back_kernel, heads, head_size),
        grid=(1,),
        out_shape=[
            jax.ShapeDtypeStruct(qkv.shape, BF16),
            jax.ShapeDtypeStruct(forget, F32),
            jax.ShapeDtypeStruct(total, F32),
        ],
        in_specs=[
            place,
            full_block(qkv.shape),
            full_block(exact.shape),
            full_block(lse.shape),
            full_block(decay.shape),
            place,
        ],
        out_specs=[place, place, full_block(total)],
        scratch_shapes=[
            pltpu.VMEM(grads.shape, BF16),
            pltpu.VMEM(qkv.shape, BF16),
            pltpu.VMEM((8, size * block), F32),
            pltpu.VMEM(forget, F32),
            pltpu.VMEM((heads, size, block, width), F32),
            pltpu.VMEM((8, size * block), F32),
        ]
        + exchange_sems(count, size) * 3
        + sum_scratch(f_size, size, *total),
        compiler_params=remote_params(ident, 56),
        cost_estimate=attend_cost(qkv, heads, 5),
        name="context_back",
    )(grads, qkv, exact, lse, decay, part)


CHUNKS = 4


def tp_places():
    me = lax.axis_index("tp")
    sibling = me + 1 - 2 * lax.rem(me, 2)
    across = lax.rem(me + 2, 4)
    diagonal = lax.rem(sibling + 2, 4)
    return me, sibling, across, diagonal


def greet(peers):
    barrier = pltpu.get_barrier_semaphore()
    for peer in peers:
        pl.semaphore_signal(barrier, inc=1, device_id={"tp": peer}, device_id_type=MESH)
    pl.semaphore_wait(barrier, len(peers))


def sending(source, target, send_sem, recv_sem, peer):
    return pltpu.make_async_remote_copy(
        src_ref=source,
        dst_ref=target,
        send_sem=send_sem,
        recv_sem=recv_sem,
        device_id={"tp": peer},
        device_id_type=MESH,
    )


def pick(step, chunks, places):
    me, sibling, across, diagonal = places
    late = step - 2 * chunks
    far = jnp.where(lax.rem(late, 2) == 0, across, diagonal)
    slot = jnp.where(step < chunks, me, jnp.where(step < 2 * chunks, sibling, far))
    chunk = jnp.where(step < 2 * chunks, lax.rem(step, chunks), late // 2)
    return slot, chunk


def gather_loop(table, sems, compute, own=None, relative=False, between=None):
    near_send, near_recv, far_send, far_recv, pass_send, pass_recv = sems
    me, sibling, across, diagonal = tp_places()
    places = (0, 1, 2, 3) if relative else (me, sibling, across, diagonal)
    mine, near_by, far_off, corner = places
    near_spot, far_spot, pass_spot = (1, 2, 3) if relative else (me, me, across)
    rows = table.shape[1] // CHUNKS

    def part(slot, chunk):
        return table.at[slot, pl.ds(pl.multiple_of(chunk * rows, rows), rows)]

    def far(chunk):
        source = part(mine, chunk)
        if own is not None:
            source = own.at[pl.ds(pl.multiple_of(chunk * rows, rows), rows)]
        return sending(source, part(far_spot, chunk), far_send.at[chunk], far_recv.at[chunk], across)

    def far_arrival(chunk):
        spot = part(far_off, chunk)
        return sending(spot, spot, far_send.at[chunk], far_recv.at[chunk], across)

    def passing(chunk):
        return sending(
            part(far_off, chunk), part(pass_spot, chunk), pass_send.at[chunk], pass_recv.at[chunk], sibling
        )

    def pass_arrival(chunk):
        spot = part(corner, chunk)
        return sending(spot, spot, pass_send.at[chunk], pass_recv.at[chunk], sibling)

    for chunk in range(CHUNKS):
        far(chunk).start()
    own = table.at[mine] if own is None else own
    near = sending(own, table.at[near_spot], near_send, near_recv, sibling)
    near.start()

    def body(step, _):
        slot, chunk = pick(step, CHUNKS, places)
        late = step - 2 * CHUNKS

        @pl.when(step == CHUNKS)
        def _():
            spot = table.at[near_by]
            sending(spot, spot, near_send, near_recv, sibling).wait_recv()

        @pl.when((late >= 0) & (lax.rem(late, 2) == 0))
        def _():
            far_arrival(chunk).wait_recv()
            passing(chunk).start()

        @pl.when((late >= 0) & (lax.rem(late, 2) == 1))
        def _():
            pass_arrival(chunk).wait_recv()

        compute(slot, chunk)
        return 0

    if between is None:
        lax.fori_loop(0, 4 * CHUNKS, body, 0)
    else:
        lax.fori_loop(0, 2 * CHUNKS, body, 0)
        for turn in range(CHUNKS):
            between(turn)
            first = 2 * (CHUNKS + turn)
            lax.fori_loop(first, first + 2, body, 0)
    near.wait_send()
    for chunk in range(CHUNKS):
        far(chunk).wait_send()
        passing(chunk).wait_send()


GATHER_SEMS = [pltpu.SemaphoreType.DMA] * 2 + [pltpu.SemaphoreType.DMA((CHUNKS,))] * 4


def scatter_loop(buffers, sems, partial, finish, relative=False, between=None):
    near_out, near_in, far_out, far_in = buffers
    near_send, near_recv, far_send, far_recv = sems
    me, sibling, across, diagonal = tp_places()
    mine, near_by, far_off, corner = (0, 1, 2, 3) if relative else (me, sibling, across, diagonal)
    rows = far_out.shape[0] // CHUNKS

    def span(chunk):
        return pl.ds(pl.multiple_of(chunk * rows, rows), rows)

    def near(half, chunk):
        return sending(
            near_out.at[half, span(chunk)],
            near_in.at[half, span(chunk)],
            near_send.at[half, chunk],
            near_recv.at[half, chunk],
            sibling,
        )

    def far(chunk):
        return sending(
            far_out.at[span(chunk)],
            far_in.at[span(chunk)],
            far_send.at[chunk],
            far_recv.at[chunk],
            across,
        )

    def body(step, _):
        phase, chunk = step // CHUNKS, lax.rem(step, CHUNKS)
        slot = jnp.where(
            phase == 0, corner, jnp.where(phase == 1, far_off, jnp.where(phase == 2, near_by, mine))
        )
        value = partial(slot, chunk)
        spot = span(chunk)

        @pl.when(lax.rem(phase, 2) == 0)
        def _():
            half = phase // 2
            near_out[half, spot] = value.astype(BF16)
            near(half, chunk).start()

        @pl.when(phase == 1)
        def _():
            near(0, chunk).wait_recv()
            far_out[spot] = (value + near_in[0, spot].astype(F32)).astype(BF16)
            far(chunk).start()

        @pl.when(phase == 3)
        def _():
            near(1, chunk).wait_recv()
            far(chunk).wait_recv()
            finish(chunk, value + near_in[1, spot].astype(F32) + far_in[spot].astype(F32))

        return 0

    if between is None:
        lax.fori_loop(0, 4 * CHUNKS, body, 0)
    else:
        lax.fori_loop(0, 3 * CHUNKS, body, 0)
        for chunk in range(CHUNKS):
            between(chunk)
            lax.fori_loop(3 * CHUNKS + chunk, 3 * CHUNKS + chunk + 1, body, 0)
    for chunk in range(CHUNKS):
        near(0, chunk).wait_send()
        near(1, chunk).wait_send()
        far(chunk).wait_send()


SCATTER_SEMS = [pltpu.SemaphoreType.DMA((2, CHUNKS))] * 2 + [pltpu.SemaphoreType.DMA((CHUNKS,))] * 2


def scatter_buffers(rows, width):
    return [
        pltpu.VMEM((2, rows, width), BF16),
        pltpu.VMEM((2, rows, width), BF16),
        pltpu.VMEM((rows, width), BF16),
        pltpu.VMEM((rows, width), BF16),
    ]


def group_peers():
    f_size, c_size = lax.axis_size("fsdp"), lax.axis_size("ctx")
    f, c = lax.axis_index("fsdp"), lax.axis_index("ctx")
    return [
        {"fsdp": lax.rem(f + i, f_size), "ctx": lax.rem(c + j, c_size)}
        for i in range(f_size)
        for j in range(c_size)
        if i or j
    ]


def greet_all(peers):
    barrier = pltpu.get_barrier_semaphore()
    for peer in peers:
        pl.semaphore_signal(barrier, inc=1, device_id=peer, device_id_type=MESH)
    pl.semaphore_wait(barrier, len(peers))


def moving(source, target, send_sem, recv_sem, peer):
    return pltpu.make_async_remote_copy(
        src_ref=source,
        dst_ref=target,
        send_sem=send_sem,
        recv_sem=recv_sem,
        device_id=peer,
        device_id_type=MESH,
    )


class WeightGather:
    def __init__(self, shard, full, sems):
        self.shard, self.full = shard, full
        self.f_size, self.c_size = lax.axis_size("fsdp"), lax.axis_size("ctx")
        self.f, self.c = lax.axis_index("fsdp"), lax.axis_index("ctx")
        self.sems = sems

    def spot(self, c, f=None):
        rows = self.shard.shape[0]
        block = (self.f if f is None else f) * self.c_size + c
        return self.full.at[pl.ds(pl.multiple_of(block * rows, rows), rows)]

    def along(self, c, hop, side, source=None):
        source = self.spot(c) if source is None else source
        peer = {"ctx": self.c + (1 if side else -1)}
        return moving(
            source, self.spot(c), self.sems[0].at[side, hop], self.sems[1].at[side, hop], peer
        )

    def over(self, c, step, source=None):
        source = self.spot(c) if source is None else source
        peer = {"fsdp": lax.rem(self.f + step, self.f_size)}
        return moving(
            source, self.spot(c), self.sems[2].at[step, c], self.sems[3].at[step, c], peer
        )

    def over_arrival(self, c, step):
        spot = self.spot(c, lax.rem(self.f + self.f_size - step, self.f_size))
        peer = {"fsdp": lax.rem(self.f + step, self.f_size)}
        return moving(spot, spot, self.sems[2].at[step, c], self.sems[3].at[step, c], peer)

    def can(self, side):
        return self.c + 1 < self.c_size if side else self.c > 0

    def holds(self, hop, side):
        return self.c - hop >= 0 if side else self.c + hop < self.c_size

    def begin(self):
        pltpu.make_async_copy(self.shard, self.spot(self.c), self.sems[4]).start()
        for side in (1, 0):

            @pl.when(self.can(side))
            def _(side=side):
                self.along(self.c, 1, side, self.shard).start()

        for step in range(1, self.f_size):
            self.over(self.c, step, self.shard).start()

    def advance(self, hop):
        for side in (1, 0):

            @pl.when(self.holds(hop, side))
            def _(side=side):
                c = self.c - hop if side else self.c + hop
                self.along(c, hop, side).wait_recv()

                @pl.when(self.can(side))
                def _():
                    self.along(c, hop + 1, side).start()

                for step in range(1, self.f_size):
                    self.over(c, step).start()

    def end(self):
        pltpu.make_async_copy(self.shard, self.spot(self.c), self.sems[4]).wait()
        for step in range(1, self.f_size):
            for c in range(self.c_size):
                self.over_arrival(c, step).wait_recv()
                self.over(c, step).wait_send()
        for side in (1, 0):

            @pl.when(self.can(side))
            def _(side=side):
                self.along(self.c, 1, side, self.shard).wait_send()

            for hop in range(1, self.c_size):

                @pl.when(self.holds(hop, side) & self.can(side))
                def _(side=side, hop=hop):
                    c = self.c - hop if side else self.c + hop
                    self.along(c, hop + 1, side).wait_send()


def weight_sems(f_size, c_size):
    dma = pltpu.SemaphoreType.DMA
    return [dma((2, c_size + 1))] * 2 + [dma((f_size, c_size))] * 2 + [dma]


class WeightSum:
    def __init__(self, part, first_column, out, refs):
        self.part, self.out = part, out
        self.stage, self.total, self.along_in = refs[:3]
        self.own_sem, self.over_send, self.over_recv, self.along_send, self.along_recv = refs[3:]
        self.f_size, self.c_size = lax.axis_size("fsdp"), lax.axis_size("ctx")
        self.f, self.c = lax.axis_index("fsdp"), lax.axis_index("ctx")
        self.rows, columns = out.shape
        self.columns = pl.ds(first_column, columns)
        self.order = [
            (self.c_size - 1 - i // 2) if i % 2 == 0 else i // 2 for i in range(self.c_size)
        ]

    def piece(self, f, c):
        row = (f * self.c_size + c) * self.rows
        return self.part.at[pl.ds(pl.multiple_of(row, self.rows), self.rows), self.columns]

    def own(self, c):
        return pltpu.make_async_copy(self.piece(self.f, c), self.stage.at[c], self.own_sem.at[c])

    def over(self, c, step):
        f = lax.rem(self.f + step, self.f_size)
        return moving(
            self.piece(f, c),
            self.total.at[step - 1, c],
            self.over_send.at[step - 1, c],
            self.over_recv.at[step - 1, c],
            {"fsdp": f},
        )

    def along(self, c, side, source=None):
        peer = {"ctx": self.c + (1 if side else -1)}
        target = self.along_in.at[side, c]
        return moving(
            target if source is None else source,
            target,
            self.along_send.at[side, c],
            self.along_recv.at[side, c],
            peer,
        )

    def begin(self):
        for c in self.order:
            self.own(c).start()
            for step in range(1, self.f_size):
                self.over(c, step).start()

    def receive(self, c):
        self.own(c).wait()
        value = self.stage[c].astype(F32)
        for step in range(1, self.f_size):
            self.over(c, step).wait_recv()
            value = value + self.total[step - 1, c].astype(F32)
        self.total[0, c] = value.astype(BF16)
        for side, end in ((1, 0), (0, self.c_size - 1)):

            @pl.when((self.c == end) & (self.c != c))
            def _(side=side):
                self.along(c, side, self.total.at[0, c]).start()

    def advance(self, c):
        for side in (1, 0):
            comes = (self.c > 0) & (self.c <= c) if side else (self.c >= c) & (self.c < self.c_size - 1)

            @pl.when(comes)
            def _(side=side):
                self.along(c, side).wait_recv()
                value = self.total[0, c].astype(F32) + self.along_in[side, c].astype(F32)

                @pl.when(self.c == c)
                def _():
                    self.total[0, c] = value.astype(BF16)

                @pl.when(self.c != c)
                def _():
                    self.along_in[side, c] = value.astype(BF16)
                    self.along(c, side).start()

    def tasks(self):
        found = []
        for turn, c in enumerate(self.order):
            found.append(functools.partial(self.receive, c))
            if turn:
                found.append(functools.partial(self.advance, self.order[turn - 1]))
        return found + [functools.partial(self.advance, self.order[-1])]

    def end(self):
        self.out[...] = self.total[0, self.c].astype(F32)
        for c in range(self.c_size):
            for step in range(1, self.f_size):
                self.over(c, step).wait_send()
            for side in (1, 0):

                @pl.when(self.c < c if side else self.c > c)
                def _(side=side):
                    self.along(c, side).wait_send()


SUM_REFS = 8


def sum_scratch(f_size, c_size, rows, columns):
    dma = pltpu.SemaphoreType.DMA
    return (
        [
            pltpu.VMEM((c_size, rows, columns), BF16),
            pltpu.VMEM((f_size - 1, c_size, rows, columns), BF16),
            pltpu.VMEM((2, c_size, rows, columns), BF16),
        ]
        + [dma((c_size,))]
        + [dma((f_size - 1, c_size))] * 2
        + [dma((2, c_size))] * 2
    )


def shared(tasks, turn, turns):
    share = -(-len(tasks) // turns)
    for task in tasks[turn * share : (turn + 1) * share]:
        task()


def startup_kernel(rows_ref, shard_ref, all_ref, full_ref, own_sem, *sems):
    me, sibling, across, diagonal = tp_places()
    greet_all([{"tp": sibling}, {"tp": across}] + group_peers())
    near_send, near_recv, far_send, far_recv, pass_send, pass_recv = sems[:6]
    gather = WeightGather(shard_ref, full_ref, sems[6:])
    size = rows_ref.shape[0] // CHUNKS
    own = pltpu.make_async_copy(rows_ref, all_ref.at[me], own_sem)
    own.start()

    def span(chunk):
        return pl.ds(chunk * size, size)

    def far(chunk):
        return sending(
            rows_ref.at[span(chunk)],
            all_ref.at[me, span(chunk)],
            far_send.at[chunk],
            far_recv.at[chunk],
            across,
        )

    def passing(chunk):
        spot = all_ref.at[across, span(chunk)]
        return sending(spot, spot, pass_send.at[chunk], pass_recv.at[chunk], sibling)

    for chunk in range(CHUNKS):
        far(chunk).start()
    gather.begin()
    near = sending(rows_ref, all_ref.at[me], near_send, near_recv, sibling)
    near.start()
    for turn in range(max(CHUNKS, gather.c_size - 1)):
        if turn < CHUNKS:
            far(turn).wait_recv()
            passing(turn).start()
        if turn + 1 < gather.c_size:
            gather.advance(turn + 1)
    near.wait()
    for chunk in range(CHUNKS):
        far(chunk).wait_send()
        passing(chunk).wait()
    own.wait()
    gather.end()


def startup(rows, shard, f_size, c_size, ident):
    place = pl.BlockSpec(memory_space=pl.ANY)
    full = (shard.shape[0] * f_size * c_size, shard.shape[1])
    return pl.pallas_call(
        startup_kernel,
        out_shape=[
            jax.ShapeDtypeStruct((4,) + rows.shape, BF16),
            jax.ShapeDtypeStruct(full, BF16),
        ],
        in_specs=[place, place],
        out_specs=[place, place],
        scratch_shapes=[pltpu.SemaphoreType.DMA] + GATHER_SEMS + weight_sems(f_size, c_size),
        compiler_params=pltpu.CompilerParams(collective_id=ident, has_side_effects=True),
        name="startup",
    )(rows, shard)


def whole(shape, column=None):
    zeros = (0,) * (len(shape) - 1)
    return pl.BlockSpec(shape, lambda i: zeros + (column or 0,), pipeline_mode=pl.Buffered(1))


def remote_params(ident, megabytes):
    return pltpu.CompilerParams(
        collective_id=ident, has_side_effects=True, vmem_limit_bytes=megabytes << 20, dimension_semantics=("arbitrary",)
    )


def project_kernel(layout, x_ref, gain_ref, w_ref, normed_ref, forget_ref, items_ref):
    seq_count, groups, width, places = layout
    x = x_ref[0].astype(F32)
    normed = (x * lax.rsqrt(jnp.mean(x * x, axis=1, keepdims=True) + epsilon) * gain_ref[...]).astype(BF16)
    normed_ref[0] = normed
    inner = groups * width
    rows = x.shape[0] // seq_count
    count = items_ref.shape[0]
    for kind in range(3):
        value = dot(normed, w_ref[:, kind * inner : (kind + 1) * inner], NN).astype(BF16)
        for slot, (s, g) in enumerate(places):
            piece = value[s * rows : (s + 1) * rows, g * width : (g + 1) * width]
            items_ref[slot % count, slot // count, kind] = piece
    forget_ref[0] = dot(normed, w_ref[:, 3 * inner :], NN)


def project(x_all, gain, full_one, layout, item_count, ctx_size):
    seq_count, groups, width, places = layout
    tp_size, rows, model_width = x_all.shape
    local = rows // seq_count
    item = jax.ShapeDtypeStruct((item_count, ctx_size, 3, tp_size * local, width), BF16)
    columns = full_one.shape[1]
    block = pl.BlockSpec((1, rows, model_width), lambda t: (t, 0, 0))
    return pl.pallas_call(
        functools.partial(project_kernel, layout),
        grid=(tp_size,),
        out_shape=[
            jax.ShapeDtypeStruct(x_all.shape, BF16),
            jax.ShapeDtypeStruct((tp_size, rows, LANES), F32),
            item,
        ],
        in_specs=[
            block,
            pl.BlockSpec((1, model_width), lambda t: (0, 0)),
            pl.BlockSpec((model_width, columns), lambda t: (0, 0), pipeline_mode=pl.Buffered(1)),
        ],
        out_specs=[
            block,
            pl.BlockSpec((1, rows, LANES), lambda t: (t, 0, 0)),
            pl.BlockSpec((item_count, ctx_size, 3, local, width), lambda t: (0, 0, 0, t, 0)),
        ],
        compiler_params=pltpu.CompilerParams(vmem_limit_bytes=48 << 20, dimension_semantics=("arbitrary",)),
        cost_estimate=pl.CostEstimate(
            flops=2 * x_all.size * columns, bytes_accessed=4 * x_all.size, transcendentals=0
        ),
        name="project",
    )(x_all, gain, full_one)


def out_kernel(layout, x_ref, gate_ref, w_ref, gain_ref, items, *refs):
    seq_count, groups, width, places = layout
    hidden_ref, normed_ref, attended_ref, mixed_ref = refs[:4]
    buffers, sems = refs[4:8], refs[8:]
    count = items.shape[0]
    me, sibling, across, diagonal = tp_places()
    greet((sibling, across))
    tp_size, rows, _ = gate_ref.shape
    local = rows // seq_count

    def mix(t, _):
        here = pl.ds(pl.multiple_of(t * local, local), local)
        for slot, (s, g) in enumerate(places[: seq_count * groups]):
            there = (t, pl.ds(s * local, local), pl.ds(g * width, width))
            value = items[slot % count, slot // count, here]
            attended_ref[there] = value
            mixed_ref[there] = (value.astype(F32) * gate_ref[there]).astype(BF16)
        return 0

    lax.fori_loop(0, tp_size, mix, 0)
    size = rows // CHUNKS

    def span(chunk):
        return pl.ds(pl.multiple_of(chunk * size, size), size)

    def partial(slot, chunk):
        return dot(mixed_ref[slot, span(chunk)], w_ref[...], NT)

    def finish(chunk, total):
        hidden = x_ref[span(chunk)].astype(F32) + total
        hidden_ref[span(chunk)] = hidden
        inverse = lax.rsqrt(jnp.mean(hidden * hidden, axis=1, keepdims=True) + epsilon)
        normed_ref[span(chunk)] = (hidden * inverse * gain_ref[...]).astype(BF16)

    scatter_loop(buffers, sems, partial, finish)


def out_project(x, gate, full_two, column, gain, items, layout, ident):
    seq_count, groups, width, places = layout
    rows, model_width = x.shape
    inner = groups * width
    tp_size = gate.shape[0]
    return pl.pallas_call(
        functools.partial(out_kernel, layout),
        grid=(1,),
        out_shape=[
            jax.ShapeDtypeStruct(x.shape, F32),
            jax.ShapeDtypeStruct(x.shape, BF16),
            jax.ShapeDtypeStruct(gate.shape, BF16),
            jax.ShapeDtypeStruct(gate.shape, BF16),
        ],
        in_specs=[
            whole(x.shape),
            whole(gate.shape),
            whole((model_width, inner), column),
            whole(gain.shape),
            whole(items.shape),
        ],
        out_specs=[whole(x.shape), whole(x.shape), whole(gate.shape), whole(gate.shape)],
        scratch_shapes=scatter_buffers(rows, model_width) + SCATTER_SEMS,
        compiler_params=remote_params(ident, 48),
        cost_estimate=pl.CostEstimate(
            flops=2 * gate.size * model_width, bytes_accessed=100 << 20, transcendentals=0
        ),
        name="out_project",
    )(x, gate, full_two, gain, items)


def mlp_kernel(normed_ref, grad_ref, gate_w, up_w, down_w, all_ref, inner_ref, pair_ref, table, own_sem, *sems):
    me, sibling, across, diagonal = tp_places()
    greet((sibling, across))
    table[0] = normed_ref[...]
    rows, hidden = table.shape[1] // CHUNKS, gate_w.shape[1]
    tile = min(hidden, 512)

    def compute(slot, chunk):
        spot = pl.ds(pl.multiple_of(chunk * rows, rows), rows)
        normed, grad = table[slot, spot], grad_ref[slot, spot]
        for start in range(0, hidden, tile):
            columns = pl.ds(start, tile)
            gate = dot(normed, gate_w[:, columns], NN)
            up = dot(normed, up_w[:, columns], NN)
            back = dot(grad, down_w[:, columns], NN)
            sig = 1.0 / (1.0 + jnp.exp(-gate))
            silu = gate * sig
            inner_ref[slot, spot, columns] = (silu * up).astype(BF16)
            pair_ref[slot, spot, columns] = (back * up * sig * (1.0 + gate * (1.0 - sig))).astype(BF16)
            pair_ref[slot, spot, pl.ds(hidden + start, tile)] = (back * silu).astype(BF16)

    gather_loop(table, sems, compute, relative=True)
    copy = pltpu.make_async_copy(table, all_ref, own_sem)
    copy.start()
    copy.wait()


def mlp(normed, grad_all, full_two, hidden, ident):
    tp_size, rows, model_width = grad_all.shape
    total = tp_size * rows
    return pl.pallas_call(
        mlp_kernel,
        grid=(1,),
        out_shape=[
            jax.ShapeDtypeStruct(grad_all.shape, BF16),
            jax.ShapeDtypeStruct((tp_size, rows, hidden), BF16),
            jax.ShapeDtypeStruct((tp_size, rows, 2 * hidden), BF16),
        ],
        in_specs=[whole(normed.shape), whole(grad_all.shape)]
        + [whole((model_width, hidden), column) for column in range(3)],
        out_specs=[
            pl.BlockSpec(memory_space=pl.ANY),
            whole((tp_size, rows, hidden)),
            whole((tp_size, rows, 2 * hidden)),
        ],
        scratch_shapes=[pltpu.VMEM(grad_all.shape, BF16), pltpu.SemaphoreType.DMA] + GATHER_SEMS,
        compiler_params=remote_params(ident, 56),
        cost_estimate=pl.CostEstimate(
            flops=6 * total * model_width * hidden, bytes_accessed=100 << 20, transcendentals=total * hidden
        ),
        name="mlp",
    )(normed, grad_all, full_two, full_two, full_two)


def mlp_back_kernel(
    pair_ref, w_ref, hidden_ref, grad_ref, gain_ref, sums_ref, out_ref, branch_ref, part_ref, sum_ref, *refs
):
    buffers, sems = refs[:4], refs[4:8]
    me, sibling, across, diagonal = tp_places()
    greet_all([{"tp": sibling}, {"tp": across}] + group_peers())
    weights = WeightSum(sums_ref, 0, sum_ref, refs[8:])
    weights.begin()
    tasks = weights.tasks()
    part_ref[...] = jnp.zeros_like(part_ref)
    size = hidden_ref.shape[0] // CHUNKS

    def span(chunk):
        return pl.ds(pl.multiple_of(chunk * size, size), size)

    def partial(slot, chunk):
        return dot(pair_ref[slot, span(chunk)], w_ref[...], NT)

    def finish(chunk, total):
        hidden = hidden_ref[span(chunk)]
        inverse = lax.rsqrt(jnp.mean(hidden * hidden, axis=1, keepdims=True) + epsilon)
        unit = hidden * inverse
        part_ref[...] += jnp.sum(total * unit, axis=0, keepdims=True)
        scaled = total * gain_ref[...]
        middle = jnp.mean(scaled * unit, axis=1, keepdims=True)
        grad = grad_ref[span(chunk)].astype(F32) + inverse * (scaled - unit * middle)
        out_ref[span(chunk)] = grad
        branch_ref[span(chunk)] = grad.astype(BF16)

    scatter_loop(
        buffers, sems, partial, finish, relative=True, between=lambda chunk: shared(tasks, chunk, CHUNKS)
    )
    weights.end()


def mlp_back(pair, full_two, hidden_state, grad_out, gain, part, f_size, c_size, ident):
    tp_size, rows, wide = pair.shape
    model_width = hidden_state.shape[1]
    total = (part.shape[0] // (f_size * c_size), part.shape[1] // 2)
    return pl.pallas_call(
        mlp_back_kernel,
        grid=(1,),
        out_shape=[
            jax.ShapeDtypeStruct(hidden_state.shape, F32),
            jax.ShapeDtypeStruct(hidden_state.shape, BF16),
            jax.ShapeDtypeStruct(gain.shape, F32),
            jax.ShapeDtypeStruct(total, F32),
        ],
        in_specs=[
            whole(pair.shape),
            whole((model_width, wide), 0),
            whole(hidden_state.shape),
            whole(grad_out.shape),
            whole(gain.shape),
            pl.BlockSpec(memory_space=pl.ANY),
        ],
        out_specs=[
            whole(hidden_state.shape),
            whole(hidden_state.shape),
            whole(gain.shape),
            whole(total),
        ],
        scratch_shapes=scatter_buffers(rows, model_width)
        + SCATTER_SEMS
        + sum_scratch(f_size, c_size, *total),
        compiler_params=remote_params(ident, 56),
        cost_estimate=pl.CostEstimate(
            flops=2 * pair.size * model_width, bytes_accessed=100 << 20, transcendentals=0
        ),
        name="mlp_back",
    )(pair, full_two, hidden_state, grad_out, gain, part)


def out_back_kernel(layout, branch_ref, w_ref, gate_ref, attended_ref, sums_ref, *refs):
    seq_count, groups, width, places = layout
    all_ref, logit_ref, items, sum_ref, table, grads, own_sem = refs[:7]
    sems = refs[7:13]
    count = items.shape[0]
    me, sibling, across, diagonal = tp_places()
    greet_all([{"tp": sibling}, {"tp": across}] + group_peers())
    weights = WeightSum(sums_ref, sum_ref.shape[1], sum_ref, refs[13:])
    weights.begin()
    tasks = weights.tasks()
    table[me] = branch_ref[...]
    tp_size, rows, _ = gate_ref.shape
    local, size = rows // seq_count, rows // CHUNKS

    def compute(slot, chunk):
        spot = pl.ds(pl.multiple_of(chunk * size, size), size)
        mixed = dot(table[slot, spot], w_ref[...], NN)
        gate = gate_ref[slot, spot]
        scaled = mixed * gate
        grads[slot, spot] = scaled.astype(BF16)
        attended = attended_ref[slot, spot].astype(F32)
        logit_ref[slot, spot] = (scaled * attended * (1.0 - gate)).astype(BF16)

    gather_loop(table, sems, compute, between=lambda turn: shared(tasks, turn, CHUNKS))
    copy = pltpu.make_async_copy(table, all_ref, own_sem)
    copy.start()

    def deal(t, _):
        here = pl.ds(pl.multiple_of(t * local, local), local)
        for slot, (s, g) in enumerate(places):
            piece = grads[t, pl.ds(s * local, local), pl.ds(g * width, width)]
            items[slot % count, slot // count, here] = piece
        return 0

    lax.fori_loop(0, tp_size, deal, 0)
    copy.wait()
    weights.end()


def out_back(branch, full_two, column, gate, attended, part, layout, item_count, f_size, ctx_size, ident):
    seq_count, groups, width, places = layout
    rows, model_width = branch.shape
    tp_size, _, inner = gate.shape
    item = (item_count, ctx_size, tp_size * rows // seq_count, width)
    table = (tp_size, rows, model_width)
    total = (part.shape[0] // (f_size * ctx_size), part.shape[1] // 2)
    return pl.pallas_call(
        functools.partial(out_back_kernel, layout),
        grid=(1,),
        out_shape=[
            jax.ShapeDtypeStruct(table, BF16),
            jax.ShapeDtypeStruct(gate.shape, BF16),
            jax.ShapeDtypeStruct(item, BF16),
            jax.ShapeDtypeStruct(total, F32),
        ],
        in_specs=[
            whole(branch.shape),
            whole((model_width, inner), column),
            whole(gate.shape),
            whole(attended.shape),
            pl.BlockSpec(memory_space=pl.ANY),
        ],
        out_specs=[pl.BlockSpec(memory_space=pl.ANY), whole(gate.shape), whole(item), whole(total)],
        scratch_shapes=[pltpu.VMEM(table, BF16), pltpu.VMEM(gate.shape, BF16), pltpu.SemaphoreType.DMA]
        + GATHER_SEMS
        + sum_scratch(f_size, ctx_size, *total),
        compiler_params=remote_params(ident, 48),
        cost_estimate=pl.CostEstimate(
            flops=2 * gate.size * model_width, bytes_accessed=100 << 20, transcendentals=0
        ),
        name="out_back",
    )(branch, full_two, gate, attended, part)


def assemble_kernel(layout, items, out_ref):
    seq_count, groups, width, places = layout
    count, local = items.shape[0], items.shape[3]
    inner = groups * width
    for slot, (s, g) in enumerate(places[: seq_count * groups]):
        for kind in range(3):
            columns = pl.ds(kind * inner + g * width, width)
            out_ref[0, pl.ds(s * local, local), columns] = items[slot % count, slot // count, kind]


def assemble(items, layout, tp_size):
    seq_count, groups, width, places = layout
    count, ctx_size, kinds, ctx_rows, _ = items.shape
    local = ctx_rows // tp_size
    shape = (tp_size, seq_count * local, kinds * groups * width)
    return pl.pallas_call(
        functools.partial(assemble_kernel, layout),
        grid=(tp_size,),
        out_shape=jax.ShapeDtypeStruct(shape, BF16),
        in_specs=[pl.BlockSpec((count, ctx_size, kinds, local, width), lambda t: (0, 0, 0, t, 0))],
        out_specs=pl.BlockSpec((1,) + shape[1:], lambda t: (t, 0, 0)),
        compiler_params=pltpu.CompilerParams(vmem_limit_bytes=32 << 20, dimension_semantics=("arbitrary",)),
        cost_estimate=pl.CostEstimate(flops=0, bytes_accessed=16 << 20, transcendentals=0),
        name="assemble",
    )(items)


def last_kernel(
    qkv_ref,
    logit_ref,
    forget_ref,
    qkv_w,
    forget_w,
    gate_w,
    x_ref,
    grad_ref,
    gain_ref,
    part_ref,
    extra_ref,
    out_ref,
    sum_ref,
    vector_ref,
    *refs,
):
    buffers, sems, (mine, near_in, group_in) = refs[:4], refs[4:8], refs[8:11]
    vector_sems, sum_refs = refs[11:15], refs[15:]
    me, sibling, across, diagonal = tp_places()
    others = group_peers()
    greet_all([{"tp": sibling}, {"tp": across}, {"tp": diagonal}] + others)
    weights = WeightSum(part_ref, 0, sum_ref, sum_refs)
    weights.begin()
    mine[...] = extra_ref[...]
    size = x_ref.shape[0] // CHUNKS

    def span(chunk):
        return pl.ds(pl.multiple_of(chunk * size, size), size)

    def partial(slot, chunk):
        value = dot(qkv_ref[slot, span(chunk)], qkv_w[...], NT)
        value = value + dot(logit_ref[slot, span(chunk)], gate_w[...], NT)
        return value + dot(forget_ref[slot, span(chunk)], forget_w[...], NT)

    def finish(chunk, total):
        x = x_ref[span(chunk)].astype(F32)
        inverse = lax.rsqrt(jnp.mean(x * x, axis=1, keepdims=True) + epsilon)
        unit = x * inverse
        mine[0:1] += jnp.sum(total * unit, axis=0, keepdims=True)
        scaled = total * gain_ref[...]
        middle = jnp.mean(scaled * unit, axis=1, keepdims=True)
        out_ref[span(chunk)] = (grad_ref[span(chunk)] + inverse * (scaled - unit * middle)).astype(BF16)

    tasks = weights.tasks()

    def between(chunk):
        shared(tasks, chunk, CHUNKS)

    scatter_loop(buffers, sems, partial, finish, between=between)
    near_send, near_recv, group_send, group_recv = vector_sems
    copies = []
    for n, peer in enumerate((sibling, across, diagonal)):
        copies.append(sending(mine, near_in.at[n], near_send.at[n], near_recv.at[n], peer))
        copies[-1].start()
    for copy in copies:
        copy.wait()
    vector_ref[...] = mine[...] + near_in[0] + near_in[1] + near_in[2]
    mine[...] = vector_ref[...]
    copies = []
    for n, peer in enumerate(others):
        copies.append(moving(mine, group_in.at[n], group_send.at[n], group_recv.at[n], peer))
        copies[-1].start()
    for n, copy in enumerate(copies):
        copy.wait()
        vector_ref[...] += group_in[n]
    weights.end()


def last(grad_qkv, grad_logit, grad_forget, full_one, full_two, column, x, grad_hidden, gain, part, extra, f_size, c_size, ident):
    rows, model_width = x.shape
    wide, inner = grad_qkv.shape[2], grad_logit.shape[2]
    shard, columns = part.shape[0] // (f_size * c_size), part.shape[1]
    dma = pltpu.SemaphoreType.DMA
    return pl.pallas_call(
        last_kernel,
        grid=(1,),
        out_shape=[
            jax.ShapeDtypeStruct(x.shape, BF16),
            jax.ShapeDtypeStruct((shard, columns), F32),
            jax.ShapeDtypeStruct(extra.shape, F32),
        ],
        in_specs=[
            whole(grad_qkv.shape),
            whole(grad_logit.shape),
            whole(grad_forget.shape),
            whole((model_width, wide), 0),
            whole((model_width, LANES), wide // LANES),
            whole((model_width, inner), column),
            whole(x.shape),
            whole(x.shape),
            whole(gain.shape),
            pl.BlockSpec(memory_space=pl.ANY),
            whole(extra.shape),
        ],
        out_specs=[whole(x.shape), whole((shard, columns)), whole(extra.shape)],
        scratch_shapes=scatter_buffers(rows, model_width)
        + SCATTER_SEMS
        + [
            pltpu.VMEM(extra.shape, F32),
            pltpu.VMEM((3,) + extra.shape, F32),
            pltpu.VMEM((f_size * c_size - 1,) + extra.shape, F32),
        ]
        + [dma((3,))] * 2
        + [dma((f_size * c_size - 1,))] * 2
        + sum_scratch(f_size, c_size, shard, columns),
        compiler_params=remote_params(ident, 60),
        cost_estimate=pl.CostEstimate(
            flops=8 * rows * model_width * (wide + inner + LANES), bytes_accessed=100 << 20, transcendentals=0
        ),
        name="last",
    )(grad_qkv, grad_logit, grad_forget, full_one, full_one, full_two, x, grad_hidden, gain, part, extra)


def to_sibling(values):
    return lax.ppermute(values, "tp", [(i, i + 1 - 2 * (i % 2)) for i in range(4)])


def to_across(values):
    return lax.ppermute(values, "tp", [(i, (i + 2) % 4) for i in range(4)])


def relative_rows(rows):
    far = to_across(rows)
    return jnp.stack([rows, to_sibling(rows), far, to_sibling(far)])


def summed_rows(partial):
    own, near, far, corner = (partial[n] for n in range(4))
    corner = to_sibling(corner.astype(BF16)).astype(F32)
    near = to_sibling(near.astype(BF16)).astype(F32)
    far = to_across((far + corner).astype(BF16)).astype(F32)
    return own + near + far


def per_device(
    layer_input,
    lengths,
    attn_gain,
    w_query,
    w_key,
    w_value,
    w_forget,
    forget_bias,
    w_gate_out,
    w_out,
    mlp_gain,
    w_gate,
    w_up,
    w_down,
    cotangent,
):
    local_rows, seq_count, model_width = layer_input.shape
    head_count = forget_bias.shape[0]
    inner_width = w_query.shape[1]
    hidden = w_gate.shape[1]
    head_size = inner_width // head_count
    tp_size = lax.axis_size("tp")
    ctx_size = lax.axis_size("ctx")
    shard_count = lax.axis_size("fsdp") * ctx_size
    ctx_rows = local_rows * tp_size
    seq_len = ctx_rows * ctx_size
    all_rows = seq_count * ctx_rows
    ctx_index = lax.axis_index("ctx")
    tp_index = lax.axis_index("tp")
    shard_index = lax.axis_index("fsdp") * ctx_size + ctx_index

    pair = LANES // head_size
    groups = head_count // pair
    width = pair * head_size
    item_count = pl.cdiv(seq_count * groups, ctx_size)
    used = seq_count * groups

    def place(slot):
        slot = slot % used
        return (slot // groups + slot % groups) % seq_count, slot % groups

    places = tuple(place(slot) for slot in range(ctx_size * item_count))
    layout = (seq_count, groups, width, places)

    fsdp_size = lax.axis_size("fsdp")
    packed_one = jnp.concatenate(
        [
            w_query,
            w_key,
            w_value,
            w_forget,
            attn_gain[:, None],
            mlp_gain[:, None],
            jnp.zeros((attn_gain.shape[0], LANES - head_count - 2), BF16),
        ],
        axis=1,
    )
    packed_two = jnp.concatenate([w_gate, w_up, w_down, w_out, w_gate_out], axis=1)
    edge = 3 * inner_width
    input_rows = layer_input.transpose(1, 0, 2).reshape(seq_count * local_rows, model_width)
    input_all, full_one = startup(input_rows, packed_one, fsdp_size, ctx_size, 1)
    gains = full_one[:, edge + head_count : edge + head_count + 2].astype(F32).T
    gain_one, gain_two = gains[0:1], gains[1:2]
    out_column = 3 * hidden // inner_width

    def by_sequence(rows):
        return rows.transpose(1, 0, 2).reshape(seq_count * local_rows, model_width)

    def by_position(rows):
        return rows.reshape(seq_count, local_rows, model_width).transpose(1, 0, 2)

    local_pos = (ctx_index * tp_size + tp_index) * local_rows + jnp.arange(
        local_rows, dtype=jnp.int32
    )
    valid_rows = (local_pos[None, :] < lengths[:, None]).astype(F32)
    valid_rows = valid_rows.reshape(seq_count * local_rows, 1)
    ctx_pos = ctx_index * ctx_rows + jnp.arange(ctx_rows, dtype=jnp.int32)
    ctx_pos = ctx_pos.reshape(tp_size, 1, local_rows)
    ctx_valid = (ctx_pos < lengths[None, :, None]).astype(F32)

    grad_out = (valid_rows * by_sequence(cotangent).astype(F32)).astype(BF16)
    grad_all = relative_rows(lax.optimization_barrier((grad_out, input_all[0, :8]))[0])
    normed_one, forget_rows, items = project(
        input_all, gain_one, full_one, layout, item_count, ctx_size
    )
    normed_flat = normed_one.reshape(all_rows, model_width)
    forget_logit = forget_rows.reshape(all_rows, LANES)[:, :head_count].T
    forget_logit = forget_logit + forget_bias.astype(F32)[:, None]
    forget_logit = forget_logit.reshape(head_count, tp_size, seq_count, local_rows)
    log_forget = (ctx_valid[None] * jax.nn.log_sigmoid(forget_logit)).astype(BF16)

    cut = log_forget.astype(F32).reshape(groups, pair, tp_size, seq_count, local_rows)
    picked = jnp.stack([cut[g, :, :, s] for s, g in places])
    picked = picked.reshape(ctx_size, item_count, pair, ctx_rows).transpose(1, 0, 2, 3)
    picked = jnp.pad(picked, ((0, 0), (0, 0), (0, 8 - pair), (0, 0)))
    attended_items, qkv, full_two, exact, lse, decay = context(
        items, picked, packed_two, fsdp_size, head_size, 7
    )
    down_w = full_two[:, 2 * hidden : 3 * hidden]
    gate_out_w = full_two[:, 3 * hidden + inner_width :]
    gate_logit = dot(normed_flat, gate_out_w, NN)
    out_gate = jax.nn.sigmoid(gate_logit).reshape(tp_size, -1, inner_width)
    hidden_state, normed_two, attended, mixed = out_project(
        input_rows, out_gate, full_two, out_column, gain_two, attended_items, layout, 2
    )
    normed_two_all, inner_act, grad_pair = mlp(normed_two, grad_all, full_two, hidden, 3)
    normed_two_flat = normed_two_all.reshape(all_rows, model_width)
    inner_flat = inner_act.reshape(all_rows, hidden)
    grad_pair_flat = grad_pair.reshape(all_rows, 2 * hidden)
    grad_flat = grad_all.reshape(all_rows, model_width)

    gate_up_part = dot(normed_two_flat, grad_pair_flat, TN).astype(BF16)
    grad_hidden, branch, mlp_gain_part, gate_sum = mlp_back(
        grad_pair, full_two, hidden_state, grad_out, gain_two, gate_up_part, fsdp_size, ctx_size, 4
    )
    feedforward = summed_rows(dot(inner_flat, down_w, NT).reshape(tp_size, -1, model_width))
    output = (valid_rows * (hidden_state + feedforward)).astype(BF16)

    branch_all, grad_gate_logit, grads, up_sum = out_back(
        branch,
        full_two,
        out_column,
        out_gate,
        attended,
        gate_up_part,
        layout,
        item_count,
        fsdp_size,
        ctx_size,
        5,
    )
    branch_flat = branch_all.reshape(all_rows, model_width)
    logit_flat = grad_gate_logit.reshape(all_rows, inner_width)

    out_part = jnp.concatenate(
        [
            dot(grad_flat, inner_flat, TN).astype(BF16),
            dot(branch_flat, mixed.reshape(all_rows, inner_width), TN).astype(BF16),
            dot(normed_flat, logit_flat, TN).astype(BF16),
        ],
        axis=1,
    )
    grad_items, forget_items, out_sum = context_back(
        grads, qkv, exact, lse, decay, out_part, fsdp_size, head_size, 8
    )
    forget_back = forget_items[:, :, :pair].astype(BF16).transpose(1, 0, 2, 3)
    forget_back = forget_back.reshape(ctx_size * item_count, pair, tp_size, local_rows)
    slots = {place(slot): slot for slot in range(used)}
    forget_back = jnp.stack(
        [
            jnp.stack([forget_back[slots[s, g]] for s in range(seq_count)], axis=2)
            for g in range(groups)
        ]
    ).reshape(head_count, tp_size, seq_count, local_rows)
    grad_forget_logit = forget_back.astype(F32) * ctx_valid[None] * jax.nn.sigmoid(-forget_logit)
    grad_forget_logit = grad_forget_logit.astype(BF16).reshape(head_count, all_rows)
    bias_part = jnp.sum(grad_forget_logit.astype(F32), axis=1)
    grad_forget_rows = jnp.pad(grad_forget_logit, ((0, LANES - head_count), (0, 0))).T
    grad_qkv = assemble(grad_items, layout, tp_size)
    grad_qkvf = jnp.concatenate([grad_qkv.reshape(all_rows, edge), grad_forget_rows], axis=1)
    bias_full = lax.dynamic_update_slice(
        jnp.zeros((1, model_width), F32), bias_part[None], (0, tp_index * head_count)
    )
    extra = jnp.concatenate(
        [jnp.zeros_like(bias_full), mlp_gain_part, bias_full, jnp.zeros((5, model_width), F32)]
    )
    input_grad, qkv_sum, vectors = last(
        grad_qkv,
        grad_gate_logit,
        grad_forget_rows.reshape(tp_size, -1, LANES),
        full_one,
        full_two,
        out_column + 1,
        input_rows,
        grad_hidden,
        gain_one,
        dot(normed_flat, grad_qkvf, TN).astype(BF16),
        extra,
        fsdp_size,
        ctx_size,
        6,
    )
    gain_one_sum, gain_two_sum, bias_sum = vectors[0], vectors[1], vectors[2]
    shard_rows = model_width // shard_count
    attn_gain_grad = lax.dynamic_slice_in_dim(gain_one_sum, shard_index * shard_rows, shard_rows, 0)
    mlp_gain_grad = lax.dynamic_slice_in_dim(gain_two_sum, shard_index * shard_rows, shard_rows, 0)
    forget_bias_grad = lax.dynamic_slice_in_dim(bias_sum, tp_index * head_count, head_count, 0)
    wide = inner_width
    return (
        by_position(output),
        by_position(input_grad),
        attn_gain_grad,
        qkv_sum[:, :wide],
        qkv_sum[:, wide : 2 * wide],
        qkv_sum[:, 2 * wide : 3 * wide],
        qkv_sum[:, 3 * wide : 3 * wide + head_count],
        forget_bias_grad,
        out_sum[:, hidden + wide :],
        out_sum[:, hidden : hidden + wide],
        mlp_gain_grad,
        gate_sum,
        up_sum,
        out_sum[:, :hidden],
    )


def solution(mesh):
    rows = P(("ctx", "tp"), "fsdp", None)
    matrix = P(("fsdp", "ctx"), "tp")
    vector = P(("fsdp", "ctx"))
    return jax.shard_map(
        per_device,
        mesh=mesh,
        in_specs=(
            rows,
            P("fsdp"),
            vector,
            matrix,
            matrix,
            matrix,
            matrix,
            P("tp"),
            matrix,
            matrix,
            vector,
            matrix,
            matrix,
            matrix,
            rows,
        ),
        out_specs=(
            rows,
            rows,
            vector,
            matrix,
            matrix,
            matrix,
            matrix,
            P("tp"),
            matrix,
            matrix,
            vector,
            matrix,
            matrix,
            matrix,
        ),
        check_vma=False,
    )
```

```python
import functools

import jax
import jax.numpy as jnp
from jax import lax
from jax.experimental import pallas as pl
from jax.experimental.pallas import tpu as pltpu
from jax.sharding import PartitionSpec as P

F32 = jnp.float32
BF16 = jnp.bfloat16
LANES = 128
MESH = pl.DeviceIdType.MESH
epsilon = 1e-06
masked_score = -1e30
NT = (((1,), (1,)), ((), ()))
NN = (((1,), (0,)), ((), ()))
TN = (((0,), (0,)), ((), ()))


def dot(left, right, dims):
    return lax.dot_general(left, right, dims, preferred_element_type=F32)


def of_head(block, head, head_size, ones_at=None):
    lane = lax.broadcasted_iota(jnp.int32, block.shape, 1)
    out = jnp.where(lane // head_size == head, block, jnp.zeros_like(block))
    if ones_at is not None:
        out = jnp.where(lane == ones_at, jnp.ones_like(block), out)
    return out


def spare_lane(head, head_size):
    return ((head + 1) % 2) * head_size


def attend_item(qkv, decay, out, exact, lse, heads, head_size):
    count, _, block, width = qkv.shape
    scale = head_size**-0.5
    row = lax.broadcasted_iota(jnp.int32, (block, block), 0)
    column = lax.broadcasted_iota(jnp.int32, (block, block), 1)
    causal = column <= row

    def query_block(i, _):
        query = qkv[i, 0]
        lanes = pl.ds(pl.multiple_of(i * block, block), block)
        result = jnp.zeros((block, width), F32)
        for head in range(heads):
            query_head = of_head(query, head, head_size)

            def step(j, carry, masked):
                top, total, acc = carry
                keys = pl.ds(pl.multiple_of(j * block, block), block)
                score = dot(query_head, qkv[j, 1], NT) * scale
                score = score - decay[head : head + 1, keys]
                if masked:
                    score = jnp.where(causal, score, masked_score)
                new_top = jnp.maximum(top, jnp.max(score, axis=1, keepdims=True))
                prob = jnp.exp(score - new_top)
                shrink = jnp.exp(top - new_top)
                total = total * shrink + jnp.sum(prob, axis=1, keepdims=True)
                acc = acc * shrink + dot(prob.astype(BF16), qkv[j, 2], NN)
                return new_top, total, acc

            carry = (
                jnp.full((block, 1), masked_score, F32),
                jnp.zeros((block, 1), F32),
                jnp.zeros((block, width), F32),
            )
            carry = lax.fori_loop(0, i, lambda j, c: step(j, c, False), carry)
            top, total, acc = step(i, carry, True)
            lane = lax.broadcasted_iota(jnp.int32, acc.shape, 1)
            result = jnp.where(lane // head_size == head, acc / total, result)
            stat = jnp.broadcast_to(top + jnp.log(total), (block, LANES)).T
            lse[head : head + 1, lanes] = stat[0:1]
        exact[i] = result
        out[i] = result.astype(BF16)
        return 0

    lax.fori_loop(0, count, query_block, 0)


def attend_item_back(qkv, grads, exact, lse, decay, dqkv, change, dq_acc, delta, heads, head_size):
    count, _, block, width = qkv.shape
    scale = head_size**-0.5
    row = lax.broadcasted_iota(jnp.int32, (block, block), 0)
    column = lax.broadcasted_iota(jnp.int32, (block, block), 1)
    causal = row <= column
    dq_acc[...] = jnp.zeros_like(dq_acc)
    change[...] = jnp.zeros_like(change)

    def prepare(i, _):
        lanes = pl.ds(pl.multiple_of(i * block, block), block)
        product = grads[i].astype(F32) * exact[i]
        lane = lax.broadcasted_iota(jnp.int32, product.shape, 1)
        for head in range(heads):
            part = jnp.where(lane // head_size == head, product, 0.0)
            part = jnp.sum(part, axis=1, keepdims=True)
            delta[head : head + 1, lanes] = jnp.broadcast_to(part, (block, LANES)).T[0:1]
        return 0

    lax.fori_loop(0, count, prepare, 0)

    def key_block(j, _):
        keys = pl.ds(pl.multiple_of(j * block, block), block)
        key = qkv[j, 1]
        value = qkv[j, 2]
        value_total = jnp.zeros((block, width), F32)
        key_total = jnp.zeros((block, width), F32)
        for head in range(heads):
            spare = spare_lane(head, head_size)
            key_ones = of_head(key, head, head_size, spare)
            fall = jnp.broadcast_to(decay[head : head + 1, keys], (LANES, block)).T[:, 0:1]

            def step(i, carry, masked):
                value_acc, key_acc = carry
                lanes = pl.ds(pl.multiple_of(i * block, block), block)
                query = qkv[i, 0]
                grad = of_head(grads[i], head, head_size)
                score = dot(key, of_head(query, head, head_size), NT) * scale
                score = score - fall - lse[head : head + 1, lanes]
                if masked:
                    score = jnp.where(causal, score, masked_score)
                prob = jnp.exp(score)
                grad_prob = dot(value, grad, NT)
                grad_score = prob * (grad_prob - delta[head : head + 1, lanes])
                grad_score = grad_score.astype(BF16)
                value_acc = value_acc + dot(prob.astype(BF16), grad, NN)
                query_ones = of_head(query, head, head_size, spare)
                key_acc = key_acc + dot(grad_score, query_ones, NN)
                dq_acc[head, i] += dot(grad_score, key_ones, TN)
                return value_acc, key_acc

            zero = jnp.zeros((block, width), F32)
            carry = step(j, (zero, zero), True)
            carry = lax.fori_loop(j + 1, count, lambda i, c: step(i, c, False), carry)
            value_acc, key_acc = carry
            value_total = value_total + value_acc
            lane = lax.broadcasted_iota(jnp.int32, key_acc.shape, 1)
            key_total = jnp.where(lane // head_size == head, key_acc, key_total)
            change[head : head + 1, keys] -= key_acc.T[spare : spare + 1]
        dqkv[j, 1] = (key_total * scale).astype(BF16)
        dqkv[j, 2] = value_total.astype(BF16)
        return 0

    lax.fori_loop(0, count, key_block, 0)

    def finish(i, _):
        lanes = pl.ds(pl.multiple_of(i * block, block), block)
        total = jnp.zeros((block, width), F32)
        for head in range(heads):
            spare = spare_lane(head, head_size)
            part = dq_acc[head, i]
            lane = lax.broadcasted_iota(jnp.int32, part.shape, 1)
            total = jnp.where(lane // head_size == head, part, total)
            change[head : head + 1, lanes] += part.T[spare : spare + 1]
        dqkv[i, 0] = (total * scale).astype(BF16)
        return 0

    lax.fori_loop(0, count, finish, 0)


def triangle(upward):
    row = lax.broadcasted_iota(jnp.int32, (LANES, LANES), 0)
    column = lax.broadcasted_iota(jnp.int32, (LANES, LANES), 1)
    keep = (row <= column) if upward else (row >= column)
    return jnp.where(keep, 1.0, 0.0).astype(BF16)


def exact_product(values, matrix):
    high = values.astype(BF16)
    rest = values - high.astype(F32)
    middle = rest.astype(BF16)
    low = (rest - middle.astype(F32)).astype(BF16)
    return dot(high, matrix, NN) + dot(middle, matrix, NN) + dot(low, matrix, NN)


def ctx_sending(source, target, send_sem, recv_sem, peer):
    return pltpu.make_async_remote_copy(
        src_ref=source,
        dst_ref=target,
        send_sem=send_sem,
        recv_sem=recv_sem,
        device_id={"ctx": peer},
        device_id_type=MESH,
    )


def ctx_greet(size):
    me = lax.axis_index("ctx")
    barrier = pltpu.get_barrier_semaphore()
    for step in range(1, size):
        peer = lax.rem(me + step, size)
        pl.semaphore_signal(barrier, inc=1, device_id={"ctx": peer}, device_id_type=MESH)
    pl.semaphore_wait(barrier, size - 1)
    return me


class Exchange:
    def __init__(self, me, size, source, target, sems):
        self.me, self.size, self.source, self.target = me, size, source, target
        self.send_sem, self.recv_sem, self.own_sem = sems

    def own(self, item):
        return pltpu.make_async_copy(
            self.source.at[item, self.me], self.target.at[item, self.me], self.own_sem.at[item]
        )

    def copy(self, item, step):
        peer = lax.rem(self.me + step, self.size)
        return ctx_sending(
            self.source.at[item, peer],
            self.target.at[item, self.me],
            self.send_sem.at[item, step],
            self.recv_sem.at[item, step],
            peer,
        )

    def start(self, item):
        self.own(item).start()
        for step in range(1, self.size):
            self.copy(item, step).start()

    def arrive(self, item):
        self.own(item).wait()
        for step in range(1, self.size):
            self.copy(item, step).wait_recv()

    def drain(self, item):
        for step in range(1, self.size):
            self.copy(item, step).wait_send()


def exchange_sems(items, size):
    return [
        pltpu.SemaphoreType.DMA((items, size)),
        pltpu.SemaphoreType.DMA((items, size)),
        pltpu.SemaphoreType.DMA((items,)),
    ]


def context_kernel(
    heads,
    head_size,
    items_ref,
    forget_ref,
    shard_ref,
    rows_ref,
    back_ref,
    qkv_ref,
    full_ref,
    table_ref,
    exact_ref,
    lse_ref,
    decay_ref,
    *refs,
):
    qkv, forget, out, save_sem = refs[:4]
    sems = refs[4:]
    count, size, _, block, width = items_ref.shape
    tp, sibling, across, diagonal = tp_places()
    greet_all([{"tp": sibling}, {"tp": across}] + group_peers())
    me = lax.axis_index("ctx")
    gather = WeightGather(shard_ref, full_ref, sems[9:14])
    rows = RowGather(rows_ref, table_ref, sems[14:])
    forgets = Exchange(me, size, forget_ref, forget, sems[0:3])
    inputs = Exchange(me, size, items_ref, qkv, sems[3:6])
    results = Exchange(me, size, out, back_ref, sems[6:9])

    @pl.loop(0, count)
    def _(item):
        forgets.start(item)

    gather.begin()
    inputs.start(0)
    rows.begin()

    @pl.loop(0, count)
    def _(item):
        forgets.arrive(item)

    @pl.loop(0, count)
    def _(item):
        upper = triangle(True)
        before = jnp.zeros((8, 1), F32)
        for start in range(0, size * block, LANES):
            part = forget[item, start // block, :, pl.ds(start % block, LANES)]
            total = before + dot(part.astype(BF16), upper, NN)
            decay_ref[item, :, pl.ds(start, LANES)] = total
            before = total[:, LANES - 1 :]

    lse_ref[...] = jnp.zeros_like(lse_ref)

    @pl.loop(0, count)
    def _(item):
        inputs.arrive(item)

        @pl.when(item + 1 < count)
        def _():
            inputs.start(item + 1)

        for hop in range(1, min(size, count + 1)):

            @pl.when(item == hop - 1)
            def _(hop=hop):
                gather.advance(hop)

        saving = pltpu.make_async_copy(qkv.at[item], qkv_ref.at[item], save_sem)
        saving.start()
        attend_item(
            qkv.at[item], decay_ref.at[item], out.at[item], exact_ref.at[item], lse_ref.at[item], heads, head_size
        )
        results.start(item)
        saving.wait()

    rows.advance()
    for hop in range(count + 1, size):
        gather.advance(hop)

    @pl.loop(0, count)
    def _(item):
        forgets.drain(item)
        inputs.drain(item)
        results.arrive(item)
        results.drain(item)

    gather.end()
    rows.end()


def full_block(shape):
    return pl.BlockSpec(shape, lambda i: (0,) * len(shape), pipeline_mode=pl.Buffered(1))


def attend_cost(items, heads, products):
    count, size, _, block, width = items.shape
    pairs = count * heads * (size * block) ** 2 // 2
    return pl.CostEstimate(
        flops=2 * products * pairs * 256, bytes_accessed=100 << 20, transcendentals=pairs
    )


def context(items, forget, shard, rows, f_size, head_size, ident):
    count, size, _, block, width = items.shape
    heads = width // head_size
    place = pl.BlockSpec(memory_space=pl.ANY)
    exact, stat = (count, size, block, width), (count, 8, size * block)
    return pl.pallas_call(
        functools.partial(context_kernel, heads, head_size),
        grid=(1,),
        out_shape=[
            jax.ShapeDtypeStruct(exact, BF16),
            jax.ShapeDtypeStruct(items.shape, BF16),
            jax.ShapeDtypeStruct((shard.shape[0] * f_size * size, shard.shape[1]), BF16),
            jax.ShapeDtypeStruct((4,) + rows.shape, BF16),
            jax.ShapeDtypeStruct(exact, F32),
            jax.ShapeDtypeStruct(stat, F32),
            jax.ShapeDtypeStruct(stat, F32),
        ],
        in_specs=[place] * 4,
        out_specs=[place, place, place, place, full_block(exact), full_block(stat), full_block(stat)],
        scratch_shapes=[
            pltpu.VMEM(items.shape, BF16),
            pltpu.VMEM(forget.shape, F32),
            pltpu.VMEM(exact, BF16),
            pltpu.SemaphoreType.DMA,
        ]
        + exchange_sems(count, size) * 3
        + weight_sems(f_size, size)
        + [pltpu.SemaphoreType.DMA((3,))] * 2
        + [pltpu.SemaphoreType.DMA],
        compiler_params=remote_params(ident, 48),
        cost_estimate=attend_cost(items, heads, 2),
        name="context",
    )(items, forget, shard, rows)


def context_back_kernel(
    heads,
    head_size,
    items_ref,
    qkv_ref,
    exact_ref,
    lse_ref,
    decay_ref,
    part_ref,
    table_ref,
    back_ref,
    forget_ref,
    sum_ref,
    rows_ref,
    *refs,
):
    grads, dqkv, change, slope, dq_acc, delta = refs[:6]
    sems = refs[6:15]
    count, size, block, width = items_ref.shape
    tp, sibling, across, diagonal = tp_places()
    greet_all([{"tp": sibling}, {"tp": across}] + group_peers())
    me = lax.axis_index("ctx")
    weights = WeightSum(part_ref, 0, sum_ref, refs[15:23])
    rows = RowSum(table_ref, rows_ref, refs[23:])
    inputs = Exchange(me, size, items_ref, grads, sems[0:3])
    results = Exchange(me, size, dqkv, back_ref, sems[3:6])
    forgets = Exchange(me, size, slope, forget_ref, sems[6:9])

    @pl.loop(0, count)
    def _(item):
        inputs.start(item)

    weights.begin()
    rows.begin()

    @pl.loop(0, count)
    def _(item):
        inputs.arrive(item)
        attend_item_back(
            qkv_ref.at[item],
            grads.at[item],
            exact_ref.at[item],
            lse_ref.at[item],
            decay_ref.at[item],
            dqkv.at[item],
            change,
            dq_acc,
            delta,
            heads,
            head_size,
        )
        results.start(item)
        lower = triangle(False)
        after = jnp.zeros((8, 1), F32)
        for start in reversed(range(0, size * block, LANES)):
            total = after + exact_product(change[:, pl.ds(start, LANES)], lower)
            slope[item, start // block, :, pl.ds(start % block, LANES)] = total
            after = total[:, 0:1]
        forgets.start(item)

        for turn in range(count):

            @pl.when(item == turn)
            def _(turn=turn):
                weights.run_share(turn, count + 1)
                if turn == 0:
                    rows.advance()

    weights.run_share(count, count + 1)

    @pl.loop(0, count)
    def _(item):
        inputs.drain(item)
        results.arrive(item)
        results.drain(item)
        forgets.arrive(item)
        forgets.drain(item)

    weights.end()
    rows.end()


def context_back(grads, qkv, exact, lse, decay, part, table, f_size, head_size, ident):
    count, size, _, block, width = qkv.shape
    heads = width // head_size
    place = pl.BlockSpec(memory_space=pl.ANY)
    forget = (count, size, 8, block)
    total = (part.shape[0] // (f_size * size), part.shape[1])
    return pl.pallas_call(
        functools.partial(context_back_kernel, heads, head_size),
        grid=(1,),
        out_shape=[
            jax.ShapeDtypeStruct(qkv.shape, BF16),
            jax.ShapeDtypeStruct(forget, F32),
            jax.ShapeDtypeStruct(total, F32),
            jax.ShapeDtypeStruct(table.shape[1:], BF16),
        ],
        in_specs=[
            place,
            full_block(qkv.shape),
            full_block(exact.shape),
            full_block(lse.shape),
            full_block(decay.shape),
            place,
            place,
        ],
        out_specs=[place, place, full_block(total), full_block(table.shape[1:])],
        scratch_shapes=[
            pltpu.VMEM(grads.shape, BF16),
            pltpu.VMEM(qkv.shape, BF16),
            pltpu.VMEM((8, size * block), F32),
            pltpu.VMEM(forget, F32),
            pltpu.VMEM((heads, size, block, width), F32),
            pltpu.VMEM((8, size * block), F32),
        ]
        + exchange_sems(count, size) * 3
        + sum_scratch(f_size, size, *total)
        + row_sum_scratch(*table.shape[1:]),
        compiler_params=remote_params(ident, 60),
        cost_estimate=attend_cost(qkv, heads, 5),
        name="context_back",
    )(grads, qkv, exact, lse, decay, part, table)


CHUNKS = 4
HALVES = 2


def tp_places():
    me = lax.axis_index("tp")
    sibling = me + 1 - 2 * lax.rem(me, 2)
    across = lax.rem(me + 2, 4)
    diagonal = lax.rem(sibling + 2, 4)
    return me, sibling, across, diagonal


def greet(peers):
    barrier = pltpu.get_barrier_semaphore()
    for peer in peers:
        pl.semaphore_signal(barrier, inc=1, device_id={"tp": peer}, device_id_type=MESH)
    pl.semaphore_wait(barrier, len(peers))


def sending(source, target, send_sem, recv_sem, peer):
    return pltpu.make_async_remote_copy(
        src_ref=source,
        dst_ref=target,
        send_sem=send_sem,
        recv_sem=recv_sem,
        device_id={"tp": peer},
        device_id_type=MESH,
    )


def pick(step, chunks, places):
    me, sibling, across, diagonal = places
    late = step - 2 * chunks
    far = jnp.where(lax.rem(late, 2) == 0, across, diagonal)
    slot = jnp.where(step < chunks, me, jnp.where(step < 2 * chunks, sibling, far))
    chunk = jnp.where(step < 2 * chunks, lax.rem(step, chunks), late // 2)
    return slot, chunk


def gather_loop(table, sems, compute, own=None, relative=False, between=None):
    near_send, near_recv, far_send, far_recv, pass_send, pass_recv = sems
    me, sibling, across, diagonal = tp_places()
    places = (0, 1, 2, 3) if relative else (me, sibling, across, diagonal)
    mine, near_by, far_off, corner = places
    near_spot, far_spot, pass_spot = (1, 2, 3) if relative else (me, me, across)
    rows = table.shape[1] // CHUNKS

    def part(slot, chunk):
        return table.at[slot, pl.ds(pl.multiple_of(chunk * rows, rows), rows)]

    def far(chunk):
        source = part(mine, chunk)
        if own is not None:
            source = own.at[pl.ds(pl.multiple_of(chunk * rows, rows), rows)]
        return sending(source, part(far_spot, chunk), far_send.at[chunk], far_recv.at[chunk], across)

    def far_arrival(chunk):
        spot = part(far_off, chunk)
        return sending(spot, spot, far_send.at[chunk], far_recv.at[chunk], across)

    def passing(chunk):
        return sending(
            part(far_off, chunk), part(pass_spot, chunk), pass_send.at[chunk], pass_recv.at[chunk], sibling
        )

    def pass_arrival(chunk):
        spot = part(corner, chunk)
        return sending(spot, spot, pass_send.at[chunk], pass_recv.at[chunk], sibling)

    for chunk in range(CHUNKS):
        far(chunk).start()
    own = table.at[mine] if own is None else own
    near = sending(own, table.at[near_spot], near_send, near_recv, sibling)
    near.start()

    def body(step, _):
        slot, chunk = pick(step, CHUNKS, places)
        late = step - 2 * CHUNKS

        @pl.when(step == CHUNKS)
        def _():
            spot = table.at[near_by]
            sending(spot, spot, near_send, near_recv, sibling).wait_recv()

        @pl.when((late >= 0) & (lax.rem(late, 2) == 0))
        def _():
            far_arrival(chunk).wait_recv()
            passing(chunk).start()

        @pl.when((late >= 0) & (lax.rem(late, 2) == 1))
        def _():
            pass_arrival(chunk).wait_recv()

        compute(slot, chunk)
        return 0

    if between is None:
        lax.fori_loop(0, 4 * CHUNKS, body, 0)
    else:
        lax.fori_loop(0, 2 * CHUNKS, body, 0)
        for turn in range(CHUNKS):
            between(turn)
            first = 2 * (CHUNKS + turn)
            lax.fori_loop(first, first + 2, body, 0)
    near.wait_send()
    for chunk in range(CHUNKS):
        far(chunk).wait_send()
        passing(chunk).wait_send()


GATHER_SEMS = [pltpu.SemaphoreType.DMA] * 2 + [pltpu.SemaphoreType.DMA((CHUNKS,))] * 4


def scatter_loop(buffers, sems, partial, finish, relative=False, between=None):
    near_out, near_in, far_out, far_in = buffers
    near_send, near_recv, far_send, far_recv = sems
    me, sibling, across, diagonal = tp_places()
    mine, near_by, far_off, corner = (0, 1, 2, 3) if relative else (me, sibling, across, diagonal)
    rows = far_out.shape[0] // CHUNKS

    def span(chunk):
        return pl.ds(pl.multiple_of(chunk * rows, rows), rows)

    def near(half, chunk):
        return sending(
            near_out.at[half, span(chunk)],
            near_in.at[half, span(chunk)],
            near_send.at[half, chunk],
            near_recv.at[half, chunk],
            sibling,
        )

    def far(chunk):
        return sending(
            far_out.at[span(chunk)],
            far_in.at[span(chunk)],
            far_send.at[chunk],
            far_recv.at[chunk],
            across,
        )

    def body(step, _):
        phase, chunk = step // CHUNKS, lax.rem(step, CHUNKS)
        slot = jnp.where(
            phase == 0, corner, jnp.where(phase == 1, far_off, jnp.where(phase == 2, near_by, mine))
        )
        value = partial(slot, chunk)
        spot = span(chunk)

        @pl.when(lax.rem(phase, 2) == 0)
        def _():
            half = phase // 2
            near_out[half, spot] = value.astype(BF16)
            near(half, chunk).start()

        @pl.when(phase == 1)
        def _():
            near(0, chunk).wait_recv()
            far_out[spot] = (value + near_in[0, spot].astype(F32)).astype(BF16)
            far(chunk).start()

        @pl.when(phase == 3)
        def _():
            near(1, chunk).wait_recv()
            far(chunk).wait_recv()
            finish(chunk, value + near_in[1, spot].astype(F32) + far_in[spot].astype(F32))

        return 0

    if between is None:
        lax.fori_loop(0, 4 * CHUNKS, body, 0)
    else:
        lax.fori_loop(0, 3 * CHUNKS, body, 0)
        for chunk in range(CHUNKS):
            between(chunk)
            lax.fori_loop(3 * CHUNKS + chunk, 3 * CHUNKS + chunk + 1, body, 0)
    for chunk in range(CHUNKS):
        near(0, chunk).wait_send()
        near(1, chunk).wait_send()
        far(chunk).wait_send()


SCATTER_SEMS = [pltpu.SemaphoreType.DMA((2, CHUNKS))] * 2 + [pltpu.SemaphoreType.DMA((CHUNKS,))] * 2


def scatter_buffers(rows, width):
    return [
        pltpu.VMEM((2, rows, width), BF16),
        pltpu.VMEM((2, rows, width), BF16),
        pltpu.VMEM((rows, width), BF16),
        pltpu.VMEM((rows, width), BF16),
    ]


def group_peers():
    f_size, c_size = lax.axis_size("fsdp"), lax.axis_size("ctx")
    f, c = lax.axis_index("fsdp"), lax.axis_index("ctx")
    return [
        {"fsdp": lax.rem(f + i, f_size), "ctx": lax.rem(c + j, c_size)}
        for i in range(f_size)
        for j in range(c_size)
        if i or j
    ]


def greet_all(peers):
    barrier = pltpu.get_barrier_semaphore()
    for peer in peers:
        pl.semaphore_signal(barrier, inc=1, device_id=peer, device_id_type=MESH)
    pl.semaphore_wait(barrier, len(peers))


def moving(source, target, send_sem, recv_sem, peer):
    return pltpu.make_async_remote_copy(
        src_ref=source,
        dst_ref=target,
        send_sem=send_sem,
        recv_sem=recv_sem,
        device_id=peer,
        device_id_type=MESH,
    )


class WeightGather:
    def __init__(self, shard, full, sems):
        self.shard, self.full = shard, full
        self.f_size, self.c_size = lax.axis_size("fsdp"), lax.axis_size("ctx")
        self.f, self.c = lax.axis_index("fsdp"), lax.axis_index("ctx")
        self.sems = sems

    def half(self, h):
        wide = self.shard.shape[1] // HALVES
        return pl.ds(h * wide, wide)

    def spot(self, c, h, f=None):
        rows = self.shard.shape[0]
        block = (self.f if f is None else f) * self.c_size + c
        return self.full.at[pl.ds(pl.multiple_of(block * rows, rows), rows), self.half(h)]

    def own(self):
        rows = self.shard.shape[0]
        block = self.f * self.c_size + self.c
        target = self.full.at[pl.ds(pl.multiple_of(block * rows, rows), rows)]
        return pltpu.make_async_copy(self.shard, target, self.sems[4])

    def along(self, c, h, hop, side, first=False):
        source = self.shard.at[:, self.half(h)] if first else self.spot(c, h)
        peer = {"ctx": self.c + (1 if side else -1)}
        send, recv = self.sems[0].at[side, hop, h], self.sems[1].at[side, hop, h]
        return moving(source, self.spot(c, h), send, recv, peer)

    def over(self, c, h, step, first=False):
        source = self.shard.at[:, self.half(h)] if first else self.spot(c, h)
        peer = {"fsdp": lax.rem(self.f + step, self.f_size)}
        send, recv = self.sems[2].at[step, c, h], self.sems[3].at[step, c, h]
        return moving(source, self.spot(c, h), send, recv, peer)

    def over_arrival(self, c, h, step):
        spot = self.spot(c, h, lax.rem(self.f + self.f_size - step, self.f_size))
        peer = {"fsdp": lax.rem(self.f + step, self.f_size)}
        return moving(spot, spot, self.sems[2].at[step, c, h], self.sems[3].at[step, c, h], peer)

    def can(self, side):
        return self.c + 1 < self.c_size if side else self.c > 0

    def holds(self, hop, side):
        return self.c - hop >= 0 if side else self.c + hop < self.c_size

    def begin(self):
        self.own().start()
        for h in range(HALVES):
            for side in (1, 0):

                @pl.when(self.can(side))
                def _(side=side):
                    self.along(self.c, h, 1, side, True).start()

            for step in range(1, self.f_size):
                self.over(self.c, h, step, True).start()

    def advance(self, hop):
        for h in range(HALVES):
            for side in (1, 0):

                @pl.when(self.holds(hop, side))
                def _(side=side):
                    c = self.c - hop if side else self.c + hop
                    self.along(c, h, hop, side).wait_recv()

                    @pl.when(self.can(side))
                    def _():
                        self.along(c, h, hop + 1, side).start()

                    for step in range(1, self.f_size):
                        self.over(c, h, step).start()

    def end(self):
        self.own().wait()
        for h in range(HALVES):
            for step in range(1, self.f_size):
                for c in range(self.c_size):
                    self.over_arrival(c, h, step).wait_recv()
                    self.over(c, h, step).wait_send()
            for side in (1, 0):

                @pl.when(self.can(side))
                def _(side=side):
                    self.along(self.c, h, 1, side, True).wait_send()

                for hop in range(1, self.c_size):

                    @pl.when(self.holds(hop, side) & self.can(side))
                    def _(side=side, hop=hop):
                        c = self.c - hop if side else self.c + hop
                        self.along(c, h, hop + 1, side).wait_send()


def weight_sems(f_size, c_size):
    dma = pltpu.SemaphoreType.DMA
    return [dma((2, c_size + 1, HALVES))] * 2 + [dma((f_size, c_size, HALVES))] * 2 + [dma]


class WeightSum:
    def __init__(self, part, first_column, out, refs):
        self.part, self.out, self.first = part, out, first_column
        self.stage, self.total, self.along_in = refs[:3]
        self.own_sem, self.over_send, self.over_recv, self.along_send, self.along_recv = refs[3:]
        self.f_size, self.c_size = lax.axis_size("fsdp"), lax.axis_size("ctx")
        self.f, self.c = lax.axis_index("fsdp"), lax.axis_index("ctx")
        self.rows, self.wide = out.shape[0], out.shape[1] // HALVES
        ends = [(self.c_size - 1 - i // 2) if i % 2 == 0 else i // 2 for i in range(self.c_size)]
        self.order = [(c, h) for c in ends for h in range(HALVES)]
        self.stages = len(self.order) + self.c_size - 1

    def piece(self, f, c, h):
        row = (f * self.c_size + c) * self.rows
        columns = pl.ds(self.first + h * self.wide, self.wide)
        return self.part.at[pl.ds(pl.multiple_of(row, self.rows), self.rows), columns]

    def own(self, c, h):
        n = c * HALVES + h
        return pltpu.make_async_copy(self.piece(self.f, c, h), self.stage.at[n], self.own_sem.at[n])

    def over(self, c, h, step):
        f, n = lax.rem(self.f + step, self.f_size), c * HALVES + h
        return moving(
            self.piece(f, c, h),
            self.total.at[step - 1, n],
            self.over_send.at[step - 1, n],
            self.over_recv.at[step - 1, n],
            {"fsdp": f},
        )

    def along(self, c, h, side, source=None):
        peer, n = {"ctx": self.c + (1 if side else -1)}, c * HALVES + h
        target = self.along_in.at[side, n]
        return moving(
            target if source is None else source,
            target,
            self.along_send.at[side, n],
            self.along_recv.at[side, n],
            peer,
        )

    def launch(self, i):
        if i < len(self.order):
            for step in range(1, self.f_size):
                self.over(*self.order[i], step).start()

    def begin(self):
        for c, h in self.order:
            self.own(c, h).start()
        self.launch(0)
        self.launch(1)

    def receive(self, i):
        c, h = self.order[i]
        n = c * HALVES + h
        self.own(c, h).wait()
        value = self.stage[n].astype(F32)
        for step in range(1, self.f_size):
            self.over(c, h, step).wait_recv()
        self.launch(i + 2)
        for step in range(1, self.f_size):
            value = value + self.total[step - 1, n].astype(F32)
        self.total[0, n] = value.astype(BF16)
        for side, end in ((1, 0), (0, self.c_size - 1)):
            if c != end:

                @pl.when(self.c == end)
                def _(side=side):
                    self.along(c, h, side, self.total.at[0, n]).start()

    def hop(self, c, h, side, device):
        n = c * HALVES + h

        @pl.when(self.c == device)
        def _():
            self.along(c, h, side).wait_recv()
            value = self.total[0, n].astype(F32) + self.along_in[side, n].astype(F32)
            if device == c:
                self.total[0, n] = value.astype(BF16)
            else:
                self.along_in[side, n] = value.astype(BF16)
                self.along(c, h, side).start()

    def run(self, n):
        if n < len(self.order):
            self.receive(n)
        for i, (c, h) in enumerate(self.order):
            if 1 <= n - i <= c:
                self.hop(c, h, 1, n - i)
            if 1 <= n - i <= self.c_size - 1 - c:
                self.hop(c, h, 0, self.c_size - 1 - (n - i))

    def run_share(self, turn, turns):
        share = -(-self.stages // turns)
        for n in range(turn * share, min(self.stages, (turn + 1) * share)):
            self.run(n)

    def end(self):
        for c in range(self.c_size):

            @pl.when(self.c == c)
            def _(c=c):
                for h in range(HALVES):
                    columns = pl.ds(h * self.wide, self.wide)
                    self.out[:, columns] = self.total[0, c * HALVES + h].astype(F32)

        for c, h in self.order:
            for step in range(1, self.f_size):
                self.over(c, h, step).wait_send()
            for side in (1, 0):

                @pl.when(self.c < c if side else self.c > c)
                def _(side=side):
                    self.along(c, h, side).wait_send()


def sum_scratch(f_size, c_size, rows, columns):
    dma, count, wide = pltpu.SemaphoreType.DMA, c_size * HALVES, columns // HALVES
    return (
        [
            pltpu.VMEM((count, rows, wide), BF16),
            pltpu.VMEM((f_size - 1, count, rows, wide), BF16),
            pltpu.VMEM((2, count, rows, wide), BF16),
        ]
        + [dma((count,))]
        + [dma((f_size - 1, count))] * 2
        + [dma((2, count))] * 2
    )


class RowGather:
    def __init__(self, rows, table, sems):
        self.rows, self.table, self.sems = rows, table, sems
        _, self.sibling, self.across, _ = tp_places()

    def own(self):
        return pltpu.make_async_copy(self.rows, self.table.at[0], self.sems[2])

    def copy(self, n):
        source = self.table.at[2] if n == 2 else self.rows
        peer = {"tp": self.across if n == 1 else self.sibling}
        return moving(source, self.table.at[n + 1], self.sems[0].at[n], self.sems[1].at[n], peer)

    def begin(self):
        self.own().start()
        self.copy(0).start()
        self.copy(1).start()

    def advance(self):
        self.copy(1).wait_recv()
        self.copy(2).start()

    def end(self):
        self.own().wait()
        self.copy(0).wait()
        self.copy(1).wait_send()
        self.copy(2).wait()


class RowSum:
    def __init__(self, table, out, refs):
        self.table, self.out = table, out
        self.mine, self.near, self.far_out, self.far_in, self.send, self.recv, self.own_sem = refs
        _, self.sibling, self.across, _ = tp_places()

    def own(self, n):
        return pltpu.make_async_copy(self.table.at[0 if n else 2], self.mine.at[n], self.own_sem.at[n])

    def copy(self, n):
        if n == 2:
            source, target, peer = self.far_out, self.far_in, self.across
        else:
            source, target, peer = self.table.at[1 if n else 3], self.near.at[n], self.sibling
        return moving(source, target, self.send.at[n], self.recv.at[n], {"tp": peer})

    def begin(self):
        for n in range(2):
            self.own(n).start()
            self.copy(n).start()

    def advance(self):
        self.own(0).wait()
        self.copy(0).wait_recv()
        self.far_out[...] = (self.mine[0].astype(F32) + self.near[0].astype(F32)).astype(BF16)
        self.copy(2).start()

    def end(self):
        self.own(1).wait()
        self.copy(1).wait_recv()
        self.copy(2).wait_recv()
        total = self.mine[1].astype(F32) + self.near[1].astype(F32)
        self.out[...] = (total + self.far_in[...].astype(F32)).astype(BF16)
        for n in range(3):
            self.copy(n).wait_send()


def row_sum_scratch(rows, width):
    dma, pair, one = pltpu.SemaphoreType.DMA, (2, rows, width), (rows, width)
    return [pltpu.VMEM(pair, BF16)] * 2 + [pltpu.VMEM(one, BF16)] * 2 + [dma((3,))] * 2 + [dma((2,))]


def startup_kernel(rows_ref, shard_ref, gain_ref, all_ref, full_ref, gains_ref, own_sem, *sems):
    me, sibling, across, diagonal = tp_places()
    others = group_peers()
    greet_all([{"tp": sibling}, {"tp": across}] + others)
    near_send, near_recv, far_send, far_recv, pass_send, pass_recv = sems[:6]
    gather = WeightGather(shard_ref, full_ref, sems[6:11])
    gain_send, gain_recv, gain_own = sems[11:]
    spot = gains_ref.at[gather.f * gather.c_size + gather.c]
    gain_copies = [
        moving(gain_ref, spot, gain_send.at[n], gain_recv.at[n], peer) for n, peer in enumerate(others)
    ]
    for copy in gain_copies:
        copy.start()
    own_gain = pltpu.make_async_copy(gain_ref, spot, gain_own)
    own_gain.start()
    size = rows_ref.shape[0] // CHUNKS
    own = pltpu.make_async_copy(rows_ref, all_ref.at[me], own_sem)
    own.start()

    def span(chunk):
        return pl.ds(chunk * size, size)

    def far(chunk):
        return sending(
            rows_ref.at[span(chunk)],
            all_ref.at[me, span(chunk)],
            far_send.at[chunk],
            far_recv.at[chunk],
            across,
        )

    def passing(chunk):
        spot = all_ref.at[across, span(chunk)]
        return sending(spot, spot, pass_send.at[chunk], pass_recv.at[chunk], sibling)

    for chunk in range(CHUNKS):
        far(chunk).start()
    gather.begin()
    near = sending(rows_ref, all_ref.at[me], near_send, near_recv, sibling)
    near.start()
    for turn in range(max(CHUNKS, gather.c_size - 1)):
        if turn < CHUNKS:
            far(turn).wait_recv()
            passing(turn).start()
        if turn + 1 < gather.c_size:
            gather.advance(turn + 1)
    near.wait()
    for chunk in range(CHUNKS):
        far(chunk).wait_send()
        passing(chunk).wait()
    own.wait()
    gather.end()
    for copy in gain_copies:
        copy.wait()
    own_gain.wait()


def startup(rows, shard, gains, f_size, c_size, ident):
    place = pl.BlockSpec(memory_space=pl.ANY)
    full = (shard.shape[0] * f_size * c_size, shard.shape[1])
    return pl.pallas_call(
        startup_kernel,
        out_shape=[
            jax.ShapeDtypeStruct((4,) + rows.shape, BF16),
            jax.ShapeDtypeStruct(full, BF16),
            jax.ShapeDtypeStruct((f_size * c_size,) + gains.shape, F32),
        ],
        in_specs=[place] * 3,
        out_specs=[place] * 3,
        scratch_shapes=[pltpu.SemaphoreType.DMA]
        + GATHER_SEMS
        + weight_sems(f_size, c_size)
        + [pltpu.SemaphoreType.DMA((f_size * c_size - 1,))] * 2
        + [pltpu.SemaphoreType.DMA],
        compiler_params=pltpu.CompilerParams(collective_id=ident, has_side_effects=True),
        name="startup",
    )(rows, shard, gains)


def whole(shape, column=None):
    zeros = (0,) * (len(shape) - 1)
    return pl.BlockSpec(shape, lambda i: zeros + (column or 0,), pipeline_mode=pl.Buffered(1))


def remote_params(ident, megabytes):
    return pltpu.CompilerParams(
        collective_id=ident, has_side_effects=True, vmem_limit_bytes=megabytes << 20, dimension_semantics=("arbitrary",)
    )


def project_kernel(layout, x_ref, gain_ref, w_ref, normed_ref, forget_ref, items_ref):
    seq_count, groups, width, places = layout
    x = x_ref[0].astype(F32)
    normed = (x * lax.rsqrt(jnp.mean(x * x, axis=1, keepdims=True) + epsilon) * gain_ref[...]).astype(BF16)
    normed_ref[0] = normed
    inner = groups * width
    rows = x.shape[0] // seq_count
    count = items_ref.shape[0]
    for kind in range(3):
        value = dot(normed, w_ref[:, kind * inner : (kind + 1) * inner], NN).astype(BF16)
        for slot, (s, g) in enumerate(places):
            piece = value[s * rows : (s + 1) * rows, g * width : (g + 1) * width]
            items_ref[slot % count, slot // count, kind] = piece
    forget_ref[0] = dot(normed, w_ref[:, 3 * inner :], NN)


def project(x_all, gain, full_one, layout, item_count, ctx_size):
    seq_count, groups, width, places = layout
    tp_size, rows, model_width = x_all.shape
    local = rows // seq_count
    item = jax.ShapeDtypeStruct((item_count, ctx_size, 3, tp_size * local, width), BF16)
    columns = full_one.shape[1]
    block = pl.BlockSpec((1, rows, model_width), lambda t: (t, 0, 0))
    return pl.pallas_call(
        functools.partial(project_kernel, layout),
        grid=(tp_size,),
        out_shape=[
            jax.ShapeDtypeStruct(x_all.shape, BF16),
            jax.ShapeDtypeStruct((tp_size, rows, LANES), F32),
            item,
        ],
        in_specs=[
            block,
            pl.BlockSpec((1, model_width), lambda t: (0, 0)),
            pl.BlockSpec((model_width, columns), lambda t: (0, 0), pipeline_mode=pl.Buffered(1)),
        ],
        out_specs=[
            block,
            pl.BlockSpec((1, rows, LANES), lambda t: (t, 0, 0)),
            pl.BlockSpec((item_count, ctx_size, 3, local, width), lambda t: (0, 0, 0, t, 0)),
        ],
        compiler_params=pltpu.CompilerParams(vmem_limit_bytes=48 << 20, dimension_semantics=("arbitrary",)),
        cost_estimate=pl.CostEstimate(
            flops=2 * x_all.size * columns, bytes_accessed=4 * x_all.size, transcendentals=0
        ),
        name="project",
    )(x_all, gain, full_one)


def out_kernel(layout, x_ref, gate_ref, w_ref, gain_ref, items, *refs):
    seq_count, groups, width, places = layout
    hidden_ref, normed_ref, attended_ref, mixed_ref = refs[:4]
    buffers, sems = refs[4:8], refs[8:]
    count = items.shape[0]
    me, sibling, across, diagonal = tp_places()
    greet((sibling, across))
    tp_size, rows, _ = gate_ref.shape
    local = rows // seq_count

    def mix(t, _):
        here = pl.ds(pl.multiple_of(t * local, local), local)
        for slot, (s, g) in enumerate(places[: seq_count * groups]):
            there = (t, pl.ds(s * local, local), pl.ds(g * width, width))
            value = items[slot % count, slot // count, here]
            attended_ref[there] = value
            mixed_ref[there] = (value.astype(F32) * gate_ref[there]).astype(BF16)
        return 0

    lax.fori_loop(0, tp_size, mix, 0)
    size = rows // CHUNKS

    def span(chunk):
        return pl.ds(pl.multiple_of(chunk * size, size), size)

    def partial(slot, chunk):
        return dot(mixed_ref[slot, span(chunk)], w_ref[...], NT)

    def finish(chunk, total):
        hidden = x_ref[span(chunk)].astype(F32) + total
        hidden_ref[span(chunk)] = hidden
        inverse = lax.rsqrt(jnp.mean(hidden * hidden, axis=1, keepdims=True) + epsilon)
        normed_ref[span(chunk)] = (hidden * inverse * gain_ref[...]).astype(BF16)

    scatter_loop(buffers, sems, partial, finish)


def out_project(x, gate, full_two, column, gain, items, layout, ident):
    seq_count, groups, width, places = layout
    rows, model_width = x.shape
    inner = groups * width
    tp_size = gate.shape[0]
    return pl.pallas_call(
        functools.partial(out_kernel, layout),
        grid=(1,),
        out_shape=[
            jax.ShapeDtypeStruct(x.shape, F32),
            jax.ShapeDtypeStruct(x.shape, BF16),
            jax.ShapeDtypeStruct(gate.shape, BF16),
            jax.ShapeDtypeStruct(gate.shape, BF16),
        ],
        in_specs=[
            whole(x.shape),
            whole(gate.shape),
            whole((model_width, inner), column),
            whole(gain.shape),
            whole(items.shape),
        ],
        out_specs=[whole(x.shape), whole(x.shape), whole(gate.shape), whole(gate.shape)],
        scratch_shapes=scatter_buffers(rows, model_width) + SCATTER_SEMS,
        compiler_params=remote_params(ident, 48),
        cost_estimate=pl.CostEstimate(
            flops=2 * gate.size * model_width, bytes_accessed=100 << 20, transcendentals=0
        ),
        name="out_project",
    )(x, gate, full_two, gain, items)


def mlp_kernel(normed_ref, grad_ref, gate_w, up_w, down_w, all_ref, inner_ref, pair_ref, table, own_sem, *sems):
    me, sibling, across, diagonal = tp_places()
    greet((sibling, across))
    table[0] = normed_ref[...]
    rows, hidden = table.shape[1] // CHUNKS, gate_w.shape[1]
    tile = min(hidden, 512)

    def compute(slot, chunk):
        spot = pl.ds(pl.multiple_of(chunk * rows, rows), rows)
        normed, grad = table[slot, spot], grad_ref[slot, spot]
        for start in range(0, hidden, tile):
            columns = pl.ds(start, tile)
            gate = dot(normed, gate_w[:, columns], NN)
            up = dot(normed, up_w[:, columns], NN)
            back = dot(grad, down_w[:, columns], NN)
            sig = 1.0 / (1.0 + jnp.exp(-gate))
            silu = gate * sig
            inner_ref[slot, spot, columns] = (silu * up).astype(BF16)
            pair_ref[slot, spot, columns] = (back * up * sig * (1.0 + gate * (1.0 - sig))).astype(BF16)
            pair_ref[slot, spot, pl.ds(hidden + start, tile)] = (back * silu).astype(BF16)

    gather_loop(table, sems, compute, relative=True)
    copy = pltpu.make_async_copy(table, all_ref, own_sem)
    copy.start()
    copy.wait()


def mlp(normed, grad_all, full_two, hidden, ident):
    tp_size, rows, model_width = grad_all.shape
    total = tp_size * rows
    return pl.pallas_call(
        mlp_kernel,
        grid=(1,),
        out_shape=[
            jax.ShapeDtypeStruct(grad_all.shape, BF16),
            jax.ShapeDtypeStruct((tp_size, rows, hidden), BF16),
            jax.ShapeDtypeStruct((tp_size, rows, 2 * hidden), BF16),
        ],
        in_specs=[whole(normed.shape), whole(grad_all.shape)]
        + [whole((model_width, hidden), column) for column in range(3)],
        out_specs=[
            pl.BlockSpec(memory_space=pl.ANY),
            whole((tp_size, rows, hidden)),
            whole((tp_size, rows, 2 * hidden)),
        ],
        scratch_shapes=[pltpu.VMEM(grad_all.shape, BF16), pltpu.SemaphoreType.DMA] + GATHER_SEMS,
        compiler_params=remote_params(ident, 56),
        cost_estimate=pl.CostEstimate(
            flops=6 * total * model_width * hidden, bytes_accessed=100 << 20, transcendentals=total * hidden
        ),
        name="mlp",
    )(normed, grad_all, full_two, full_two, full_two)


def mlp_back_kernel(
    pair_ref, w_ref, hidden_ref, grad_ref, gain_ref, sums_ref, out_ref, branch_ref, part_ref, sum_ref, *refs
):
    buffers, sems = refs[:4], refs[4:8]
    me, sibling, across, diagonal = tp_places()
    greet_all([{"tp": sibling}, {"tp": across}] + group_peers())
    weights = WeightSum(sums_ref, 0, sum_ref, refs[8:])
    weights.begin()
    part_ref[...] = jnp.zeros_like(part_ref)
    size = hidden_ref.shape[0] // CHUNKS

    def span(chunk):
        return pl.ds(pl.multiple_of(chunk * size, size), size)

    def partial(slot, chunk):
        return dot(pair_ref[slot, span(chunk)], w_ref[...], NT)

    def finish(chunk, total):
        hidden = hidden_ref[span(chunk)]
        inverse = lax.rsqrt(jnp.mean(hidden * hidden, axis=1, keepdims=True) + epsilon)
        unit = hidden * inverse
        part_ref[...] += jnp.sum(total * unit, axis=0, keepdims=True)
        scaled = total * gain_ref[...]
        middle = jnp.mean(scaled * unit, axis=1, keepdims=True)
        grad = grad_ref[span(chunk)].astype(F32) + inverse * (scaled - unit * middle)
        out_ref[span(chunk)] = grad
        branch_ref[span(chunk)] = grad.astype(BF16)

    scatter_loop(
        buffers, sems, partial, finish, relative=True, between=lambda turn: weights.run_share(turn, CHUNKS)
    )
    weights.end()


def mlp_back(pair, full_two, hidden_state, grad_out, gain, part, f_size, c_size, ident):
    tp_size, rows, wide = pair.shape
    model_width = hidden_state.shape[1]
    total = (part.shape[0] // (f_size * c_size), part.shape[1] // 2)
    return pl.pallas_call(
        mlp_back_kernel,
        grid=(1,),
        out_shape=[
            jax.ShapeDtypeStruct(hidden_state.shape, F32),
            jax.ShapeDtypeStruct(hidden_state.shape, BF16),
            jax.ShapeDtypeStruct(gain.shape, F32),
            jax.ShapeDtypeStruct(total, F32),
        ],
        in_specs=[
            whole(pair.shape),
            whole((model_width, wide), 0),
            whole(hidden_state.shape),
            whole(grad_out.shape),
            whole(gain.shape),
            pl.BlockSpec(memory_space=pl.ANY),
        ],
        out_specs=[
            whole(hidden_state.shape),
            whole(hidden_state.shape),
            whole(gain.shape),
            whole(total),
        ],
        scratch_shapes=scatter_buffers(rows, model_width)
        + SCATTER_SEMS
        + sum_scratch(f_size, c_size, *total),
        compiler_params=remote_params(ident, 56),
        cost_estimate=pl.CostEstimate(
            flops=2 * pair.size * model_width, bytes_accessed=100 << 20, transcendentals=0
        ),
        name="mlp_back",
    )(pair, full_two, hidden_state, grad_out, gain, part)


def out_back_kernel(layout, branch_ref, w_ref, gate_ref, attended_ref, sums_ref, *refs):
    seq_count, groups, width, places = layout
    all_ref, logit_ref, items, sum_ref, table, grads, own_sem = refs[:7]
    sems = refs[7:13]
    count = items.shape[0]
    me, sibling, across, diagonal = tp_places()
    greet_all([{"tp": sibling}, {"tp": across}] + group_peers())
    weights = WeightSum(sums_ref, sum_ref.shape[1], sum_ref, refs[13:])
    weights.begin()
    table[me] = branch_ref[...]
    tp_size, rows, _ = gate_ref.shape
    local, size = rows // seq_count, rows // CHUNKS

    def compute(slot, chunk):
        spot = pl.ds(pl.multiple_of(chunk * size, size), size)
        mixed = dot(table[slot, spot], w_ref[...], NN)
        gate = gate_ref[slot, spot]
        scaled = mixed * gate
        grads[slot, spot] = scaled.astype(BF16)
        attended = attended_ref[slot, spot].astype(F32)
        logit_ref[slot, spot] = (scaled * attended * (1.0 - gate)).astype(BF16)

    gather_loop(table, sems, compute, between=lambda turn: weights.run_share(turn, CHUNKS))
    copy = pltpu.make_async_copy(table, all_ref, own_sem)
    copy.start()

    def deal(t, _):
        here = pl.ds(pl.multiple_of(t * local, local), local)
        for slot, (s, g) in enumerate(places):
            piece = grads[t, pl.ds(s * local, local), pl.ds(g * width, width)]
            items[slot % count, slot // count, here] = piece
        return 0

    lax.fori_loop(0, tp_size, deal, 0)
    copy.wait()
    weights.end()


def out_back(branch, full_two, column, gate, attended, part, layout, item_count, f_size, ctx_size, ident):
    seq_count, groups, width, places = layout
    rows, model_width = branch.shape
    tp_size, _, inner = gate.shape
    item = (item_count, ctx_size, tp_size * rows // seq_count, width)
    table = (tp_size, rows, model_width)
    total = (part.shape[0] // (f_size * ctx_size), part.shape[1] // 2)
    return pl.pallas_call(
        functools.partial(out_back_kernel, layout),
        grid=(1,),
        out_shape=[
            jax.ShapeDtypeStruct(table, BF16),
            jax.ShapeDtypeStruct(gate.shape, BF16),
            jax.ShapeDtypeStruct(item, BF16),
            jax.ShapeDtypeStruct(total, F32),
        ],
        in_specs=[
            whole(branch.shape),
            whole((model_width, inner), column),
            whole(gate.shape),
            whole(attended.shape),
            pl.BlockSpec(memory_space=pl.ANY),
        ],
        out_specs=[pl.BlockSpec(memory_space=pl.ANY), whole(gate.shape), whole(item), whole(total)],
        scratch_shapes=[pltpu.VMEM(table, BF16), pltpu.VMEM(gate.shape, BF16), pltpu.SemaphoreType.DMA]
        + GATHER_SEMS
        + sum_scratch(f_size, ctx_size, *total),
        compiler_params=remote_params(ident, 48),
        cost_estimate=pl.CostEstimate(
            flops=2 * gate.size * model_width, bytes_accessed=100 << 20, transcendentals=0
        ),
        name="out_back",
    )(branch, full_two, gate, attended, part)


def assemble_kernel(layout, items, out_ref):
    seq_count, groups, width, places = layout
    count, local = items.shape[0], items.shape[3]
    inner = groups * width
    for slot, (s, g) in enumerate(places[: seq_count * groups]):
        for kind in range(3):
            columns = pl.ds(kind * inner + g * width, width)
            out_ref[0, pl.ds(s * local, local), columns] = items[slot % count, slot // count, kind]


def assemble(items, layout, tp_size):
    seq_count, groups, width, places = layout
    count, ctx_size, kinds, ctx_rows, _ = items.shape
    local = ctx_rows // tp_size
    shape = (tp_size, seq_count * local, kinds * groups * width)
    return pl.pallas_call(
        functools.partial(assemble_kernel, layout),
        grid=(tp_size,),
        out_shape=jax.ShapeDtypeStruct(shape, BF16),
        in_specs=[pl.BlockSpec((count, ctx_size, kinds, local, width), lambda t: (0, 0, 0, t, 0))],
        out_specs=pl.BlockSpec((1,) + shape[1:], lambda t: (t, 0, 0)),
        compiler_params=pltpu.CompilerParams(vmem_limit_bytes=32 << 20, dimension_semantics=("arbitrary",)),
        cost_estimate=pl.CostEstimate(flops=0, bytes_accessed=16 << 20, transcendentals=0),
        name="assemble",
    )(items)


def last_kernel(
    qkv_ref,
    logit_ref,
    forget_ref,
    qkv_w,
    forget_w,
    gate_w,
    x_ref,
    grad_ref,
    gain_ref,
    part_ref,
    extra_ref,
    out_ref,
    sum_ref,
    vector_ref,
    *refs,
):
    buffers, sems, (mine, near_in, group_in) = refs[:4], refs[4:8], refs[8:11]
    vector_sems, sum_refs = refs[11:15], refs[15:]
    me, sibling, across, diagonal = tp_places()
    others = group_peers()
    greet_all([{"tp": sibling}, {"tp": across}, {"tp": diagonal}] + others)
    weights = WeightSum(part_ref, 0, sum_ref, sum_refs)
    weights.begin()
    mine[...] = extra_ref[...]
    size = x_ref.shape[0] // CHUNKS

    def span(chunk):
        return pl.ds(pl.multiple_of(chunk * size, size), size)

    def partial(slot, chunk):
        value = dot(qkv_ref[slot, span(chunk)], qkv_w[...], NT)
        value = value + dot(logit_ref[slot, span(chunk)], gate_w[...], NT)
        return value + dot(forget_ref[slot, span(chunk)], forget_w[...], NT)

    def finish(chunk, total):
        x = x_ref[span(chunk)].astype(F32)
        inverse = lax.rsqrt(jnp.mean(x * x, axis=1, keepdims=True) + epsilon)
        unit = x * inverse
        mine[0:1] += jnp.sum(total * unit, axis=0, keepdims=True)
        scaled = total * gain_ref[...]
        middle = jnp.mean(scaled * unit, axis=1, keepdims=True)
        out_ref[span(chunk)] = (grad_ref[span(chunk)] + inverse * (scaled - unit * middle)).astype(BF16)

    scatter_loop(
        buffers, sems, partial, finish, between=lambda turn: weights.run_share(turn, CHUNKS)
    )
    near_send, near_recv, group_send, group_recv = vector_sems
    copies = []
    for n, peer in enumerate((sibling, across, diagonal)):
        copies.append(sending(mine, near_in.at[n], near_send.at[n], near_recv.at[n], peer))
        copies[-1].start()
    for copy in copies:
        copy.wait()
    vector_ref[...] = mine[...] + near_in[0] + near_in[1] + near_in[2]
    mine[...] = vector_ref[...]
    copies = []
    for n, peer in enumerate(others):
        copies.append(moving(mine, group_in.at[n], group_send.at[n], group_recv.at[n], peer))
        copies[-1].start()
    for n, copy in enumerate(copies):
        copy.wait()
        vector_ref[...] += group_in[n]
    weights.end()


def last(grad_qkv, grad_logit, grad_forget, full_one, full_two, column, x, grad_hidden, gain, part, extra, f_size, c_size, ident):
    rows, model_width = x.shape
    wide, inner = grad_qkv.shape[2], grad_logit.shape[2]
    shard, columns = part.shape[0] // (f_size * c_size), part.shape[1]
    dma = pltpu.SemaphoreType.DMA
    return pl.pallas_call(
        last_kernel,
        grid=(1,),
        out_shape=[
            jax.ShapeDtypeStruct(x.shape, BF16),
            jax.ShapeDtypeStruct((shard, columns), F32),
            jax.ShapeDtypeStruct(extra.shape, F32),
        ],
        in_specs=[
            whole(grad_qkv.shape),
            whole(grad_logit.shape),
            whole(grad_forget.shape),
            whole((model_width, wide), 0),
            whole((model_width, LANES), wide // LANES),
            whole((model_width, inner), column),
            whole(x.shape),
            whole(x.shape),
            whole(gain.shape),
            pl.BlockSpec(memory_space=pl.ANY),
            whole(extra.shape),
        ],
        out_specs=[whole(x.shape), whole((shard, columns)), whole(extra.shape)],
        scratch_shapes=scatter_buffers(rows, model_width)
        + SCATTER_SEMS
        + [
            pltpu.VMEM(extra.shape, F32),
            pltpu.VMEM((3,) + extra.shape, F32),
            pltpu.VMEM((f_size * c_size - 1,) + extra.shape, F32),
        ]
        + [dma((3,))] * 2
        + [dma((f_size * c_size - 1,))] * 2
        + sum_scratch(f_size, c_size, shard, columns),
        compiler_params=remote_params(ident, 60),
        cost_estimate=pl.CostEstimate(
            flops=8 * rows * model_width * (wide + inner + LANES), bytes_accessed=100 << 20, transcendentals=0
        ),
        name="last",
    )(grad_qkv, grad_logit, grad_forget, full_one, full_one, full_two, x, grad_hidden, gain, part, extra)


def per_device(
    layer_input,
    lengths,
    attn_gain,
    w_query,
    w_key,
    w_value,
    w_forget,
    forget_bias,
    w_gate_out,
    w_out,
    mlp_gain,
    w_gate,
    w_up,
    w_down,
    cotangent,
):
    local_rows, seq_count, model_width = layer_input.shape
    head_count = forget_bias.shape[0]
    inner_width = w_query.shape[1]
    hidden = w_gate.shape[1]
    head_size = inner_width // head_count
    tp_size = lax.axis_size("tp")
    ctx_size = lax.axis_size("ctx")
    shard_count = lax.axis_size("fsdp") * ctx_size
    ctx_rows = local_rows * tp_size
    seq_len = ctx_rows * ctx_size
    all_rows = seq_count * ctx_rows
    ctx_index = lax.axis_index("ctx")
    tp_index = lax.axis_index("tp")
    shard_index = lax.axis_index("fsdp") * ctx_size + ctx_index

    pair = LANES // head_size
    groups = head_count // pair
    width = pair * head_size
    item_count = pl.cdiv(seq_count * groups, ctx_size)
    used = seq_count * groups

    def place(slot):
        slot = slot % used
        return (slot // groups + slot % groups) % seq_count, slot % groups

    places = tuple(place(slot) for slot in range(ctx_size * item_count))
    layout = (seq_count, groups, width, places)

    fsdp_size = lax.axis_size("fsdp")
    packed_one = jnp.concatenate(
        [
            w_query,
            w_key,
            w_value,
            w_forget,
            jnp.zeros((attn_gain.shape[0], LANES - head_count), BF16),
        ],
        axis=1,
    )
    packed_two = jnp.concatenate([w_gate, w_up, w_down, w_out, w_gate_out], axis=1)
    edge = 3 * inner_width
    input_rows = layer_input.transpose(1, 0, 2).reshape(seq_count * local_rows, model_width)
    shard_rows = model_width // shard_count
    own_gains = jnp.stack([attn_gain, mlp_gain]).astype(F32)
    own_gains = jnp.pad(own_gains, ((0, 6), (0, -shard_rows % LANES)))
    input_all, full_one, gains = startup(
        input_rows, packed_one, own_gains, fsdp_size, ctx_size, 1
    )
    gain_one = gains[:, 0, :shard_rows].reshape(1, model_width)
    gain_two = gains[:, 1, :shard_rows].reshape(1, model_width)
    out_column = 3 * hidden // inner_width

    def by_sequence(rows):
        return rows.transpose(1, 0, 2).reshape(seq_count * local_rows, model_width)

    def by_position(rows):
        return rows.reshape(seq_count, local_rows, model_width).transpose(1, 0, 2)

    local_pos = (ctx_index * tp_size + tp_index) * local_rows + jnp.arange(
        local_rows, dtype=jnp.int32
    )
    valid_rows = (local_pos[None, :] < lengths[:, None]).astype(F32)
    valid_rows = valid_rows.reshape(seq_count * local_rows, 1)
    ctx_pos = ctx_index * ctx_rows + jnp.arange(ctx_rows, dtype=jnp.int32)
    ctx_pos = ctx_pos.reshape(tp_size, 1, local_rows)
    ctx_valid = (ctx_pos < lengths[None, :, None]).astype(F32)

    grad_out = (valid_rows * by_sequence(cotangent).astype(F32)).astype(BF16)
    normed_one, forget_rows, items = project(
        input_all, gain_one, full_one, layout, item_count, ctx_size
    )
    normed_flat = normed_one.reshape(all_rows, model_width)
    forget_logit = forget_rows.reshape(all_rows, LANES)[:, :head_count].T
    forget_logit = forget_logit + forget_bias.astype(F32)[:, None]
    forget_logit = forget_logit.reshape(head_count, tp_size, seq_count, local_rows)
    log_forget = (ctx_valid[None] * jax.nn.log_sigmoid(forget_logit)).astype(BF16)

    cut = log_forget.astype(F32).reshape(groups, pair, tp_size, seq_count, local_rows)
    picked = jnp.stack([cut[g, :, :, s] for s, g in places])
    picked = picked.reshape(ctx_size, item_count, pair, ctx_rows).transpose(1, 0, 2, 3)
    picked = jnp.pad(picked, ((0, 0), (0, 0), (0, 8 - pair), (0, 0)))
    attended_items, qkv, full_two, grad_all, exact, lse, decay = context(
        items, picked, packed_two, grad_out, fsdp_size, head_size, 7
    )
    down_w = full_two[:, 2 * hidden : 3 * hidden]
    gate_out_w = full_two[:, 3 * hidden + inner_width :]
    gate_logit = dot(normed_flat, gate_out_w, NN)
    out_gate = jax.nn.sigmoid(gate_logit).reshape(tp_size, -1, inner_width)
    hidden_state, normed_two, attended, mixed = out_project(
        input_rows, out_gate, full_two, out_column, gain_two, attended_items, layout, 2
    )
    normed_two_all, inner_act, grad_pair = mlp(normed_two, grad_all, full_two, hidden, 3)
    normed_two_flat = normed_two_all.reshape(all_rows, model_width)
    inner_flat = inner_act.reshape(all_rows, hidden)
    grad_pair_flat = grad_pair.reshape(all_rows, 2 * hidden)
    grad_flat = grad_all.reshape(all_rows, model_width)

    gate_up_part = dot(normed_two_flat, grad_pair_flat, TN).astype(BF16)
    grad_hidden, branch, mlp_gain_part, gate_sum = mlp_back(
        grad_pair, full_two, hidden_state, grad_out, gain_two, gate_up_part, fsdp_size, ctx_size, 4
    )
    feedforward_part = dot(inner_flat, down_w, NT).astype(BF16)
    branch_all, grad_gate_logit, grads, up_sum = out_back(
        branch,
        full_two,
        out_column,
        out_gate,
        attended,
        gate_up_part,
        layout,
        item_count,
        fsdp_size,
        ctx_size,
        5,
    )
    branch_flat = branch_all.reshape(all_rows, model_width)
    logit_flat = grad_gate_logit.reshape(all_rows, inner_width)

    out_part = jnp.concatenate(
        [
            dot(grad_flat, inner_flat, TN).astype(BF16),
            dot(branch_flat, mixed.reshape(all_rows, inner_width), TN).astype(BF16),
            dot(normed_flat, logit_flat, TN).astype(BF16),
        ],
        axis=1,
    )
    grad_items, forget_items, out_sum, feedforward = context_back(
        grads,
        qkv,
        exact,
        lse,
        decay,
        out_part,
        feedforward_part.reshape(tp_size, -1, model_width),
        fsdp_size,
        head_size,
        8,
    )
    output = (valid_rows * (hidden_state + feedforward.astype(F32))).astype(BF16)
    forget_back = forget_items[:, :, :pair].astype(BF16).transpose(1, 0, 2, 3)
    forget_back = forget_back.reshape(ctx_size * item_count, pair, tp_size, local_rows)
    slots = {place(slot): slot for slot in range(used)}
    forget_back = jnp.stack(
        [
            jnp.stack([forget_back[slots[s, g]] for s in range(seq_count)], axis=2)
            for g in range(groups)
        ]
    ).reshape(head_count, tp_size, seq_count, local_rows)
    grad_forget_logit = forget_back.astype(F32) * ctx_valid[None] * jax.nn.sigmoid(-forget_logit)
    grad_forget_logit = grad_forget_logit.astype(BF16).reshape(head_count, all_rows)
    bias_part = jnp.sum(grad_forget_logit.astype(F32), axis=1)
    grad_forget_rows = jnp.pad(grad_forget_logit, ((0, LANES - head_count), (0, 0))).T
    grad_qkv = assemble(grad_items, layout, tp_size)
    grad_qkvf = jnp.concatenate([grad_qkv.reshape(all_rows, edge), grad_forget_rows], axis=1)
    bias_full = lax.dynamic_update_slice(
        jnp.zeros((1, model_width), F32), bias_part[None], (0, tp_index * head_count)
    )
    extra = jnp.concatenate(
        [jnp.zeros_like(bias_full), mlp_gain_part, bias_full, jnp.zeros((5, model_width), F32)]
    )
    input_grad, qkv_sum, vectors = last(
        grad_qkv,
        grad_gate_logit,
        grad_forget_rows.reshape(tp_size, -1, LANES),
        full_one,
        full_two,
        out_column + 1,
        input_rows,
        grad_hidden,
        gain_one,
        dot(normed_flat, grad_qkvf, TN).astype(BF16),
        extra,
        fsdp_size,
        ctx_size,
        6,
    )
    gain_one_sum, gain_two_sum, bias_sum = vectors[0], vectors[1], vectors[2]
    attn_gain_grad = lax.dynamic_slice_in_dim(gain_one_sum, shard_index * shard_rows, shard_rows, 0)
    mlp_gain_grad = lax.dynamic_slice_in_dim(gain_two_sum, shard_index * shard_rows, shard_rows, 0)
    forget_bias_grad = lax.dynamic_slice_in_dim(bias_sum, tp_index * head_count, head_count, 0)
    wide = inner_width
    return (
        by_position(output),
        by_position(input_grad),
        attn_gain_grad,
        qkv_sum[:, :wide],
        qkv_sum[:, wide : 2 * wide],
        qkv_sum[:, 2 * wide : 3 * wide],
        qkv_sum[:, 3 * wide : 3 * wide + head_count],
        forget_bias_grad,
        out_sum[:, hidden + wide :],
        out_sum[:, hidden : hidden + wide],
        mlp_gain_grad,
        gate_sum,
        up_sum,
        out_sum[:, :hidden],
    )


def solution(mesh):
    rows = P(("ctx", "tp"), "fsdp", None)
    matrix = P(("fsdp", "ctx"), "tp")
    vector = P(("fsdp", "ctx"))
    return jax.shard_map(
        per_device,
        mesh=mesh,
        in_specs=(
            rows,
            P("fsdp"),
            vector,
            matrix,
            matrix,
            matrix,
            matrix,
            P("tp"),
            matrix,
            matrix,
            vector,
            matrix,
            matrix,
            matrix,
            rows,
        ),
        out_specs=(
            rows,
            rows,
            vector,
            matrix,
            matrix,
            matrix,
            matrix,
            P("tp"),
            matrix,
            matrix,
            vector,
            matrix,
            matrix,
            matrix,
        ),
        check_vma=False,
    )
```

```python
import functools

import jax
import jax.numpy as jnp
from jax import lax
from jax.experimental import pallas as pl
from jax.experimental.pallas import tpu as pltpu
from jax.sharding import PartitionSpec as P

F32 = jnp.float32
BF16 = jnp.bfloat16
LANES = 128
MESH = pl.DeviceIdType.MESH
epsilon = 1e-06
masked_score = -1e30
NT = (((1,), (1,)), ((), ()))
NN = (((1,), (0,)), ((), ()))
TN = (((0,), (0,)), ((), ()))


def dot(left, right, dims):
    return lax.dot_general(left, right, dims, preferred_element_type=F32)


def of_head(block, head, head_size, ones_at=None):
    lane = lax.broadcasted_iota(jnp.int32, block.shape, 1)
    out = jnp.where(lane // head_size == head, block, jnp.zeros_like(block))
    if ones_at is not None:
        out = jnp.where(lane == ones_at, jnp.ones_like(block), out)
    return out


def spare_lane(head, head_size):
    return ((head + 1) % 2) * head_size


def attend_item(qkv, decay, out, exact, lse, heads, head_size):
    count, _, block, width = qkv.shape
    scale = head_size**-0.5
    row = lax.broadcasted_iota(jnp.int32, (block, block), 0)
    column = lax.broadcasted_iota(jnp.int32, (block, block), 1)
    causal = column <= row

    def query_block(i, _):
        query = qkv[i, 0]
        lanes = pl.ds(pl.multiple_of(i * block, block), block)
        result = jnp.zeros((block, width), F32)
        for head in range(heads):
            query_head = of_head(query, head, head_size)

            def step(j, carry, masked):
                top, total, acc = carry
                keys = pl.ds(pl.multiple_of(j * block, block), block)
                score = dot(query_head, qkv[j, 1], NT) * scale
                score = score - decay[head : head + 1, keys]
                if masked:
                    score = jnp.where(causal, score, masked_score)
                new_top = jnp.maximum(top, jnp.max(score, axis=1, keepdims=True))
                prob = jnp.exp(score - new_top)
                shrink = jnp.exp(top - new_top)
                total = total * shrink + jnp.sum(prob, axis=1, keepdims=True)
                acc = acc * shrink + dot(prob.astype(BF16), qkv[j, 2], NN)
                return new_top, total, acc

            carry = (
                jnp.full((block, 1), masked_score, F32),
                jnp.zeros((block, 1), F32),
                jnp.zeros((block, width), F32),
            )
            carry = lax.fori_loop(0, i, lambda j, c: step(j, c, False), carry)
            top, total, acc = step(i, carry, True)
            lane = lax.broadcasted_iota(jnp.int32, acc.shape, 1)
            result = jnp.where(lane // head_size == head, acc / total, result)
            stat = jnp.broadcast_to(top + jnp.log(total), (block, LANES)).T
            lse[head : head + 1, lanes] = stat[0:1]
        exact[i] = result
        out[i] = result.astype(BF16)
        return 0

    lax.fori_loop(0, count, query_block, 0)


def attend_item_back(qkv, grads, exact, lse, decay, dqkv, change, dq_acc, delta, heads, head_size):
    count, _, block, width = qkv.shape
    scale = head_size**-0.5
    row = lax.broadcasted_iota(jnp.int32, (block, block), 0)
    column = lax.broadcasted_iota(jnp.int32, (block, block), 1)
    causal = row <= column
    dq_acc[...] = jnp.zeros_like(dq_acc)
    change[...] = jnp.zeros_like(change)

    def prepare(i, _):
        lanes = pl.ds(pl.multiple_of(i * block, block), block)
        product = grads[i].astype(F32) * exact[i]
        lane = lax.broadcasted_iota(jnp.int32, product.shape, 1)
        for head in range(heads):
            part = jnp.where(lane // head_size == head, product, 0.0)
            part = jnp.sum(part, axis=1, keepdims=True)
            delta[head : head + 1, lanes] = jnp.broadcast_to(part, (block, LANES)).T[0:1]
        return 0

    lax.fori_loop(0, count, prepare, 0)

    def key_block(j, _):
        keys = pl.ds(pl.multiple_of(j * block, block), block)
        key = qkv[j, 1]
        value = qkv[j, 2]
        value_total = jnp.zeros((block, width), F32)
        key_total = jnp.zeros((block, width), F32)
        for head in range(heads):
            spare = spare_lane(head, head_size)
            key_ones = of_head(key, head, head_size, spare)
            fall = jnp.broadcast_to(decay[head : head + 1, keys], (LANES, block)).T[:, 0:1]

            def step(i, carry, masked):
                value_acc, key_acc = carry
                lanes = pl.ds(pl.multiple_of(i * block, block), block)
                query = qkv[i, 0]
                grad = of_head(grads[i], head, head_size)
                score = dot(key, of_head(query, head, head_size), NT) * scale
                score = score - fall - lse[head : head + 1, lanes]
                if masked:
                    score = jnp.where(causal, score, masked_score)
                prob = jnp.exp(score)
                grad_prob = dot(value, grad, NT)
                grad_score = prob * (grad_prob - delta[head : head + 1, lanes])
                grad_score = grad_score.astype(BF16)
                value_acc = value_acc + dot(prob.astype(BF16), grad, NN)
                query_ones = of_head(query, head, head_size, spare)
                key_acc = key_acc + dot(grad_score, query_ones, NN)
                dq_acc[head, i] += dot(grad_score, key_ones, TN)
                return value_acc, key_acc

            zero = jnp.zeros((block, width), F32)
            carry = step(j, (zero, zero), True)
            carry = lax.fori_loop(j + 1, count, lambda i, c: step(i, c, False), carry)
            value_acc, key_acc = carry
            value_total = value_total + value_acc
            lane = lax.broadcasted_iota(jnp.int32, key_acc.shape, 1)
            key_total = jnp.where(lane // head_size == head, key_acc, key_total)
            change[head : head + 1, keys] -= key_acc.T[spare : spare + 1]
        dqkv[j, 1] = (key_total * scale).astype(BF16)
        dqkv[j, 2] = value_total.astype(BF16)
        return 0

    lax.fori_loop(0, count, key_block, 0)

    def finish(i, _):
        lanes = pl.ds(pl.multiple_of(i * block, block), block)
        total = jnp.zeros((block, width), F32)
        for head in range(heads):
            spare = spare_lane(head, head_size)
            part = dq_acc[head, i]
            lane = lax.broadcasted_iota(jnp.int32, part.shape, 1)
            total = jnp.where(lane // head_size == head, part, total)
            change[head : head + 1, lanes] += part.T[spare : spare + 1]
        dqkv[i, 0] = (total * scale).astype(BF16)
        return 0

    lax.fori_loop(0, count, finish, 0)


def triangle(upward):
    row = lax.broadcasted_iota(jnp.int32, (LANES, LANES), 0)
    column = lax.broadcasted_iota(jnp.int32, (LANES, LANES), 1)
    keep = (row <= column) if upward else (row >= column)
    return jnp.where(keep, 1.0, 0.0).astype(BF16)


def exact_product(values, matrix):
    high = values.astype(BF16)
    rest = values - high.astype(F32)
    middle = rest.astype(BF16)
    low = (rest - middle.astype(F32)).astype(BF16)
    return dot(high, matrix, NN) + dot(middle, matrix, NN) + dot(low, matrix, NN)


def ctx_sending(source, target, send_sem, recv_sem, peer):
    return pltpu.make_async_remote_copy(
        src_ref=source,
        dst_ref=target,
        send_sem=send_sem,
        recv_sem=recv_sem,
        device_id={"ctx": peer},
        device_id_type=MESH,
    )


def ctx_greet(size):
    me = lax.axis_index("ctx")
    barrier = pltpu.get_barrier_semaphore()
    for step in range(1, size):
        peer = lax.rem(me + step, size)
        pl.semaphore_signal(barrier, inc=1, device_id={"ctx": peer}, device_id_type=MESH)
    pl.semaphore_wait(barrier, size - 1)
    return me


class Exchange:
    def __init__(self, me, size, source, target, sems):
        self.me, self.size, self.source, self.target = me, size, source, target
        self.send_sem, self.recv_sem, self.own_sem = sems

    def own(self, item):
        return pltpu.make_async_copy(
            self.source.at[item, self.me], self.target.at[item, self.me], self.own_sem.at[item]
        )

    def copy(self, item, step):
        peer = lax.rem(self.me + step, self.size)
        return ctx_sending(
            self.source.at[item, peer],
            self.target.at[item, self.me],
            self.send_sem.at[item, step],
            self.recv_sem.at[item, step],
            peer,
        )

    def start(self, item):
        self.own(item).start()
        for step in range(1, self.size):
            self.copy(item, step).start()

    def arrive(self, item):
        self.own(item).wait()
        for step in range(1, self.size):
            self.copy(item, step).wait_recv()

    def drain(self, item):
        for step in range(1, self.size):
            self.copy(item, step).wait_send()


def exchange_sems(items, size):
    return [
        pltpu.SemaphoreType.DMA((items, size)),
        pltpu.SemaphoreType.DMA((items, size)),
        pltpu.SemaphoreType.DMA((items,)),
    ]


def context_kernel(
    heads,
    head_size,
    items_ref,
    forget_ref,
    shard_ref,
    out_shard_ref,
    rows_ref,
    back_ref,
    qkv_ref,
    full_ref,
    full_out_ref,
    table_ref,
    exact_ref,
    lse_ref,
    decay_ref,
    *refs,
):
    qkv, forget, out, save_sem = refs[:4]
    sems = refs[4:]
    count, size, _, block, width = items_ref.shape
    tp, sibling, across, diagonal = tp_places()
    greet_all([{"tp": sibling}, {"tp": across}] + group_peers())
    me = lax.axis_index("ctx")
    gathers = (
        WeightGather(out_shard_ref, full_out_ref, sems[9:14]),
        WeightGather(shard_ref, full_ref, sems[14:19]),
    )
    rows = RowGather(rows_ref, table_ref, sems[19:])
    forgets = Exchange(me, size, forget_ref, forget, sems[0:3])
    inputs = Exchange(me, size, items_ref, qkv, sems[3:6])
    results = Exchange(me, size, out, back_ref, sems[6:9])

    @pl.loop(0, count)
    def _(item):
        forgets.start(item)

    for gather in gathers:
        gather.begin()
    inputs.start(0)
    rows.begin()

    @pl.loop(0, count)
    def _(item):
        forgets.arrive(item)

    @pl.loop(0, count)
    def _(item):
        upper = triangle(True)
        before = jnp.zeros((8, 1), F32)
        for start in range(0, size * block, LANES):
            part = forget[item, start // block, :, pl.ds(start % block, LANES)]
            total = before + dot(part.astype(BF16), upper, NN)
            decay_ref[item, :, pl.ds(start, LANES)] = total
            before = total[:, LANES - 1 :]

    lse_ref[...] = jnp.zeros_like(lse_ref)

    @pl.loop(0, count)
    def _(item):
        inputs.arrive(item)

        @pl.when(item + 1 < count)
        def _():
            inputs.start(item + 1)

        for hop in range(1, min(size, count + 1)):

            @pl.when(item == hop - 1)
            def _(hop=hop):
                for gather in gathers:
                    gather.advance(hop)

        saving = pltpu.make_async_copy(qkv.at[item], qkv_ref.at[item], save_sem)
        saving.start()
        attend_item(
            qkv.at[item], decay_ref.at[item], out.at[item], exact_ref.at[item], lse_ref.at[item], heads, head_size
        )
        results.start(item)
        saving.wait()

    rows.advance()
    for hop in range(count + 1, size):
        for gather in gathers:
            gather.advance(hop)

    @pl.loop(0, count)
    def _(item):
        forgets.drain(item)
        inputs.drain(item)
        results.arrive(item)
        results.drain(item)

    for gather in gathers:
        gather.end()
    rows.end()


def full_block(shape):
    return pl.BlockSpec(shape, lambda i: (0,) * len(shape), pipeline_mode=pl.Buffered(1))


def attend_cost(items, heads, products):
    count, size, _, block, width = items.shape
    pairs = count * heads * (size * block) ** 2 // 2
    return pl.CostEstimate(
        flops=2 * products * pairs * 256, bytes_accessed=100 << 20, transcendentals=pairs
    )


def context(items, forget, shard, out_shard, rows, f_size, head_size, ident):
    count, size, _, block, width = items.shape
    heads = width // head_size
    place = pl.BlockSpec(memory_space=pl.ANY)
    exact, stat = (count, size, block, width), (count, 8, size * block)
    return pl.pallas_call(
        functools.partial(context_kernel, heads, head_size),
        grid=(1,),
        out_shape=[
            jax.ShapeDtypeStruct(exact, BF16),
            jax.ShapeDtypeStruct(items.shape, BF16),
            jax.ShapeDtypeStruct((shard.shape[0] * f_size * size, shard.shape[1]), BF16),
            jax.ShapeDtypeStruct((shard.shape[0] * f_size * size, out_shard.shape[1]), BF16),
            jax.ShapeDtypeStruct((4,) + rows.shape, BF16),
            jax.ShapeDtypeStruct(exact, F32),
            jax.ShapeDtypeStruct(stat, F32),
            jax.ShapeDtypeStruct(stat, F32),
        ],
        in_specs=[place] * 5,
        out_specs=[place, place, place, place, place, full_block(exact), full_block(stat), full_block(stat)],
        scratch_shapes=[
            pltpu.VMEM(items.shape, BF16),
            pltpu.VMEM(forget.shape, F32),
            pltpu.VMEM(exact, BF16),
            pltpu.SemaphoreType.DMA,
        ]
        + exchange_sems(count, size) * 3
        + weight_sems(f_size, size) * 2
        + [pltpu.SemaphoreType.DMA((3,))] * 2
        + [pltpu.SemaphoreType.DMA],
        compiler_params=remote_params(ident, 48),
        cost_estimate=attend_cost(items, heads, 2),
        name="context",
    )(items, forget, shard, out_shard, rows)


def context_back_kernel(
    heads,
    head_size,
    items_ref,
    qkv_ref,
    exact_ref,
    lse_ref,
    decay_ref,
    part_ref,
    table_ref,
    back_ref,
    forget_ref,
    sum_ref,
    rows_ref,
    *refs,
):
    grads, dqkv, change, slope, dq_acc, delta = refs[:6]
    sems = refs[6:15]
    count, size, block, width = items_ref.shape
    tp, sibling, across, diagonal = tp_places()
    greet_all([{"tp": sibling}, {"tp": across}] + group_peers())
    me = lax.axis_index("ctx")
    weights = WeightSum(part_ref, 0, sum_ref, refs[15:23])
    rows = RowSum(table_ref, rows_ref, refs[23:])
    inputs = Exchange(me, size, items_ref, grads, sems[0:3])
    results = Exchange(me, size, dqkv, back_ref, sems[3:6])
    forgets = Exchange(me, size, slope, forget_ref, sems[6:9])

    inputs.start(0)
    weights.begin()
    rows.begin()

    @pl.loop(0, count)
    def _(item):
        inputs.arrive(item)

        @pl.when(item + 1 < count)
        def _():
            inputs.start(item + 1)

        attend_item_back(
            qkv_ref.at[item],
            grads.at[item],
            exact_ref.at[item],
            lse_ref.at[item],
            decay_ref.at[item],
            dqkv.at[item],
            change,
            dq_acc,
            delta,
            heads,
            head_size,
        )
        results.start(item)
        lower = triangle(False)
        after = jnp.zeros((8, 1), F32)
        for start in reversed(range(0, size * block, LANES)):
            total = after + exact_product(change[:, pl.ds(start, LANES)], lower)
            slope[item, start // block, :, pl.ds(start % block, LANES)] = total
            after = total[:, 0:1]
        forgets.start(item)

        for turn in range(count):

            @pl.when(item == turn)
            def _(turn=turn):
                weights.run_share(turn, count + 1)
                if turn == 0:
                    rows.advance()

    weights.run_share(count, count + 1)

    @pl.loop(0, count)
    def _(item):
        inputs.drain(item)
        results.arrive(item)
        results.drain(item)
        forgets.arrive(item)
        forgets.drain(item)

    weights.end()
    rows.end()


def context_back(grads, qkv, exact, lse, decay, part, table, f_size, head_size, ident):
    count, size, _, block, width = qkv.shape
    heads = width // head_size
    place = pl.BlockSpec(memory_space=pl.ANY)
    forget = (count, size, 8, block)
    total = (part.shape[0] // (f_size * size), part.shape[1])
    return pl.pallas_call(
        functools.partial(context_back_kernel, heads, head_size),
        grid=(1,),
        out_shape=[
            jax.ShapeDtypeStruct(qkv.shape, BF16),
            jax.ShapeDtypeStruct(forget, F32),
            jax.ShapeDtypeStruct(total, F32),
            jax.ShapeDtypeStruct(table.shape[1:], BF16),
        ],
        in_specs=[
            place,
            full_block(qkv.shape),
            full_block(exact.shape),
            full_block(lse.shape),
            full_block(decay.shape),
            place,
            place,
        ],
        out_specs=[place, place, full_block(total), full_block(table.shape[1:])],
        scratch_shapes=[
            pltpu.VMEM(grads.shape, BF16),
            pltpu.VMEM(qkv.shape, BF16),
            pltpu.VMEM((8, size * block), F32),
            pltpu.VMEM(forget, F32),
            pltpu.VMEM((heads, size, block, width), F32),
            pltpu.VMEM((8, size * block), F32),
        ]
        + exchange_sems(count, size) * 3
        + sum_scratch(f_size, size, *total)
        + row_sum_scratch(*table.shape[1:]),
        compiler_params=remote_params(ident, 60),
        cost_estimate=attend_cost(qkv, heads, 5),
        name="context_back",
    )(grads, qkv, exact, lse, decay, part, table)


CHUNKS = 4
HALVES = 2


def tp_places():
    me = lax.axis_index("tp")
    sibling = me + 1 - 2 * lax.rem(me, 2)
    across = lax.rem(me + 2, 4)
    diagonal = lax.rem(sibling + 2, 4)
    return me, sibling, across, diagonal


def greet(peers):
    barrier = pltpu.get_barrier_semaphore()
    for peer in peers:
        pl.semaphore_signal(barrier, inc=1, device_id={"tp": peer}, device_id_type=MESH)
    pl.semaphore_wait(barrier, len(peers))


def sending(source, target, send_sem, recv_sem, peer):
    return pltpu.make_async_remote_copy(
        src_ref=source,
        dst_ref=target,
        send_sem=send_sem,
        recv_sem=recv_sem,
        device_id={"tp": peer},
        device_id_type=MESH,
    )


def pick(step, chunks, places):
    me, sibling, across, diagonal = places
    late = step - 2 * chunks
    far = jnp.where(lax.rem(late, 2) == 0, across, diagonal)
    slot = jnp.where(step < chunks, me, jnp.where(step < 2 * chunks, sibling, far))
    chunk = jnp.where(step < 2 * chunks, lax.rem(step, chunks), late // 2)
    return slot, chunk


def gather_loop(table, sems, compute, own=None, relative=False, between=None):
    near_send, near_recv, far_send, far_recv, pass_send, pass_recv = sems
    me, sibling, across, diagonal = tp_places()
    places = (0, 1, 2, 3) if relative else (me, sibling, across, diagonal)
    mine, near_by, far_off, corner = places
    near_spot, far_spot, pass_spot = (1, 2, 3) if relative else (me, me, across)
    rows = table.shape[1] // CHUNKS

    def part(slot, chunk):
        return table.at[slot, pl.ds(pl.multiple_of(chunk * rows, rows), rows)]

    def far(chunk):
        source = part(mine, chunk)
        if own is not None:
            source = own.at[pl.ds(pl.multiple_of(chunk * rows, rows), rows)]
        return sending(source, part(far_spot, chunk), far_send.at[chunk], far_recv.at[chunk], across)

    def far_arrival(chunk):
        spot = part(far_off, chunk)
        return sending(spot, spot, far_send.at[chunk], far_recv.at[chunk], across)

    def passing(chunk):
        return sending(
            part(far_off, chunk), part(pass_spot, chunk), pass_send.at[chunk], pass_recv.at[chunk], sibling
        )

    def pass_arrival(chunk):
        spot = part(corner, chunk)
        return sending(spot, spot, pass_send.at[chunk], pass_recv.at[chunk], sibling)

    for chunk in range(CHUNKS):
        far(chunk).start()
    own = table.at[mine] if own is None else own
    near = sending(own, table.at[near_spot], near_send, near_recv, sibling)
    near.start()

    def body(step, _):
        slot, chunk = pick(step, CHUNKS, places)
        late = step - 2 * CHUNKS

        @pl.when(step == CHUNKS)
        def _():
            spot = table.at[near_by]
            sending(spot, spot, near_send, near_recv, sibling).wait_recv()

        @pl.when((late >= 0) & (lax.rem(late, 2) == 0))
        def _():
            far_arrival(chunk).wait_recv()
            passing(chunk).start()

        @pl.when((late >= 0) & (lax.rem(late, 2) == 1))
        def _():
            pass_arrival(chunk).wait_recv()

        compute(slot, chunk)
        return 0

    if between is None:
        lax.fori_loop(0, 4 * CHUNKS, body, 0)
    else:
        lax.fori_loop(0, 2 * CHUNKS, body, 0)
        between()
        lax.fori_loop(2 * CHUNKS, 4 * CHUNKS, body, 0)
    near.wait_send()
    for chunk in range(CHUNKS):
        far(chunk).wait_send()
        passing(chunk).wait_send()


GATHER_SEMS = [pltpu.SemaphoreType.DMA] * 2 + [pltpu.SemaphoreType.DMA((CHUNKS,))] * 4


def scatter_loop(buffers, sems, partial, finish, relative=False, between=None):
    near_out, near_in, far_out, far_in = buffers
    near_send, near_recv, far_send, far_recv = sems
    me, sibling, across, diagonal = tp_places()
    mine, near_by, far_off, corner = (0, 1, 2, 3) if relative else (me, sibling, across, diagonal)
    rows = far_out.shape[0] // CHUNKS

    def span(chunk):
        return pl.ds(pl.multiple_of(chunk * rows, rows), rows)

    def near(half, chunk):
        return sending(
            near_out.at[half, span(chunk)],
            near_in.at[half, span(chunk)],
            near_send.at[half, chunk],
            near_recv.at[half, chunk],
            sibling,
        )

    def far(chunk):
        return sending(
            far_out.at[span(chunk)],
            far_in.at[span(chunk)],
            far_send.at[chunk],
            far_recv.at[chunk],
            across,
        )

    def body(step, _):
        phase, chunk = step // CHUNKS, lax.rem(step, CHUNKS)
        slot = jnp.where(
            phase == 0, corner, jnp.where(phase == 1, far_off, jnp.where(phase == 2, near_by, mine))
        )
        value = partial(slot, chunk)
        spot = span(chunk)

        @pl.when(lax.rem(phase, 2) == 0)
        def _():
            half = phase // 2
            near_out[half, spot] = value.astype(BF16)
            near(half, chunk).start()

        @pl.when(phase == 1)
        def _():
            near(0, chunk).wait_recv()
            far_out[spot] = (value + near_in[0, spot].astype(F32)).astype(BF16)
            far(chunk).start()

        @pl.when(phase == 3)
        def _():
            near(1, chunk).wait_recv()

            far(chunk).wait_recv()
            finish(chunk, value + near_in[1, spot].astype(F32) + far_in[spot].astype(F32))

        return 0

    if between is None:
        lax.fori_loop(0, 4 * CHUNKS, body, 0)
    else:
        lax.fori_loop(0, 2 * CHUNKS, body, 0)
        for phase in (2, 3):
            between(phase)
            lax.fori_loop(phase * CHUNKS, (phase + 1) * CHUNKS, body, 0)
    for chunk in range(CHUNKS):
        near(0, chunk).wait_send()
        near(1, chunk).wait_send()
        far(chunk).wait_send()


SCATTER_SEMS = [pltpu.SemaphoreType.DMA((2, CHUNKS))] * 2 + [pltpu.SemaphoreType.DMA((CHUNKS,))] * 2


def scatter_buffers(rows, width):
    return [
        pltpu.VMEM((2, rows, width), BF16),
        pltpu.VMEM((2, rows, width), BF16),
        pltpu.VMEM((rows, width), BF16),
        pltpu.VMEM((rows, width), BF16),
    ]


def group_peers():
    f_size, c_size = lax.axis_size("fsdp"), lax.axis_size("ctx")
    f, c = lax.axis_index("fsdp"), lax.axis_index("ctx")
    return [
        {"fsdp": lax.rem(f + i, f_size), "ctx": lax.rem(c + j, c_size)}
        for i in range(f_size)
        for j in range(c_size)
        if i or j
    ]


def greet_all(peers):
    barrier = pltpu.get_barrier_semaphore()
    for peer in peers:
        pl.semaphore_signal(barrier, inc=1, device_id=peer, device_id_type=MESH)
    pl.semaphore_wait(barrier, len(peers))


def moving(source, target, send_sem, recv_sem, peer):
    return pltpu.make_async_remote_copy(
        src_ref=source,
        dst_ref=target,
        send_sem=send_sem,
        recv_sem=recv_sem,
        device_id=peer,
        device_id_type=MESH,
    )


class WeightGather:
    def __init__(self, shard, full, sems):
        self.shard, self.full = shard, full
        self.f_size, self.c_size = lax.axis_size("fsdp"), lax.axis_size("ctx")
        self.f, self.c = lax.axis_index("fsdp"), lax.axis_index("ctx")
        self.sems = sems

    def half(self, h):
        wide = self.shard.shape[1] // HALVES
        return pl.ds(h * wide, wide)

    def spot(self, c, h, f=None):
        rows = self.shard.shape[0]
        block = (self.f if f is None else f) * self.c_size + c
        return self.full.at[pl.ds(pl.multiple_of(block * rows, rows), rows), self.half(h)]

    def own(self):
        rows = self.shard.shape[0]
        block = self.f * self.c_size + self.c
        target = self.full.at[pl.ds(pl.multiple_of(block * rows, rows), rows)]
        return pltpu.make_async_copy(self.shard, target, self.sems[4])

    def along(self, c, h, hop, side, first=False):
        source = self.shard.at[:, self.half(h)] if first else self.spot(c, h)
        peer = {"ctx": self.c + (1 if side else -1)}
        send, recv = self.sems[0].at[side, hop, h], self.sems[1].at[side, hop, h]
        return moving(source, self.spot(c, h), send, recv, peer)

    def over(self, c, h, step, first=False):
        source = self.shard.at[:, self.half(h)] if first else self.spot(c, h)
        peer = {"fsdp": lax.rem(self.f + step, self.f_size)}
        send, recv = self.sems[2].at[step, c, h], self.sems[3].at[step, c, h]
        return moving(source, self.spot(c, h), send, recv, peer)

    def over_arrival(self, c, h, step):
        spot = self.spot(c, h, lax.rem(self.f + self.f_size - step, self.f_size))
        peer = {"fsdp": lax.rem(self.f + step, self.f_size)}
        return moving(spot, spot, self.sems[2].at[step, c, h], self.sems[3].at[step, c, h], peer)

    def can(self, side):
        return self.c + 1 < self.c_size if side else self.c > 0

    def holds(self, hop, side):
        return self.c - hop >= 0 if side else self.c + hop < self.c_size

    def begin(self):
        self.own().start()
        for h in range(HALVES):
            for side in (1, 0):

                @pl.when(self.can(side))
                def _(side=side):
                    self.along(self.c, h, 1, side, True).start()

            for step in range(1, self.f_size):
                self.over(self.c, h, step, True).start()

    def advance(self, hop):
        for h in range(HALVES):
            for side in (1, 0):

                @pl.when(self.holds(hop, side))
                def _(side=side):
                    c = self.c - hop if side else self.c + hop
                    self.along(c, h, hop, side).wait_recv()

                    @pl.when(self.can(side))
                    def _():
                        self.along(c, h, hop + 1, side).start()

                    for step in range(1, self.f_size):
                        self.over(c, h, step).start()

    def end(self):
        self.own().wait()
        for h in range(HALVES):
            for step in range(1, self.f_size):
                for c in range(self.c_size):
                    self.over_arrival(c, h, step).wait_recv()
                    self.over(c, h, step).wait_send()
            for side in (1, 0):

                @pl.when(self.can(side))
                def _(side=side):
                    self.along(self.c, h, 1, side, True).wait_send()

                for hop in range(1, self.c_size):

                    @pl.when(self.holds(hop, side) & self.can(side))
                    def _(side=side, hop=hop):
                        c = self.c - hop if side else self.c + hop
                        self.along(c, h, hop + 1, side).wait_send()


def weight_sems(f_size, c_size):
    dma = pltpu.SemaphoreType.DMA
    return [dma((2, c_size + 1, HALVES))] * 2 + [dma((f_size, c_size, HALVES))] * 2 + [dma]


class WeightSum:
    def __init__(self, part, first_column, out, refs):
        self.part, self.out, self.first = part, out, first_column
        self.stage, self.total, self.along_in = refs[:3]
        self.own_sem, self.over_send, self.over_recv, self.along_send, self.along_recv = refs[3:]
        self.f_size, self.c_size = lax.axis_size("fsdp"), lax.axis_size("ctx")
        self.f, self.c = lax.axis_index("fsdp"), lax.axis_index("ctx")
        self.rows, self.wide = out.shape[0], out.shape[1] // HALVES
        ends = [(self.c_size - 1 - i // 2) if i % 2 == 0 else i // 2 for i in range(self.c_size)]
        self.order = [(c, h) for c in ends for h in range(HALVES)]
        self.stages = len(self.order) + self.c_size - 1

    def piece(self, f, c, h):
        row = (f * self.c_size + c) * self.rows
        columns = pl.ds(self.first + h * self.wide, self.wide)
        return self.part.at[pl.ds(pl.multiple_of(row, self.rows), self.rows), columns]

    def own(self, c, h):
        n = c * HALVES + h
        return pltpu.make_async_copy(self.piece(self.f, c, h), self.stage.at[n], self.own_sem.at[n])

    def over(self, c, h, step):
        f, n = lax.rem(self.f + step, self.f_size), c * HALVES + h
        return moving(
            self.piece(f, c, h),
            self.total.at[step - 1, n],
            self.over_send.at[step - 1, n],
            self.over_recv.at[step - 1, n],
            {"fsdp": f},
        )

    def along(self, c, h, side, source=None):
        peer, n = {"ctx": self.c + (1 if side else -1)}, c * HALVES + h
        target = self.along_in.at[side, n]
        return moving(
            target if source is None else source,
            target,
            self.along_send.at[side, n],
            self.along_recv.at[side, n],
            peer,
        )

    def launch(self, i):
        if i < len(self.order):
            for step in range(1, self.f_size):
                self.over(*self.order[i], step).start()

    def begin(self):
        for c, h in self.order:
            self.own(c, h).start()
        self.launch(0)
        self.launch(1)

    def receive(self, i):
        c, h = self.order[i]
        n = c * HALVES + h
        self.own(c, h).wait()
        value = self.stage[n].astype(F32)
        for step in range(1, self.f_size):
            self.over(c, h, step).wait_recv()
        self.launch(i + 2)
        for step in range(1, self.f_size):
            value = value + self.total[step - 1, n].astype(F32)
        self.total[0, n] = value.astype(BF16)
        for side, end in ((1, 0), (0, self.c_size - 1)):
            if c != end:

                @pl.when(self.c == end)
                def _(side=side):
                    self.along(c, h, side, self.total.at[0, n]).start()

    def hop(self, c, h, side, device):
        n = c * HALVES + h

        @pl.when(self.c == device)
        def _():
            self.along(c, h, side).wait_recv()
            value = self.total[0, n].astype(F32) + self.along_in[side, n].astype(F32)
            if device == c:
                self.total[0, n] = value.astype(BF16)
            else:
                self.along_in[side, n] = value.astype(BF16)
                self.along(c, h, side).start()

    def run(self, n):
        if n < len(self.order):
            self.receive(n)
        for i, (c, h) in enumerate(self.order):
            if 1 <= n - i <= c:
                self.hop(c, h, 1, n - i)
            if 1 <= n - i <= self.c_size - 1 - c:
                self.hop(c, h, 0, self.c_size - 1 - (n - i))

    def run_to(self, first, last):
        for n in range(min(first, self.stages), min(last, self.stages)):
            self.run(n)

    def run_share(self, turn, turns):
        share = -(-self.stages // turns)
        self.run_to(turn * share, (turn + 1) * share)

    def end(self):
        for c in range(self.c_size):

            @pl.when(self.c == c)
            def _(c=c):
                for h in range(HALVES):
                    columns = pl.ds(h * self.wide, self.wide)
                    self.out[:, columns] = self.total[0, c * HALVES + h].astype(F32)

        for c, h in self.order:
            for step in range(1, self.f_size):
                self.over(c, h, step).wait_send()
            for side in (1, 0):

                @pl.when(self.c < c if side else self.c > c)
                def _(side=side):
                    self.along(c, h, side).wait_send()


def sum_scratch(f_size, c_size, rows, columns):
    dma, count, wide = pltpu.SemaphoreType.DMA, c_size * HALVES, columns // HALVES
    return (
        [
            pltpu.VMEM((count, rows, wide), BF16),
            pltpu.VMEM((f_size - 1, count, rows, wide), BF16),
            pltpu.VMEM((2, count, rows, wide), BF16),
        ]
        + [dma((count,))]
        + [dma((f_size - 1, count))] * 2
        + [dma((2, count))] * 2
    )


class Fetch:
    def __init__(self, pairs, sem):
        self.copies = [
            pltpu.make_async_copy(source, target, sem.at[n]) for n, (source, target) in enumerate(pairs)
        ]
        for copy in self.copies:
            copy.start()

    def wait(self):
        for copy in self.copies:
            copy.wait()


class RowGather:
    def __init__(self, rows, table, sems):
        self.rows, self.table, self.sems = rows, table, sems
        _, self.sibling, self.across, _ = tp_places()

    def own(self):
        return pltpu.make_async_copy(self.rows, self.table.at[0], self.sems[2])

    def copy(self, n):
        source = self.table.at[2] if n == 2 else self.rows
        peer = {"tp": self.across if n == 1 else self.sibling}
        return moving(source, self.table.at[n + 1], self.sems[0].at[n], self.sems[1].at[n], peer)

    def begin(self):
        self.own().start()
        self.copy(0).start()
        self.copy(1).start()

    def advance(self):
        self.copy(1).wait_recv()
        self.copy(2).start()

    def end(self):
        self.own().wait()
        self.copy(0).wait()
        self.copy(1).wait_send()
        self.copy(2).wait()


class RowSum:
    def __init__(self, table, out, refs):
        self.table, self.out = table, out
        self.mine, self.near, self.far_out, self.far_in, self.send, self.recv, self.own_sem = refs
        _, self.sibling, self.across, _ = tp_places()

    def own(self, n):
        return pltpu.make_async_copy(self.table.at[0 if n else 2], self.mine.at[n], self.own_sem.at[n])

    def copy(self, n):
        if n == 2:
            source, target, peer = self.far_out, self.far_in, self.across
        else:
            source, target, peer = self.table.at[1 if n else 3], self.near.at[n], self.sibling
        return moving(source, target, self.send.at[n], self.recv.at[n], {"tp": peer})

    def begin(self):
        for n in range(2):
            self.own(n).start()
            self.copy(n).start()

    def advance(self):
        self.own(0).wait()
        self.copy(0).wait_recv()
        self.far_out[...] = (self.mine[0].astype(F32) + self.near[0].astype(F32)).astype(BF16)
        self.copy(2).start()

    def end(self):
        self.own(1).wait()
        self.copy(1).wait_recv()
        self.copy(2).wait_recv()
        total = self.mine[1].astype(F32) + self.near[1].astype(F32)
        self.out[...] = (total + self.far_in[...].astype(F32)).astype(BF16)
        for n in range(3):
            self.copy(n).wait_send()


def row_sum_scratch(rows, width):
    dma, pair, one = pltpu.SemaphoreType.DMA, (2, rows, width), (rows, width)
    return [pltpu.VMEM(pair, BF16)] * 2 + [pltpu.VMEM(one, BF16)] * 2 + [dma((3,))] * 2 + [dma((2,))]


def startup_kernel(rows_ref, shard_ref, gain_ref, all_ref, full_ref, gains_ref, own_sem, *sems):
    me, sibling, across, diagonal = tp_places()
    others = group_peers()
    greet_all([{"tp": sibling}, {"tp": across}] + others)
    near_send, near_recv, far_send, far_recv, pass_send, pass_recv = sems[:6]
    gather = WeightGather(shard_ref, full_ref, sems[6:11])
    gain_send, gain_recv, gain_own = sems[11:]
    spot = gains_ref.at[gather.f * gather.c_size + gather.c]
    gain_copies = [
        moving(gain_ref, spot, gain_send.at[n], gain_recv.at[n], peer) for n, peer in enumerate(others)
    ]
    for copy in gain_copies:
        copy.start()
    own_gain = pltpu.make_async_copy(gain_ref, spot, gain_own)
    own_gain.start()
    size = rows_ref.shape[0] // CHUNKS
    own = pltpu.make_async_copy(rows_ref, all_ref.at[me], own_sem)
    own.start()

    def span(chunk):
        return pl.ds(chunk * size, size)

    def far(chunk):
        return sending(
            rows_ref.at[span(chunk)],
            all_ref.at[me, span(chunk)],
            far_send.at[chunk],
            far_recv.at[chunk],
            across,
        )

    def passing(chunk):
        spot = all_ref.at[across, span(chunk)]
        return sending(spot, spot, pass_send.at[chunk], pass_recv.at[chunk], sibling)

    gather.begin()
    far(0).start()
    near = sending(rows_ref, all_ref.at[me], near_send, near_recv, sibling)
    near.start()
    for turn in range(max(CHUNKS, gather.c_size - 1)):
        if turn < CHUNKS:
            far(turn).wait_recv()
            if turn + 1 < CHUNKS:
                far(turn + 1).start()
            passing(turn).start()
        if turn + 1 < gather.c_size:
            gather.advance(turn + 1)
    near.wait()
    for chunk in range(CHUNKS):
        far(chunk).wait_send()
        passing(chunk).wait()
    own.wait()
    gather.end()
    for copy in gain_copies:
        copy.wait()
    own_gain.wait()


def startup(rows, shard, gains, f_size, c_size, ident):
    place = pl.BlockSpec(memory_space=pl.ANY)
    full = (shard.shape[0] * f_size * c_size, shard.shape[1])
    return pl.pallas_call(
        startup_kernel,
        out_shape=[
            jax.ShapeDtypeStruct((4,) + rows.shape, BF16),
            jax.ShapeDtypeStruct(full, BF16),
            jax.ShapeDtypeStruct((f_size * c_size,) + gains.shape, F32),
        ],
        in_specs=[place] * 3,
        out_specs=[place] * 3,
        scratch_shapes=[pltpu.SemaphoreType.DMA]
        + GATHER_SEMS
        + weight_sems(f_size, c_size)
        + [pltpu.SemaphoreType.DMA((f_size * c_size - 1,))] * 2
        + [pltpu.SemaphoreType.DMA],
        compiler_params=pltpu.CompilerParams(collective_id=ident, has_side_effects=True),
        name="startup",
    )(rows, shard, gains)


def whole(shape, column=None):
    zeros = (0,) * (len(shape) - 1)
    return pl.BlockSpec(shape, lambda i: zeros + (column or 0,), pipeline_mode=pl.Buffered(1))


def remote_params(ident, megabytes):
    return pltpu.CompilerParams(
        collective_id=ident, has_side_effects=True, vmem_limit_bytes=megabytes << 20, dimension_semantics=("arbitrary",)
    )


def project_kernel(layout, x_ref, gain_ref, w_ref, normed_ref, forget_ref, items_ref):
    seq_count, groups, width, places = layout
    x = x_ref[0].astype(F32)
    normed = (x * lax.rsqrt(jnp.mean(x * x, axis=1, keepdims=True) + epsilon) * gain_ref[...]).astype(BF16)
    normed_ref[0] = normed
    inner = groups * width
    rows = x.shape[0] // seq_count
    count = items_ref.shape[0]
    for kind in range(3):
        value = dot(normed, w_ref[:, kind * inner : (kind + 1) * inner], NN).astype(BF16)
        for slot, (s, g) in enumerate(places):
            piece = value[s * rows : (s + 1) * rows, g * width : (g + 1) * width]
            items_ref[slot % count, slot // count, kind] = piece
    forget_ref[0] = dot(normed, w_ref[:, 3 * inner :], NN)


def project(x_all, gain, full_one, layout, item_count, ctx_size):
    seq_count, groups, width, places = layout
    tp_size, rows, model_width = x_all.shape
    local = rows // seq_count
    item = jax.ShapeDtypeStruct((item_count, ctx_size, 3, tp_size * local, width), BF16)
    columns = full_one.shape[1]
    block = pl.BlockSpec((1, rows, model_width), lambda t: (t, 0, 0))
    return pl.pallas_call(
        functools.partial(project_kernel, layout),
        grid=(tp_size,),
        out_shape=[
            jax.ShapeDtypeStruct(x_all.shape, BF16),
            jax.ShapeDtypeStruct((tp_size, rows, LANES), F32),
            item,
        ],
        in_specs=[
            block,
            pl.BlockSpec((1, model_width), lambda t: (0, 0)),
            pl.BlockSpec((model_width, columns), lambda t: (0, 0), pipeline_mode=pl.Buffered(1)),
        ],
        out_specs=[
            block,
            pl.BlockSpec((1, rows, LANES), lambda t: (t, 0, 0)),
            pl.BlockSpec((item_count, ctx_size, 3, local, width), lambda t: (0, 0, 0, t, 0)),
        ],
        compiler_params=pltpu.CompilerParams(vmem_limit_bytes=48 << 20, dimension_semantics=("arbitrary",)),
        cost_estimate=pl.CostEstimate(
            flops=2 * x_all.size * columns, bytes_accessed=4 * x_all.size, transcendentals=0
        ),
        name="project",
    )(x_all, gain, full_one)


def out_kernel(layout, x_ref, gate_ref, w_ref, gain_ref, items, shard_ref, *refs):
    seq_count, groups, width, places = layout
    hidden_ref, normed_ref, attended_ref, mixed_ref, full_ref = refs[:5]
    buffers, sems = refs[5:9], refs[9:13]
    count = items.shape[0]
    me, sibling, across, diagonal = tp_places()
    greet_all([{"tp": sibling}, {"tp": across}] + group_peers())
    gather = WeightGather(shard_ref, full_ref, refs[13:])
    gather.begin()
    tp_size, rows, _ = gate_ref.shape
    local = rows // seq_count

    def mix(t, _):
        here = pl.ds(pl.multiple_of(t * local, local), local)
        for slot, (s, g) in enumerate(places[: seq_count * groups]):
            there = (t, pl.ds(s * local, local), pl.ds(g * width, width))
            value = items[slot % count, slot // count, here]
            attended_ref[there] = value
            mixed_ref[there] = (value.astype(F32) * gate_ref[there]).astype(BF16)
        return 0

    lax.fori_loop(0, tp_size, mix, 0)
    size = rows // CHUNKS

    def span(chunk):
        return pl.ds(pl.multiple_of(chunk * size, size), size)

    def partial(slot, chunk):
        return dot(mixed_ref[slot, span(chunk)], w_ref[...], NT)

    def finish(chunk, total):
        hidden = x_ref[span(chunk)].astype(F32) + total
        hidden_ref[span(chunk)] = hidden
        inverse = lax.rsqrt(jnp.mean(hidden * hidden, axis=1, keepdims=True) + epsilon)
        normed_ref[span(chunk)] = (hidden * inverse * gain_ref[...]).astype(BF16)

    def between(phase):
        if phase == 2:
            gather.advance(1)
        else:
            for hop in range(2, gather.c_size):
                gather.advance(hop)

    scatter_loop(buffers, sems, partial, finish, between=between)
    gather.end()


def out_project(x, gate, full_out, gain, items, shard, layout, f_size, c_size, ident):
    seq_count, groups, width, places = layout
    rows, model_width = x.shape
    inner = groups * width
    tp_size = gate.shape[0]
    return pl.pallas_call(
        functools.partial(out_kernel, layout),
        grid=(1,),
        out_shape=[
            jax.ShapeDtypeStruct(x.shape, F32),
            jax.ShapeDtypeStruct(x.shape, BF16),
            jax.ShapeDtypeStruct(gate.shape, BF16),
            jax.ShapeDtypeStruct(gate.shape, BF16),
            jax.ShapeDtypeStruct((model_width, shard.shape[1]), BF16),
        ],
        in_specs=[
            whole(x.shape),
            whole(gate.shape),
            whole((model_width, inner), 0),
            whole(gain.shape),
            whole(items.shape),
            pl.BlockSpec(memory_space=pl.ANY),
        ],
        out_specs=[
            whole(x.shape),
            whole(x.shape),
            whole(gate.shape),
            whole(gate.shape),
            pl.BlockSpec(memory_space=pl.ANY),
        ],
        scratch_shapes=scatter_buffers(rows, model_width)
        + SCATTER_SEMS
        + weight_sems(f_size, c_size),
        compiler_params=remote_params(ident, 48),
        cost_estimate=pl.CostEstimate(
            flops=2 * gate.size * model_width, bytes_accessed=100 << 20, transcendentals=0
        ),
        name="out_project",
    )(x, gate, full_out, gain, items, shard)


def mlp_kernel(normed_ref, grad_ref, gate_w, up_w, down_w, all_ref, inner_ref, pair_ref, table, own_sem, *sems):
    me, sibling, across, diagonal = tp_places()
    greet((sibling, across))
    table[0] = normed_ref[...]
    rows, hidden = table.shape[1] // CHUNKS, gate_w.shape[1]
    tile = min(hidden, 512)

    def compute(slot, chunk):
        spot = pl.ds(pl.multiple_of(chunk * rows, rows), rows)
        normed, grad = table[slot, spot], grad_ref[slot, spot]
        for start in range(0, hidden, tile):
            columns = pl.ds(start, tile)
            gate = dot(normed, gate_w[:, columns], NN)
            up = dot(normed, up_w[:, columns], NN)
            back = dot(grad, down_w[:, columns], NN)
            sig = 1.0 / (1.0 + jnp.exp(-gate))
            silu = gate * sig
            inner_ref[slot, spot, columns] = (silu * up).astype(BF16)
            pair_ref[slot, spot, columns] = (back * up * sig * (1.0 + gate * (1.0 - sig))).astype(BF16)
            pair_ref[slot, spot, pl.ds(hidden + start, tile)] = (back * silu).astype(BF16)

    gather_loop(table, sems, compute, relative=True)
    copy = pltpu.make_async_copy(table, all_ref, own_sem)
    copy.start()
    copy.wait()


def mlp(normed, grad_all, full_two, full_down, hidden, ident):
    tp_size, rows, model_width = grad_all.shape
    total = tp_size * rows
    return pl.pallas_call(
        mlp_kernel,
        grid=(1,),
        out_shape=[
            jax.ShapeDtypeStruct(grad_all.shape, BF16),
            jax.ShapeDtypeStruct((tp_size, rows, hidden), BF16),
            jax.ShapeDtypeStruct((tp_size, rows, 2 * hidden), BF16),
        ],
        in_specs=[whole(normed.shape), whole(grad_all.shape)]
        + [whole((model_width, hidden), column) for column in (0, 1, 0)],
        out_specs=[
            pl.BlockSpec(memory_space=pl.ANY),
            whole((tp_size, rows, hidden)),
            whole((tp_size, rows, 2 * hidden)),
        ],
        scratch_shapes=[pltpu.VMEM(grad_all.shape, BF16), pltpu.SemaphoreType.DMA] + GATHER_SEMS,
        compiler_params=remote_params(ident, 56),
        cost_estimate=pl.CostEstimate(
            flops=6 * total * model_width * hidden, bytes_accessed=100 << 20, transcendentals=total * hidden
        ),
        name="mlp",
    )(normed, grad_all, full_two, full_two, full_down)


def mlp_back_kernel(
    pair_hbm, w_hbm, hidden_hbm, grad_hbm, gain_ref, sums_ref, out_ref, branch_ref, part_ref, sum_ref, *refs
):
    buffers, sems = refs[:4], refs[4:8]
    pair_ref, w_ref, hidden_ref, grad_ref, fetch_sem = refs[8:13]
    columns = pl.ds(0, w_ref.shape[1])
    fetch = Fetch(
        [
            (pair_hbm, pair_ref),
            (w_hbm.at[:, columns], w_ref),
            (hidden_hbm, hidden_ref),
            (grad_hbm, grad_ref),
        ],
        fetch_sem,
    )
    me, sibling, across, diagonal = tp_places()
    greet_all([{"tp": sibling}, {"tp": across}] + group_peers())
    weights = WeightSum(sums_ref, 0, sum_ref, refs[13:])
    weights.begin()
    fetch.wait()
    part_ref[...] = jnp.zeros_like(part_ref)
    size = hidden_ref.shape[0] // CHUNKS

    def span(chunk):
        return pl.ds(pl.multiple_of(chunk * size, size), size)

    def partial(slot, chunk):
        return dot(pair_ref[slot, span(chunk)], w_ref[...], NT)

    def finish(chunk, total):
        hidden = hidden_ref[span(chunk)]
        inverse = lax.rsqrt(jnp.mean(hidden * hidden, axis=1, keepdims=True) + epsilon)
        unit = hidden * inverse
        part_ref[...] += jnp.sum(total * unit, axis=0, keepdims=True)
        scaled = total * gain_ref[...]
        middle = jnp.mean(scaled * unit, axis=1, keepdims=True)
        grad = grad_ref[span(chunk)].astype(F32) + inverse * (scaled - unit * middle)
        out_ref[span(chunk)] = grad
        branch_ref[span(chunk)] = grad.astype(BF16)

    def between(phase):
        if phase == 2:
            weights.run_to(0, 3)
        else:
            weights.run_to(3, weights.stages)

    scatter_loop(buffers, sems, partial, finish, relative=True, between=between)
    weights.end()


def mlp_back(pair, full_two, hidden_state, grad_out, gain, part, f_size, c_size, ident):
    tp_size, rows, wide = pair.shape
    model_width = hidden_state.shape[1]
    place = pl.BlockSpec(memory_space=pl.ANY)
    total = (part.shape[0] // (f_size * c_size), part.shape[1] // 2)
    return pl.pallas_call(
        mlp_back_kernel,
        grid=(1,),
        out_shape=[
            jax.ShapeDtypeStruct(hidden_state.shape, F32),
            jax.ShapeDtypeStruct(hidden_state.shape, BF16),
            jax.ShapeDtypeStruct(gain.shape, F32),
            jax.ShapeDtypeStruct(total, F32),
        ],
        in_specs=[
            place,
            place,
            place,
            place,
            whole(gain.shape),
            place,
        ],
        out_specs=[
            whole(hidden_state.shape),
            whole(hidden_state.shape),
            whole(gain.shape),
            whole(total),
        ],
        scratch_shapes=scatter_buffers(rows, model_width)
        + SCATTER_SEMS
        + [
            pltpu.VMEM(pair.shape, BF16),
            pltpu.VMEM((model_width, wide), BF16),
            pltpu.VMEM(hidden_state.shape, F32),
            pltpu.VMEM(grad_out.shape, BF16),
            pltpu.SemaphoreType.DMA((4,)),
        ]
        + sum_scratch(f_size, c_size, *total),
        compiler_params=remote_params(ident, 60),
        cost_estimate=pl.CostEstimate(
            flops=2 * pair.size * model_width, bytes_accessed=100 << 20, transcendentals=0
        ),
        name="mlp_back",
    )(pair, full_two, hidden_state, grad_out, gain, part)


def out_back_kernel(layout, branch_ref, w_ref, gate_ref, attended_ref, sums_ref, *refs):
    seq_count, groups, width, places = layout
    all_ref, logit_ref, items, sum_ref, table, grads, own_sem = refs[:7]
    sems = refs[7:13]
    count = items.shape[0]
    me, sibling, across, diagonal = tp_places()
    greet_all([{"tp": sibling}, {"tp": across}] + group_peers())
    weights = WeightSum(sums_ref, sum_ref.shape[1], sum_ref, refs[13:])
    weights.begin()
    table[me] = branch_ref[...]
    tp_size, rows, _ = gate_ref.shape
    local, size = rows // seq_count, rows // CHUNKS

    def compute(slot, chunk):
        spot = pl.ds(pl.multiple_of(chunk * size, size), size)
        mixed = dot(table[slot, spot], w_ref[...], NN)
        gate = gate_ref[slot, spot]
        scaled = mixed * gate
        grads[slot, spot] = scaled.astype(BF16)
        attended = attended_ref[slot, spot].astype(F32)
        logit_ref[slot, spot] = (scaled * attended * (1.0 - gate)).astype(BF16)

    gather_loop(table, sems, compute, between=lambda: weights.run_share(0, 1))
    copy = pltpu.make_async_copy(table, all_ref, own_sem)
    copy.start()

    def deal(t, _):
        here = pl.ds(pl.multiple_of(t * local, local), local)
        for slot, (s, g) in enumerate(places):
            piece = grads[t, pl.ds(s * local, local), pl.ds(g * width, width)]
            items[slot % count, slot // count, here] = piece
        return 0

    lax.fori_loop(0, tp_size, deal, 0)
    copy.wait()
    weights.end()


def out_back(branch, full_out, gate, attended, part, layout, item_count, f_size, ctx_size, ident):
    seq_count, groups, width, places = layout
    rows, model_width = branch.shape
    tp_size, _, inner = gate.shape
    item = (item_count, ctx_size, tp_size * rows // seq_count, width)
    table = (tp_size, rows, model_width)
    total = (part.shape[0] // (f_size * ctx_size), part.shape[1] // 2)
    return pl.pallas_call(
        functools.partial(out_back_kernel, layout),
        grid=(1,),
        out_shape=[
            jax.ShapeDtypeStruct(table, BF16),
            jax.ShapeDtypeStruct(gate.shape, BF16),
            jax.ShapeDtypeStruct(item, BF16),
            jax.ShapeDtypeStruct(total, F32),
        ],
        in_specs=[
            whole(branch.shape),
            whole((model_width, inner), 0),
            whole(gate.shape),
            whole(attended.shape),
            pl.BlockSpec(memory_space=pl.ANY),
        ],
        out_specs=[pl.BlockSpec(memory_space=pl.ANY), whole(gate.shape), whole(item), whole(total)],
        scratch_shapes=[pltpu.VMEM(table, BF16), pltpu.VMEM(gate.shape, BF16), pltpu.SemaphoreType.DMA]
        + GATHER_SEMS
        + sum_scratch(f_size, ctx_size, *total),
        compiler_params=remote_params(ident, 48),
        cost_estimate=pl.CostEstimate(
            flops=2 * gate.size * model_width, bytes_accessed=100 << 20, transcendentals=0
        ),
        name="out_back",
    )(branch, full_out, gate, attended, part)


def assemble_kernel(layout, items, out_ref):
    seq_count, groups, width, places = layout
    count, local = items.shape[0], items.shape[3]
    inner = groups * width
    for slot, (s, g) in enumerate(places[: seq_count * groups]):
        for kind in range(3):
            columns = pl.ds(kind * inner + g * width, width)
            out_ref[0, pl.ds(s * local, local), columns] = items[slot % count, slot // count, kind]


def assemble(items, layout, tp_size):
    seq_count, groups, width, places = layout
    count, ctx_size, kinds, ctx_rows, _ = items.shape
    local = ctx_rows // tp_size
    shape = (tp_size, seq_count * local, kinds * groups * width)
    return pl.pallas_call(
        functools.partial(assemble_kernel, layout),
        grid=(tp_size,),
        out_shape=jax.ShapeDtypeStruct(shape, BF16),
        in_specs=[pl.BlockSpec((count, ctx_size, kinds, local, width), lambda t: (0, 0, 0, t, 0))],
        out_specs=pl.BlockSpec((1,) + shape[1:], lambda t: (t, 0, 0)),
        compiler_params=pltpu.CompilerParams(vmem_limit_bytes=32 << 20, dimension_semantics=("arbitrary",)),
        cost_estimate=pl.CostEstimate(flops=0, bytes_accessed=16 << 20, transcendentals=0),
        name="assemble",
    )(items)


def last_kernel(
    qkv_hbm,
    logit_hbm,
    forget_hbm,
    qkv_w_hbm,
    gate_w_hbm,
    x_hbm,
    grad_hbm,
    gain_ref,
    part_ref,
    extra_ref,
    out_ref,
    sum_ref,
    vector_ref,
    *refs,
):
    buffers, sems, (mine, near_in, group_in) = refs[:4], refs[4:8], refs[8:11]
    vector_sems = refs[11:15]
    qkv_ref, logit_ref, forget_ref, qkv_w, gate_w, x_ref, grad_ref, fetch_sem = refs[15:23]
    inner = gate_w.shape[1]
    fetch = Fetch(
        [
            (qkv_hbm, qkv_ref),
            (qkv_w_hbm, qkv_w),
            (logit_hbm, logit_ref),
            (forget_hbm, forget_ref),
            (gate_w_hbm.at[:, pl.ds(inner, inner)], gate_w),
            (x_hbm, x_ref),
            (grad_hbm, grad_ref),
        ],
        fetch_sem,
    )
    me, sibling, across, diagonal = tp_places()
    others = group_peers()
    greet_all([{"tp": sibling}, {"tp": across}, {"tp": diagonal}] + others)
    weights = WeightSum(part_ref, 0, sum_ref, refs[23:])
    weights.begin()
    fetch.wait()
    wide = qkv_ref.shape[2]
    mine[...] = extra_ref[...]
    size = x_ref.shape[0] // CHUNKS

    def span(chunk):
        return pl.ds(pl.multiple_of(chunk * size, size), size)

    def partial(slot, chunk):
        value = dot(qkv_ref[slot, span(chunk)], qkv_w[:, :wide], NT)
        value = value + dot(logit_ref[slot, span(chunk)], gate_w[...], NT)
        return value + dot(forget_ref[slot, span(chunk)], qkv_w[:, wide:], NT)

    def finish(chunk, total):
        x = x_ref[span(chunk)].astype(F32)
        inverse = lax.rsqrt(jnp.mean(x * x, axis=1, keepdims=True) + epsilon)
        unit = x * inverse
        mine[0:1] += jnp.sum(total * unit, axis=0, keepdims=True)
        scaled = total * gain_ref[...]
        middle = jnp.mean(scaled * unit, axis=1, keepdims=True)
        out_ref[span(chunk)] = (grad_ref[span(chunk)] + inverse * (scaled - unit * middle)).astype(BF16)

    stages = weights.stages
    late = max(3, stages - 4)

    def between(phase):
        if phase == 2:
            weights.run_to(0, 3)
        else:
            weights.run_to(3, late)

    scatter_loop(buffers, sems, partial, finish, between=between)
    near_send, near_recv, group_send, group_recv = vector_sems
    copies = []
    for n, peer in enumerate((sibling, across, diagonal)):
        copies.append(sending(mine, near_in.at[n], near_send.at[n], near_recv.at[n], peer))
        copies[-1].start()
    weights.run_to(late, late + 2)
    for copy in copies:
        copy.wait()
    vector_ref[...] = mine[...] + near_in[0] + near_in[1] + near_in[2]
    mine[...] = vector_ref[...]
    copies = []
    for n, peer in enumerate(others):
        copies.append(moving(mine, group_in.at[n], group_send.at[n], group_recv.at[n], peer))
        copies[-1].start()
    weights.run_to(late + 2, stages)
    for n, copy in enumerate(copies):
        copy.wait()
        vector_ref[...] += group_in[n]
    weights.end()


def last(grad_qkv, grad_logit, grad_forget, full_one, full_out, x, grad_hidden, gain, part, extra, f_size, c_size, ident):
    rows, model_width = x.shape
    wide, inner = grad_qkv.shape[2], grad_logit.shape[2]
    shard, columns = part.shape[0] // (f_size * c_size), part.shape[1]
    dma = pltpu.SemaphoreType.DMA
    place = pl.BlockSpec(memory_space=pl.ANY)
    return pl.pallas_call(
        last_kernel,
        grid=(1,),
        out_shape=[
            jax.ShapeDtypeStruct(x.shape, BF16),
            jax.ShapeDtypeStruct((shard, columns), F32),
            jax.ShapeDtypeStruct(extra.shape, F32),
        ],
        in_specs=[
            place,
            place,
            place,
            place,
            place,
            place,
            place,
            whole(gain.shape),
            place,
            whole(extra.shape),
        ],
        out_specs=[whole(x.shape), whole((shard, columns)), whole(extra.shape)],
        scratch_shapes=scatter_buffers(rows, model_width)
        + SCATTER_SEMS
        + [
            pltpu.VMEM(extra.shape, F32),
            pltpu.VMEM((3,) + extra.shape, F32),
            pltpu.VMEM((f_size * c_size - 1,) + extra.shape, F32),
        ]
        + [dma((3,))] * 2
        + [dma((f_size * c_size - 1,))] * 2
        + [
            pltpu.VMEM(grad_qkv.shape, BF16),
            pltpu.VMEM(grad_logit.shape, BF16),
            pltpu.VMEM(grad_forget.shape, BF16),
            pltpu.VMEM(full_one.shape, BF16),
            pltpu.VMEM((model_width, inner), BF16),
            pltpu.VMEM(x.shape, BF16),
            pltpu.VMEM(x.shape, F32),
            dma((7,)),
        ]
        + sum_scratch(f_size, c_size, shard, columns),
        compiler_params=remote_params(ident, 60),
        cost_estimate=pl.CostEstimate(
            flops=8 * rows * model_width * (wide + inner + LANES), bytes_accessed=100 << 20, transcendentals=0
        ),
        name="last",
    )(grad_qkv, grad_logit, grad_forget, full_one, full_out, x, grad_hidden, gain, part, extra)


def per_device(
    layer_input,
    lengths,
    attn_gain,
    w_query,
    w_key,
    w_value,
    w_forget,
    forget_bias,
    w_gate_out,
    w_out,
    mlp_gain,
    w_gate,
    w_up,
    w_down,
    cotangent,
):
    local_rows, seq_count, model_width = layer_input.shape
    head_count = forget_bias.shape[0]
    inner_width = w_query.shape[1]
    hidden = w_gate.shape[1]
    head_size = inner_width // head_count
    tp_size = lax.axis_size("tp")
    ctx_size = lax.axis_size("ctx")
    shard_count = lax.axis_size("fsdp") * ctx_size
    ctx_rows = local_rows * tp_size
    seq_len = ctx_rows * ctx_size
    all_rows = seq_count * ctx_rows
    ctx_index = lax.axis_index("ctx")
    tp_index = lax.axis_index("tp")
    shard_index = lax.axis_index("fsdp") * ctx_size + ctx_index

    pair = LANES // head_size
    groups = head_count // pair
    width = pair * head_size
    item_count = pl.cdiv(seq_count * groups, ctx_size)
    used = seq_count * groups

    def place(slot):
        slot = slot % used
        return (slot // groups + slot % groups) % seq_count, slot % groups

    places = tuple(place(slot) for slot in range(ctx_size * item_count))
    layout = (seq_count, groups, width, places)

    fsdp_size = lax.axis_size("fsdp")
    packed_one = jnp.concatenate(
        [
            w_query,
            w_key,
            w_value,
            w_forget,
            jnp.zeros((attn_gain.shape[0], LANES - head_count), BF16),
        ],
        axis=1,
    )
    packed_two = jnp.concatenate([w_gate, w_up], axis=1)
    packed_out = jnp.concatenate([w_out, w_gate_out], axis=1)
    edge = 3 * inner_width
    input_rows = layer_input.transpose(1, 0, 2).reshape(seq_count * local_rows, model_width)
    shard_rows = model_width // shard_count
    own_gains = jnp.stack([attn_gain, mlp_gain]).astype(F32)
    own_gains = jnp.pad(own_gains, ((0, 6), (0, -shard_rows % LANES)))
    input_all, full_one, gains = startup(
        input_rows, packed_one, own_gains, fsdp_size, ctx_size, 1
    )
    gain_one = gains[:, 0, :shard_rows].reshape(1, model_width)
    gain_two = gains[:, 1, :shard_rows].reshape(1, model_width)

    def by_sequence(rows):
        return rows.transpose(1, 0, 2).reshape(seq_count * local_rows, model_width)

    def by_position(rows):
        return rows.reshape(seq_count, local_rows, model_width).transpose(1, 0, 2)

    local_pos = (ctx_index * tp_size + tp_index) * local_rows + jnp.arange(
        local_rows, dtype=jnp.int32
    )
    valid_rows = (local_pos[None, :] < lengths[:, None]).astype(F32)
    valid_rows = valid_rows.reshape(seq_count * local_rows, 1)
    ctx_pos = ctx_index * ctx_rows + jnp.arange(ctx_rows, dtype=jnp.int32)
    ctx_pos = ctx_pos.reshape(tp_size, 1, local_rows)
    ctx_valid = (ctx_pos < lengths[None, :, None]).astype(F32)

    grad_out = (valid_rows * by_sequence(cotangent).astype(F32)).astype(BF16)
    normed_one, forget_rows, items = project(
        input_all, gain_one, full_one, layout, item_count, ctx_size
    )
    normed_flat = normed_one.reshape(all_rows, model_width)
    forget_logit = forget_rows.reshape(all_rows, LANES)[:, :head_count].T
    forget_logit = forget_logit + forget_bias.astype(F32)[:, None]
    forget_logit = forget_logit.reshape(head_count, tp_size, seq_count, local_rows)
    log_forget = (ctx_valid[None] * jax.nn.log_sigmoid(forget_logit)).astype(BF16)

    cut = log_forget.astype(F32).reshape(groups, pair, tp_size, seq_count, local_rows)
    picked = jnp.stack([cut[g, :, :, s] for s, g in places])
    picked = picked.reshape(ctx_size, item_count, pair, ctx_rows).transpose(1, 0, 2, 3)
    picked = jnp.pad(picked, ((0, 0), (0, 0), (0, 8 - pair), (0, 0)))
    attended_items, qkv, full_two, full_out, grad_all, exact, lse, decay = context(
        items, picked, packed_two, packed_out, grad_out, fsdp_size, head_size, 7
    )
    gate_out_w = full_out[:, inner_width:]
    gate_logit = dot(normed_flat, gate_out_w, NN)
    out_gate = jax.nn.sigmoid(gate_logit).reshape(tp_size, -1, inner_width)
    hidden_state, normed_two, attended, mixed, down_w = out_project(
        input_rows,
        out_gate,
        full_out,
        gain_two,
        attended_items,
        w_down,
        layout,
        fsdp_size,
        ctx_size,
        2,
    )
    normed_two_all, inner_act, grad_pair = mlp(normed_two, grad_all, full_two, down_w, hidden, 3)
    normed_two_flat = normed_two_all.reshape(all_rows, model_width)
    inner_flat = inner_act.reshape(all_rows, hidden)
    grad_pair_flat = grad_pair.reshape(all_rows, 2 * hidden)
    grad_flat = grad_all.reshape(all_rows, model_width)

    gate_up_part = dot(normed_two_flat, grad_pair_flat, TN).astype(BF16)
    grad_hidden, branch, mlp_gain_part, gate_sum = mlp_back(
        grad_pair, full_two, hidden_state, grad_out, gain_two, gate_up_part, fsdp_size, ctx_size, 4
    )
    feedforward_part = dot(inner_flat, down_w, NT).astype(BF16)
    branch_all, grad_gate_logit, grads, up_sum = out_back(
        branch,
        full_out,
        out_gate,
        attended,
        gate_up_part,
        layout,
        item_count,
        fsdp_size,
        ctx_size,
        5,
    )
    branch_flat = branch_all.reshape(all_rows, model_width)
    logit_flat = grad_gate_logit.reshape(all_rows, inner_width)

    out_part = jnp.concatenate(
        [
            dot(grad_flat, inner_flat, TN).astype(BF16),
            dot(branch_flat, mixed.reshape(all_rows, inner_width), TN).astype(BF16),
            dot(normed_flat, logit_flat, TN).astype(BF16),
        ],
        axis=1,
    )
    grad_items, forget_items, out_sum, feedforward = context_back(
        grads,
        qkv,
        exact,
        lse,
        decay,
        out_part,
        feedforward_part.reshape(tp_size, -1, model_width),
        fsdp_size,
        head_size,
        8,
    )
    output = (valid_rows * (hidden_state + feedforward.astype(F32))).astype(BF16)
    forget_back = forget_items[:, :, :pair].astype(BF16).transpose(1, 0, 2, 3)
    forget_back = forget_back.reshape(ctx_size * item_count, pair, tp_size, local_rows)
    slots = {place(slot): slot for slot in range(used)}
    forget_back = jnp.stack(
        [
            jnp.stack([forget_back[slots[s, g]] for s in range(seq_count)], axis=2)
            for g in range(groups)
        ]
    ).reshape(head_count, tp_size, seq_count, local_rows)
    grad_forget_logit = forget_back.astype(F32) * ctx_valid[None] * jax.nn.sigmoid(-forget_logit)
    grad_forget_logit = grad_forget_logit.astype(BF16).reshape(head_count, all_rows)
    bias_part = jnp.sum(grad_forget_logit.astype(F32), axis=1)
    grad_forget_rows = jnp.pad(grad_forget_logit, ((0, LANES - head_count), (0, 0))).T
    grad_qkv = assemble(grad_items, layout, tp_size)
    grad_qkvf = jnp.concatenate([grad_qkv.reshape(all_rows, edge), grad_forget_rows], axis=1)
    bias_full = lax.dynamic_update_slice(
        jnp.zeros((1, model_width), F32), bias_part[None], (0, tp_index * head_count)
    )
    extra = jnp.concatenate(
        [jnp.zeros_like(bias_full), mlp_gain_part, bias_full, jnp.zeros((5, model_width), F32)]
    )
    input_grad, qkv_sum, vectors = last(
        grad_qkv,
        grad_gate_logit,
        grad_forget_rows.reshape(tp_size, -1, LANES),
        full_one,
        full_out,
        input_rows,
        grad_hidden,
        gain_one,
        dot(normed_flat, grad_qkvf, TN).astype(BF16),
        extra,
        fsdp_size,
        ctx_size,
        6,
    )
    gain_one_sum, gain_two_sum, bias_sum = vectors[0], vectors[1], vectors[2]
    attn_gain_grad = lax.dynamic_slice_in_dim(gain_one_sum, shard_index * shard_rows, shard_rows, 0)
    mlp_gain_grad = lax.dynamic_slice_in_dim(gain_two_sum, shard_index * shard_rows, shard_rows, 0)
    forget_bias_grad = lax.dynamic_slice_in_dim(bias_sum, tp_index * head_count, head_count, 0)
    wide = inner_width
    return (
        by_position(output),
        by_position(input_grad),
        attn_gain_grad,
        qkv_sum[:, :wide],
        qkv_sum[:, wide : 2 * wide],
        qkv_sum[:, 2 * wide : 3 * wide],
        qkv_sum[:, 3 * wide : 3 * wide + head_count],
        forget_bias_grad,
        out_sum[:, hidden + wide :],
        out_sum[:, hidden : hidden + wide],
        mlp_gain_grad,
        gate_sum,
        up_sum,
        out_sum[:, :hidden],
    )


def solution(mesh):
    rows = P(("ctx", "tp"), "fsdp", None)
    matrix = P(("fsdp", "ctx"), "tp")
    vector = P(("fsdp", "ctx"))
    return jax.shard_map(
        per_device,
        mesh=mesh,
        in_specs=(
            rows,
            P("fsdp"),
            vector,
            matrix,
            matrix,
            matrix,
            matrix,
            P("tp"),
            matrix,
            matrix,
            vector,
            matrix,
            matrix,
            matrix,
            rows,
        ),
        out_specs=(
            rows,
            rows,
            vector,
            matrix,
            matrix,
            matrix,
            matrix,
            P("tp"),
            matrix,
            matrix,
            vector,
            matrix,
            matrix,
            matrix,
        ),
        check_vma=False,
    )
```

```python
import functools

import jax
import jax.numpy as jnp
from jax import lax
from jax.experimental import pallas as pl
from jax.experimental.pallas import tpu as pltpu
from jax.sharding import PartitionSpec as P

F32 = jnp.float32
BF16 = jnp.bfloat16
LANES = 128
MESH = pl.DeviceIdType.MESH
epsilon = 1e-06
masked_score = -1e30
NT = (((1,), (1,)), ((), ()))
NN = (((1,), (0,)), ((), ()))
TN = (((0,), (0,)), ((), ()))


def dot(left, right, dims):
    return lax.dot_general(left, right, dims, preferred_element_type=F32)


def of_head(block, head, head_size, ones_at=None):
    lane = lax.broadcasted_iota(jnp.int32, block.shape, 1)
    out = jnp.where(lane // head_size == head, block, jnp.zeros_like(block))
    if ones_at is not None:
        out = jnp.where(lane == ones_at, jnp.ones_like(block), out)
    return out


def spare_lane(head, head_size):
    return ((head + 1) % 2) * head_size


def attend_item(qkv, decay, out, exact, lse, heads, head_size):
    count, _, block, width = qkv.shape
    scale = head_size**-0.5
    row = lax.broadcasted_iota(jnp.int32, (block, block), 0)
    column = lax.broadcasted_iota(jnp.int32, (block, block), 1)
    causal = column <= row

    def query_block(i, _):
        query = qkv[i, 0]
        lanes = pl.ds(pl.multiple_of(i * block, block), block)
        result = jnp.zeros((block, width), F32)
        for head in range(heads):
            query_head = of_head(query, head, head_size)

            def step(j, carry, masked):
                top, total, acc = carry
                keys = pl.ds(pl.multiple_of(j * block, block), block)
                score = dot(query_head, qkv[j, 1], NT) * scale
                score = score - decay[head : head + 1, keys]
                if masked:
                    score = jnp.where(causal, score, masked_score)
                new_top = jnp.maximum(top, jnp.max(score, axis=1, keepdims=True))
                prob = jnp.exp(score - new_top)
                shrink = jnp.exp(top - new_top)
                total = total * shrink + jnp.sum(prob, axis=1, keepdims=True)
                acc = acc * shrink + dot(prob.astype(BF16), qkv[j, 2], NN)
                return new_top, total, acc

            carry = (
                jnp.full((block, 1), masked_score, F32),
                jnp.zeros((block, 1), F32),
                jnp.zeros((block, width), F32),
            )
            carry = lax.fori_loop(0, i, lambda j, c: step(j, c, False), carry)
            top, total, acc = step(i, carry, True)
            lane = lax.broadcasted_iota(jnp.int32, acc.shape, 1)
            result = jnp.where(lane // head_size == head, acc / total, result)
            stat = jnp.broadcast_to(top + jnp.log(total), (block, LANES)).T
            lse[head : head + 1, lanes] = stat[0:1]
        exact[i] = result
        out[i] = result.astype(BF16)
        return 0

    lax.fori_loop(0, count, query_block, 0)


def attend_item_back(qkv, grads, exact, lse, decay, dqkv, change, dq_acc, delta, heads, head_size):
    count, _, block, width = qkv.shape
    scale = head_size**-0.5
    row = lax.broadcasted_iota(jnp.int32, (block, block), 0)
    column = lax.broadcasted_iota(jnp.int32, (block, block), 1)
    causal = row <= column
    dq_acc[...] = jnp.zeros_like(dq_acc)
    change[...] = jnp.zeros_like(change)

    def prepare(i, _):
        lanes = pl.ds(pl.multiple_of(i * block, block), block)
        product = grads[i].astype(F32) * exact[i]
        lane = lax.broadcasted_iota(jnp.int32, product.shape, 1)
        for head in range(heads):
            part = jnp.where(lane // head_size == head, product, 0.0)
            part = jnp.sum(part, axis=1, keepdims=True)
            delta[head : head + 1, lanes] = jnp.broadcast_to(part, (block, LANES)).T[0:1]
        return 0

    lax.fori_loop(0, count, prepare, 0)

    def key_block(j, _):
        keys = pl.ds(pl.multiple_of(j * block, block), block)
        key = qkv[j, 1]
        value = qkv[j, 2]
        value_total = jnp.zeros((block, width), F32)
        key_total = jnp.zeros((block, width), F32)
        for head in range(heads):
            spare = spare_lane(head, head_size)
            key_ones = of_head(key, head, head_size, spare)
            fall = jnp.broadcast_to(decay[head : head + 1, keys], (LANES, block)).T[:, 0:1]

            def step(i, carry, masked):
                value_acc, key_acc = carry
                lanes = pl.ds(pl.multiple_of(i * block, block), block)
                query = qkv[i, 0]
                grad = of_head(grads[i], head, head_size)
                score = dot(key, of_head(query, head, head_size), NT) * scale
                score = score - fall - lse[head : head + 1, lanes]
                if masked:
                    score = jnp.where(causal, score, masked_score)
                prob = jnp.exp(score)
                grad_prob = dot(value, grad, NT)
                grad_score = prob * (grad_prob - delta[head : head + 1, lanes])
                grad_score = grad_score.astype(BF16)
                value_acc = value_acc + dot(prob.astype(BF16), grad, NN)
                query_ones = of_head(query, head, head_size, spare)
                key_acc = key_acc + dot(grad_score, query_ones, NN)
                dq_acc[head, i] += dot(grad_score, key_ones, TN)
                return value_acc, key_acc

            zero = jnp.zeros((block, width), F32)
            carry = step(j, (zero, zero), True)
            carry = lax.fori_loop(j + 1, count, lambda i, c: step(i, c, False), carry)
            value_acc, key_acc = carry
            value_total = value_total + value_acc
            lane = lax.broadcasted_iota(jnp.int32, key_acc.shape, 1)
            key_total = jnp.where(lane // head_size == head, key_acc, key_total)
            change[head : head + 1, keys] -= key_acc.T[spare : spare + 1]
        dqkv[j, 1] = (key_total * scale).astype(BF16)
        dqkv[j, 2] = value_total.astype(BF16)
        return 0

    lax.fori_loop(0, count, key_block, 0)

    def finish(i, _):
        lanes = pl.ds(pl.multiple_of(i * block, block), block)
        total = jnp.zeros((block, width), F32)
        for head in range(heads):
            spare = spare_lane(head, head_size)
            part = dq_acc[head, i]
            lane = lax.broadcasted_iota(jnp.int32, part.shape, 1)
            total = jnp.where(lane // head_size == head, part, total)
            change[head : head + 1, lanes] += part.T[spare : spare + 1]
        dqkv[i, 0] = (total * scale).astype(BF16)
        return 0

    lax.fori_loop(0, count, finish, 0)


def triangle(upward):
    row = lax.broadcasted_iota(jnp.int32, (LANES, LANES), 0)
    column = lax.broadcasted_iota(jnp.int32, (LANES, LANES), 1)
    keep = (row <= column) if upward else (row >= column)
    return jnp.where(keep, 1.0, 0.0).astype(BF16)


def exact_product(values, matrix):
    high = values.astype(BF16)
    rest = values - high.astype(F32)
    middle = rest.astype(BF16)
    low = (rest - middle.astype(F32)).astype(BF16)
    return dot(high, matrix, NN) + dot(middle, matrix, NN) + dot(low, matrix, NN)


def ctx_sending(source, target, send_sem, recv_sem, peer):
    return pltpu.make_async_remote_copy(
        src_ref=source,
        dst_ref=target,
        send_sem=send_sem,
        recv_sem=recv_sem,
        device_id={"ctx": peer},
        device_id_type=MESH,
    )


def ctx_greet(size):
    me = lax.axis_index("ctx")
    barrier = pltpu.get_barrier_semaphore()
    for step in range(1, size):
        peer = lax.rem(me + step, size)
        pl.semaphore_signal(barrier, inc=1, device_id={"ctx": peer}, device_id_type=MESH)
    pl.semaphore_wait(barrier, size - 1)
    return me


class Exchange:
    def __init__(self, me, size, source, target, sems):
        self.me, self.size, self.source, self.target = me, size, source, target
        self.send_sem, self.recv_sem, self.own_sem = sems

    def own(self, item):
        return pltpu.make_async_copy(
            self.source.at[item, self.me], self.target.at[item, self.me], self.own_sem.at[item]
        )

    def copy(self, item, step):
        peer = lax.rem(self.me + step, self.size)
        return ctx_sending(
            self.source.at[item, peer],
            self.target.at[item, self.me],
            self.send_sem.at[item, step],
            self.recv_sem.at[item, step],
            peer,
        )

    def start(self, item):
        for step in range(1, self.size):
            self.copy(item, step).start()
        self.own(item).start()

    def arrive(self, item):
        self.own(item).wait()
        for step in range(1, self.size):
            self.copy(item, step).wait_recv()

    def drain(self, item):
        for step in range(1, self.size):
            self.copy(item, step).wait_send()


def exchange_sems(items, size):
    return [
        pltpu.SemaphoreType.DMA((items, size)),
        pltpu.SemaphoreType.DMA((items, size)),
        pltpu.SemaphoreType.DMA((items,)),
    ]


def context_kernel(
    heads,
    head_size,
    items_ref,
    forget_ref,
    gate_ref,
    up_ref,
    out_w_ref,
    gate_out_ref,
    rows_ref,
    back_ref,
    qkv_ref,
    full_ref,
    full_out_ref,
    table_ref,
    exact_ref,
    lse_ref,
    decay_ref,
    *refs,
):
    qkv, forget, out, save_sem = refs[:4]
    sems = refs[4:]
    count, size, _, block, width = items_ref.shape
    tp, sibling, across, diagonal = tp_places()
    greet_all([{"tp": sibling}, {"tp": across}] + group_peers())
    me = lax.axis_index("ctx")
    gathers = (
        WeightGather((out_w_ref, gate_out_ref), full_out_ref, sems[9:14]),
        WeightGather((gate_ref, up_ref), full_ref, sems[14:19]),
    )
    rows = RowGather(rows_ref, table_ref, sems[19:])
    forgets = Exchange(me, size, forget_ref, forget, sems[0:3])
    inputs = Exchange(me, size, items_ref, qkv, sems[3:6])
    results = Exchange(me, size, out, back_ref, sems[6:9])

    @pl.loop(0, count)
    def _(item):
        forgets.start(item)

    for gather in gathers:
        gather.begin()
    inputs.start(0)
    rows.begin()

    @pl.loop(0, count)
    def _(item):
        forgets.arrive(item)

    @pl.loop(0, count)
    def _(item):
        upper = triangle(True)
        before = jnp.zeros((8, 1), F32)
        for start in range(0, size * block, LANES):
            part = forget[item, start // block, :, pl.ds(start % block, LANES)]
            total = before + dot(part.astype(BF16), upper, NN)
            decay_ref[item, :, pl.ds(start, LANES)] = total
            before = total[:, LANES - 1 :]

    lse_ref[...] = jnp.zeros_like(lse_ref)

    @pl.loop(0, count)
    def _(item):
        inputs.arrive(item)

        @pl.when(item + 1 < count)
        def _():
            inputs.start(item + 1)

        for hop in range(1, min(size, count + 1)):

            @pl.when(item == hop - 1)
            def _(hop=hop):
                for gather in gathers:
                    gather.advance(hop)

        saving = pltpu.make_async_copy(qkv.at[item], qkv_ref.at[item], save_sem)
        saving.start()
        attend_item(
            qkv.at[item], decay_ref.at[item], out.at[item], exact_ref.at[item], lse_ref.at[item], heads, head_size
        )
        results.start(item)
        saving.wait()

    rows.advance()
    for hop in range(count + 1, size):
        for gather in gathers:
            gather.advance(hop)

    @pl.loop(0, count)
    def _(item):
        forgets.drain(item)
        inputs.drain(item)
        results.arrive(item)
        results.drain(item)

    for gather in gathers:
        gather.end()
    rows.end()


def full_block(shape):
    return pl.BlockSpec(shape, lambda i: (0,) * len(shape), pipeline_mode=pl.Buffered(1))


def attend_cost(items, heads, products):
    count, size, _, block, width = items.shape
    pairs = count * heads * (size * block) ** 2 // 2
    return pl.CostEstimate(
        flops=2 * products * pairs * 256, bytes_accessed=100 << 20, transcendentals=pairs
    )


def context(items, forget, shards, rows, f_size, head_size, ident):
    count, size, _, block, width = items.shape
    full = shards[0].shape[0] * f_size * size
    heads = width // head_size
    place = pl.BlockSpec(memory_space=pl.ANY)
    exact, stat = (count, size, block, width), (count, 8, size * block)
    return pl.pallas_call(
        functools.partial(context_kernel, heads, head_size),
        grid=(1,),
        out_shape=[
            jax.ShapeDtypeStruct(exact, BF16),
            jax.ShapeDtypeStruct(items.shape, BF16),
            jax.ShapeDtypeStruct((full, 2 * shards[0].shape[1]), BF16),
            jax.ShapeDtypeStruct((full, 2 * shards[2].shape[1]), BF16),
            jax.ShapeDtypeStruct((4,) + rows.shape, BF16),
            jax.ShapeDtypeStruct(exact, F32),
            jax.ShapeDtypeStruct(stat, F32),
            jax.ShapeDtypeStruct(stat, F32),
        ],
        in_specs=[place, place]
        + [full_block(shard.shape) for shard in shards]
        + [full_block(rows.shape)],
        out_specs=[place, place, place, place, place, full_block(exact), full_block(stat), full_block(stat)],
        scratch_shapes=[
            pltpu.VMEM(items.shape, BF16),
            pltpu.VMEM(forget.shape, F32),
            pltpu.VMEM(exact, BF16),
            pltpu.SemaphoreType.DMA,
        ]
        + exchange_sems(count, size) * 3
        + weight_sems(f_size, size, 2) * 2
        + [pltpu.SemaphoreType.DMA((3,))] * 2
        + [pltpu.SemaphoreType.DMA],
        compiler_params=remote_params(ident, 48),
        cost_estimate=attend_cost(items, heads, 2),
        name="context",
    )(items, forget, *shards, rows)


def context_back_kernel(
    heads,
    head_size,
    items_ref,
    qkv_ref,
    exact_ref,
    lse_ref,
    decay_ref,
    down_ref,
    part_ref,
    table_ref,
    back_ref,
    forget_ref,
    down_sum_ref,
    sum_ref,
    rows_ref,
    *refs,
):
    grads, dqkv, change, slope, dq_acc, delta = refs[:6]
    sems = refs[6:15]
    count, size, block, width = items_ref.shape
    tp, sibling, across, diagonal = tp_places()
    greet_all([{"tp": sibling}, {"tp": across}] + group_peers())
    me = lax.axis_index("ctx")
    sums = (
        WeightSum(part_ref, 0, sum_ref, refs[15:23]),
        WeightSum(down_ref, 0, down_sum_ref, refs[23:31]),
    )
    rows = RowSum(table_ref, rows_ref, refs[31:])
    inputs = Exchange(me, size, items_ref, grads, sems[0:3])
    results = Exchange(me, size, dqkv, back_ref, sems[3:6])
    forgets = Exchange(me, size, slope, forget_ref, sems[6:9])

    inputs.start(0)
    for weights in sums:
        weights.begin()
    rows.begin()

    @pl.loop(0, count)
    def _(item):
        inputs.arrive(item)

        @pl.when(item + 1 < count)
        def _():
            inputs.start(item + 1)

        attend_item_back(
            qkv_ref.at[item],
            grads.at[item],
            exact_ref.at[item],
            lse_ref.at[item],
            decay_ref.at[item],
            dqkv.at[item],
            change,
            dq_acc,
            delta,
            heads,
            head_size,
        )
        results.start(item)
        lower = triangle(False)
        after = jnp.zeros((8, 1), F32)
        for start in reversed(range(0, size * block, LANES)):
            total = after + exact_product(change[:, pl.ds(start, LANES)], lower)
            slope[item, start // block, :, pl.ds(start % block, LANES)] = total
            after = total[:, 0:1]
        forgets.start(item)

        for turn in range(count):

            @pl.when(item == turn)
            def _(turn=turn):
                for weights in sums:
                    weights.run_share(turn, count + 1)
                if turn == 0:
                    rows.advance()

    share = -(-sums[0].stages // (count + 1))
    for n in range(count * share, sums[0].stages):
        for weights in sums:
            weights.run(n)

    @pl.loop(0, count)
    def _(item):
        inputs.drain(item)
        results.arrive(item)
        results.drain(item)
        forgets.arrive(item)
        forgets.drain(item)

    for weights in sums:
        weights.end()
    rows.end()


def context_back(grads, qkv, exact, lse, decay, down, part, table, f_size, head_size, ident):
    count, size, _, block, width = qkv.shape
    heads = width // head_size
    place = pl.BlockSpec(memory_space=pl.ANY)
    forget = (count, size, 8, block)
    total = (part.shape[0] // (f_size * size), part.shape[1])
    down_total = (total[0], down.shape[1])
    return pl.pallas_call(
        functools.partial(context_back_kernel, heads, head_size),
        grid=(1,),
        out_shape=[
            jax.ShapeDtypeStruct(qkv.shape, BF16),
            jax.ShapeDtypeStruct(forget, F32),
            jax.ShapeDtypeStruct(down_total, F32),
            jax.ShapeDtypeStruct(total, F32),
            jax.ShapeDtypeStruct(table.shape[1:], BF16),
        ],
        in_specs=[
            place,
            full_block(qkv.shape),
            full_block(exact.shape),
            full_block(lse.shape),
            full_block(decay.shape),
            place,
            place,
            place,
        ],
        out_specs=[
            place,
            place,
            full_block(down_total),
            full_block(total),
            full_block(table.shape[1:]),
        ],
        scratch_shapes=[
            pltpu.VMEM(grads.shape, BF16),
            pltpu.VMEM(qkv.shape, BF16),
            pltpu.VMEM((8, size * block), F32),
            pltpu.VMEM(forget, F32),
            pltpu.VMEM((heads, size, block, width), F32),
            pltpu.VMEM((8, size * block), F32),
        ]
        + exchange_sems(count, size) * 3
        + sum_scratch(f_size, size, *total)
        + sum_scratch(f_size, size, *down_total)
        + row_sum_scratch(*table.shape[1:]),
        compiler_params=remote_params(ident, 60),
        cost_estimate=attend_cost(qkv, heads, 5),
        name="context_back",
    )(grads, qkv, exact, lse, decay, down, part, table)


CHUNKS = 4
HALVES = 2


def tp_places():
    me = lax.axis_index("tp")
    sibling = me + 1 - 2 * lax.rem(me, 2)
    across = lax.rem(me + 2, 4)
    diagonal = lax.rem(sibling + 2, 4)
    return me, sibling, across, diagonal


def greet(peers):
    barrier = pltpu.get_barrier_semaphore()
    for peer in peers:
        pl.semaphore_signal(barrier, inc=1, device_id={"tp": peer}, device_id_type=MESH)
    pl.semaphore_wait(barrier, len(peers))


def sending(source, target, send_sem, recv_sem, peer):
    return pltpu.make_async_remote_copy(
        src_ref=source,
        dst_ref=target,
        send_sem=send_sem,
        recv_sem=recv_sem,
        device_id={"tp": peer},
        device_id_type=MESH,
    )


def pick(step, chunks, places):
    me, sibling, across, diagonal = places
    late = step - 2 * chunks
    far = jnp.where(lax.rem(late, 2) == 0, across, diagonal)
    slot = jnp.where(step < chunks, me, jnp.where(step < 2 * chunks, sibling, far))
    chunk = jnp.where(step < 2 * chunks, lax.rem(step, chunks), late // 2)
    return slot, chunk


def gather_loop(table, sems, compute, own=None, relative=False, between=None, ready=None):
    near_send, near_recv, far_send, far_recv, pass_send, pass_recv = sems
    me, sibling, across, diagonal = tp_places()
    places = (0, 1, 2, 3) if relative else (me, sibling, across, diagonal)
    mine, near_by, far_off, corner = places
    near_spot, far_spot, pass_spot = (1, 2, 3) if relative else (me, me, across)
    rows = table.shape[1] // CHUNKS

    def part(slot, chunk):
        return table.at[slot, pl.ds(pl.multiple_of(chunk * rows, rows), rows)]

    def far(chunk):
        source = part(mine, chunk)
        if own is not None:
            source = own.at[pl.ds(pl.multiple_of(chunk * rows, rows), rows)]
        return sending(source, part(far_spot, chunk), far_send.at[chunk], far_recv.at[chunk], across)

    def far_arrival(chunk):
        spot = part(far_off, chunk)
        return sending(spot, spot, far_send.at[chunk], far_recv.at[chunk], across)

    def passing(chunk):
        return sending(
            part(far_off, chunk), part(pass_spot, chunk), pass_send.at[chunk], pass_recv.at[chunk], sibling
        )

    def pass_arrival(chunk):
        spot = part(corner, chunk)
        return sending(spot, spot, pass_send.at[chunk], pass_recv.at[chunk], sibling)

    for chunk in range(CHUNKS):
        far(chunk).start()
    own = table.at[mine] if own is None else own
    near = sending(own, table.at[near_spot], near_send, near_recv, sibling)
    near.start()
    if ready is not None:
        ready()

    def body(step, _):
        slot, chunk = pick(step, CHUNKS, places)
        late = step - 2 * CHUNKS

        @pl.when(step == CHUNKS)
        def _():
            spot = table.at[near_by]
            sending(spot, spot, near_send, near_recv, sibling).wait_recv()

        @pl.when((late >= 0) & (lax.rem(late, 2) == 0))
        def _():
            far_arrival(chunk).wait_recv()
            passing(chunk).start()

        @pl.when((late >= 0) & (lax.rem(late, 2) == 1))
        def _():
            pass_arrival(chunk).wait_recv()

        compute(slot, chunk)
        return 0

    if between is None:
        lax.fori_loop(0, 4 * CHUNKS, body, 0)
    else:
        lax.fori_loop(0, 2 * CHUNKS, body, 0)
        between()
        lax.fori_loop(2 * CHUNKS, 4 * CHUNKS, body, 0)
    near.wait_send()
    for chunk in range(CHUNKS):
        far(chunk).wait_send()
        passing(chunk).wait_send()


GATHER_SEMS = [pltpu.SemaphoreType.DMA] * 2 + [pltpu.SemaphoreType.DMA((CHUNKS,))] * 4


def scatter_loop(buffers, sems, partial, finish, relative=False, between=None):
    near_out, near_in, far_out, far_in = buffers
    near_send, near_recv, far_send, far_recv = sems
    me, sibling, across, diagonal = tp_places()
    mine, near_by, far_off, corner = (0, 1, 2, 3) if relative else (me, sibling, across, diagonal)
    rows = far_out.shape[0] // CHUNKS

    def span(chunk):
        return pl.ds(pl.multiple_of(chunk * rows, rows), rows)

    def near(half, chunk):
        return sending(
            near_out.at[half, span(chunk)],
            near_in.at[half, span(chunk)],
            near_send.at[half, chunk],
            near_recv.at[half, chunk],
            sibling,
        )

    def far(chunk):
        return sending(
            far_out.at[span(chunk)],
            far_in.at[span(chunk)],
            far_send.at[chunk],
            far_recv.at[chunk],
            across,
        )

    def body(step, _):
        phase, chunk = step // CHUNKS, lax.rem(step, CHUNKS)
        slot = jnp.where(
            phase == 0, corner, jnp.where(phase == 1, far_off, jnp.where(phase == 2, near_by, mine))
        )
        value = partial(slot, chunk)
        spot = span(chunk)

        @pl.when(lax.rem(phase, 2) == 0)
        def _():
            half = phase // 2
            near_out[half, spot] = value.astype(BF16)
            near(half, chunk).start()

        @pl.when(phase == 1)
        def _():
            near(0, chunk).wait_recv()
            far_out[spot] = (value + near_in[0, spot].astype(F32)).astype(BF16)
            far(chunk).start()

        @pl.when(phase == 3)
        def _():
            near(1, chunk).wait_recv()

            far(chunk).wait_recv()
            finish(chunk, value + near_in[1, spot].astype(F32) + far_in[spot].astype(F32))

        return 0

    if between is None:
        lax.fori_loop(0, 4 * CHUNKS, body, 0)
    else:
        lax.fori_loop(0, CHUNKS, body, 0)
        for phase in (1, 2, 3):
            between(phase)
            lax.fori_loop(phase * CHUNKS, (phase + 1) * CHUNKS, body, 0)
    for chunk in range(CHUNKS):
        near(0, chunk).wait_send()
        near(1, chunk).wait_send()
        far(chunk).wait_send()


SCATTER_SEMS = [pltpu.SemaphoreType.DMA((2, CHUNKS))] * 2 + [pltpu.SemaphoreType.DMA((CHUNKS,))] * 2


def scatter_buffers(rows, width):
    return [
        pltpu.VMEM((2, rows, width), BF16),
        pltpu.VMEM((2, rows, width), BF16),
        pltpu.VMEM((rows, width), BF16),
        pltpu.VMEM((rows, width), BF16),
    ]


def group_peers():
    f_size, c_size = lax.axis_size("fsdp"), lax.axis_size("ctx")
    f, c = lax.axis_index("fsdp"), lax.axis_index("ctx")
    return [
        {"fsdp": lax.rem(f + i, f_size), "ctx": lax.rem(c + j, c_size)}
        for i in range(f_size)
        for j in range(c_size)
        if i or j
    ]


def greet_all(peers):
    barrier = pltpu.get_barrier_semaphore()
    for peer in peers:
        pl.semaphore_signal(barrier, inc=1, device_id=peer, device_id_type=MESH)
    pl.semaphore_wait(barrier, len(peers))


def moving(source, target, send_sem, recv_sem, peer):
    return pltpu.make_async_remote_copy(
        src_ref=source,
        dst_ref=target,
        send_sem=send_sem,
        recv_sem=recv_sem,
        device_id=peer,
        device_id_type=MESH,
    )


class WeightGather:
    def __init__(self, shards, full, sems):
        self.shards, self.full = shards, full
        widths = [shard.shape[1] for shard in shards]
        self.columns = [pl.ds(sum(widths[:h]), width) for h, width in enumerate(widths)]
        self.f_size, self.c_size = lax.axis_size("fsdp"), lax.axis_size("ctx")
        self.f, self.c = lax.axis_index("fsdp"), lax.axis_index("ctx")
        self.sems = sems

    def spot(self, c, h, f=None):
        rows = self.shards[0].shape[0]
        block = (self.f if f is None else f) * self.c_size + c
        return self.full.at[pl.ds(pl.multiple_of(block * rows, rows), rows), self.columns[h]]

    def own(self, h):
        return pltpu.make_async_copy(self.shards[h], self.spot(self.c, h), self.sems[4].at[h])

    def along(self, c, h, hop, side, first=False):
        source = self.shards[h] if first else self.spot(c, h)
        peer = {"ctx": self.c + (1 if side else -1)}
        send, recv = self.sems[0].at[side, hop, h], self.sems[1].at[side, hop, h]
        return moving(source, self.spot(c, h), send, recv, peer)

    def over(self, c, h, step, first=False):
        source = self.shards[h] if first else self.spot(c, h)
        peer = {"fsdp": lax.rem(self.f + step, self.f_size)}
        send, recv = self.sems[2].at[step, c, h], self.sems[3].at[step, c, h]
        return moving(source, self.spot(c, h), send, recv, peer)

    def over_arrival(self, c, h, step):
        spot = self.spot(c, h, lax.rem(self.f + self.f_size - step, self.f_size))
        peer = {"fsdp": lax.rem(self.f + step, self.f_size)}
        return moving(spot, spot, self.sems[2].at[step, c, h], self.sems[3].at[step, c, h], peer)

    def can(self, side):
        return self.c + 1 < self.c_size if side else self.c > 0

    def holds(self, hop, side):
        return self.c - hop >= 0 if side else self.c + hop < self.c_size

    def begin(self):
        for h in range(len(self.shards)):
            for side in (1, 0):

                @pl.when(self.can(side))
                def _(side=side):
                    self.along(self.c, h, 1, side, True).start()

            for step in range(1, self.f_size):
                self.over(self.c, h, step, True).start()

        for h in range(len(self.shards)):
            self.own(h).start()

    def advance(self, hop):
        for h in range(len(self.shards)):
            for side in (1, 0):

                @pl.when(self.holds(hop, side))
                def _(side=side):
                    c = self.c - hop if side else self.c + hop
                    self.along(c, h, hop, side).wait_recv()

                    @pl.when(self.can(side))
                    def _():
                        self.along(c, h, hop + 1, side).start()

                    for step in range(1, self.f_size):
                        self.over(c, h, step).start()

    def end(self):
        for h in range(len(self.shards)):
            self.own(h).wait()
            for step in range(1, self.f_size):
                for c in range(self.c_size):
                    self.over_arrival(c, h, step).wait_recv()
                    self.over(c, h, step).wait_send()
            for side in (1, 0):

                @pl.when(self.can(side))
                def _(side=side):
                    self.along(self.c, h, 1, side, True).wait_send()

                for hop in range(1, self.c_size):

                    @pl.when(self.holds(hop, side) & self.can(side))
                    def _(side=side, hop=hop):
                        c = self.c - hop if side else self.c + hop
                        self.along(c, h, hop + 1, side).wait_send()


def weight_sems(f_size, c_size, parts):
    dma = pltpu.SemaphoreType.DMA
    return [dma((2, c_size + 1, parts))] * 2 + [dma((f_size, c_size, parts))] * 2 + [dma((parts,))]


class WeightSum:
    def __init__(self, part, first_column, out, refs):
        self.part, self.out, self.first = part, out, first_column
        self.stage, self.total, self.along_in = refs[:3]
        self.own_sem, self.over_send, self.over_recv, self.along_send, self.along_recv = refs[3:]
        self.f_size, self.c_size = lax.axis_size("fsdp"), lax.axis_size("ctx")
        self.f, self.c = lax.axis_index("fsdp"), lax.axis_index("ctx")
        self.rows, self.wide = out.shape[0], out.shape[1] // HALVES
        ends = [(self.c_size - 1 - i // 2) if i % 2 == 0 else i // 2 for i in range(self.c_size)]
        self.order = [(c, h) for c in ends for h in range(HALVES)]
        self.stages = len(self.order) + self.c_size - 1

    def piece(self, f, c, h):
        row = (f * self.c_size + c) * self.rows
        columns = pl.ds(self.first + h * self.wide, self.wide)
        return self.part.at[pl.ds(pl.multiple_of(row, self.rows), self.rows), columns]

    def own(self, c, h):
        n = c * HALVES + h
        return pltpu.make_async_copy(self.piece(self.f, c, h), self.stage.at[n], self.own_sem.at[n])

    def over(self, c, h, step):
        f, n = lax.rem(self.f + step, self.f_size), c * HALVES + h
        return moving(
            self.piece(f, c, h),
            self.total.at[step - 1, n],
            self.over_send.at[step - 1, n],
            self.over_recv.at[step - 1, n],
            {"fsdp": f},
        )

    def along(self, c, h, side, source=None):
        peer, n = {"ctx": self.c + (1 if side else -1)}, c * HALVES + h
        target = self.along_in.at[side, n]
        return moving(
            target if source is None else source,
            target,
            self.along_send.at[side, n],
            self.along_recv.at[side, n],
            peer,
        )

    def begin(self):
        for c, h in self.order:
            for step in range(1, self.f_size):
                self.over(c, h, step).start()
        for c, h in self.order:
            self.own(c, h).start()

    def receive(self, i):
        c, h = self.order[i]
        n = c * HALVES + h
        self.own(c, h).wait()
        value = self.stage[n].astype(F32)
        for step in range(1, self.f_size):
            self.over(c, h, step).wait_recv()
        for step in range(1, self.f_size):
            value = value + self.total[step - 1, n].astype(F32)
        self.total[0, n] = value.astype(BF16)
        for side, end in ((1, 0), (0, self.c_size - 1)):
            if c != end:

                @pl.when(self.c == end)
                def _(side=side):
                    self.along(c, h, side, self.total.at[0, n]).start()

    def hop(self, c, h, side, device):
        n = c * HALVES + h

        @pl.when(self.c == device)
        def _():
            self.along(c, h, side).wait_recv()
            value = self.total[0, n].astype(F32) + self.along_in[side, n].astype(F32)
            if device == c:
                self.total[0, n] = value.astype(BF16)
            else:
                self.along_in[side, n] = value.astype(BF16)
                self.along(c, h, side).start()

    def run(self, n):
        if n < len(self.order):
            self.receive(n)
        for i, (c, h) in enumerate(self.order):
            if 1 <= n - i <= c:
                self.hop(c, h, 1, n - i)
            if 1 <= n - i <= self.c_size - 1 - c:
                self.hop(c, h, 0, self.c_size - 1 - (n - i))

    def run_to(self, first, last):
        for n in range(min(first, self.stages), min(last, self.stages)):
            self.run(n)

    def run_share(self, turn, turns):
        share = -(-self.stages // turns)
        self.run_to(turn * share, (turn + 1) * share)

    def end(self):
        for c in range(self.c_size):

            @pl.when(self.c == c)
            def _(c=c):
                for h in range(HALVES):
                    columns = pl.ds(h * self.wide, self.wide)
                    self.out[:, columns] = self.total[0, c * HALVES + h].astype(F32)

        for c, h in self.order:
            for step in range(1, self.f_size):
                self.over(c, h, step).wait_send()
            for side in (1, 0):

                @pl.when(self.c < c if side else self.c > c)
                def _(side=side):
                    self.along(c, h, side).wait_send()


def sum_scratch(f_size, c_size, rows, columns):
    dma, count, wide = pltpu.SemaphoreType.DMA, c_size * HALVES, columns // HALVES
    return (
        [
            pltpu.VMEM((count, rows, wide), BF16),
            pltpu.VMEM((f_size - 1, count, rows, wide), BF16),
            pltpu.VMEM((2, count, rows, wide), BF16),
        ]
        + [dma((count,))]
        + [dma((f_size - 1, count))] * 2
        + [dma((2, count))] * 2
    )


class Fetch:
    def __init__(self, pairs, sem):
        self.copies = [
            pltpu.make_async_copy(source, target, sem.at[n]) for n, (source, target) in enumerate(pairs)
        ]
        for copy in self.copies:
            copy.start()

    def wait(self):
        for copy in self.copies:
            copy.wait()


class RowGather:
    def __init__(self, rows, table, sems):
        self.rows, self.table, self.sems = rows, table, sems
        _, self.sibling, self.across, _ = tp_places()

    def own(self):
        return pltpu.make_async_copy(self.rows, self.table.at[0], self.sems[2])

    def copy(self, n):
        source = self.table.at[2] if n == 2 else self.rows
        peer = {"tp": self.across if n == 1 else self.sibling}
        return moving(source, self.table.at[n + 1], self.sems[0].at[n], self.sems[1].at[n], peer)

    def begin(self):
        self.copy(1).start()
        self.copy(0).start()
        self.own().start()

    def advance(self):
        self.copy(1).wait_recv()
        self.copy(2).start()

    def end(self):
        self.own().wait()
        self.copy(0).wait()
        self.copy(1).wait_send()
        self.copy(2).wait()


class RowSum:
    def __init__(self, table, out, refs):
        self.table, self.out = table, out
        self.mine, self.near, self.far_out, self.far_in, self.send, self.recv, self.own_sem = refs
        _, self.sibling, self.across, _ = tp_places()

    def own(self, n):
        return pltpu.make_async_copy(self.table.at[0 if n else 2], self.mine.at[n], self.own_sem.at[n])

    def copy(self, n):
        if n == 2:
            source, target, peer = self.far_out, self.far_in, self.across
        else:
            source, target, peer = self.table.at[1 if n else 3], self.near.at[n], self.sibling
        return moving(source, target, self.send.at[n], self.recv.at[n], {"tp": peer})

    def begin(self):
        for n in range(2):
            self.copy(n).start()
        for n in range(2):
            self.own(n).start()

    def advance(self):
        self.own(0).wait()
        self.copy(0).wait_recv()
        self.far_out[...] = (self.mine[0].astype(F32) + self.near[0].astype(F32)).astype(BF16)
        self.copy(2).start()

    def end(self):
        self.own(1).wait()
        self.copy(1).wait_recv()
        self.copy(2).wait_recv()
        total = self.mine[1].astype(F32) + self.near[1].astype(F32)
        self.out[...] = (total + self.far_in[...].astype(F32)).astype(BF16)
        for n in range(3):
            self.copy(n).wait_send()


def row_sum_scratch(rows, width):
    dma, pair, one = pltpu.SemaphoreType.DMA, (2, rows, width), (rows, width)
    return [pltpu.VMEM(pair, BF16)] * 2 + [pltpu.VMEM(one, BF16)] * 2 + [dma((3,))] * 2 + [dma((2,))]


def startup_kernel(parts, rows_ref, gain_ref, *refs):
    shards, (all_ref, full_ref, gains_ref, own_sem) = refs[:parts], refs[parts : parts + 4]
    sems = refs[parts + 4 :]
    me, sibling, across, diagonal = tp_places()
    others = group_peers()
    greet_all([{"tp": sibling}, {"tp": across}] + others)
    near_send, near_recv, far_send, far_recv, pass_send, pass_recv = sems[:6]
    gather = WeightGather(shards, full_ref, sems[6:11])
    gain_send, gain_recv, gain_own = sems[11:]
    spot = gains_ref.at[gather.f * gather.c_size + gather.c]
    gain_copies = [
        moving(gain_ref, spot, gain_send.at[n], gain_recv.at[n], peer) for n, peer in enumerate(others)
    ]
    own_gain = pltpu.make_async_copy(gain_ref, spot, gain_own)
    size = rows_ref.shape[0] // CHUNKS
    own = pltpu.make_async_copy(rows_ref, all_ref.at[me], own_sem)

    def span(chunk):
        return pl.ds(chunk * size, size)

    def far(chunk):
        return sending(
            rows_ref.at[span(chunk)],
            all_ref.at[me, span(chunk)],
            far_send.at[chunk],
            far_recv.at[chunk],
            across,
        )

    def passing(chunk):
        spot = all_ref.at[across, span(chunk)]
        return sending(spot, spot, pass_send.at[chunk], pass_recv.at[chunk], sibling)

    gather.begin()
    far(0).start()
    for copy in gain_copies:
        copy.start()
    own_gain.start()
    near = sending(rows_ref, all_ref.at[me], near_send, near_recv, sibling)
    near.start()
    own.start()
    for turn in range(max(CHUNKS, gather.c_size - 1)):
        if turn < CHUNKS:
            far(turn).wait_recv()
            if turn + 1 < CHUNKS:
                far(turn + 1).start()
            passing(turn).start()
        if turn + 1 < gather.c_size:
            gather.advance(turn + 1)
    near.wait()
    for chunk in range(CHUNKS):
        far(chunk).wait_send()
        passing(chunk).wait()
    own.wait()
    gather.end()
    for copy in gain_copies:
        copy.wait()
    own_gain.wait()


def startup(rows, gains, shards, f_size, c_size, ident):
    place = pl.BlockSpec(memory_space=pl.ANY)
    full = (shards[0].shape[0] * f_size * c_size, sum(shard.shape[1] for shard in shards))
    return pl.pallas_call(
        functools.partial(startup_kernel, len(shards)),
        out_shape=[
            jax.ShapeDtypeStruct((4,) + rows.shape, BF16),
            jax.ShapeDtypeStruct(full, BF16),
            jax.ShapeDtypeStruct((f_size * c_size,) + gains.shape, F32),
        ],
        in_specs=[pl.BlockSpec(memory_space=pltpu.VMEM)] * (2 + len(shards)),
        out_specs=[place] * 3,
        scratch_shapes=[pltpu.SemaphoreType.DMA]
        + GATHER_SEMS
        + weight_sems(f_size, c_size, len(shards))
        + [pltpu.SemaphoreType.DMA((f_size * c_size - 1,))] * 2
        + [pltpu.SemaphoreType.DMA],
        compiler_params=pltpu.CompilerParams(
            collective_id=ident, has_side_effects=True, vmem_limit_bytes=32 << 20
        ),
        name="startup",
    )(rows, gains, *shards)


def whole(shape, column=None):
    zeros = (0,) * (len(shape) - 1)
    return pl.BlockSpec(shape, lambda i: zeros + (column or 0,), pipeline_mode=pl.Buffered(1))


def remote_params(ident, megabytes):
    return pltpu.CompilerParams(
        collective_id=ident, has_side_effects=True, vmem_limit_bytes=megabytes << 20, dimension_semantics=("arbitrary",)
    )


def project_kernel(layout, x_ref, gain_ref, w_ref, normed_ref, forget_ref, items_ref):
    seq_count, groups, width, places = layout
    x = x_ref[0].astype(F32)
    normed = (x * lax.rsqrt(jnp.mean(x * x, axis=1, keepdims=True) + epsilon) * gain_ref[...]).astype(BF16)
    normed_ref[0] = normed
    inner = groups * width
    rows = x.shape[0] // seq_count
    count = items_ref.shape[0]
    for kind in range(3):
        value = dot(normed, w_ref[:, kind * inner : (kind + 1) * inner], NN).astype(BF16)
        for slot, (s, g) in enumerate(places):
            piece = value[s * rows : (s + 1) * rows, g * width : (g + 1) * width]
            items_ref[slot % count, slot // count, kind] = piece
    forget_ref[0] = dot(normed, w_ref[:, 3 * inner :], NN)


def project(x_all, gain, full_one, layout, item_count, ctx_size):
    seq_count, groups, width, places = layout
    tp_size, rows, model_width = x_all.shape
    local = rows // seq_count
    item = jax.ShapeDtypeStruct((item_count, ctx_size, 3, tp_size * local, width), BF16)
    columns = full_one.shape[1]
    block = pl.BlockSpec((1, rows, model_width), lambda t: (t, 0, 0))
    return pl.pallas_call(
        functools.partial(project_kernel, layout),
        grid=(tp_size,),
        out_shape=[
            jax.ShapeDtypeStruct(x_all.shape, BF16),
            jax.ShapeDtypeStruct((tp_size, rows, LANES), F32),
            item,
        ],
        in_specs=[
            block,
            pl.BlockSpec((1, model_width), lambda t: (0, 0)),
            pl.BlockSpec((model_width, columns), lambda t: (0, 0), pipeline_mode=pl.Buffered(1)),
        ],
        out_specs=[
            block,
            pl.BlockSpec((1, rows, LANES), lambda t: (t, 0, 0)),
            pl.BlockSpec((item_count, ctx_size, 3, local, width), lambda t: (0, 0, 0, t, 0)),
        ],
        compiler_params=pltpu.CompilerParams(vmem_limit_bytes=48 << 20, dimension_semantics=("arbitrary",)),
        cost_estimate=pl.CostEstimate(
            flops=2 * x_all.size * columns, bytes_accessed=4 * x_all.size, transcendentals=0
        ),
        name="project",
    )(x_all, gain, full_one)


def out_kernel(layout, x_ref, gate_ref, w_ref, gain_ref, items, shard_ref, *refs):
    seq_count, groups, width, places = layout
    hidden_ref, normed_ref, attended_ref, mixed_ref, full_ref = refs[:5]
    buffers, sems = refs[5:9], refs[9:13]
    count = items.shape[0]
    me, sibling, across, diagonal = tp_places()
    greet_all([{"tp": sibling}, {"tp": across}] + group_peers())
    gather = WeightGather((shard_ref,), full_ref, refs[13:])
    gather.begin()
    tp_size, rows, _ = gate_ref.shape
    local = rows // seq_count

    def mix(t, _):
        here = pl.ds(pl.multiple_of(t * local, local), local)
        for slot, (s, g) in enumerate(places[: seq_count * groups]):
            there = (t, pl.ds(s * local, local), pl.ds(g * width, width))
            value = items[slot % count, slot // count, here]
            attended_ref[there] = value
            mixed_ref[there] = (value.astype(F32) * gate_ref[there]).astype(BF16)
        return 0

    lax.fori_loop(0, tp_size, mix, 0)
    size = rows // CHUNKS

    def span(chunk):
        return pl.ds(pl.multiple_of(chunk * size, size), size)

    def partial(slot, chunk):
        return dot(mixed_ref[slot, span(chunk)], w_ref[...], NT)

    def finish(chunk, total):
        hidden = x_ref[span(chunk)].astype(F32) + total
        hidden_ref[span(chunk)] = hidden
        inverse = lax.rsqrt(jnp.mean(hidden * hidden, axis=1, keepdims=True) + epsilon)
        normed_ref[span(chunk)] = (hidden * inverse * gain_ref[...]).astype(BF16)

    def between(phase):
        if phase < 3:
            gather.advance(phase)
        else:
            for hop in range(3, gather.c_size):
                gather.advance(hop)

    scatter_loop(buffers, sems, partial, finish, between=between)
    gather.end()


def out_project(x, gate, full_out, gain, items, shard, layout, f_size, c_size, ident):
    seq_count, groups, width, places = layout
    rows, model_width = x.shape
    inner = groups * width
    tp_size = gate.shape[0]
    return pl.pallas_call(
        functools.partial(out_kernel, layout),
        grid=(1,),
        out_shape=[
            jax.ShapeDtypeStruct(x.shape, F32),
            jax.ShapeDtypeStruct(x.shape, BF16),
            jax.ShapeDtypeStruct(gate.shape, BF16),
            jax.ShapeDtypeStruct(gate.shape, BF16),
            jax.ShapeDtypeStruct((model_width, shard.shape[1]), BF16),
        ],
        in_specs=[
            whole(x.shape),
            whole(gate.shape),
            whole((model_width, inner), 0),
            whole(gain.shape),
            whole(items.shape),
            whole(shard.shape),
        ],
        out_specs=[
            whole(x.shape),
            whole(x.shape),
            whole(gate.shape),
            whole(gate.shape),
            pl.BlockSpec(memory_space=pl.ANY),
        ],
        scratch_shapes=scatter_buffers(rows, model_width)
        + SCATTER_SEMS
        + weight_sems(f_size, c_size, 1),
        compiler_params=remote_params(ident, 48),
        cost_estimate=pl.CostEstimate(
            flops=2 * gate.size * model_width, bytes_accessed=100 << 20, transcendentals=0
        ),
        name="out_project",
    )(x, gate, full_out, gain, items, shard)


def mlp_kernel(
    normed_ref, grad_hbm, gate_hbm, down_hbm, all_ref, inner_hbm, pair_hbm, table, inner_ref, pair_ref, *refs
):
    grad_ref, both_w, down_w, fetch_sem, out_sem = refs[:5]
    sems = refs[5:]
    fetch = Fetch([(gate_hbm, both_w), (grad_hbm, grad_ref), (down_hbm, down_w)], fetch_sem)
    me, sibling, across, diagonal = tp_places()
    greet((sibling, across))
    table[0] = normed_ref[...]
    rows, hidden = table.shape[1] // CHUNKS, down_w.shape[1]
    tile = min(hidden, 512)

    def writing(n, slot, chunk):
        here = (slot, pl.ds(pl.multiple_of(chunk * rows, rows), rows))
        source, target = ((inner_ref, inner_hbm), (pair_ref, pair_hbm), (table, all_ref))[n]
        return pltpu.make_async_copy(source.at[here], target.at[here], out_sem.at[n, slot, chunk])

    def compute(slot, chunk):
        spot = pl.ds(pl.multiple_of(chunk * rows, rows), rows)
        normed, grad = table[slot, spot], grad_ref[slot, spot]
        for start in range(0, hidden, tile):
            columns = pl.ds(start, tile)
            gate = dot(normed, both_w[:, columns], NN)
            up = dot(normed, both_w[:, pl.ds(hidden + start, tile)], NN)
            back = dot(grad, down_w[:, columns], NN)
            sig = 1.0 / (1.0 + jnp.exp(-gate))
            silu = gate * sig
            inner_ref[slot, spot, columns] = (silu * up).astype(BF16)
            pair_ref[slot, spot, columns] = (back * up * sig * (1.0 + gate * (1.0 - sig))).astype(BF16)
            pair_ref[slot, spot, pl.ds(hidden + start, tile)] = (back * silu).astype(BF16)
        for n in range(3):
            writing(n, slot, chunk).start()

    gather_loop(table, sems, compute, relative=True, ready=fetch.wait)
    for n in range(3):

        @pl.loop(0, 4 * CHUNKS)
        def _(step):
            writing(n, step // CHUNKS, lax.rem(step, CHUNKS)).wait()


def mlp(normed, grad_all, full_two, full_down, hidden, ident):
    tp_size, rows, model_width = grad_all.shape
    total = tp_size * rows
    place = pl.BlockSpec(memory_space=pl.ANY)
    inner, pair = (tp_size, rows, hidden), (tp_size, rows, 2 * hidden)
    dma = pltpu.SemaphoreType.DMA
    return pl.pallas_call(
        mlp_kernel,
        grid=(1,),
        out_shape=[
            jax.ShapeDtypeStruct(grad_all.shape, BF16),
            jax.ShapeDtypeStruct(inner, BF16),
            jax.ShapeDtypeStruct(pair, BF16),
        ],
        in_specs=[whole(normed.shape), place, place, place],
        out_specs=[place] * 3,
        scratch_shapes=[
            pltpu.VMEM(grad_all.shape, BF16),
            pltpu.VMEM(inner, BF16),
            pltpu.VMEM(pair, BF16),
            pltpu.VMEM(grad_all.shape, BF16),
            pltpu.VMEM((model_width, 2 * hidden), BF16),
            pltpu.VMEM((model_width, hidden), BF16),
            dma((3,)),
            dma((3, tp_size, CHUNKS)),
        ]
        + GATHER_SEMS,
        compiler_params=remote_params(ident, 56),
        cost_estimate=pl.CostEstimate(
            flops=6 * total * model_width * hidden, bytes_accessed=100 << 20, transcendentals=total * hidden
        ),
        name="mlp",
    )(normed, grad_all, full_two, full_down)


def mlp_back_kernel(
    pair_hbm, w_hbm, hidden_hbm, grad_hbm, gain_ref, sums_ref, out_ref, branch_ref, part_ref, sum_ref, *refs
):
    buffers, sems = refs[:4], refs[4:8]
    pair_ref, w_ref, hidden_ref, grad_ref, fetch_sem = refs[8:13]
    columns = pl.ds(0, w_ref.shape[1])
    fetch = Fetch(
        [
            (pair_hbm, pair_ref),
            (w_hbm.at[:, columns], w_ref),
            (hidden_hbm, hidden_ref),
            (grad_hbm, grad_ref),
        ],
        fetch_sem,
    )
    me, sibling, across, diagonal = tp_places()
    greet_all([{"tp": sibling}, {"tp": across}] + group_peers())
    weights = WeightSum(sums_ref, 0, sum_ref, refs[13:])
    weights.begin()
    fetch.wait()
    part_ref[...] = jnp.zeros_like(part_ref)
    size = hidden_ref.shape[0] // CHUNKS

    def span(chunk):
        return pl.ds(pl.multiple_of(chunk * size, size), size)

    def partial(slot, chunk):
        return dot(pair_ref[slot, span(chunk)], w_ref[...], NT)

    def finish(chunk, total):
        hidden = hidden_ref[span(chunk)]
        inverse = lax.rsqrt(jnp.mean(hidden * hidden, axis=1, keepdims=True) + epsilon)
        unit = hidden * inverse
        part_ref[...] += jnp.sum(total * unit, axis=0, keepdims=True)
        scaled = total * gain_ref[...]
        middle = jnp.mean(scaled * unit, axis=1, keepdims=True)
        grad = grad_ref[span(chunk)].astype(F32) + inverse * (scaled - unit * middle)
        out_ref[span(chunk)] = grad
        branch_ref[span(chunk)] = grad.astype(BF16)

    def between(phase):
        if phase < 3:
            weights.run_to(2 * phase - 2, 2 * phase)
        else:
            weights.run_to(4, weights.stages)

    scatter_loop(buffers, sems, partial, finish, relative=True, between=between)
    weights.end()


def mlp_back(pair, full_two, hidden_state, grad_out, gain, part, f_size, c_size, ident):
    tp_size, rows, wide = pair.shape
    model_width = hidden_state.shape[1]
    place = pl.BlockSpec(memory_space=pl.ANY)
    total = (part.shape[0] // (f_size * c_size), part.shape[1] // 2)
    return pl.pallas_call(
        mlp_back_kernel,
        grid=(1,),
        out_shape=[
            jax.ShapeDtypeStruct(hidden_state.shape, F32),
            jax.ShapeDtypeStruct(hidden_state.shape, BF16),
            jax.ShapeDtypeStruct(gain.shape, F32),
            jax.ShapeDtypeStruct(total, F32),
        ],
        in_specs=[
            place,
            place,
            place,
            place,
            whole(gain.shape),
            place,
        ],
        out_specs=[
            whole(hidden_state.shape),
            whole(hidden_state.shape),
            whole(gain.shape),
            whole(total),
        ],
        scratch_shapes=scatter_buffers(rows, model_width)
        + SCATTER_SEMS
        + [
            pltpu.VMEM(pair.shape, BF16),
            pltpu.VMEM((model_width, wide), BF16),
            pltpu.VMEM(hidden_state.shape, F32),
            pltpu.VMEM(grad_out.shape, BF16),
            pltpu.SemaphoreType.DMA((4,)),
        ]
        + sum_scratch(f_size, c_size, *total),
        compiler_params=remote_params(ident, 60),
        cost_estimate=pl.CostEstimate(
            flops=2 * pair.size * model_width, bytes_accessed=100 << 20, transcendentals=0
        ),
        name="mlp_back",
    )(pair, full_two, hidden_state, grad_out, gain, part)


def out_back_kernel(
    layout,
    branch_ref,
    w_ref,
    gate_ref,
    attended_ref,
    sums_ref,
    inner_hbm,
    down_hbm,
    grad_hbm,
    all_ref,
    logit_ref,
    items,
    sum_ref,
    forward_hbm,
    part_hbm,
    *refs,
):
    seq_count, groups, width, places = layout
    table, grads, own_sem = refs[:3]
    sems = refs[3:9]
    inner_ref, down_w, grad_ref, forward, part, fetch_sem, write_sem = refs[9:16]
    count = items.shape[0]
    me, sibling, across, diagonal = tp_places()
    greet_all([{"tp": sibling}, {"tp": across}] + group_peers())
    weights = WeightSum(sums_ref, sum_ref.shape[1], sum_ref, refs[16:])
    weights.begin()
    table[me] = branch_ref[...]
    tp_size, rows, _ = gate_ref.shape
    local, size = rows // seq_count, rows // CHUNKS
    model_width, hidden = part.shape
    tile = 2 * LANES
    steps, tiles = 4 * CHUNKS, model_width // tile
    fetches = []

    def begin_fetch():
        fetches.append(
            Fetch([(inner_hbm, inner_ref), (down_hbm, down_w), (grad_hbm, grad_ref)], fetch_sem)
        )

    def compute(slot, chunk):
        spot = pl.ds(pl.multiple_of(chunk * size, size), size)
        mixed = dot(table[slot, spot], w_ref[...], NN)
        gate = gate_ref[slot, spot]
        scaled = mixed * gate
        grads[slot, spot] = scaled.astype(BF16)
        attended = attended_ref[slot, spot].astype(F32)
        logit_ref[slot, spot] = (scaled * attended * (1.0 - gate)).astype(BF16)

    def project_down(step, _):
        slot, chunk = step // CHUNKS, lax.rem(step, CHUNKS)
        spot = pl.ds(pl.multiple_of(chunk * size, size), size)
        forward[slot, spot] = dot(inner_ref[slot, spot], down_w[...], NT).astype(BF16)
        return 0

    def down_grad(n, _):
        columns = pl.ds(pl.multiple_of(n * tile, tile), tile)
        left = grad_ref[:, :, columns].reshape(tp_size * rows, tile)
        right = inner_ref[...].reshape(tp_size * rows, hidden)
        part[columns] = dot(left, right, TN).astype(BF16)
        return 0

    last = weights.stages
    middle = max(1, last - 4)

    def stage(n):
        weights.run(n)
        lax.fori_loop(n * steps // last, (n + 1) * steps // last, project_down, 0)
        lax.fori_loop(n * tiles // last, (n + 1) * tiles // last, down_grad, 0)

    def between():
        fetches[0].wait()
        for n in range(middle):
            stage(n)

    gather_loop(table, sems, compute, between=between, ready=begin_fetch)
    copies = [
        pltpu.make_async_copy(table, all_ref, own_sem),
        pltpu.make_async_copy(forward, forward_hbm, write_sem.at[0]),
        pltpu.make_async_copy(part, part_hbm, write_sem.at[1]),
    ]
    copies[0].start()

    def deal(t, _):
        here = pl.ds(pl.multiple_of(t * local, local), local)
        for slot, (s, g) in enumerate(places):
            piece = grads[t, pl.ds(s * local, local), pl.ds(g * width, width)]
            items[slot % count, slot // count, here] = piece
        return 0

    lax.fori_loop(0, tp_size, deal, 0)
    for n in range(middle, last):
        stage(n)
    for copy in copies[1:]:
        copy.start()
    for copy in copies:
        copy.wait()
    weights.end()


def out_back(
    branch, full_out, gate, attended, part, inner_act, down_w, grad_all, layout, item_count, f_size, ctx_size, ident
):
    seq_count, groups, width, places = layout
    rows, model_width = branch.shape
    tp_size, _, inner = gate.shape
    item = (item_count, ctx_size, tp_size * rows // seq_count, width)
    table = (tp_size, rows, model_width)
    total = (part.shape[0] // (f_size * ctx_size), part.shape[1] // 2)
    place = pl.BlockSpec(memory_space=pl.ANY)
    dma = pltpu.SemaphoreType.DMA
    return pl.pallas_call(
        functools.partial(out_back_kernel, layout),
        grid=(1,),
        out_shape=[
            jax.ShapeDtypeStruct(table, BF16),
            jax.ShapeDtypeStruct(gate.shape, BF16),
            jax.ShapeDtypeStruct(item, BF16),
            jax.ShapeDtypeStruct(total, F32),
            jax.ShapeDtypeStruct(table, BF16),
            jax.ShapeDtypeStruct(down_w.shape, BF16),
        ],
        in_specs=[
            whole(branch.shape),
            whole((model_width, inner), 0),
            whole(gate.shape),
            whole(attended.shape),
            place,
            place,
            place,
            place,
        ],
        out_specs=[place, whole(gate.shape), whole(item), whole(total), place, place],
        scratch_shapes=[pltpu.VMEM(table, BF16), pltpu.VMEM(gate.shape, BF16), dma]
        + GATHER_SEMS
        + [
            pltpu.VMEM(inner_act.shape, BF16),
            pltpu.VMEM(down_w.shape, BF16),
            pltpu.VMEM(table, BF16),
            pltpu.VMEM(table, BF16),
            pltpu.VMEM(down_w.shape, BF16),
            dma((3,)),
            dma((2,)),
        ]
        + sum_scratch(f_size, ctx_size, *total),
        compiler_params=remote_params(ident, 60),
        cost_estimate=pl.CostEstimate(
            flops=2 * gate.size * model_width, bytes_accessed=100 << 20, transcendentals=0
        ),
        name="out_back",
    )(branch, full_out, gate, attended, part, inner_act, down_w, grad_all)


def assemble_kernel(layout, items, out_ref):
    seq_count, groups, width, places = layout
    count, local = items.shape[0], items.shape[3]
    inner = groups * width
    for slot, (s, g) in enumerate(places[: seq_count * groups]):
        for kind in range(3):
            columns = pl.ds(kind * inner + g * width, width)
            out_ref[0, pl.ds(s * local, local), columns] = items[slot % count, slot // count, kind]


def assemble(items, layout, tp_size):
    seq_count, groups, width, places = layout
    count, ctx_size, kinds, ctx_rows, _ = items.shape
    local = ctx_rows // tp_size
    shape = (tp_size, seq_count * local, kinds * groups * width)
    return pl.pallas_call(
        functools.partial(assemble_kernel, layout),
        grid=(tp_size,),
        out_shape=jax.ShapeDtypeStruct(shape, BF16),
        in_specs=[pl.BlockSpec((count, ctx_size, kinds, local, width), lambda t: (0, 0, 0, t, 0))],
        out_specs=pl.BlockSpec((1,) + shape[1:], lambda t: (t, 0, 0)),
        compiler_params=pltpu.CompilerParams(vmem_limit_bytes=32 << 20, dimension_semantics=("arbitrary",)),
        cost_estimate=pl.CostEstimate(flops=0, bytes_accessed=16 << 20, transcendentals=0),
        name="assemble",
    )(items)


def last_kernel(
    qkv_hbm,
    logit_hbm,
    forget_hbm,
    qkv_w_hbm,
    gate_w_hbm,
    x_hbm,
    grad_hbm,
    gain_ref,
    part_ref,
    extra_ref,
    out_ref,
    sum_ref,
    vector_ref,
    *refs,
):
    buffers, sems, (mine, near_in, group_in) = refs[:4], refs[4:8], refs[8:11]
    vector_sems = refs[11:15]
    qkv_ref, logit_ref, forget_ref, qkv_w, gate_w, x_ref, grad_ref, fetch_sem = refs[15:23]
    inner = gate_w.shape[1]
    fetch = Fetch(
        [
            (qkv_hbm, qkv_ref),
            (qkv_w_hbm, qkv_w),
            (logit_hbm, logit_ref),
            (forget_hbm, forget_ref),
            (gate_w_hbm.at[:, pl.ds(inner, inner)], gate_w),
            (x_hbm, x_ref),
            (grad_hbm, grad_ref),
        ],
        fetch_sem,
    )
    me, sibling, across, diagonal = tp_places()
    others = group_peers()
    greet_all([{"tp": sibling}, {"tp": across}, {"tp": diagonal}] + others)
    weights = WeightSum(part_ref, 0, sum_ref, refs[23:])
    weights.begin()
    fetch.wait()
    wide = qkv_ref.shape[2]
    mine[...] = extra_ref[...]
    size = x_ref.shape[0] // CHUNKS

    def span(chunk):
        return pl.ds(pl.multiple_of(chunk * size, size), size)

    def partial(slot, chunk):
        value = dot(qkv_ref[slot, span(chunk)], qkv_w[:, :wide], NT)
        value = value + dot(logit_ref[slot, span(chunk)], gate_w[...], NT)
        return value + dot(forget_ref[slot, span(chunk)], qkv_w[:, wide:], NT)

    def finish(chunk, total):
        x = x_ref[span(chunk)].astype(F32)
        inverse = lax.rsqrt(jnp.mean(x * x, axis=1, keepdims=True) + epsilon)
        unit = x * inverse
        mine[0:1] += jnp.sum(total * unit, axis=0, keepdims=True)
        scaled = total * gain_ref[...]
        middle = jnp.mean(scaled * unit, axis=1, keepdims=True)
        out_ref[span(chunk)] = (grad_ref[span(chunk)] + inverse * (scaled - unit * middle)).astype(BF16)

    stages = weights.stages
    late = max(4, stages - 4)

    def between(phase):
        if phase < 3:
            weights.run_to(2 * phase - 2, 2 * phase)
        else:
            weights.run_to(4, late)

    scatter_loop(buffers, sems, partial, finish, between=between)
    near_send, near_recv, group_send, group_recv = vector_sems
    copies = []
    for n, peer in enumerate((sibling, across, diagonal)):
        copies.append(sending(mine, near_in.at[n], near_send.at[n], near_recv.at[n], peer))
        copies[-1].start()
    weights.run_to(late, late + 2)
    for copy in copies:
        copy.wait()
    vector_ref[...] = mine[...] + near_in[0] + near_in[1] + near_in[2]
    mine[...] = vector_ref[...]
    copies = []
    for n, peer in enumerate(others):
        copies.append(moving(mine, group_in.at[n], group_send.at[n], group_recv.at[n], peer))
        copies[-1].start()
    weights.run_to(late + 2, stages)
    for n, copy in enumerate(copies):
        copy.wait()
        vector_ref[...] += group_in[n]
    weights.end()


def last(grad_qkv, grad_logit, grad_forget, full_one, full_out, x, grad_hidden, gain, part, extra, f_size, c_size, ident):
    rows, model_width = x.shape
    wide, inner = grad_qkv.shape[2], grad_logit.shape[2]
    shard, columns = part.shape[0] // (f_size * c_size), part.shape[1]
    dma = pltpu.SemaphoreType.DMA
    place = pl.BlockSpec(memory_space=pl.ANY)
    return pl.pallas_call(
        last_kernel,
        grid=(1,),
        out_shape=[
            jax.ShapeDtypeStruct(x.shape, BF16),
            jax.ShapeDtypeStruct((shard, columns), F32),
            jax.ShapeDtypeStruct(extra.shape, F32),
        ],
        in_specs=[
            place,
            place,
            place,
            place,
            place,
            place,
            place,
            whole(gain.shape),
            place,
            whole(extra.shape),
        ],
        out_specs=[whole(x.shape), whole((shard, columns)), whole(extra.shape)],
        scratch_shapes=scatter_buffers(rows, model_width)
        + SCATTER_SEMS
        + [
            pltpu.VMEM(extra.shape, F32),
            pltpu.VMEM((3,) + extra.shape, F32),
            pltpu.VMEM((f_size * c_size - 1,) + extra.shape, F32),
        ]
        + [dma((3,))] * 2
        + [dma((f_size * c_size - 1,))] * 2
        + [
            pltpu.VMEM(grad_qkv.shape, BF16),
            pltpu.VMEM(grad_logit.shape, BF16),
            pltpu.VMEM(grad_forget.shape, BF16),
            pltpu.VMEM(full_one.shape, BF16),
            pltpu.VMEM((model_width, inner), BF16),
            pltpu.VMEM(x.shape, BF16),
            pltpu.VMEM(x.shape, F32),
            dma((7,)),
        ]
        + sum_scratch(f_size, c_size, shard, columns),
        compiler_params=remote_params(ident, 60),
        cost_estimate=pl.CostEstimate(
            flops=8 * rows * model_width * (wide + inner + LANES), bytes_accessed=100 << 20, transcendentals=0
        ),
        name="last",
    )(grad_qkv, grad_logit, grad_forget, full_one, full_out, x, grad_hidden, gain, part, extra)


def per_device(
    layer_input,
    lengths,
    attn_gain,
    w_query,
    w_key,
    w_value,
    w_forget,
    forget_bias,
    w_gate_out,
    w_out,
    mlp_gain,
    w_gate,
    w_up,
    w_down,
    cotangent,
):
    local_rows, seq_count, model_width = layer_input.shape
    head_count = forget_bias.shape[0]
    inner_width = w_query.shape[1]
    hidden = w_gate.shape[1]
    head_size = inner_width // head_count
    tp_size = lax.axis_size("tp")
    ctx_size = lax.axis_size("ctx")
    shard_count = lax.axis_size("fsdp") * ctx_size
    ctx_rows = local_rows * tp_size
    seq_len = ctx_rows * ctx_size
    all_rows = seq_count * ctx_rows
    ctx_index = lax.axis_index("ctx")
    tp_index = lax.axis_index("tp")
    shard_index = lax.axis_index("fsdp") * ctx_size + ctx_index

    pair = LANES // head_size
    groups = head_count // pair
    width = pair * head_size
    item_count = pl.cdiv(seq_count * groups, ctx_size)
    used = seq_count * groups

    def place(slot):
        slot = slot % used
        return (slot // groups + slot % groups) % seq_count, slot % groups

    places = tuple(place(slot) for slot in range(ctx_size * item_count))
    layout = (seq_count, groups, width, places)

    fsdp_size = lax.axis_size("fsdp")
    wide_forget = jnp.pad(w_forget, ((0, 0), (0, LANES - head_count)))
    edge = 3 * inner_width
    input_rows = layer_input.transpose(1, 0, 2).reshape(seq_count * local_rows, model_width)
    shard_rows = model_width // shard_count
    own_gains = jnp.stack([attn_gain, mlp_gain]).astype(F32)
    own_gains = jnp.pad(own_gains, ((0, 6), (0, -shard_rows % LANES)))
    input_all, full_one, gains = startup(
        input_rows, own_gains, (w_query, w_key, w_value, wide_forget), fsdp_size, ctx_size, 1
    )
    gain_one = gains[:, 0, :shard_rows].reshape(1, model_width)
    gain_two = gains[:, 1, :shard_rows].reshape(1, model_width)

    def by_sequence(rows):
        return rows.transpose(1, 0, 2).reshape(seq_count * local_rows, model_width)

    def by_position(rows):
        return rows.reshape(seq_count, local_rows, model_width).transpose(1, 0, 2)

    local_pos = (ctx_index * tp_size + tp_index) * local_rows + jnp.arange(
        local_rows, dtype=jnp.int32
    )
    valid_rows = (local_pos[None, :] < lengths[:, None]).astype(F32)
    valid_rows = valid_rows.reshape(seq_count * local_rows, 1)
    ctx_pos = ctx_index * ctx_rows + jnp.arange(ctx_rows, dtype=jnp.int32)
    ctx_pos = ctx_pos.reshape(tp_size, 1, local_rows)
    ctx_valid = (ctx_pos < lengths[None, :, None]).astype(F32)

    grad_out = (valid_rows * by_sequence(cotangent).astype(F32)).astype(BF16)
    normed_one, forget_rows, items = project(
        input_all, gain_one, full_one, layout, item_count, ctx_size
    )
    normed_flat = normed_one.reshape(all_rows, model_width)
    forget_logit = forget_rows.reshape(all_rows, LANES)[:, :head_count].T
    forget_logit = forget_logit + forget_bias.astype(F32)[:, None]
    forget_logit = forget_logit.reshape(head_count, tp_size, seq_count, local_rows)
    log_forget = (ctx_valid[None] * jax.nn.log_sigmoid(forget_logit)).astype(BF16)

    cut = log_forget.astype(F32).reshape(groups, pair, tp_size, seq_count, local_rows)
    picked = jnp.stack([cut[g, :, :, s] for s, g in places])
    picked = picked.reshape(ctx_size, item_count, pair, ctx_rows).transpose(1, 0, 2, 3)
    picked = jnp.pad(picked, ((0, 0), (0, 0), (0, 8 - pair), (0, 0)))
    attended_items, qkv, full_two, full_out, grad_all, exact, lse, decay = context(
        items,
        picked,
        (w_gate, w_up, w_out, w_gate_out),
        grad_out,
        fsdp_size,
        head_size,
        7,
    )
    gate_out_w = full_out[:, inner_width:]
    gate_logit = dot(normed_flat, gate_out_w, NN)
    out_gate = jax.nn.sigmoid(gate_logit).reshape(tp_size, -1, inner_width)
    hidden_state, normed_two, attended, mixed, down_w = out_project(
        input_rows,
        out_gate,
        full_out,
        gain_two,
        attended_items,
        w_down,
        layout,
        fsdp_size,
        ctx_size,
        2,
    )
    normed_two_all, inner_act, grad_pair = mlp(normed_two, grad_all, full_two, down_w, hidden, 3)
    normed_two_flat = normed_two_all.reshape(all_rows, model_width)
    grad_pair_flat = grad_pair.reshape(all_rows, 2 * hidden)

    gate_up_part = dot(normed_two_flat, grad_pair_flat, TN).astype(BF16)
    grad_hidden, branch, mlp_gain_part, gate_sum = mlp_back(
        grad_pair, full_two, hidden_state, grad_out, gain_two, gate_up_part, fsdp_size, ctx_size, 4
    )
    branch_all, grad_gate_logit, grads, up_sum, feedforward_part, down_part = out_back(
        branch,
        full_out,
        out_gate,
        attended,
        gate_up_part,
        inner_act,
        down_w,
        grad_all,
        layout,
        item_count,
        fsdp_size,
        ctx_size,
        5,
    )
    branch_flat = branch_all.reshape(all_rows, model_width)
    logit_flat = grad_gate_logit.reshape(all_rows, inner_width)

    out_part = jnp.concatenate(
        [
            dot(branch_flat, mixed.reshape(all_rows, inner_width), TN).astype(BF16),
            dot(normed_flat, logit_flat, TN).astype(BF16),
        ],
        axis=1,
    )
    grad_items, forget_items, down_sum, out_sum, feedforward = context_back(
        grads,
        qkv,
        exact,
        lse,
        decay,
        down_part,
        out_part,
        feedforward_part,
        fsdp_size,
        head_size,
        8,
    )
    output = (valid_rows * (hidden_state + feedforward.astype(F32))).astype(BF16)
    forget_back = forget_items[:, :, :pair].astype(BF16).transpose(1, 0, 2, 3)
    forget_back = forget_back.reshape(ctx_size * item_count, pair, tp_size, local_rows)
    slots = {place(slot): slot for slot in range(used)}
    forget_back = jnp.stack(
        [
            jnp.stack([forget_back[slots[s, g]] for s in range(seq_count)], axis=2)
            for g in range(groups)
        ]
    ).reshape(head_count, tp_size, seq_count, local_rows)
    grad_forget_logit = forget_back.astype(F32) * ctx_valid[None] * jax.nn.sigmoid(-forget_logit)
    grad_forget_logit = grad_forget_logit.astype(BF16).reshape(head_count, all_rows)
    bias_part = jnp.sum(grad_forget_logit.astype(F32), axis=1)
    grad_forget_rows = jnp.pad(grad_forget_logit, ((0, LANES - head_count), (0, 0))).T
    grad_qkv = assemble(grad_items, layout, tp_size)
    grad_qkvf = jnp.concatenate([grad_qkv.reshape(all_rows, edge), grad_forget_rows], axis=1)
    bias_full = lax.dynamic_update_slice(
        jnp.zeros((1, model_width), F32), bias_part[None], (0, tp_index * head_count)
    )
    extra = jnp.concatenate(
        [jnp.zeros_like(bias_full), mlp_gain_part, bias_full, jnp.zeros((5, model_width), F32)]
    )
    input_grad, qkv_sum, vectors = last(
        grad_qkv,
        grad_gate_logit,
        grad_forget_rows.reshape(tp_size, -1, LANES),
        full_one,
        full_out,
        input_rows,
        grad_hidden,
        gain_one,
        dot(normed_flat, grad_qkvf, TN).astype(BF16),
        extra,
        fsdp_size,
        ctx_size,
        6,
    )
    gain_one_sum, gain_two_sum, bias_sum = vectors[0], vectors[1], vectors[2]
    attn_gain_grad = lax.dynamic_slice_in_dim(gain_one_sum, shard_index * shard_rows, shard_rows, 0)
    mlp_gain_grad = lax.dynamic_slice_in_dim(gain_two_sum, shard_index * shard_rows, shard_rows, 0)
    forget_bias_grad = lax.dynamic_slice_in_dim(bias_sum, tp_index * head_count, head_count, 0)
    wide = inner_width
    return (
        by_position(output),
        by_position(input_grad),
        attn_gain_grad,
        qkv_sum[:, :wide],
        qkv_sum[:, wide : 2 * wide],
        qkv_sum[:, 2 * wide : 3 * wide],
        qkv_sum[:, 3 * wide : 3 * wide + head_count],
        forget_bias_grad,
        out_sum[:, wide:],
        out_sum[:, :wide],
        mlp_gain_grad,
        gate_sum,
        up_sum,
        down_sum,
    )


def solution(mesh):
    rows = P(("ctx", "tp"), "fsdp", None)
    matrix = P(("fsdp", "ctx"), "tp")
    vector = P(("fsdp", "ctx"))
    return jax.shard_map(
        per_device,
        mesh=mesh,
        in_specs=(
            rows,
            P("fsdp"),
            vector,
            matrix,
            matrix,
            matrix,
            matrix,
            P("tp"),
            matrix,
            matrix,
            vector,
            matrix,
            matrix,
            matrix,
            rows,
        ),
        out_specs=(
            rows,
            rows,
            vector,
            matrix,
            matrix,
            matrix,
            matrix,
            P("tp"),
            matrix,
            matrix,
            vector,
            matrix,
            matrix,
            matrix,
        ),
        check_vma=False,
    )
```

```python
import functools

import jax
import jax.numpy as jnp
from jax import lax
from jax.experimental import pallas as pl
from jax.experimental.pallas import tpu as pltpu
from jax.sharding import PartitionSpec as P

F32 = jnp.float32
BF16 = jnp.bfloat16
LANES = 128
MESH = pl.DeviceIdType.MESH
epsilon = 1e-06
masked_score = -1e30
NT = (((1,), (1,)), ((), ()))
NN = (((1,), (0,)), ((), ()))
TN = (((0,), (0,)), ((), ()))


def dot(left, right, dims):
    return lax.dot_general(left, right, dims, preferred_element_type=F32)


def of_head(block, head, head_size, ones_at=None):
    lane = lax.broadcasted_iota(jnp.int32, block.shape, 1)
    out = jnp.where(lane // head_size == head, block, jnp.zeros_like(block))
    if ones_at is not None:
        out = jnp.where(lane == ones_at, jnp.ones_like(block), out)
    return out


def spare_lane(head, head_size):
    return ((head + 1) % 2) * head_size


def attend_item(qkv, decay, out, exact, lse, heads, head_size):
    count, _, block, width = qkv.shape
    scale = head_size**-0.5
    row = lax.broadcasted_iota(jnp.int32, (block, block), 0)
    column = lax.broadcasted_iota(jnp.int32, (block, block), 1)
    causal = column <= row

    def query_block(i, _):
        query = qkv[i, 0]
        lanes = pl.ds(pl.multiple_of(i * block, block), block)
        result = jnp.zeros((block, width), F32)
        for head in range(heads):
            query_head = of_head(query, head, head_size)

            def step(j, carry, masked):
                top, total, acc = carry
                keys = pl.ds(pl.multiple_of(j * block, block), block)
                score = dot(query_head, qkv[j, 1], NT) * scale
                score = score - decay[head : head + 1, keys]
                if masked:
                    score = jnp.where(causal, score, masked_score)
                new_top = jnp.maximum(top, jnp.max(score, axis=1, keepdims=True))
                prob = jnp.exp(score - new_top)
                shrink = jnp.exp(top - new_top)
                total = total * shrink + jnp.sum(prob, axis=1, keepdims=True)
                acc = acc * shrink + dot(prob.astype(BF16), qkv[j, 2], NN)
                return new_top, total, acc

            carry = (
                jnp.full((block, 1), masked_score, F32),
                jnp.zeros((block, 1), F32),
                jnp.zeros((block, width), F32),
            )
            carry = lax.fori_loop(0, i, lambda j, c: step(j, c, False), carry)
            top, total, acc = step(i, carry, True)
            lane = lax.broadcasted_iota(jnp.int32, acc.shape, 1)
            result = jnp.where(lane // head_size == head, acc / total, result)
            stat = jnp.broadcast_to(top + jnp.log(total), (block, LANES)).T
            lse[head : head + 1, lanes] = stat[0:1]
        exact[i] = result
        out[i] = result.astype(BF16)
        return 0

    lax.fori_loop(0, count, query_block, 0)


def attend_item_back(qkv, grads, exact, lse, decay, dqkv, change, dq_acc, delta, heads, head_size):
    count, _, block, width = qkv.shape
    scale = head_size**-0.5
    row = lax.broadcasted_iota(jnp.int32, (block, block), 0)
    column = lax.broadcasted_iota(jnp.int32, (block, block), 1)
    causal = row <= column
    dq_acc[...] = jnp.zeros_like(dq_acc)
    change[...] = jnp.zeros_like(change)

    def prepare(i, _):
        lanes = pl.ds(pl.multiple_of(i * block, block), block)
        product = grads[i].astype(F32) * exact[i]
        lane = lax.broadcasted_iota(jnp.int32, product.shape, 1)
        for head in range(heads):
            part = jnp.where(lane // head_size == head, product, 0.0)
            part = jnp.sum(part, axis=1, keepdims=True)
            delta[head : head + 1, lanes] = jnp.broadcast_to(part, (block, LANES)).T[0:1]
        return 0

    lax.fori_loop(0, count, prepare, 0)

    def key_block(j, _):
        keys = pl.ds(pl.multiple_of(j * block, block), block)
        key = qkv[j, 1]
        value = qkv[j, 2]
        value_total = jnp.zeros((block, width), F32)
        key_total = jnp.zeros((block, width), F32)
        for head in range(heads):
            spare = spare_lane(head, head_size)
            key_ones = of_head(key, head, head_size, spare)
            fall = jnp.broadcast_to(decay[head : head + 1, keys], (LANES, block)).T[:, 0:1]

            def step(i, carry, masked):
                value_acc, key_acc = carry
                lanes = pl.ds(pl.multiple_of(i * block, block), block)
                query = qkv[i, 0]
                grad = of_head(grads[i], head, head_size)
                score = dot(key, of_head(query, head, head_size), NT) * scale
                score = score - fall - lse[head : head + 1, lanes]
                if masked:
                    score = jnp.where(causal, score, masked_score)
                prob = jnp.exp(score)
                grad_prob = dot(value, grad, NT)
                grad_score = prob * (grad_prob - delta[head : head + 1, lanes])
                grad_score = grad_score.astype(BF16)
                value_acc = value_acc + dot(prob.astype(BF16), grad, NN)
                query_ones = of_head(query, head, head_size, spare)
                key_acc = key_acc + dot(grad_score, query_ones, NN)
                dq_acc[head, i] += dot(grad_score, key_ones, TN)
                return value_acc, key_acc

            zero = jnp.zeros((block, width), F32)
            carry = step(j, (zero, zero), True)
            carry = lax.fori_loop(j + 1, count, lambda i, c: step(i, c, False), carry)
            value_acc, key_acc = carry
            value_total = value_total + value_acc
            lane = lax.broadcasted_iota(jnp.int32, key_acc.shape, 1)
            key_total = jnp.where(lane // head_size == head, key_acc, key_total)
            change[head : head + 1, keys] -= key_acc.T[spare : spare + 1]
        dqkv[j, 1] = (key_total * scale).astype(BF16)
        dqkv[j, 2] = value_total.astype(BF16)
        return 0

    lax.fori_loop(0, count, key_block, 0)

    def finish(i, _):
        lanes = pl.ds(pl.multiple_of(i * block, block), block)
        total = jnp.zeros((block, width), F32)
        for head in range(heads):
            spare = spare_lane(head, head_size)
            part = dq_acc[head, i]
            lane = lax.broadcasted_iota(jnp.int32, part.shape, 1)
            total = jnp.where(lane // head_size == head, part, total)
            change[head : head + 1, lanes] += part.T[spare : spare + 1]
        dqkv[i, 0] = (total * scale).astype(BF16)
        return 0

    lax.fori_loop(0, count, finish, 0)


def triangle(upward):
    row = lax.broadcasted_iota(jnp.int32, (LANES, LANES), 0)
    column = lax.broadcasted_iota(jnp.int32, (LANES, LANES), 1)
    keep = (row <= column) if upward else (row >= column)
    return jnp.where(keep, 1.0, 0.0).astype(BF16)


def exact_product(values, matrix):
    high = values.astype(BF16)
    rest = values - high.astype(F32)
    middle = rest.astype(BF16)
    low = (rest - middle.astype(F32)).astype(BF16)
    return dot(high, matrix, NN) + dot(middle, matrix, NN) + dot(low, matrix, NN)


def ctx_sending(source, target, send_sem, recv_sem, peer):
    return pltpu.make_async_remote_copy(
        src_ref=source,
        dst_ref=target,
        send_sem=send_sem,
        recv_sem=recv_sem,
        device_id={"ctx": peer},
        device_id_type=MESH,
    )


def ctx_greet(size):
    me = lax.axis_index("ctx")
    barrier = pltpu.get_barrier_semaphore()
    for step in range(1, size):
        peer = lax.rem(me + step, size)
        pl.semaphore_signal(barrier, inc=1, device_id={"ctx": peer}, device_id_type=MESH)
    pl.semaphore_wait(barrier, size - 1)
    return me


class Exchange:
    def __init__(self, me, size, source, target, sems):
        self.me, self.size, self.source, self.target = me, size, source, target
        self.send_sem, self.recv_sem, self.own_sem = sems

    def own(self, item):
        return pltpu.make_async_copy(
            self.source.at[item, self.me], self.target.at[item, self.me], self.own_sem.at[item]
        )

    def copy(self, item, step):
        peer = lax.rem(self.me + step, self.size)
        return ctx_sending(
            self.source.at[item, peer],
            self.target.at[item, self.me],
            self.send_sem.at[item, step],
            self.recv_sem.at[item, step],
            peer,
        )

    def start(self, item):
        for step in range(1, self.size):
            self.copy(item, step).start()
        self.own(item).start()

    def arrive(self, item):
        self.own(item).wait()
        for step in range(1, self.size):
            self.copy(item, step).wait_recv()

    def drain(self, item):
        for step in range(1, self.size):
            self.copy(item, step).wait_send()


def exchange_sems(items, size):
    return [
        pltpu.SemaphoreType.DMA((items, size)),
        pltpu.SemaphoreType.DMA((items, size)),
        pltpu.SemaphoreType.DMA((items,)),
    ]


def context_kernel(
    heads,
    head_size,
    items_ref,
    forget_ref,
    gate_ref,
    up_ref,
    out_w_ref,
    gate_out_ref,
    rows_ref,
    normed_hbm,
    back_ref,
    qkv_ref,
    full_ref,
    full_out_ref,
    table_ref,
    exact_ref,
    lse_ref,
    decay_ref,
    out_gate_ref,
    *refs,
):
    qkv, forget, out, normed, gate_w, fetch_sem, save_sem = refs[:7]
    sems = refs[7:]
    count, size, _, block, width = items_ref.shape
    tp, sibling, across, diagonal = tp_places()
    greet_all([{"tp": sibling}, {"tp": across}] + group_peers())
    me = lax.axis_index("ctx")
    gathers = (
        WeightGather((out_w_ref, gate_out_ref), full_out_ref, sems[9:14]),
        WeightGather((gate_ref, up_ref), full_ref, sems[14:19]),
    )
    rows = RowGather(rows_ref, table_ref, sems[19:])
    fetch = Fetch([(normed_hbm, normed)], fetch_sem)
    forgets = Exchange(me, size, forget_ref, forget, sems[0:3])
    inputs = Exchange(me, size, items_ref, qkv, sems[3:6])
    results = Exchange(me, size, out, back_ref, sems[6:9])

    @pl.loop(0, count)
    def _(item):
        forgets.start(item)

    for gather in gathers:
        gather.begin()
    inputs.start(0)
    rows.begin()

    @pl.loop(0, count)
    def _(item):
        forgets.arrive(item)

    @pl.loop(0, count)
    def _(item):
        upper = triangle(True)
        before = jnp.zeros((8, 1), F32)
        for start in range(0, size * block, LANES):
            part = forget[item, start // block, :, pl.ds(start % block, LANES)]
            total = before + dot(part.astype(BF16), upper, NN)
            decay_ref[item, :, pl.ds(start, LANES)] = total
            before = total[:, LANES - 1 :]

    lse_ref[...] = jnp.zeros_like(lse_ref)

    @pl.loop(0, count)
    def _(item):
        inputs.arrive(item)

        @pl.when(item + 1 < count)
        def _():
            inputs.start(item + 1)

        for hop in range(1, min(size, count + 1)):

            @pl.when(item == hop - 1)
            def _(hop=hop):
                for gather in gathers:
                    gather.advance(hop)

        saving = pltpu.make_async_copy(qkv.at[item], qkv_ref.at[item], save_sem)
        saving.start()
        attend_item(
            qkv.at[item], decay_ref.at[item], out.at[item], exact_ref.at[item], lse_ref.at[item], heads, head_size
        )
        results.start(item)
        saving.wait()

    rows.advance()
    for hop in range(count + 1, size):
        for gather in gathers:
            gather.advance(hop)

    gathers[0].end()
    inner = gate_w.shape[1]
    copy = pltpu.make_async_copy(full_out_ref.at[:, pl.ds(inner, inner)], gate_w, fetch_sem.at[1])
    copy.start()
    fetch.wait()
    copy.wait()
    step_rows = normed.shape[1] // CHUNKS

    @pl.loop(0, 4 * CHUNKS)
    def _(step):
        spot = pl.ds(pl.multiple_of(lax.rem(step, CHUNKS) * step_rows, step_rows), step_rows)
        logit = dot(normed[step // CHUNKS, spot], gate_w[...], NN)
        out_gate_ref[step // CHUNKS, spot] = 1.0 / (1.0 + jnp.exp(-logit))

    @pl.loop(0, count)
    def _(item):
        forgets.drain(item)
        inputs.drain(item)
        results.arrive(item)
        results.drain(item)

    gathers[1].end()
    rows.end()


def full_block(shape):
    return pl.BlockSpec(shape, lambda i: (0,) * len(shape), pipeline_mode=pl.Buffered(1))


def attend_cost(items, heads, products):
    count, size, _, block, width = items.shape
    pairs = count * heads * (size * block) ** 2 // 2
    return pl.CostEstimate(
        flops=2 * products * pairs * 256, bytes_accessed=100 << 20, transcendentals=pairs
    )


def context(items, forget, shards, rows, normed, f_size, head_size, ident):
    count, size, _, block, width = items.shape
    full = shards[0].shape[0] * f_size * size
    gate = normed.shape[:2] + shards[3].shape[1:]
    heads = width // head_size
    place = pl.BlockSpec(memory_space=pl.ANY)
    exact, stat = (count, size, block, width), (count, 8, size * block)
    return pl.pallas_call(
        functools.partial(context_kernel, heads, head_size),
        grid=(1,),
        out_shape=[
            jax.ShapeDtypeStruct(exact, BF16),
            jax.ShapeDtypeStruct(items.shape, BF16),
            jax.ShapeDtypeStruct((full, 2 * shards[0].shape[1]), BF16),
            jax.ShapeDtypeStruct((full, 2 * shards[2].shape[1]), BF16),
            jax.ShapeDtypeStruct((4,) + rows.shape, BF16),
            jax.ShapeDtypeStruct(exact, F32),
            jax.ShapeDtypeStruct(stat, F32),
            jax.ShapeDtypeStruct(stat, F32),
            jax.ShapeDtypeStruct(gate, F32),
        ],
        in_specs=[place, place]
        + [full_block(shard.shape) for shard in shards]
        + [full_block(rows.shape), place],
        out_specs=[place] * 5
        + [full_block(exact), full_block(stat), full_block(stat), full_block(gate)],
        scratch_shapes=[
            pltpu.VMEM(items.shape, BF16),
            pltpu.VMEM(forget.shape, F32),
            pltpu.VMEM(exact, BF16),
            pltpu.VMEM(normed.shape, BF16),
            pltpu.VMEM((full, shards[3].shape[1]), BF16),
            pltpu.SemaphoreType.DMA((2,)),
            pltpu.SemaphoreType.DMA,
        ]
        + exchange_sems(count, size) * 3
        + weight_sems(f_size, size, 2) * 2
        + [pltpu.SemaphoreType.DMA((3,))] * 2
        + [pltpu.SemaphoreType.DMA],
        compiler_params=remote_params(ident, 48),
        cost_estimate=attend_cost(items, heads, 2),
        name="context",
    )(items, forget, *shards, rows, normed)


def context_back_kernel(
    heads,
    head_size,
    items_ref,
    qkv_ref,
    exact_ref,
    lse_ref,
    decay_ref,
    down_ref,
    part_ref,
    inner_hbm,
    down_w_hbm,
    back_ref,
    forget_ref,
    down_sum_ref,
    sum_ref,
    rows_ref,
    *refs,
):
    grads, dqkv, change, slope, dq_acc, delta = refs[:6]
    sems = refs[6:15]
    count, size, block, width = items_ref.shape
    inner, down_w, table, fetch_sem = refs[36:]
    fetch = Fetch([(inner_hbm, inner), (down_w_hbm, down_w)], fetch_sem)
    tp, sibling, across, diagonal = tp_places()
    greet_all([{"tp": sibling}, {"tp": across}] + group_peers())
    me = lax.axis_index("ctx")
    sums = (
        WeightSum(part_ref, 0, sum_ref, refs[15:23]),
        WeightSum(down_ref, 0, down_sum_ref, refs[23:31]),
    )
    rows = RowSum(table, rows_ref, refs[31:36])
    inputs = Exchange(me, size, items_ref, grads, sems[0:3])
    results = Exchange(me, size, dqkv, back_ref, sems[3:6])
    forgets = Exchange(me, size, slope, forget_ref, sems[6:9])

    inputs.start(0)
    for weights in sums:
        weights.begin()
    fetch.wait()
    step_rows = inner.shape[1] // CHUNKS

    @pl.loop(0, 4 * CHUNKS)
    def _(step):
        spot = pl.ds(pl.multiple_of(lax.rem(step, CHUNKS) * step_rows, step_rows), step_rows)
        forward = dot(inner[step // CHUNKS, spot], down_w[...], NT)
        table[step // CHUNKS, spot] = forward.astype(BF16)

    rows.begin()

    @pl.loop(0, count)
    def _(item):
        inputs.arrive(item)

        @pl.when(item + 1 < count)
        def _():
            inputs.start(item + 1)

        attend_item_back(
            qkv_ref.at[item],
            grads.at[item],
            exact_ref.at[item],
            lse_ref.at[item],
            decay_ref.at[item],
            dqkv.at[item],
            change,
            dq_acc,
            delta,
            heads,
            head_size,
        )
        @pl.when(item > 0)
        def _():
            results.start(item)

        lower = triangle(False)
        after = jnp.zeros((8, 1), F32)
        for start in reversed(range(0, size * block, LANES)):
            total = after + exact_product(change[:, pl.ds(start, LANES)], lower)
            slope[item, start // block, :, pl.ds(start % block, LANES)] = total
            after = total[:, 0:1]
        forgets.start(item)

        for turn in range(count):

            @pl.when(item == turn)
            def _(turn=turn):
                for weights in sums:
                    weights.run_round(turn)
                if turn == 0:
                    results.start(0)
                    rows.advance()

    for n in range(count, sums[0].rounds()):
        for weights in sums:
            weights.run_round(n)

    @pl.loop(0, count)
    def _(item):
        inputs.drain(item)
        results.arrive(item)
        results.drain(item)
        forgets.arrive(item)
        forgets.drain(item)

    for weights in sums:
        weights.end()
    rows.end()


def context_back(grads, qkv, exact, lse, decay, down, part, inner_act, down_w, f_size, head_size, ident):
    count, size, _, block, width = qkv.shape
    heads = width // head_size
    place = pl.BlockSpec(memory_space=pl.ANY)
    forget = (count, size, 8, block)
    total = (part.shape[0] // (f_size * size), part.shape[1])
    down_total = (total[0], down.shape[1])
    table = inner_act.shape[:2] + down_w.shape[:1]
    return pl.pallas_call(
        functools.partial(context_back_kernel, heads, head_size),
        grid=(1,),
        out_shape=[
            jax.ShapeDtypeStruct(qkv.shape, BF16),
            jax.ShapeDtypeStruct(forget, F32),
            jax.ShapeDtypeStruct(down_total, F32),
            jax.ShapeDtypeStruct(total, F32),
            jax.ShapeDtypeStruct(table[1:], BF16),
        ],
        in_specs=[
            place,
            full_block(qkv.shape),
            full_block(exact.shape),
            full_block(lse.shape),
            full_block(decay.shape),
            place,
            place,
            place,
            place,
        ],
        out_specs=[
            place,
            place,
            full_block(down_total),
            full_block(total),
            full_block(table[1:]),
        ],
        scratch_shapes=[
            pltpu.VMEM(grads.shape, BF16),
            pltpu.VMEM(qkv.shape, BF16),
            pltpu.VMEM((8, size * block), F32),
            pltpu.VMEM(forget, F32),
            pltpu.VMEM((heads, size, block, width), F32),
            pltpu.VMEM((8, size * block), F32),
        ]
        + exchange_sems(count, size) * 3
        + sum_scratch(f_size, size, *total)
        + sum_scratch(f_size, size, *down_total)
        + row_sum_scratch(*table[1:])
        + [
            pltpu.VMEM(inner_act.shape, BF16),
            pltpu.VMEM(down_w.shape, BF16),
            pltpu.VMEM(table, BF16),
            pltpu.SemaphoreType.DMA((2,)),
        ],
        compiler_params=remote_params(ident, 62),
        cost_estimate=attend_cost(qkv, heads, 5),
        name="context_back",
    )(grads, qkv, exact, lse, decay, down, part, inner_act, down_w)


CHUNKS = 4
HALVES = 2
SUM_CHUNKS = 2


def tp_places():
    me = lax.axis_index("tp")
    sibling = me + 1 - 2 * lax.rem(me, 2)
    across = lax.rem(me + 2, 4)
    diagonal = lax.rem(sibling + 2, 4)
    return me, sibling, across, diagonal


def greet(peers):
    barrier = pltpu.get_barrier_semaphore()
    for peer in peers:
        pl.semaphore_signal(barrier, inc=1, device_id={"tp": peer}, device_id_type=MESH)
    pl.semaphore_wait(barrier, len(peers))


def sending(source, target, send_sem, recv_sem, peer):
    return pltpu.make_async_remote_copy(
        src_ref=source,
        dst_ref=target,
        send_sem=send_sem,
        recv_sem=recv_sem,
        device_id={"tp": peer},
        device_id_type=MESH,
    )


def pick(step, chunks, places):
    me, sibling, across, diagonal = places
    late = step - 2 * chunks
    far = jnp.where(lax.rem(late, 2) == 0, across, diagonal)
    slot = jnp.where(step < chunks, me, jnp.where(step < 2 * chunks, sibling, far))
    chunk = jnp.where(step < 2 * chunks, lax.rem(step, chunks), late // 2)
    return slot, chunk


def gather_loop(table, sems, compute, own=None, relative=False, between=None, ready=None):
    near_send, near_recv, far_send, far_recv, pass_send, pass_recv = sems
    me, sibling, across, diagonal = tp_places()
    places = (0, 1, 2, 3) if relative else (me, sibling, across, diagonal)
    mine, near_by, far_off, corner = places
    near_spot, far_spot, pass_spot = (1, 2, 3) if relative else (me, me, across)
    rows = table.shape[1] // CHUNKS

    def part(slot, chunk):
        return table.at[slot, pl.ds(pl.multiple_of(chunk * rows, rows), rows)]

    def far(chunk):
        source = part(mine, chunk)
        if own is not None:
            source = own.at[pl.ds(pl.multiple_of(chunk * rows, rows), rows)]
        return sending(source, part(far_spot, chunk), far_send.at[chunk], far_recv.at[chunk], across)

    def far_arrival(chunk):
        spot = part(far_off, chunk)
        return sending(spot, spot, far_send.at[chunk], far_recv.at[chunk], across)

    def passing(chunk):
        return sending(
            part(far_off, chunk), part(pass_spot, chunk), pass_send.at[chunk], pass_recv.at[chunk], sibling
        )

    def pass_arrival(chunk):
        spot = part(corner, chunk)
        return sending(spot, spot, pass_send.at[chunk], pass_recv.at[chunk], sibling)

    for chunk in range(CHUNKS):
        far(chunk).start()
    own = table.at[mine] if own is None else own
    near = sending(own, table.at[near_spot], near_send, near_recv, sibling)
    near.start()
    if ready is not None:
        ready()

    def body(step, _):
        slot, chunk = pick(step, CHUNKS, places)
        late = step - 2 * CHUNKS

        @pl.when(step == CHUNKS)
        def _():
            spot = table.at[near_by]
            sending(spot, spot, near_send, near_recv, sibling).wait_recv()

        @pl.when((late >= 0) & (lax.rem(late, 2) == 0))
        def _():
            far_arrival(chunk).wait_recv()
            passing(chunk).start()

        @pl.when((late >= 0) & (lax.rem(late, 2) == 1))
        def _():
            pass_arrival(chunk).wait_recv()

        compute(slot, chunk)
        return 0

    if between is None:
        lax.fori_loop(0, 4 * CHUNKS, body, 0)
    else:
        lax.fori_loop(0, 2 * CHUNKS, body, 0)
        between()
        lax.fori_loop(2 * CHUNKS, 4 * CHUNKS, body, 0)
    near.wait_send()
    for chunk in range(CHUNKS):
        far(chunk).wait_send()
        passing(chunk).wait_send()


GATHER_SEMS = [pltpu.SemaphoreType.DMA] * 2 + [pltpu.SemaphoreType.DMA((CHUNKS,))] * 4


def scatter_loop(buffers, sems, partial, finish, relative=False, between=None):
    near_out, near_in, far_out, far_in = buffers
    near_send, near_recv, far_send, far_recv = sems
    me, sibling, across, diagonal = tp_places()
    mine, near_by, far_off, corner = (0, 1, 2, 3) if relative else (me, sibling, across, diagonal)
    rows = far_out.shape[0] // SUM_CHUNKS

    def span(chunk):
        return pl.ds(pl.multiple_of(chunk * rows, rows), rows)

    def near(half, chunk):
        return sending(
            near_out.at[half, span(chunk)],
            near_in.at[half, span(chunk)],
            near_send.at[half, chunk],
            near_recv.at[half, chunk],
            sibling,
        )

    def far(chunk):
        return sending(
            far_out.at[span(chunk)],
            far_in.at[span(chunk)],
            far_send.at[chunk],
            far_recv.at[chunk],
            across,
        )

    def body(step, _):
        phase, chunk = step // SUM_CHUNKS, lax.rem(step, SUM_CHUNKS)
        slot = jnp.where(
            phase == 0, corner, jnp.where(phase == 1, far_off, jnp.where(phase == 2, near_by, mine))
        )
        value = partial(slot, chunk)
        spot = span(chunk)

        @pl.when(lax.rem(phase, 2) == 0)
        def _():
            half = phase // 2
            near_out[half, spot] = value.astype(BF16)
            near(half, chunk).start()

        @pl.when(phase == 1)
        def _():
            near(0, chunk).wait_recv()
            far_out[spot] = (value + near_in[0, spot].astype(F32)).astype(BF16)
            far(chunk).start()

        @pl.when(phase == 3)
        def _():
            near(1, chunk).wait_recv()

            far(chunk).wait_recv()
            finish(chunk, value + near_in[1, spot].astype(F32) + far_in[spot].astype(F32))

        return 0

    if between is None:
        lax.fori_loop(0, 4 * SUM_CHUNKS, body, 0)
    else:
        lax.fori_loop(0, SUM_CHUNKS, body, 0)
        for phase in (1, 2, 3):
            between(phase)
            lax.fori_loop(phase * SUM_CHUNKS, (phase + 1) * SUM_CHUNKS, body, 0)
    for chunk in range(SUM_CHUNKS):
        near(0, chunk).wait_send()
        near(1, chunk).wait_send()
        far(chunk).wait_send()


SCATTER_SEMS = [pltpu.SemaphoreType.DMA((2, SUM_CHUNKS))] * 2 + [pltpu.SemaphoreType.DMA((SUM_CHUNKS,))] * 2


def scatter_buffers(rows, width):
    return [
        pltpu.VMEM((2, rows, width), BF16),
        pltpu.VMEM((2, rows, width), BF16),
        pltpu.VMEM((rows, width), BF16),
        pltpu.VMEM((rows, width), BF16),
    ]


def group_peers():
    f_size, c_size = lax.axis_size("fsdp"), lax.axis_size("ctx")
    f, c = lax.axis_index("fsdp"), lax.axis_index("ctx")
    return [
        {"fsdp": lax.rem(f + i, f_size), "ctx": lax.rem(c + j, c_size)}
        for i in range(f_size)
        for j in range(c_size)
        if i or j
    ]


def greet_all(peers):
    barrier = pltpu.get_barrier_semaphore()
    for peer in peers:
        pl.semaphore_signal(barrier, inc=1, device_id=peer, device_id_type=MESH)
    pl.semaphore_wait(barrier, len(peers))


def moving(source, target, send_sem, recv_sem, peer):
    return pltpu.make_async_remote_copy(
        src_ref=source,
        dst_ref=target,
        send_sem=send_sem,
        recv_sem=recv_sem,
        device_id=peer,
        device_id_type=MESH,
    )


class WeightGather:
    def __init__(self, shards, full, sems):
        self.shards, self.full = shards, full
        widths = [shard.shape[1] for shard in shards]
        self.columns = [pl.ds(sum(widths[:h]), width) for h, width in enumerate(widths)]
        self.f_size, self.c_size = lax.axis_size("fsdp"), lax.axis_size("ctx")
        self.f, self.c = lax.axis_index("fsdp"), lax.axis_index("ctx")
        self.sems = sems

    def spot(self, c, h, f=None):
        rows = self.shards[0].shape[0]
        block = (self.f if f is None else f) * self.c_size + c
        return self.full.at[pl.ds(pl.multiple_of(block * rows, rows), rows), self.columns[h]]

    def own(self, h):
        return pltpu.make_async_copy(self.shards[h], self.spot(self.c, h), self.sems[4].at[h])

    def along(self, c, h, hop, side, first=False):
        source = self.shards[h] if first else self.spot(c, h)
        peer = {"ctx": self.c + (1 if side else -1)}
        send, recv = self.sems[0].at[side, hop, h], self.sems[1].at[side, hop, h]
        return moving(source, self.spot(c, h), send, recv, peer)

    def over(self, c, h, step, first=False):
        source = self.shards[h] if first else self.spot(c, h)
        peer = {"fsdp": lax.rem(self.f + step, self.f_size)}
        send, recv = self.sems[2].at[step, c, h], self.sems[3].at[step, c, h]
        return moving(source, self.spot(c, h), send, recv, peer)

    def over_arrival(self, c, h, step):
        spot = self.spot(c, h, lax.rem(self.f + self.f_size - step, self.f_size))
        peer = {"fsdp": lax.rem(self.f + step, self.f_size)}
        return moving(spot, spot, self.sems[2].at[step, c, h], self.sems[3].at[step, c, h], peer)

    def can(self, side):
        return self.c + 1 < self.c_size if side else self.c > 0

    def holds(self, hop, side):
        return self.c - hop >= 0 if side else self.c + hop < self.c_size

    def begin(self):
        for h in range(len(self.shards)):
            for side in (1, 0):

                @pl.when(self.can(side))
                def _(side=side):
                    self.along(self.c, h, 1, side, True).start()

            for step in range(1, self.f_size):
                self.over(self.c, h, step, True).start()

        for h in range(len(self.shards)):
            self.own(h).start()

    def advance(self, hop):
        for h in range(len(self.shards)):
            for side in (1, 0):

                @pl.when(self.holds(hop, side))
                def _(side=side):
                    c = self.c - hop if side else self.c + hop
                    self.along(c, h, hop, side).wait_recv()

                    @pl.when(self.can(side))
                    def _():
                        self.along(c, h, hop + 1, side).start()

                    for step in range(1, self.f_size):
                        self.over(c, h, step).start()

    def end(self):
        for h in range(len(self.shards)):
            self.own(h).wait()
            for step in range(1, self.f_size):
                for c in range(self.c_size):
                    self.over_arrival(c, h, step).wait_recv()
                    self.over(c, h, step).wait_send()
            for side in (1, 0):

                @pl.when(self.can(side))
                def _(side=side):
                    self.along(self.c, h, 1, side, True).wait_send()

                for hop in range(1, self.c_size):

                    @pl.when(self.holds(hop, side) & self.can(side))
                    def _(side=side, hop=hop):
                        c = self.c - hop if side else self.c + hop
                        self.along(c, h, hop + 1, side).wait_send()


def weight_sems(f_size, c_size, parts):
    dma = pltpu.SemaphoreType.DMA
    return [dma((2, c_size + 1, parts))] * 2 + [dma((f_size, c_size, parts))] * 2 + [dma((parts,))]


class WeightSum:
    def __init__(self, part, first_column, out, refs):
        self.part, self.out, self.first = part, out, first_column
        self.stage, self.total, self.along_in = refs[:3]
        self.own_sem, self.over_send, self.over_recv, self.along_send, self.along_recv = refs[3:]
        self.f_size, self.c_size = lax.axis_size("fsdp"), lax.axis_size("ctx")
        self.f, self.c = lax.axis_index("fsdp"), lax.axis_index("ctx")
        self.rows, self.wide = out.shape[0], out.shape[1] // HALVES
        ends = [(self.c_size - 1 - i // 2) if i % 2 == 0 else i // 2 for i in range(self.c_size)]
        self.order = [(c, h) for c in ends for h in range(HALVES)]
        self.stages = len(self.order) + self.c_size - 1

    def piece(self, f, c, h):
        row = (f * self.c_size + c) * self.rows
        columns = pl.ds(self.first + h * self.wide, self.wide)
        return self.part.at[pl.ds(pl.multiple_of(row, self.rows), self.rows), columns]

    def own(self, c, h):
        n = c * HALVES + h
        return pltpu.make_async_copy(self.piece(self.f, c, h), self.stage.at[n], self.own_sem.at[n])

    def over(self, c, h, step):
        f, n = lax.rem(self.f + step, self.f_size), c * HALVES + h
        return moving(
            self.piece(f, c, h),
            self.total.at[step - 1, n],
            self.over_send.at[step - 1, n],
            self.over_recv.at[step - 1, n],
            {"fsdp": f},
        )

    def along(self, c, h, side, source=None):
        peer, n = {"ctx": self.c + (1 if side else -1)}, c * HALVES + h
        target = self.along_in.at[side, n]
        return moving(
            target if source is None else source,
            target,
            self.along_send.at[side, n],
            self.along_recv.at[side, n],
            peer,
        )

    def begin(self):
        for c, h in self.order:
            for step in range(1, self.f_size):
                self.over(c, h, step).start()
        for c, h in self.order:
            self.own(c, h).start()

    def receive(self, i):
        c, h = self.order[i]
        n = c * HALVES + h
        self.own(c, h).wait()
        value = self.stage[n].astype(F32)
        for step in range(1, self.f_size):
            self.over(c, h, step).wait_recv()
        for step in range(1, self.f_size):
            value = value + self.total[step - 1, n].astype(F32)
        self.total[0, n] = value.astype(BF16)
        for side, end in ((1, 0), (0, self.c_size - 1)):
            if c != end:

                @pl.when(self.c == end)
                def _(side=side):
                    self.along(c, h, side, self.total.at[0, n]).start()

    def hop(self, c, h, side, device):
        n = c * HALVES + h

        @pl.when(self.c == device)
        def _():
            self.along(c, h, side).wait_recv()
            value = self.total[0, n].astype(F32) + self.along_in[side, n].astype(F32)
            if device == c:
                self.total[0, n] = value.astype(BF16)
            else:
                self.along_in[side, n] = value.astype(BF16)
                self.along(c, h, side).start()

    def run(self, n):
        if n < len(self.order):
            self.receive(n)
        for i, (c, h) in enumerate(self.order):
            if 1 <= n - i <= c:
                self.hop(c, h, 1, n - i)
            if 1 <= n - i <= self.c_size - 1 - c:
                self.hop(c, h, 0, self.c_size - 1 - (n - i))

    def run_to(self, first, last):
        for n in range(min(first, self.stages), min(last, self.stages)):
            self.run(n)

    def rounds(self):
        return self.c_size + 1

    def run_round(self, n):
        count = len(self.order)
        for i, (c, h) in enumerate(self.order):
            hop = n if i < 5 * count // 8 else n - 1
            if hop == 0:
                self.receive(i)
            if 1 <= hop <= c:
                self.hop(c, h, 1, hop)
            if 1 <= hop <= self.c_size - 1 - c:
                self.hop(c, h, 0, self.c_size - 1 - hop)

    def end(self):
        for c in range(self.c_size):

            @pl.when(self.c == c)
            def _(c=c):
                for h in range(HALVES):
                    columns = pl.ds(h * self.wide, self.wide)
                    self.out[:, columns] = self.total[0, c * HALVES + h].astype(F32)

        for c, h in self.order:
            for step in range(1, self.f_size):
                self.over(c, h, step).wait_send()
            for side in (1, 0):

                @pl.when(self.c < c if side else self.c > c)
                def _(side=side):
                    self.along(c, h, side).wait_send()


def sum_scratch(f_size, c_size, rows, columns):
    dma, count, wide = pltpu.SemaphoreType.DMA, c_size * HALVES, columns // HALVES
    return (
        [
            pltpu.VMEM((count, rows, wide), BF16),
            pltpu.VMEM((f_size - 1, count, rows, wide), BF16),
            pltpu.VMEM((2, count, rows, wide), BF16),
        ]
        + [dma((count,))]
        + [dma((f_size - 1, count))] * 2
        + [dma((2, count))] * 2
    )


class Fetch:
    def __init__(self, pairs, sem):
        self.copies = [
            pltpu.make_async_copy(source, target, sem.at[n]) for n, (source, target) in enumerate(pairs)
        ]
        for copy in self.copies:
            copy.start()

    def wait(self):
        for copy in self.copies:
            copy.wait()


class RowGather:
    def __init__(self, rows, table, sems):
        self.rows, self.table, self.sems = rows, table, sems
        _, self.sibling, self.across, _ = tp_places()

    def own(self):
        return pltpu.make_async_copy(self.rows, self.table.at[0], self.sems[2])

    def copy(self, n):
        source = self.table.at[2] if n == 2 else self.rows
        peer = {"tp": self.across if n == 1 else self.sibling}
        return moving(source, self.table.at[n + 1], self.sems[0].at[n], self.sems[1].at[n], peer)

    def begin(self):
        self.copy(1).start()
        self.copy(0).start()
        self.own().start()

    def advance(self):
        self.copy(1).wait_recv()
        self.copy(2).start()

    def end(self):
        self.own().wait()
        self.copy(0).wait()
        self.copy(1).wait_send()
        self.copy(2).wait()


class RowSum:
    def __init__(self, table, out, refs):
        self.table, self.out = table, out
        self.near, self.far_out, self.far_in, self.send, self.recv = refs
        _, self.sibling, self.across, _ = tp_places()

    def copy(self, n):
        if n == 2:
            source, target, peer = self.far_out, self.far_in, self.across
        else:
            source, target, peer = self.table.at[1 if n else 3], self.near.at[n], self.sibling
        return moving(source, target, self.send.at[n], self.recv.at[n], {"tp": peer})

    def begin(self):
        for n in range(2):
            self.copy(n).start()

    def advance(self):
        self.copy(0).wait_recv()
        self.far_out[...] = (self.table[2].astype(F32) + self.near[0].astype(F32)).astype(BF16)
        self.copy(2).start()

    def end(self):
        self.copy(1).wait_recv()
        self.copy(2).wait_recv()
        total = self.table[0].astype(F32) + self.near[1].astype(F32)
        self.out[...] = (total + self.far_in[...].astype(F32)).astype(BF16)
        for n in range(3):
            self.copy(n).wait_send()


def row_sum_scratch(rows, width):
    dma, pair, one = pltpu.SemaphoreType.DMA, (2, rows, width), (rows, width)
    return [pltpu.VMEM(pair, BF16)] + [pltpu.VMEM(one, BF16)] * 2 + [dma((3,))] * 2


def startup_kernel(parts, rows_ref, gain_ref, *refs):
    shards, (all_ref, full_ref, gains_ref, own_sem) = refs[:parts], refs[parts : parts + 4]
    sems = refs[parts + 4 :]
    me, sibling, across, diagonal = tp_places()
    others = group_peers()
    greet_all([{"tp": sibling}, {"tp": across}] + others)
    near_send, near_recv, far_send, far_recv, pass_send, pass_recv = sems[:6]
    gather = WeightGather(shards, full_ref, sems[6:11])
    gain_send, gain_recv, gain_own = sems[11:]
    spot = gains_ref.at[gather.f * gather.c_size + gather.c]
    gain_copies = [
        moving(gain_ref, spot, gain_send.at[n], gain_recv.at[n], peer) for n, peer in enumerate(others)
    ]
    own_gain = pltpu.make_async_copy(gain_ref, spot, gain_own)
    size = rows_ref.shape[0] // CHUNKS
    own = pltpu.make_async_copy(rows_ref, all_ref.at[me], own_sem)

    def span(chunk):
        return pl.ds(chunk * size, size)

    def far(chunk):
        return sending(
            rows_ref.at[span(chunk)],
            all_ref.at[me, span(chunk)],
            far_send.at[chunk],
            far_recv.at[chunk],
            across,
        )

    def passing(chunk):
        spot = all_ref.at[across, span(chunk)]
        return sending(spot, spot, pass_send.at[chunk], pass_recv.at[chunk], sibling)

    gather.begin()
    far(0).start()
    for copy in gain_copies:
        copy.start()
    own_gain.start()
    near = sending(rows_ref, all_ref.at[me], near_send, near_recv, sibling)
    near.start()
    own.start()
    for turn in range(max(CHUNKS, gather.c_size - 1)):
        if turn < CHUNKS:
            far(turn).wait_recv()
            if turn + 1 < CHUNKS:
                far(turn + 1).start()
            passing(turn).start()
        if turn + 1 < gather.c_size:
            gather.advance(turn + 1)
    near.wait()
    for chunk in range(CHUNKS):
        far(chunk).wait_send()
        passing(chunk).wait()
    own.wait()
    gather.end()
    for copy in gain_copies:
        copy.wait()
    own_gain.wait()


def startup(rows, gains, shards, f_size, c_size, ident):
    place = pl.BlockSpec(memory_space=pl.ANY)
    full = (shards[0].shape[0] * f_size * c_size, sum(shard.shape[1] for shard in shards))
    return pl.pallas_call(
        functools.partial(startup_kernel, len(shards)),
        out_shape=[
            jax.ShapeDtypeStruct((4,) + rows.shape, BF16),
            jax.ShapeDtypeStruct(full, BF16),
            jax.ShapeDtypeStruct((f_size * c_size,) + gains.shape, F32),
        ],
        in_specs=[pl.BlockSpec(memory_space=pltpu.VMEM)] * (2 + len(shards)),
        out_specs=[pl.BlockSpec(memory_space=pltpu.HBM)] * 2 + [place],
        scratch_shapes=[pltpu.SemaphoreType.DMA]
        + GATHER_SEMS
        + weight_sems(f_size, c_size, len(shards))
        + [pltpu.SemaphoreType.DMA((f_size * c_size - 1,))] * 2
        + [pltpu.SemaphoreType.DMA],
        compiler_params=pltpu.CompilerParams(
            collective_id=ident, has_side_effects=True, vmem_limit_bytes=32 << 20
        ),
        name="startup",
    )(rows, gains, *shards)


def whole(shape, column=None):
    zeros = (0,) * (len(shape) - 1)
    return pl.BlockSpec(shape, lambda i: zeros + (column or 0,), pipeline_mode=pl.Buffered(1))


def remote_params(ident, megabytes):
    return pltpu.CompilerParams(
        collective_id=ident, has_side_effects=True, vmem_limit_bytes=megabytes << 20, dimension_semantics=("arbitrary",)
    )


def project_kernel(layout, x_ref, gain_ref, w_ref, normed_ref, forget_ref, items_ref):
    seq_count, groups, width, places = layout
    x = x_ref[0].astype(F32)
    normed = (x * lax.rsqrt(jnp.mean(x * x, axis=1, keepdims=True) + epsilon) * gain_ref[...]).astype(BF16)
    normed_ref[0] = normed
    inner = groups * width
    rows = x.shape[0] // seq_count
    count = items_ref.shape[0]
    for kind in range(3):
        value = dot(normed, w_ref[:, kind * inner : (kind + 1) * inner], NN).astype(BF16)
        for slot, (s, g) in enumerate(places):
            piece = value[s * rows : (s + 1) * rows, g * width : (g + 1) * width]
            items_ref[slot % count, slot // count, kind] = piece
    forget_ref[0] = dot(normed, w_ref[:, 3 * inner :], NN)


def project(x_all, gain, full_one, layout, item_count, ctx_size):
    seq_count, groups, width, places = layout
    tp_size, rows, model_width = x_all.shape
    local = rows // seq_count
    item = jax.ShapeDtypeStruct((item_count, ctx_size, 3, tp_size * local, width), BF16)
    columns = full_one.shape[1]
    block = pl.BlockSpec((1, rows, model_width), lambda t: (t, 0, 0))
    return pl.pallas_call(
        functools.partial(project_kernel, layout),
        grid=(tp_size,),
        out_shape=[
            jax.ShapeDtypeStruct(x_all.shape, BF16),
            jax.ShapeDtypeStruct((tp_size, rows, LANES), F32),
            item,
        ],
        in_specs=[
            block,
            pl.BlockSpec((1, model_width), lambda t: (0, 0)),
            pl.BlockSpec((model_width, columns), lambda t: (0, 0), pipeline_mode=pl.Buffered(1)),
        ],
        out_specs=[
            block,
            pl.BlockSpec((1, rows, LANES), lambda t: (t, 0, 0)),
            pl.BlockSpec((item_count, ctx_size, 3, local, width), lambda t: (0, 0, 0, t, 0)),
        ],
        compiler_params=pltpu.CompilerParams(vmem_limit_bytes=48 << 20, dimension_semantics=("arbitrary",)),
        cost_estimate=pl.CostEstimate(
            flops=2 * x_all.size * columns, bytes_accessed=4 * x_all.size, transcendentals=0
        ),
        name="project",
    )(x_all, gain, full_one)


def out_kernel(layout, x_ref, gate_ref, w_ref, gain_ref, items, shard_ref, *refs):
    seq_count, groups, width, places = layout
    hidden_ref, normed_ref, attended_ref, mixed_ref, full_ref = refs[:5]
    buffers, sems = refs[5:9], refs[9:13]
    count = items.shape[0]
    me, sibling, across, diagonal = tp_places()
    greet_all([{"tp": sibling}, {"tp": across}] + group_peers())
    gather = WeightGather((shard_ref,), full_ref, refs[13:])
    gather.begin()
    tp_size, rows, _ = gate_ref.shape
    local = rows // seq_count

    def mix(t, _):
        here = pl.ds(pl.multiple_of(t * local, local), local)
        for slot, (s, g) in enumerate(places[: seq_count * groups]):
            there = (t, pl.ds(s * local, local), pl.ds(g * width, width))
            value = items[slot % count, slot // count, here]
            attended_ref[there] = value
            mixed_ref[there] = (value.astype(F32) * gate_ref[there]).astype(BF16)
        return 0

    lax.fori_loop(0, tp_size, mix, 0)
    size = rows // SUM_CHUNKS

    def span(chunk):
        return pl.ds(pl.multiple_of(chunk * size, size), size)

    def partial(slot, chunk):
        return dot(mixed_ref[slot, span(chunk)], w_ref[...], NT)

    def finish(chunk, total):
        hidden = x_ref[span(chunk)].astype(F32) + total
        hidden_ref[span(chunk)] = hidden
        inverse = lax.rsqrt(jnp.mean(hidden * hidden, axis=1, keepdims=True) + epsilon)
        normed_ref[span(chunk)] = (hidden * inverse * gain_ref[...]).astype(BF16)

    def between(phase):
        if phase < 3:
            gather.advance(phase)
        else:
            for hop in range(3, gather.c_size):
                gather.advance(hop)

    scatter_loop(buffers, sems, partial, finish, between=between)
    gather.end()


def out_project(x, gate, full_out, gain, items, shard, layout, f_size, c_size, ident):
    seq_count, groups, width, places = layout
    rows, model_width = x.shape
    inner = groups * width
    tp_size = gate.shape[0]
    return pl.pallas_call(
        functools.partial(out_kernel, layout),
        grid=(1,),
        out_shape=[
            jax.ShapeDtypeStruct(x.shape, F32),
            jax.ShapeDtypeStruct(x.shape, BF16),
            jax.ShapeDtypeStruct(gate.shape, BF16),
            jax.ShapeDtypeStruct(gate.shape, BF16),
            jax.ShapeDtypeStruct((model_width, shard.shape[1]), BF16),
        ],
        in_specs=[
            whole(x.shape),
            whole(gate.shape),
            whole((model_width, inner), 0),
            whole(gain.shape),
            whole(items.shape),
            whole(shard.shape),
        ],
        out_specs=[
            whole(x.shape),
            whole(x.shape),
            whole(gate.shape),
            whole(gate.shape),
            pl.BlockSpec(memory_space=pl.ANY),
        ],
        scratch_shapes=scatter_buffers(rows, model_width)
        + SCATTER_SEMS
        + weight_sems(f_size, c_size, 1),
        compiler_params=remote_params(ident, 48),
        cost_estimate=pl.CostEstimate(
            flops=2 * gate.size * model_width, bytes_accessed=100 << 20, transcendentals=0
        ),
        name="out_project",
    )(x, gate, full_out, gain, items, shard)


def mlp_kernel(
    normed_ref, grad_hbm, gate_hbm, down_hbm, all_ref, inner_hbm, pair_hbm, table, inner_ref, pair_ref, *refs
):
    grad_ref, both_w, down_w, fetch_sem, out_sem = refs[:5]
    sems = refs[5:]
    fetch = Fetch([(gate_hbm, both_w), (grad_hbm, grad_ref), (down_hbm, down_w)], fetch_sem)
    me, sibling, across, diagonal = tp_places()
    greet((sibling, across))
    table[0] = normed_ref[...]
    rows, hidden = table.shape[1] // CHUNKS, down_w.shape[1]
    tile = min(hidden, 512)

    def writing(n, slot, chunk):
        here = (slot, pl.ds(pl.multiple_of(chunk * rows, rows), rows))
        source, target = ((inner_ref, inner_hbm), (pair_ref, pair_hbm), (table, all_ref))[n]
        return pltpu.make_async_copy(source.at[here], target.at[here], out_sem.at[n, slot, chunk])

    def compute(slot, chunk):
        spot = pl.ds(pl.multiple_of(chunk * rows, rows), rows)
        normed, grad = table[slot, spot], grad_ref[slot, spot]
        for start in range(0, hidden, tile):
            columns = pl.ds(start, tile)
            gate = dot(normed, both_w[:, columns], NN)
            up = dot(normed, both_w[:, pl.ds(hidden + start, tile)], NN)
            back = dot(grad, down_w[:, columns], NN)
            sig = 1.0 / (1.0 + jnp.exp(-gate))
            silu = gate * sig
            inner_ref[slot, spot, columns] = (silu * up).astype(BF16)
            pair_ref[slot, spot, columns] = (back * up * sig * (1.0 + gate * (1.0 - sig))).astype(BF16)
            pair_ref[slot, spot, pl.ds(hidden + start, tile)] = (back * silu).astype(BF16)
        for n in range(3):
            writing(n, slot, chunk).start()

    gather_loop(table, sems, compute, relative=True, ready=fetch.wait)
    for n in range(3):

        @pl.loop(0, 4 * CHUNKS)
        def _(step):
            writing(n, step // CHUNKS, lax.rem(step, CHUNKS)).wait()


def mlp(normed, grad_all, full_two, full_down, hidden, ident):
    tp_size, rows, model_width = grad_all.shape
    total = tp_size * rows
    place = pl.BlockSpec(memory_space=pl.ANY)
    inner, pair = (tp_size, rows, hidden), (tp_size, rows, 2 * hidden)
    dma = pltpu.SemaphoreType.DMA
    return pl.pallas_call(
        mlp_kernel,
        grid=(1,),
        out_shape=[
            jax.ShapeDtypeStruct(grad_all.shape, BF16),
            jax.ShapeDtypeStruct(inner, BF16),
            jax.ShapeDtypeStruct(pair, BF16),
        ],
        in_specs=[whole(normed.shape), place, place, place],
        out_specs=[place] * 3,
        scratch_shapes=[
            pltpu.VMEM(grad_all.shape, BF16),
            pltpu.VMEM(inner, BF16),
            pltpu.VMEM(pair, BF16),
            pltpu.VMEM(grad_all.shape, BF16),
            pltpu.VMEM((model_width, 2 * hidden), BF16),
            pltpu.VMEM((model_width, hidden), BF16),
            dma((3,)),
            dma((3, tp_size, CHUNKS)),
        ]
        + GATHER_SEMS,
        compiler_params=remote_params(ident, 56),
        cost_estimate=pl.CostEstimate(
            flops=6 * total * model_width * hidden, bytes_accessed=100 << 20, transcendentals=total * hidden
        ),
        name="mlp",
    )(normed, grad_all, full_two, full_down)


def mlp_back_kernel(
    pair_hbm, w_hbm, hidden_hbm, grad_hbm, gain_ref, sums_ref, out_ref, branch_ref, part_ref, sum_ref, *refs
):
    buffers, sems = refs[:4], refs[4:8]
    pair_ref, w_ref, hidden_ref, grad_ref, fetch_sem = refs[8:13]
    columns = pl.ds(0, w_ref.shape[1])
    fetch = Fetch(
        [
            (pair_hbm, pair_ref),
            (w_hbm.at[:, columns], w_ref),
            (hidden_hbm, hidden_ref),
            (grad_hbm, grad_ref),
        ],
        fetch_sem,
    )
    me, sibling, across, diagonal = tp_places()
    greet_all([{"tp": sibling}, {"tp": across}] + group_peers())
    weights = WeightSum(sums_ref, 0, sum_ref, refs[13:])
    weights.begin()
    fetch.wait()
    part_ref[...] = jnp.zeros_like(part_ref)
    size = hidden_ref.shape[0] // SUM_CHUNKS

    def span(chunk):
        return pl.ds(pl.multiple_of(chunk * size, size), size)

    def partial(slot, chunk):
        return dot(pair_ref[slot, span(chunk)], w_ref[...], NT)

    def finish(chunk, total):
        hidden = hidden_ref[span(chunk)]
        inverse = lax.rsqrt(jnp.mean(hidden * hidden, axis=1, keepdims=True) + epsilon)
        unit = hidden * inverse
        part_ref[...] += jnp.sum(total * unit, axis=0, keepdims=True)
        scaled = total * gain_ref[...]
        middle = jnp.mean(scaled * unit, axis=1, keepdims=True)
        grad = grad_ref[span(chunk)].astype(F32) + inverse * (scaled - unit * middle)
        out_ref[span(chunk)] = grad
        branch_ref[span(chunk)] = grad.astype(BF16)

    def between(phase):
        if phase < 3:
            weights.run_to(2 * phase - 2, 2 * phase)
        else:
            weights.run_to(4, weights.stages)

    scatter_loop(buffers, sems, partial, finish, relative=True, between=between)
    weights.end()


def mlp_back(pair, full_two, hidden_state, grad_out, gain, part, f_size, c_size, ident):
    tp_size, rows, wide = pair.shape
    model_width = hidden_state.shape[1]
    place = pl.BlockSpec(memory_space=pl.ANY)
    total = (part.shape[0] // (f_size * c_size), part.shape[1] // 2)
    return pl.pallas_call(
        mlp_back_kernel,
        grid=(1,),
        out_shape=[
            jax.ShapeDtypeStruct(hidden_state.shape, F32),
            jax.ShapeDtypeStruct(hidden_state.shape, BF16),
            jax.ShapeDtypeStruct(gain.shape, F32),
            jax.ShapeDtypeStruct(total, F32),
        ],
        in_specs=[
            place,
            place,
            place,
            place,
            whole(gain.shape),
            place,
        ],
        out_specs=[
            whole(hidden_state.shape),
            whole(hidden_state.shape),
            whole(gain.shape),
            whole(total),
        ],
        scratch_shapes=scatter_buffers(rows, model_width)
        + SCATTER_SEMS
        + [
            pltpu.VMEM(pair.shape, BF16),
            pltpu.VMEM((model_width, wide), BF16),
            pltpu.VMEM(hidden_state.shape, F32),
            pltpu.VMEM(grad_out.shape, BF16),
            pltpu.SemaphoreType.DMA((4,)),
        ]
        + sum_scratch(f_size, c_size, *total),
        compiler_params=remote_params(ident, 60),
        cost_estimate=pl.CostEstimate(
            flops=2 * pair.size * model_width, bytes_accessed=100 << 20, transcendentals=0
        ),
        name="mlp_back",
    )(pair, full_two, hidden_state, grad_out, gain, part)


def out_back_kernel(
    layout,
    branch_ref,
    w_ref,
    gate_ref,
    attended_ref,
    sums_ref,
    inner_hbm,
    grad_hbm,
    all_ref,
    logit_ref,
    items,
    sum_ref,
    part_hbm,
    *refs,
):
    seq_count, groups, width, places = layout
    table, grads, own_sem = refs[:3]
    sems = refs[3:9]
    inner_ref, grad_ref, part, fetch_sem, write_sem = refs[9:14]
    count = items.shape[0]
    me, sibling, across, diagonal = tp_places()
    greet_all([{"tp": sibling}, {"tp": across}] + group_peers())
    weights = WeightSum(sums_ref, sum_ref.shape[1], sum_ref, refs[14:])
    weights.begin()
    table[me] = branch_ref[...]
    tp_size, rows, _ = gate_ref.shape
    local, size = rows // seq_count, rows // CHUNKS
    model_width, hidden = part.shape
    tile = 2 * LANES
    tiles = model_width // tile
    fetches = []

    def begin_fetch():
        fetches.append(
            Fetch([(inner_hbm, inner_ref), (grad_hbm, grad_ref)], fetch_sem)
        )

    def compute(slot, chunk):
        spot = pl.ds(pl.multiple_of(chunk * size, size), size)
        mixed = dot(table[slot, spot], w_ref[...], NN)
        gate = gate_ref[slot, spot]
        scaled = mixed * gate
        grads[slot, spot] = scaled.astype(BF16)
        attended = attended_ref[slot, spot].astype(F32)
        logit_ref[slot, spot] = (scaled * attended * (1.0 - gate)).astype(BF16)

    def down_grad(n, _):
        columns = pl.ds(pl.multiple_of(n * tile, tile), tile)
        left = grad_ref[:, :, columns].reshape(tp_size * rows, tile)
        right = inner_ref[...].reshape(tp_size * rows, hidden)
        part[columns] = dot(left, right, TN).astype(BF16)
        return 0

    last = weights.stages
    middle = max(1, last - 4)

    def stage(n):
        weights.run(n)
        lax.fori_loop(n * tiles // last, (n + 1) * tiles // last, down_grad, 0)

    def between():
        fetches[0].wait()
        for n in range(middle):
            stage(n)

    gather_loop(table, sems, compute, between=between, ready=begin_fetch)
    copies = [
        pltpu.make_async_copy(table, all_ref, own_sem),
        pltpu.make_async_copy(part, part_hbm, write_sem),
    ]
    copies[0].start()

    def deal(t, _):
        here = pl.ds(pl.multiple_of(t * local, local), local)
        for slot, (s, g) in enumerate(places):
            piece = grads[t, pl.ds(s * local, local), pl.ds(g * width, width)]
            items[slot % count, slot // count, here] = piece
        return 0

    lax.fori_loop(0, tp_size, deal, 0)
    for n in range(middle, last):
        stage(n)
    for copy in copies[1:]:
        copy.start()
    for copy in copies:
        copy.wait()
    weights.end()


def out_back(
    branch, full_out, gate, attended, part, inner_act, grad_all, layout, item_count, f_size, ctx_size, ident
):
    seq_count, groups, width, places = layout
    rows, model_width = branch.shape
    tp_size, _, inner = gate.shape
    item = (item_count, ctx_size, tp_size * rows // seq_count, width)
    table = (tp_size, rows, model_width)
    down = (model_width, inner_act.shape[2])
    total = (part.shape[0] // (f_size * ctx_size), part.shape[1] // 2)
    place = pl.BlockSpec(memory_space=pl.ANY)
    dma = pltpu.SemaphoreType.DMA
    return pl.pallas_call(
        functools.partial(out_back_kernel, layout),
        grid=(1,),
        out_shape=[
            jax.ShapeDtypeStruct(table, BF16),
            jax.ShapeDtypeStruct(gate.shape, BF16),
            jax.ShapeDtypeStruct(item, BF16),
            jax.ShapeDtypeStruct(total, F32),
            jax.ShapeDtypeStruct(down, BF16),
        ],
        in_specs=[
            whole(branch.shape),
            whole((model_width, inner), 0),
            whole(gate.shape),
            whole(attended.shape),
            place,
            place,
            place,
        ],
        out_specs=[place, whole(gate.shape), whole(item), whole(total), place],
        scratch_shapes=[pltpu.VMEM(table, BF16), pltpu.VMEM(gate.shape, BF16), dma]
        + GATHER_SEMS
        + [
            pltpu.VMEM(inner_act.shape, BF16),
            pltpu.VMEM(table, BF16),
            pltpu.VMEM(down, BF16),
            dma((2,)),
            dma,
        ]
        + sum_scratch(f_size, ctx_size, *total),
        compiler_params=remote_params(ident, 60),
        cost_estimate=pl.CostEstimate(
            flops=2 * gate.size * model_width, bytes_accessed=100 << 20, transcendentals=0
        ),
        name="out_back",
    )(branch, full_out, gate, attended, part, inner_act, grad_all)


def assemble_kernel(layout, items, out_ref):
    seq_count, groups, width, places = layout
    count, local = items.shape[0], items.shape[3]
    inner = groups * width
    for slot, (s, g) in enumerate(places[: seq_count * groups]):
        for kind in range(3):
            columns = pl.ds(kind * inner + g * width, width)
            out_ref[0, pl.ds(s * local, local), columns] = items[slot % count, slot // count, kind]


def assemble(items, layout, tp_size):
    seq_count, groups, width, places = layout
    count, ctx_size, kinds, ctx_rows, _ = items.shape
    local = ctx_rows // tp_size
    shape = (tp_size, seq_count * local, kinds * groups * width)
    return pl.pallas_call(
        functools.partial(assemble_kernel, layout),
        grid=(tp_size,),
        out_shape=jax.ShapeDtypeStruct(shape, BF16),
        in_specs=[pl.BlockSpec((count, ctx_size, kinds, local, width), lambda t: (0, 0, 0, t, 0))],
        out_specs=pl.BlockSpec((1,) + shape[1:], lambda t: (t, 0, 0)),
        compiler_params=pltpu.CompilerParams(vmem_limit_bytes=32 << 20, dimension_semantics=("arbitrary",)),
        cost_estimate=pl.CostEstimate(flops=0, bytes_accessed=16 << 20, transcendentals=0),
        name="assemble",
    )(items)


def last_kernel(
    qkv_hbm,
    logit_hbm,
    forget_hbm,
    qkv_w_hbm,
    gate_w_hbm,
    x_hbm,
    grad_hbm,
    gain_ref,
    part_ref,
    extra_ref,
    out_ref,
    sum_ref,
    vector_ref,
    *refs,
):
    buffers, sems, (mine, near_in, group_in) = refs[:4], refs[4:8], refs[8:11]
    vector_sems = refs[11:15]
    qkv_ref, logit_ref, forget_ref, qkv_w, gate_w, x_ref, grad_ref, fetch_sem = refs[15:23]
    inner = gate_w.shape[1]
    fetch = Fetch(
        [
            (qkv_hbm, qkv_ref),
            (qkv_w_hbm, qkv_w),
            (logit_hbm, logit_ref),
            (forget_hbm, forget_ref),
            (gate_w_hbm.at[:, pl.ds(inner, inner)], gate_w),
            (x_hbm, x_ref),
            (grad_hbm, grad_ref),
        ],
        fetch_sem,
    )
    me, sibling, across, diagonal = tp_places()
    others = group_peers()
    greet_all([{"tp": sibling}, {"tp": across}, {"tp": diagonal}] + others)
    weights = WeightSum(part_ref, 0, sum_ref, refs[23:])
    weights.begin()
    fetch.wait()
    wide = qkv_ref.shape[2]
    mine[...] = extra_ref[...]
    size = x_ref.shape[0] // SUM_CHUNKS

    def span(chunk):
        return pl.ds(pl.multiple_of(chunk * size, size), size)

    def partial(slot, chunk):
        value = dot(qkv_ref[slot, span(chunk)], qkv_w[:, :wide], NT)
        value = value + dot(logit_ref[slot, span(chunk)], gate_w[...], NT)
        return value + dot(forget_ref[slot, span(chunk)], qkv_w[:, wide:], NT)

    def finish(chunk, total):
        x = x_ref[span(chunk)].astype(F32)
        inverse = lax.rsqrt(jnp.mean(x * x, axis=1, keepdims=True) + epsilon)
        unit = x * inverse
        mine[0:1] += jnp.sum(total * unit, axis=0, keepdims=True)
        scaled = total * gain_ref[...]
        middle = jnp.mean(scaled * unit, axis=1, keepdims=True)
        out_ref[span(chunk)] = (grad_ref[span(chunk)] + inverse * (scaled - unit * middle)).astype(BF16)

    stages = weights.stages
    late = max(4, stages - 4)

    def between(phase):
        if phase < 3:
            weights.run_to(2 * phase - 2, 2 * phase)
        else:
            weights.run_to(4, late)

    scatter_loop(buffers, sems, partial, finish, between=between)
    near_send, near_recv, group_send, group_recv = vector_sems
    copies = []
    for n, peer in enumerate((sibling, across, diagonal)):
        copies.append(sending(mine, near_in.at[n], near_send.at[n], near_recv.at[n], peer))
        copies[-1].start()
    weights.run_to(late, late + 2)
    for copy in copies:
        copy.wait()
    vector_ref[...] = mine[...] + near_in[0] + near_in[1] + near_in[2]
    mine[...] = vector_ref[...]
    copies = []
    for n, peer in enumerate(others):
        copies.append(moving(mine, group_in.at[n], group_send.at[n], group_recv.at[n], peer))
        copies[-1].start()
    weights.run_to(late + 2, stages)
    for n, copy in enumerate(copies):
        copy.wait()
        vector_ref[...] += group_in[n]
    weights.end()


def last(grad_qkv, grad_logit, grad_forget, full_one, full_out, x, grad_hidden, gain, part, extra, f_size, c_size, ident):
    rows, model_width = x.shape
    wide, inner = grad_qkv.shape[2], grad_logit.shape[2]
    shard, columns = part.shape[0] // (f_size * c_size), part.shape[1]
    dma = pltpu.SemaphoreType.DMA
    place = pl.BlockSpec(memory_space=pl.ANY)
    return pl.pallas_call(
        last_kernel,
        grid=(1,),
        out_shape=[
            jax.ShapeDtypeStruct(x.shape, BF16),
            jax.ShapeDtypeStruct((shard, columns), F32),
            jax.ShapeDtypeStruct(extra.shape, F32),
        ],
        in_specs=[
            place,
            place,
            place,
            place,
            place,
            place,
            place,
            whole(gain.shape),
            place,
            whole(extra.shape),
        ],
        out_specs=[whole(x.shape), whole((shard, columns)), whole(extra.shape)],
        scratch_shapes=scatter_buffers(rows, model_width)
        + SCATTER_SEMS
        + [
            pltpu.VMEM(extra.shape, F32),
            pltpu.VMEM((3,) + extra.shape, F32),
            pltpu.VMEM((f_size * c_size - 1,) + extra.shape, F32),
        ]
        + [dma((3,))] * 2
        + [dma((f_size * c_size - 1,))] * 2
        + [
            pltpu.VMEM(grad_qkv.shape, BF16),
            pltpu.VMEM(grad_logit.shape, BF16),
            pltpu.VMEM(grad_forget.shape, BF16),
            pltpu.VMEM(full_one.shape, BF16),
            pltpu.VMEM((model_width, inner), BF16),
            pltpu.VMEM(x.shape, BF16),
            pltpu.VMEM(x.shape, F32),
            dma((7,)),
        ]
        + sum_scratch(f_size, c_size, shard, columns),
        compiler_params=remote_params(ident, 60),
        cost_estimate=pl.CostEstimate(
            flops=8 * rows * model_width * (wide + inner + LANES), bytes_accessed=100 << 20, transcendentals=0
        ),
        name="last",
    )(grad_qkv, grad_logit, grad_forget, full_one, full_out, x, grad_hidden, gain, part, extra)


def per_device(
    layer_input,
    lengths,
    attn_gain,
    w_query,
    w_key,
    w_value,
    w_forget,
    forget_bias,
    w_gate_out,
    w_out,
    mlp_gain,
    w_gate,
    w_up,
    w_down,
    cotangent,
):
    local_rows, seq_count, model_width = layer_input.shape
    head_count = forget_bias.shape[0]
    inner_width = w_query.shape[1]
    hidden = w_gate.shape[1]
    head_size = inner_width // head_count
    tp_size = lax.axis_size("tp")
    ctx_size = lax.axis_size("ctx")
    shard_count = lax.axis_size("fsdp") * ctx_size
    ctx_rows = local_rows * tp_size
    seq_len = ctx_rows * ctx_size
    all_rows = seq_count * ctx_rows
    ctx_index = lax.axis_index("ctx")
    tp_index = lax.axis_index("tp")
    shard_index = lax.axis_index("fsdp") * ctx_size + ctx_index

    pair = LANES // head_size
    groups = head_count // pair
    width = pair * head_size
    item_count = pl.cdiv(seq_count * groups, ctx_size)
    used = seq_count * groups

    def place(slot):
        slot = slot % used
        return (slot // groups + slot % groups) % seq_count, slot % groups

    places = tuple(place(slot) for slot in range(ctx_size * item_count))
    layout = (seq_count, groups, width, places)

    fsdp_size = lax.axis_size("fsdp")
    wide_forget = jnp.pad(w_forget, ((0, 0), (0, LANES - head_count)))
    edge = 3 * inner_width
    input_rows = layer_input.transpose(1, 0, 2).reshape(seq_count * local_rows, model_width)
    shard_rows = model_width // shard_count
    own_gains = jnp.stack([attn_gain, mlp_gain]).astype(F32)
    own_gains = jnp.pad(own_gains, ((0, 6), (0, -shard_rows % LANES)))
    input_all, full_one, gains = startup(
        input_rows, own_gains, (w_query, w_key, w_value, wide_forget), fsdp_size, ctx_size, 1
    )
    gain_one = gains[:, 0, :shard_rows].reshape(1, model_width)
    gain_two = gains[:, 1, :shard_rows].reshape(1, model_width)

    def by_sequence(rows):
        return rows.transpose(1, 0, 2).reshape(seq_count * local_rows, model_width)

    def by_position(rows):
        return rows.reshape(seq_count, local_rows, model_width).transpose(1, 0, 2)

    local_pos = (ctx_index * tp_size + tp_index) * local_rows + jnp.arange(
        local_rows, dtype=jnp.int32
    )
    valid_rows = (local_pos[None, :] < lengths[:, None]).astype(F32)
    valid_rows = valid_rows.reshape(seq_count * local_rows, 1)
    ctx_pos = ctx_index * ctx_rows + jnp.arange(ctx_rows, dtype=jnp.int32)
    ctx_pos = ctx_pos.reshape(tp_size, 1, local_rows)
    ctx_valid = (ctx_pos < lengths[None, :, None]).astype(F32)

    grad_out = (valid_rows * by_sequence(cotangent).astype(F32)).astype(BF16)
    normed_one, forget_rows, items = project(
        input_all, gain_one, full_one, layout, item_count, ctx_size
    )
    normed_flat = normed_one.reshape(all_rows, model_width)
    forget_logit = forget_rows.reshape(all_rows, LANES)[:, :head_count].T
    forget_logit = forget_logit + forget_bias.astype(F32)[:, None]
    forget_logit = forget_logit.reshape(head_count, tp_size, seq_count, local_rows)
    log_forget = (ctx_valid[None] * jax.nn.log_sigmoid(forget_logit)).astype(BF16)

    cut = log_forget.astype(F32).reshape(groups, pair, tp_size, seq_count, local_rows)
    picked = jnp.stack([cut[g, :, :, s] for s, g in places])
    picked = picked.reshape(ctx_size, item_count, pair, ctx_rows).transpose(1, 0, 2, 3)
    picked = jnp.pad(picked, ((0, 0), (0, 0), (0, 8 - pair), (0, 0)))
    attended_items, qkv, full_two, full_out, grad_all, exact, lse, decay, out_gate = context(
        items,
        picked,
        (w_gate, w_up, w_out, w_gate_out),
        grad_out,
        normed_one,
        fsdp_size,
        head_size,
        7,
    )
    hidden_state, normed_two, attended, mixed, down_w = out_project(
        input_rows,
        out_gate,
        full_out,
        gain_two,
        attended_items,
        w_down,
        layout,
        fsdp_size,
        ctx_size,
        2,
    )
    normed_two_all, inner_act, grad_pair = mlp(normed_two, grad_all, full_two, down_w, hidden, 3)
    normed_two_flat = normed_two_all.reshape(all_rows, model_width)
    grad_pair_flat = grad_pair.reshape(all_rows, 2 * hidden)

    gate_up_part = dot(normed_two_flat, grad_pair_flat, TN).astype(BF16)
    grad_hidden, branch, mlp_gain_part, gate_sum = mlp_back(
        grad_pair, full_two, hidden_state, grad_out, gain_two, gate_up_part, fsdp_size, ctx_size, 4
    )
    branch_all, grad_gate_logit, grads, up_sum, down_part = out_back(
        branch,
        full_out,
        out_gate,
        attended,
        gate_up_part,
        inner_act,
        grad_all,
        layout,
        item_count,
        fsdp_size,
        ctx_size,
        5,
    )
    branch_flat = branch_all.reshape(all_rows, model_width)
    logit_flat = grad_gate_logit.reshape(all_rows, inner_width)

    out_part = jnp.concatenate(
        [
            dot(branch_flat, mixed.reshape(all_rows, inner_width), TN).astype(BF16),
            dot(normed_flat, logit_flat, TN).astype(BF16),
        ],
        axis=1,
    )
    grad_items, forget_items, down_sum, out_sum, feedforward = context_back(
        grads,
        qkv,
        exact,
        lse,
        decay,
        down_part,
        out_part,
        inner_act,
        down_w,
        fsdp_size,
        head_size,
        8,
    )
    output = (valid_rows * (hidden_state + feedforward.astype(F32))).astype(BF16)
    forget_back = forget_items[:, :, :pair].astype(BF16).transpose(1, 0, 2, 3)
    forget_back = forget_back.reshape(ctx_size * item_count, pair, tp_size, local_rows)
    slots = {place(slot): slot for slot in range(used)}
    forget_back = jnp.stack(
        [
            jnp.stack([forget_back[slots[s, g]] for s in range(seq_count)], axis=2)
            for g in range(groups)
        ]
    ).reshape(head_count, tp_size, seq_count, local_rows)
    grad_forget_logit = forget_back.astype(F32) * ctx_valid[None] * jax.nn.sigmoid(-forget_logit)
    grad_forget_logit = grad_forget_logit.astype(BF16).reshape(head_count, all_rows)
    bias_part = jnp.sum(grad_forget_logit.astype(F32), axis=1)
    grad_forget_rows = jnp.pad(grad_forget_logit, ((0, LANES - head_count), (0, 0))).T
    grad_qkv = assemble(grad_items, layout, tp_size)
    grad_qkvf = jnp.concatenate([grad_qkv.reshape(all_rows, edge), grad_forget_rows], axis=1)
    bias_full = lax.dynamic_update_slice(
        jnp.zeros((1, model_width), F32), bias_part[None], (0, tp_index * head_count)
    )
    extra = jnp.concatenate(
        [jnp.zeros_like(bias_full), mlp_gain_part, bias_full, jnp.zeros((5, model_width), F32)]
    )
    input_grad, qkv_sum, vectors = last(
        grad_qkv,
        grad_gate_logit,
        grad_forget_rows.reshape(tp_size, -1, LANES),
        full_one,
        full_out,
        input_rows,
        grad_hidden,
        gain_one,
        dot(normed_flat, grad_qkvf, TN).astype(BF16),
        extra,
        fsdp_size,
        ctx_size,
        6,
    )
    gain_one_sum, gain_two_sum, bias_sum = vectors[0], vectors[1], vectors[2]
    attn_gain_grad = lax.dynamic_slice_in_dim(gain_one_sum, shard_index * shard_rows, shard_rows, 0)
    mlp_gain_grad = lax.dynamic_slice_in_dim(gain_two_sum, shard_index * shard_rows, shard_rows, 0)
    forget_bias_grad = lax.dynamic_slice_in_dim(bias_sum, tp_index * head_count, head_count, 0)
    wide = inner_width
    return (
        by_position(output),
        by_position(input_grad),
        attn_gain_grad,
        qkv_sum[:, :wide],
        qkv_sum[:, wide : 2 * wide],
        qkv_sum[:, 2 * wide : 3 * wide],
        qkv_sum[:, 3 * wide : 3 * wide + head_count],
        forget_bias_grad,
        out_sum[:, wide:],
        out_sum[:, :wide],
        mlp_gain_grad,
        gate_sum,
        up_sum,
        down_sum,
    )


def solution(mesh):
    rows = P(("ctx", "tp"), "fsdp", None)
    matrix = P(("fsdp", "ctx"), "tp")
    vector = P(("fsdp", "ctx"))
    return jax.shard_map(
        per_device,
        mesh=mesh,
        in_specs=(
            rows,
            P("fsdp"),
            vector,
            matrix,
            matrix,
            matrix,
            matrix,
            P("tp"),
            matrix,
            matrix,
            vector,
            matrix,
            matrix,
            matrix,
            rows,
        ),
        out_specs=(
            rows,
            rows,
            vector,
            matrix,
            matrix,
            matrix,
            matrix,
            P("tp"),
            matrix,
            matrix,
            vector,
            matrix,
            matrix,
            matrix,
        ),
        check_vma=False,
    )
```

```python
import functools

import jax
import jax.numpy as jnp
from jax import lax
from jax.experimental import pallas as pl
from jax.experimental.pallas import tpu as pltpu
from jax.sharding import PartitionSpec as P

F32 = jnp.float32
BF16 = jnp.bfloat16
LANES = 128
MESH = pl.DeviceIdType.MESH
epsilon = 1e-06
masked_score = -1e30
NT = (((1,), (1,)), ((), ()))
NN = (((1,), (0,)), ((), ()))
TN = (((0,), (0,)), ((), ()))


def dot(left, right, dims):
    return lax.dot_general(left, right, dims, preferred_element_type=F32)


def of_head(block, head, head_size, ones_at=None):
    lane = lax.broadcasted_iota(jnp.int32, block.shape, 1)
    out = jnp.where(lane // head_size == head, block, jnp.zeros_like(block))
    if ones_at is not None:
        out = jnp.where(lane == ones_at, jnp.ones_like(block), out)
    return out


def spare_lane(head, head_size):
    return ((head + 1) % 2) * head_size


def attend_item(qkv, decay, out, exact, lse, heads, head_size):
    count, _, block, width = qkv.shape
    scale = head_size**-0.5
    row = lax.broadcasted_iota(jnp.int32, (block, block), 0)
    column = lax.broadcasted_iota(jnp.int32, (block, block), 1)
    causal = column <= row

    def query_block(i, _):
        query = qkv[i, 0]
        lanes = pl.ds(pl.multiple_of(i * block, block), block)
        result = jnp.zeros((block, width), F32)
        for head in range(heads):
            query_head = of_head(query, head, head_size)

            def step(j, carry, masked):
                top, total, acc = carry
                keys = pl.ds(pl.multiple_of(j * block, block), block)
                score = dot(query_head, qkv[j, 1], NT) * scale
                score = score - decay[head : head + 1, keys]
                if masked:
                    score = jnp.where(causal, score, masked_score)
                new_top = jnp.maximum(top, jnp.max(score, axis=1, keepdims=True))
                prob = jnp.exp(score - new_top)
                shrink = jnp.exp(top - new_top)
                total = total * shrink + jnp.sum(prob, axis=1, keepdims=True)
                acc = acc * shrink + dot(prob.astype(BF16), qkv[j, 2], NN)
                return new_top, total, acc

            carry = (
                jnp.full((block, 1), masked_score, F32),
                jnp.zeros((block, 1), F32),
                jnp.zeros((block, width), F32),
            )
            carry = lax.fori_loop(0, i, lambda j, c: step(j, c, False), carry)
            top, total, acc = step(i, carry, True)
            lane = lax.broadcasted_iota(jnp.int32, acc.shape, 1)
            result = jnp.where(lane // head_size == head, acc / total, result)
            stat = jnp.broadcast_to(top + jnp.log(total), (block, LANES)).T
            lse[head : head + 1, lanes] = stat[0:1]
        exact[i] = result
        out[i] = result.astype(BF16)
        return 0

    lax.fori_loop(0, count, query_block, 0)


def attend_item_back(qkv, grads, exact, lse, decay, dqkv, change, dq_acc, delta, heads, head_size):
    count, _, block, width = qkv.shape
    scale = head_size**-0.5
    row = lax.broadcasted_iota(jnp.int32, (block, block), 0)
    column = lax.broadcasted_iota(jnp.int32, (block, block), 1)
    causal = row <= column
    dq_acc[...] = jnp.zeros_like(dq_acc)
    change[...] = jnp.zeros_like(change)

    def prepare(i, _):
        lanes = pl.ds(pl.multiple_of(i * block, block), block)
        product = grads[i].astype(F32) * exact[i]
        lane = lax.broadcasted_iota(jnp.int32, product.shape, 1)
        for head in range(heads):
            part = jnp.where(lane // head_size == head, product, 0.0)
            part = jnp.sum(part, axis=1, keepdims=True)
            delta[head : head + 1, lanes] = jnp.broadcast_to(part, (block, LANES)).T[0:1]
        return 0

    lax.fori_loop(0, count, prepare, 0)

    def key_block(j, _):
        keys = pl.ds(pl.multiple_of(j * block, block), block)
        key = qkv[j, 1]
        value = qkv[j, 2]
        value_total = jnp.zeros((block, width), F32)
        key_total = jnp.zeros((block, width), F32)
        for head in range(heads):
            spare = spare_lane(head, head_size)
            key_ones = of_head(key, head, head_size, spare)
            fall = jnp.broadcast_to(decay[head : head + 1, keys], (LANES, block)).T[:, 0:1]

            def step(i, carry, masked):
                value_acc, key_acc = carry
                lanes = pl.ds(pl.multiple_of(i * block, block), block)
                query = qkv[i, 0]
                grad = of_head(grads[i], head, head_size)
                score = dot(key, of_head(query, head, head_size), NT) * scale
                score = score - fall - lse[head : head + 1, lanes]
                if masked:
                    score = jnp.where(causal, score, masked_score)
                prob = jnp.exp(score)
                grad_prob = dot(value, grad, NT)
                grad_score = prob * (grad_prob - delta[head : head + 1, lanes])
                grad_score = grad_score.astype(BF16)
                value_acc = value_acc + dot(prob.astype(BF16), grad, NN)
                query_ones = of_head(query, head, head_size, spare)
                key_acc = key_acc + dot(grad_score, query_ones, NN)
                dq_acc[head, i] += dot(grad_score, key_ones, TN)
                return value_acc, key_acc

            zero = jnp.zeros((block, width), F32)
            carry = step(j, (zero, zero), True)
            carry = lax.fori_loop(j + 1, count, lambda i, c: step(i, c, False), carry)
            value_acc, key_acc = carry
            value_total = value_total + value_acc
            lane = lax.broadcasted_iota(jnp.int32, key_acc.shape, 1)
            key_total = jnp.where(lane // head_size == head, key_acc, key_total)
            change[head : head + 1, keys] -= key_acc.T[spare : spare + 1]
        dqkv[j, 1] = (key_total * scale).astype(BF16)
        dqkv[j, 2] = value_total.astype(BF16)
        return 0

    lax.fori_loop(0, count, key_block, 0)

    def finish(i, _):
        lanes = pl.ds(pl.multiple_of(i * block, block), block)
        total = jnp.zeros((block, width), F32)
        for head in range(heads):
            spare = spare_lane(head, head_size)
            part = dq_acc[head, i]
            lane = lax.broadcasted_iota(jnp.int32, part.shape, 1)
            total = jnp.where(lane // head_size == head, part, total)
            change[head : head + 1, lanes] += part.T[spare : spare + 1]
        dqkv[i, 0] = (total * scale).astype(BF16)
        return 0

    lax.fori_loop(0, count, finish, 0)


def triangle(upward):
    row = lax.broadcasted_iota(jnp.int32, (LANES, LANES), 0)
    column = lax.broadcasted_iota(jnp.int32, (LANES, LANES), 1)
    keep = (row <= column) if upward else (row >= column)
    return jnp.where(keep, 1.0, 0.0).astype(BF16)


def exact_product(values, matrix):
    high = values.astype(BF16)
    rest = values - high.astype(F32)
    middle = rest.astype(BF16)
    low = (rest - middle.astype(F32)).astype(BF16)
    return dot(high, matrix, NN) + dot(middle, matrix, NN) + dot(low, matrix, NN)


def ctx_sending(source, target, send_sem, recv_sem, peer):
    return pltpu.make_async_remote_copy(
        src_ref=source,
        dst_ref=target,
        send_sem=send_sem,
        recv_sem=recv_sem,
        device_id={"ctx": peer},
        device_id_type=MESH,
    )


def ctx_greet(size):
    me = lax.axis_index("ctx")
    barrier = pltpu.get_barrier_semaphore()
    for step in range(1, size):
        peer = lax.rem(me + step, size)
        pl.semaphore_signal(barrier, inc=1, device_id={"ctx": peer}, device_id_type=MESH)
    pl.semaphore_wait(barrier, size - 1)
    return me


class Exchange:
    def __init__(self, me, size, source, target, sems):
        self.me, self.size, self.source, self.target = me, size, source, target
        self.send_sem, self.recv_sem, self.own_sem = sems

    def own(self, item):
        return pltpu.make_async_copy(
            self.source.at[item, self.me], self.target.at[item, self.me], self.own_sem.at[item]
        )

    def copy(self, item, step):
        peer = lax.rem(self.me + step, self.size)
        return ctx_sending(
            self.source.at[item, peer],
            self.target.at[item, self.me],
            self.send_sem.at[item, step],
            self.recv_sem.at[item, step],
            peer,
        )

    def start(self, item):
        for step in range(1, self.size):
            self.copy(item, step).start()
        self.own(item).start()

    def arrive(self, item):
        self.own(item).wait()
        for step in range(1, self.size):
            self.copy(item, step).wait_recv()

    def drain(self, item):
        for step in range(1, self.size):
            self.copy(item, step).wait_send()


def exchange_sems(items, size):
    return [
        pltpu.SemaphoreType.DMA((items, size)),
        pltpu.SemaphoreType.DMA((items, size)),
        pltpu.SemaphoreType.DMA((items,)),
    ]


def context_kernel(
    heads,
    head_size,
    items_ref,
    forget_ref,
    gate_ref,
    up_ref,
    out_w_ref,
    gate_out_ref,
    rows_ref,
    normed_hbm,
    back_ref,
    qkv_ref,
    full_ref,
    full_out_ref,
    table_ref,
    exact_ref,
    lse_ref,
    decay_ref,
    out_gate_ref,
    *refs,
):
    qkv, forget, out, normed, gate_w, fetch_sem, save_sem = refs[:7]
    sems = refs[7:]
    count, size, _, block, width = items_ref.shape
    tp, sibling, across, diagonal = tp_places()
    greet_all([{"tp": sibling}, {"tp": across}] + group_peers())
    me = lax.axis_index("ctx")
    gathers = (
        WeightGather((out_w_ref, gate_out_ref), full_out_ref, sems[9:14]),
        WeightGather((gate_ref, up_ref), full_ref, sems[14:19]),
    )
    rows = RowGather(rows_ref, table_ref, sems[19:])
    fetch = Fetch([(normed_hbm, normed)], fetch_sem)
    forgets = Exchange(me, size, forget_ref, forget, sems[0:3])
    inputs = Exchange(me, size, items_ref, qkv, sems[3:6])
    results = Exchange(me, size, out, back_ref, sems[6:9])

    @pl.loop(0, count)
    def _(item):
        forgets.start(item)

    for gather in gathers:
        gather.begin()
    inputs.start(0)
    rows.begin()

    @pl.loop(0, count)
    def _(item):
        forgets.arrive(item)

    @pl.loop(0, count)
    def _(item):
        upper = triangle(True)
        before = jnp.zeros((8, 1), F32)
        for start in range(0, size * block, LANES):
            part = forget[item, start // block, :, pl.ds(start % block, LANES)]
            total = before + dot(part.astype(BF16), upper, NN)
            decay_ref[item, :, pl.ds(start, LANES)] = total
            before = total[:, LANES - 1 :]

    lse_ref[...] = jnp.zeros_like(lse_ref)

    @pl.loop(0, count)
    def _(item):
        inputs.arrive(item)

        @pl.when(item + 1 < count)
        def _():
            inputs.start(item + 1)

        for hop in range(1, min(size, count + 1)):

            @pl.when(item == hop - 1)
            def _(hop=hop):
                for gather in gathers:
                    gather.advance(hop)

        saving = pltpu.make_async_copy(qkv.at[item], qkv_ref.at[item], save_sem)
        saving.start()
        attend_item(
            qkv.at[item], decay_ref.at[item], out.at[item], exact_ref.at[item], lse_ref.at[item], heads, head_size
        )
        results.start(item)
        saving.wait()

    rows.advance()
    for hop in range(count + 1, size):
        for gather in gathers:
            gather.advance(hop)

    gathers[0].end()
    inner = gate_w.shape[1]
    copy = pltpu.make_async_copy(full_out_ref.at[:, pl.ds(inner, inner)], gate_w, fetch_sem.at[1])
    copy.start()
    fetch.wait()
    copy.wait()
    step_rows = normed.shape[1] // CHUNKS

    @pl.loop(0, 4 * CHUNKS)
    def _(step):
        spot = pl.ds(pl.multiple_of(lax.rem(step, CHUNKS) * step_rows, step_rows), step_rows)
        logit = dot(normed[step // CHUNKS, spot], gate_w[...], NN)
        out_gate_ref[step // CHUNKS, spot] = 1.0 / (1.0 + jnp.exp(-logit))

    @pl.loop(0, count)
    def _(item):
        forgets.drain(item)
        inputs.drain(item)
        results.arrive(item)
        results.drain(item)

    gathers[1].end()
    rows.end()


def full_block(shape):
    return pl.BlockSpec(shape, lambda i: (0,) * len(shape), pipeline_mode=pl.Buffered(1))


def attend_cost(items, heads, products):
    count, size, _, block, width = items.shape
    pairs = count * heads * (size * block) ** 2 // 2
    return pl.CostEstimate(
        flops=2 * products * pairs * 256, bytes_accessed=100 << 20, transcendentals=pairs
    )


def context(items, forget, shards, rows, normed, f_size, head_size, ident):
    count, size, _, block, width = items.shape
    full = shards[0].shape[0] * f_size * size
    gate = normed.shape[:2] + shards[3].shape[1:]
    heads = width // head_size
    place = pl.BlockSpec(memory_space=pl.ANY)
    exact, stat = (count, size, block, width), (count, 8, size * block)
    return pl.pallas_call(
        functools.partial(context_kernel, heads, head_size),
        grid=(1,),
        out_shape=[
            jax.ShapeDtypeStruct(exact, BF16),
            jax.ShapeDtypeStruct(items.shape, BF16),
            jax.ShapeDtypeStruct((full, 2 * shards[0].shape[1]), BF16),
            jax.ShapeDtypeStruct((full, 2 * shards[2].shape[1]), BF16),
            jax.ShapeDtypeStruct((4,) + rows.shape, BF16),
            jax.ShapeDtypeStruct(exact, F32),
            jax.ShapeDtypeStruct(stat, F32),
            jax.ShapeDtypeStruct(stat, F32),
            jax.ShapeDtypeStruct(gate, F32),
        ],
        in_specs=[place, place]
        + [full_block(shard.shape) for shard in shards]
        + [full_block(rows.shape), place],
        out_specs=[place] * 5
        + [full_block(exact), full_block(stat), full_block(stat), full_block(gate)],
        scratch_shapes=[
            pltpu.VMEM(items.shape, BF16),
            pltpu.VMEM(forget.shape, F32),
            pltpu.VMEM(exact, BF16),
            pltpu.VMEM(normed.shape, BF16),
            pltpu.VMEM((full, shards[3].shape[1]), BF16),
            pltpu.SemaphoreType.DMA((2,)),
            pltpu.SemaphoreType.DMA,
        ]
        + exchange_sems(count, size) * 3
        + weight_sems(f_size, size, 2) * 2
        + [pltpu.SemaphoreType.DMA((3,))] * 2
        + [pltpu.SemaphoreType.DMA],
        compiler_params=remote_params(ident, 48),
        cost_estimate=attend_cost(items, heads, 2),
        name="context",
    )(items, forget, *shards, rows, normed)


def context_back_kernel(
    heads,
    head_size,
    items_ref,
    qkv_ref,
    exact_ref,
    lse_ref,
    decay_ref,
    down_ref,
    part_ref,
    inner_hbm,
    down_w_hbm,
    back_ref,
    forget_ref,
    down_sum_ref,
    sum_ref,
    rows_ref,
    *refs,
):
    grads, dqkv, change, slope, dq_acc, delta = refs[:6]
    sems = refs[6:15]
    count, size, block, width = items_ref.shape
    inner, down_w, table, fetch_sem = refs[36:]
    fetch = Fetch([(inner_hbm, inner), (down_w_hbm, down_w)], fetch_sem)
    tp, sibling, across, diagonal = tp_places()
    greet_all([{"tp": sibling}, {"tp": across}] + group_peers())
    me = lax.axis_index("ctx")
    sums = (
        WeightSum(part_ref, 0, sum_ref, refs[15:23]),
        WeightSum(down_ref, 0, down_sum_ref, refs[23:31]),
    )
    rows = RowSum(table, rows_ref, refs[31:36])
    inputs = Exchange(me, size, items_ref, grads, sems[0:3])
    results = Exchange(me, size, dqkv, back_ref, sems[3:6])
    forgets = Exchange(me, size, slope, forget_ref, sems[6:9])

    inputs.start(0)
    for weights in sums:
        weights.begin()
    fetch.wait()
    step_rows = inner.shape[1] // CHUNKS

    @pl.loop(0, 4 * CHUNKS)
    def _(step):
        spot = pl.ds(pl.multiple_of(lax.rem(step, CHUNKS) * step_rows, step_rows), step_rows)
        forward = dot(inner[step // CHUNKS, spot], down_w[...], NT)
        table[step // CHUNKS, spot] = forward.astype(BF16)

    rows.begin()

    @pl.loop(0, count)
    def _(item):
        inputs.arrive(item)

        @pl.when(item + 1 < count)
        def _():
            inputs.start(item + 1)

        attend_item_back(
            qkv_ref.at[item],
            grads.at[item],
            exact_ref.at[item],
            lse_ref.at[item],
            decay_ref.at[item],
            dqkv.at[item],
            change,
            dq_acc,
            delta,
            heads,
            head_size,
        )
        @pl.when(item > 0)
        def _():
            results.start(item)

        lower = triangle(False)
        after = jnp.zeros((8, 1), F32)
        for start in reversed(range(0, size * block, LANES)):
            total = after + exact_product(change[:, pl.ds(start, LANES)], lower)
            slope[item, start // block, :, pl.ds(start % block, LANES)] = total
            after = total[:, 0:1]
        forgets.start(item)

        for turn in range(count):

            @pl.when(item == turn)
            def _(turn=turn):
                for weights in sums:
                    weights.run_round(turn)
                if turn == 0:
                    results.start(0)
                    rows.advance()

    for n in range(count, sums[0].rounds()):
        for weights in sums:
            weights.run_round(n)

    @pl.loop(0, count)
    def _(item):
        inputs.drain(item)
        results.arrive(item)
        results.drain(item)
        forgets.arrive(item)
        forgets.drain(item)

    for weights in sums:
        weights.end()
    rows.end()


def context_back(grads, qkv, exact, lse, decay, down, part, inner_act, down_w, f_size, head_size, ident):
    count, size, _, block, width = qkv.shape
    heads = width // head_size
    place = pl.BlockSpec(memory_space=pl.ANY)
    forget = (count, size, 8, block)
    total = (part.shape[0] // (f_size * size), part.shape[1])
    down_total = (total[0], down.shape[1])
    table = inner_act.shape[:2] + down_w.shape[:1]
    return pl.pallas_call(
        functools.partial(context_back_kernel, heads, head_size),
        grid=(1,),
        out_shape=[
            jax.ShapeDtypeStruct(qkv.shape, BF16),
            jax.ShapeDtypeStruct(forget, F32),
            jax.ShapeDtypeStruct(down_total, F32),
            jax.ShapeDtypeStruct(total, F32),
            jax.ShapeDtypeStruct(table[1:], BF16),
        ],
        in_specs=[
            place,
            full_block(qkv.shape),
            full_block(exact.shape),
            full_block(lse.shape),
            full_block(decay.shape),
            place,
            place,
            place,
            place,
        ],
        out_specs=[
            place,
            place,
            full_block(down_total),
            full_block(total),
            full_block(table[1:]),
        ],
        scratch_shapes=[
            pltpu.VMEM(grads.shape, BF16),
            pltpu.VMEM(qkv.shape, BF16),
            pltpu.VMEM((8, size * block), F32),
            pltpu.VMEM(forget, F32),
            pltpu.VMEM((heads, size, block, width), F32),
            pltpu.VMEM((8, size * block), F32),
        ]
        + exchange_sems(count, size) * 3
        + sum_scratch(f_size, size, *total)
        + sum_scratch(f_size, size, *down_total)
        + row_sum_scratch(*table[1:])
        + [
            pltpu.VMEM(inner_act.shape, BF16),
            pltpu.VMEM(down_w.shape, BF16),
            pltpu.VMEM(table, BF16),
            pltpu.SemaphoreType.DMA((2,)),
        ],
        compiler_params=remote_params(ident, 62),
        cost_estimate=attend_cost(qkv, heads, 5),
        name="context_back",
    )(grads, qkv, exact, lse, decay, down, part, inner_act, down_w)


CHUNKS = 4
HALVES = 2
SUM_CHUNKS = 2


def tp_places():
    me = lax.axis_index("tp")
    sibling = me + 1 - 2 * lax.rem(me, 2)
    across = lax.rem(me + 2, 4)
    diagonal = lax.rem(sibling + 2, 4)
    return me, sibling, across, diagonal


def greet(peers):
    barrier = pltpu.get_barrier_semaphore()
    for peer in peers:
        pl.semaphore_signal(barrier, inc=1, device_id={"tp": peer}, device_id_type=MESH)
    pl.semaphore_wait(barrier, len(peers))


def sending(source, target, send_sem, recv_sem, peer):
    return pltpu.make_async_remote_copy(
        src_ref=source,
        dst_ref=target,
        send_sem=send_sem,
        recv_sem=recv_sem,
        device_id={"tp": peer},
        device_id_type=MESH,
    )


def pick(step, chunks, places):
    me, sibling, across, diagonal = places
    late = step - 2 * chunks
    far = jnp.where(lax.rem(late, 2) == 0, across, diagonal)
    slot = jnp.where(step < chunks, me, jnp.where(step < 2 * chunks, sibling, far))
    chunk = jnp.where(step < 2 * chunks, lax.rem(step, chunks), late // 2)
    return slot, chunk


def gather_loop(table, sems, compute, own=None, relative=False, between=None, ready=None):
    near_send, near_recv, far_send, far_recv, pass_send, pass_recv = sems
    me, sibling, across, diagonal = tp_places()
    places = (0, 1, 2, 3) if relative else (me, sibling, across, diagonal)
    mine, near_by, far_off, corner = places
    near_spot, far_spot, pass_spot = (1, 2, 3) if relative else (me, me, across)
    rows = table.shape[1] // CHUNKS

    def part(slot, chunk):
        return table.at[slot, pl.ds(pl.multiple_of(chunk * rows, rows), rows)]

    def far(chunk):
        source = part(mine, chunk)
        if own is not None:
            source = own.at[pl.ds(pl.multiple_of(chunk * rows, rows), rows)]
        return sending(source, part(far_spot, chunk), far_send.at[chunk], far_recv.at[chunk], across)

    def far_arrival(chunk):
        spot = part(far_off, chunk)
        return sending(spot, spot, far_send.at[chunk], far_recv.at[chunk], across)

    def passing(chunk):
        return sending(
            part(far_off, chunk), part(pass_spot, chunk), pass_send.at[chunk], pass_recv.at[chunk], sibling
        )

    def pass_arrival(chunk):
        spot = part(corner, chunk)
        return sending(spot, spot, pass_send.at[chunk], pass_recv.at[chunk], sibling)

    for chunk in range(CHUNKS):
        far(chunk).start()
    own = table.at[mine] if own is None else own
    near = sending(own, table.at[near_spot], near_send, near_recv, sibling)
    near.start()
    if ready is not None:
        ready()

    def body(step, _):
        slot, chunk = pick(step, CHUNKS, places)
        late = step - 2 * CHUNKS

        @pl.when(step == CHUNKS)
        def _():
            spot = table.at[near_by]
            sending(spot, spot, near_send, near_recv, sibling).wait_recv()

        @pl.when((late >= 0) & (lax.rem(late, 2) == 0))
        def _():
            far_arrival(chunk).wait_recv()
            passing(chunk).start()

        @pl.when((late >= 0) & (lax.rem(late, 2) == 1))
        def _():
            pass_arrival(chunk).wait_recv()

        compute(slot, chunk)
        return 0

    if between is None:
        lax.fori_loop(0, 4 * CHUNKS, body, 0)
    else:
        lax.fori_loop(0, 2 * CHUNKS, body, 0)
        between()
        lax.fori_loop(2 * CHUNKS, 4 * CHUNKS, body, 0)
    near.wait_send()
    for chunk in range(CHUNKS):
        far(chunk).wait_send()
        passing(chunk).wait_send()


GATHER_SEMS = [pltpu.SemaphoreType.DMA] * 2 + [pltpu.SemaphoreType.DMA((CHUNKS,))] * 4


def scatter_loop(buffers, sems, partial, finish, relative=False, between=None):
    near_out, near_in, far_out, far_in = buffers
    near_send, near_recv, far_send, far_recv = sems
    me, sibling, across, diagonal = tp_places()
    mine, near_by, far_off, corner = (0, 1, 2, 3) if relative else (me, sibling, across, diagonal)
    rows = far_out.shape[0] // SUM_CHUNKS

    def span(chunk):
        return pl.ds(pl.multiple_of(chunk * rows, rows), rows)

    def near(half, chunk):
        return sending(
            near_out.at[half, span(chunk)],
            near_in.at[half, span(chunk)],
            near_send.at[half, chunk],
            near_recv.at[half, chunk],
            sibling,
        )

    def far(chunk):
        return sending(
            far_out.at[span(chunk)],
            far_in.at[span(chunk)],
            far_send.at[chunk],
            far_recv.at[chunk],
            across,
        )

    def body(step, _):
        phase, chunk = step // SUM_CHUNKS, lax.rem(step, SUM_CHUNKS)
        slot = jnp.where(
            phase == 0, corner, jnp.where(phase == 1, far_off, jnp.where(phase == 2, near_by, mine))
        )
        value = partial(slot, chunk)
        spot = span(chunk)

        @pl.when(lax.rem(phase, 2) == 0)
        def _():
            half = phase // 2
            near_out[half, spot] = value.astype(BF16)
            near(half, chunk).start()

        @pl.when(phase == 1)
        def _():
            near(0, chunk).wait_recv()
            far_out[spot] = (value + near_in[0, spot].astype(F32)).astype(BF16)
            far(chunk).start()

        @pl.when(phase == 3)
        def _():
            near(1, chunk).wait_recv()

            far(chunk).wait_recv()
            finish(chunk, value + near_in[1, spot].astype(F32) + far_in[spot].astype(F32))

        return 0

    if between is None:
        lax.fori_loop(0, 4 * SUM_CHUNKS, body, 0)
    else:
        lax.fori_loop(0, SUM_CHUNKS, body, 0)
        for phase in (1, 2, 3):
            between(phase)
            lax.fori_loop(phase * SUM_CHUNKS, (phase + 1) * SUM_CHUNKS, body, 0)
    for chunk in range(SUM_CHUNKS):
        near(0, chunk).wait_send()
        near(1, chunk).wait_send()
        far(chunk).wait_send()


SCATTER_SEMS = [pltpu.SemaphoreType.DMA((2, SUM_CHUNKS))] * 2 + [pltpu.SemaphoreType.DMA((SUM_CHUNKS,))] * 2


def scatter_buffers(rows, width):
    return [
        pltpu.VMEM((2, rows, width), BF16),
        pltpu.VMEM((2, rows, width), BF16),
        pltpu.VMEM((rows, width), BF16),
        pltpu.VMEM((rows, width), BF16),
    ]


def group_peers():
    f_size, c_size = lax.axis_size("fsdp"), lax.axis_size("ctx")
    f, c = lax.axis_index("fsdp"), lax.axis_index("ctx")
    return [
        {"fsdp": lax.rem(f + i, f_size), "ctx": lax.rem(c + j, c_size)}
        for i in range(f_size)
        for j in range(c_size)
        if i or j
    ]


def greet_all(peers):
    barrier = pltpu.get_barrier_semaphore()
    for peer in peers:
        pl.semaphore_signal(barrier, inc=1, device_id=peer, device_id_type=MESH)
    pl.semaphore_wait(barrier, len(peers))


def moving(source, target, send_sem, recv_sem, peer):
    return pltpu.make_async_remote_copy(
        src_ref=source,
        dst_ref=target,
        send_sem=send_sem,
        recv_sem=recv_sem,
        device_id=peer,
        device_id_type=MESH,
    )


class WeightGather:
    def __init__(self, shards, full, sems):
        self.shards, self.full = shards, full
        widths = [shard.shape[1] for shard in shards]
        self.columns = [pl.ds(sum(widths[:h]), width) for h, width in enumerate(widths)]
        self.f_size, self.c_size = lax.axis_size("fsdp"), lax.axis_size("ctx")
        self.f, self.c = lax.axis_index("fsdp"), lax.axis_index("ctx")
        self.sems = sems

    def spot(self, c, h, f=None):
        rows = self.shards[0].shape[0]
        block = (self.f if f is None else f) * self.c_size + c
        return self.full.at[pl.ds(pl.multiple_of(block * rows, rows), rows), self.columns[h]]

    def own(self, h):
        return pltpu.make_async_copy(self.shards[h], self.spot(self.c, h), self.sems[4].at[h])

    def along(self, c, h, hop, side, first=False):
        source = self.shards[h] if first else self.spot(c, h)
        peer = {"ctx": self.c + (1 if side else -1)}
        send, recv = self.sems[0].at[side, hop, h], self.sems[1].at[side, hop, h]
        return moving(source, self.spot(c, h), send, recv, peer)

    def over(self, c, h, step, first=False):
        source = self.shards[h] if first else self.spot(c, h)
        peer = {"fsdp": lax.rem(self.f + step, self.f_size)}
        send, recv = self.sems[2].at[step, c, h], self.sems[3].at[step, c, h]
        return moving(source, self.spot(c, h), send, recv, peer)

    def over_arrival(self, c, h, step):
        spot = self.spot(c, h, lax.rem(self.f + self.f_size - step, self.f_size))
        peer = {"fsdp": lax.rem(self.f + step, self.f_size)}
        return moving(spot, spot, self.sems[2].at[step, c, h], self.sems[3].at[step, c, h], peer)

    def can(self, side):
        return self.c + 1 < self.c_size if side else self.c > 0

    def holds(self, hop, side):
        return self.c - hop >= 0 if side else self.c + hop < self.c_size

    def begin(self):
        for h in range(len(self.shards)):
            for side in (1, 0):

                @pl.when(self.can(side))
                def _(side=side):
                    self.along(self.c, h, 1, side, True).start()

            for step in range(1, self.f_size):
                self.over(self.c, h, step, True).start()

        for h in range(len(self.shards)):
            self.own(h).start()

    def advance(self, hop):
        for h in range(len(self.shards)):
            for side in (1, 0):

                @pl.when(self.holds(hop, side))
                def _(side=side):
                    c = self.c - hop if side else self.c + hop
                    self.along(c, h, hop, side).wait_recv()

                    @pl.when(self.can(side))
                    def _():
                        self.along(c, h, hop + 1, side).start()

                    for step in range(1, self.f_size):
                        self.over(c, h, step).start()

    def end(self):
        for h in range(len(self.shards)):
            self.own(h).wait()
            for step in range(1, self.f_size):
                for c in range(self.c_size):
                    self.over_arrival(c, h, step).wait_recv()
                    self.over(c, h, step).wait_send()
            for side in (1, 0):

                @pl.when(self.can(side))
                def _(side=side):
                    self.along(self.c, h, 1, side, True).wait_send()

                for hop in range(1, self.c_size):

                    @pl.when(self.holds(hop, side) & self.can(side))
                    def _(side=side, hop=hop):
                        c = self.c - hop if side else self.c + hop
                        self.along(c, h, hop + 1, side).wait_send()


def weight_sems(f_size, c_size, parts):
    dma = pltpu.SemaphoreType.DMA
    return [dma((2, c_size + 1, parts))] * 2 + [dma((f_size, c_size, parts))] * 2 + [dma((parts,))]


class WeightSum:
    def __init__(self, part, first_column, out, refs):
        self.part, self.out, self.first = part, out, first_column
        self.stage, self.total, self.along_in = refs[:3]
        self.own_sem, self.over_send, self.over_recv, self.along_send, self.along_recv = refs[3:]
        self.f_size, self.c_size = lax.axis_size("fsdp"), lax.axis_size("ctx")
        self.f, self.c = lax.axis_index("fsdp"), lax.axis_index("ctx")
        self.rows, self.wide = out.shape[0], out.shape[1] // HALVES
        ends = [(self.c_size - 1 - i // 2) if i % 2 == 0 else i // 2 for i in range(self.c_size)]
        self.order = [(c, h) for c in ends for h in range(HALVES)]
        self.stages = len(self.order) + self.c_size - 1

    def piece(self, f, c, h):
        row = (f * self.c_size + c) * self.rows
        columns = pl.ds(self.first + h * self.wide, self.wide)
        return self.part.at[pl.ds(pl.multiple_of(row, self.rows), self.rows), columns]

    def own(self, c, h):
        n = c * HALVES + h
        return pltpu.make_async_copy(self.piece(self.f, c, h), self.stage.at[n], self.own_sem.at[n])

    def over(self, c, h, step):
        f, n = lax.rem(self.f + step, self.f_size), c * HALVES + h
        return moving(
            self.piece(f, c, h),
            self.total.at[step - 1, n],
            self.over_send.at[step - 1, n],
            self.over_recv.at[step - 1, n],
            {"fsdp": f},
        )

    def along(self, c, h, side, source=None):
        peer, n = {"ctx": self.c + (1 if side else -1)}, c * HALVES + h
        target = self.along_in.at[side, n]
        return moving(
            target if source is None else source,
            target,
            self.along_send.at[side, n],
            self.along_recv.at[side, n],
            peer,
        )

    def begin(self):
        for c, h in self.order:
            for step in range(1, self.f_size):
                self.over(c, h, step).start()
        for c, h in self.order:
            self.own(c, h).start()

    def receive(self, i):
        c, h = self.order[i]
        n = c * HALVES + h
        self.own(c, h).wait()
        value = self.stage[n].astype(F32)
        for step in range(1, self.f_size):
            self.over(c, h, step).wait_recv()
        for step in range(1, self.f_size):
            value = value + self.total[step - 1, n].astype(F32)
        self.total[0, n] = value.astype(BF16)
        for side, end in ((1, 0), (0, self.c_size - 1)):
            if c != end:

                @pl.when(self.c == end)
                def _(side=side):
                    self.along(c, h, side, self.total.at[0, n]).start()

    def hop(self, c, h, side, device):
        n = c * HALVES + h

        @pl.when(self.c == device)
        def _():
            self.along(c, h, side).wait_recv()
            value = self.total[0, n].astype(F32) + self.along_in[side, n].astype(F32)
            if device == c:
                self.total[0, n] = value.astype(BF16)
            else:
                self.along_in[side, n] = value.astype(BF16)
                self.along(c, h, side).start()

    def run(self, n):
        if n < len(self.order):
            self.receive(n)
        for i, (c, h) in enumerate(self.order):
            if 1 <= n - i <= c:
                self.hop(c, h, 1, n - i)
            if 1 <= n - i <= self.c_size - 1 - c:
                self.hop(c, h, 0, self.c_size - 1 - (n - i))

    def run_to(self, first, last):
        for n in range(min(first, self.stages), min(last, self.stages)):
            self.run(n)

    def rounds(self):
        return self.c_size + 1

    def run_round(self, n):
        count = len(self.order)
        for i, (c, h) in enumerate(self.order):
            hop = n if i < 5 * count // 8 else n - 1
            if hop == 0:
                self.receive(i)
            if 1 <= hop <= c:
                self.hop(c, h, 1, hop)
            if 1 <= hop <= self.c_size - 1 - c:
                self.hop(c, h, 0, self.c_size - 1 - hop)

    def end(self):
        for c in range(self.c_size):

            @pl.when(self.c == c)
            def _(c=c):
                for h in range(HALVES):
                    columns = pl.ds(h * self.wide, self.wide)
                    self.out[:, columns] = self.total[0, c * HALVES + h].astype(F32)

        for c, h in self.order:
            for step in range(1, self.f_size):
                self.over(c, h, step).wait_send()
            for side in (1, 0):

                @pl.when(self.c < c if side else self.c > c)
                def _(side=side):
                    self.along(c, h, side).wait_send()


def sum_scratch(f_size, c_size, rows, columns):
    dma, count, wide = pltpu.SemaphoreType.DMA, c_size * HALVES, columns // HALVES
    return (
        [
            pltpu.VMEM((count, rows, wide), BF16),
            pltpu.VMEM((f_size - 1, count, rows, wide), BF16),
            pltpu.VMEM((2, count, rows, wide), BF16),
        ]
        + [dma((count,))]
        + [dma((f_size - 1, count))] * 2
        + [dma((2, count))] * 2
    )


class Fetch:
    def __init__(self, pairs, sem):
        self.copies = [
            pltpu.make_async_copy(source, target, sem.at[n]) for n, (source, target) in enumerate(pairs)
        ]
        for copy in self.copies:
            copy.start()

    def wait(self):
        for copy in self.copies:
            copy.wait()


class RowGather:
    def __init__(self, rows, table, sems):
        self.rows, self.table, self.sems = rows, table, sems
        _, self.sibling, self.across, _ = tp_places()

    def own(self):
        return pltpu.make_async_copy(self.rows, self.table.at[0], self.sems[2])

    def copy(self, n):
        source = self.table.at[2] if n == 2 else self.rows
        peer = {"tp": self.across if n == 1 else self.sibling}
        return moving(source, self.table.at[n + 1], self.sems[0].at[n], self.sems[1].at[n], peer)

    def begin(self):
        self.copy(1).start()
        self.copy(0).start()
        self.own().start()

    def advance(self):
        self.copy(1).wait_recv()
        self.copy(2).start()

    def end(self):
        self.own().wait()
        self.copy(0).wait()
        self.copy(1).wait_send()
        self.copy(2).wait()


class RowSum:
    def __init__(self, table, out, refs):
        self.table, self.out = table, out
        self.near, self.far_out, self.far_in, self.send, self.recv = refs
        _, self.sibling, self.across, _ = tp_places()

    def copy(self, n):
        if n == 2:
            source, target, peer = self.far_out, self.far_in, self.across
        else:
            source, target, peer = self.table.at[1 if n else 3], self.near.at[n], self.sibling
        return moving(source, target, self.send.at[n], self.recv.at[n], {"tp": peer})

    def begin(self):
        for n in range(2):
            self.copy(n).start()

    def advance(self):
        self.copy(0).wait_recv()
        self.far_out[...] = (self.table[2].astype(F32) + self.near[0].astype(F32)).astype(BF16)
        self.copy(2).start()

    def end(self):
        self.copy(1).wait_recv()
        self.copy(2).wait_recv()
        total = self.table[0].astype(F32) + self.near[1].astype(F32)
        self.out[...] = (total + self.far_in[...].astype(F32)).astype(BF16)
        for n in range(3):
            self.copy(n).wait_send()


def row_sum_scratch(rows, width):
    dma, pair, one = pltpu.SemaphoreType.DMA, (2, rows, width), (rows, width)
    return [pltpu.VMEM(pair, BF16)] + [pltpu.VMEM(one, BF16)] * 2 + [dma((3,))] * 2


def startup_kernel(parts, rows_ref, gain_ref, *refs):
    shards, (all_ref, full_ref, gains_ref, own_sem) = refs[:parts], refs[parts : parts + 4]
    sems = refs[parts + 4 :]
    me, sibling, across, diagonal = tp_places()
    others = group_peers()
    greet_all([{"tp": sibling}, {"tp": across}] + others)
    near_send, near_recv, far_send, far_recv, pass_send, pass_recv = sems[:6]
    gather = WeightGather(shards, full_ref, sems[6:11])
    gain_send, gain_recv, gain_own = sems[11:]
    spot = gains_ref.at[gather.f * gather.c_size + gather.c]
    gain_copies = [
        moving(gain_ref, spot, gain_send.at[n], gain_recv.at[n], peer) for n, peer in enumerate(others)
    ]
    own_gain = pltpu.make_async_copy(gain_ref, spot, gain_own)
    size = rows_ref.shape[0] // CHUNKS
    own = pltpu.make_async_copy(rows_ref, all_ref.at[me], own_sem)

    def span(chunk):
        return pl.ds(chunk * size, size)

    def far(chunk):
        return sending(
            rows_ref.at[span(chunk)],
            all_ref.at[me, span(chunk)],
            far_send.at[chunk],
            far_recv.at[chunk],
            across,
        )

    def passing(chunk):
        spot = all_ref.at[across, span(chunk)]
        return sending(spot, spot, pass_send.at[chunk], pass_recv.at[chunk], sibling)

    gather.begin()
    far(0).start()
    for copy in gain_copies:
        copy.start()
    own_gain.start()
    near = sending(rows_ref, all_ref.at[me], near_send, near_recv, sibling)
    near.start()
    own.start()
    for turn in range(max(CHUNKS, gather.c_size - 1)):
        if turn < CHUNKS:
            far(turn).wait_recv()
            if turn + 1 < CHUNKS:
                far(turn + 1).start()
            passing(turn).start()
        if turn + 1 < gather.c_size:
            gather.advance(turn + 1)
    near.wait()
    for chunk in range(CHUNKS):
        far(chunk).wait_send()
        passing(chunk).wait()
    own.wait()
    gather.end()
    for copy in gain_copies:
        copy.wait()
    own_gain.wait()


def startup(rows, gains, shards, f_size, c_size, ident):
    place = pl.BlockSpec(memory_space=pl.ANY)
    full = (shards[0].shape[0] * f_size * c_size, sum(shard.shape[1] for shard in shards))
    return pl.pallas_call(
        functools.partial(startup_kernel, len(shards)),
        out_shape=[
            jax.ShapeDtypeStruct((4,) + rows.shape, BF16),
            jax.ShapeDtypeStruct(full, BF16),
            jax.ShapeDtypeStruct((f_size * c_size,) + gains.shape, F32),
        ],
        in_specs=[pl.BlockSpec(memory_space=pltpu.VMEM)] * (2 + len(shards)),
        out_specs=[pl.BlockSpec(memory_space=pltpu.HBM)] * 2 + [place],
        scratch_shapes=[pltpu.SemaphoreType.DMA]
        + GATHER_SEMS
        + weight_sems(f_size, c_size, len(shards))
        + [pltpu.SemaphoreType.DMA((f_size * c_size - 1,))] * 2
        + [pltpu.SemaphoreType.DMA],
        compiler_params=pltpu.CompilerParams(
            collective_id=ident, has_side_effects=True, vmem_limit_bytes=32 << 20
        ),
        name="startup",
    )(rows, gains, *shards)


def whole(shape, column=None):
    zeros = (0,) * (len(shape) - 1)
    return pl.BlockSpec(shape, lambda i: zeros + (column or 0,), pipeline_mode=pl.Buffered(1))


def remote_params(ident, megabytes):
    return pltpu.CompilerParams(
        collective_id=ident, has_side_effects=True, vmem_limit_bytes=megabytes << 20, dimension_semantics=("arbitrary",)
    )


def project_kernel(layout, x_ref, gain_ref, w_ref, normed_ref, forget_ref, items_ref):
    seq_count, groups, width, places = layout
    x = x_ref[0].astype(F32)
    normed = (x * lax.rsqrt(jnp.mean(x * x, axis=1, keepdims=True) + epsilon) * gain_ref[...]).astype(BF16)
    normed_ref[0] = normed
    inner = groups * width
    rows = x.shape[0] // seq_count
    count = items_ref.shape[0]
    product = dot(normed, w_ref[...], NN)
    forget_ref[0] = product[:, 3 * inner :]
    for kind in range(3):
        value = product[:, kind * inner : (kind + 1) * inner].astype(BF16)
        for slot, (s, g) in enumerate(places):
            piece = value[s * rows : (s + 1) * rows, g * width : (g + 1) * width]
            items_ref[slot % count, slot // count, kind] = piece


def project(x_all, gain, full_one, layout, item_count, ctx_size):
    seq_count, groups, width, places = layout
    tp_size, rows, model_width = x_all.shape
    local = rows // seq_count
    item = jax.ShapeDtypeStruct((item_count, ctx_size, 3, tp_size * local, width), BF16)
    columns = full_one.shape[1]
    block = pl.BlockSpec((1, rows, model_width), lambda t: (t, 0, 0))
    return pl.pallas_call(
        functools.partial(project_kernel, layout),
        grid=(tp_size,),
        out_shape=[
            jax.ShapeDtypeStruct(x_all.shape, BF16),
            jax.ShapeDtypeStruct((tp_size, rows, LANES), F32),
            item,
        ],
        in_specs=[
            block,
            pl.BlockSpec((1, model_width), lambda t: (0, 0)),
            pl.BlockSpec((model_width, columns), lambda t: (0, 0), pipeline_mode=pl.Buffered(1)),
        ],
        out_specs=[
            block,
            pl.BlockSpec((1, rows, LANES), lambda t: (t, 0, 0)),
            pl.BlockSpec((item_count, ctx_size, 3, local, width), lambda t: (0, 0, 0, t, 0)),
        ],
        compiler_params=pltpu.CompilerParams(vmem_limit_bytes=48 << 20, dimension_semantics=("arbitrary",)),
        cost_estimate=pl.CostEstimate(
            flops=2 * x_all.size * columns, bytes_accessed=4 * x_all.size, transcendentals=0
        ),
        name="project",
    )(x_all, gain, full_one)


def out_kernel(layout, x_ref, gate_ref, w_ref, gain_ref, items, shard_ref, *refs):
    seq_count, groups, width, places = layout
    hidden_ref, normed_ref, attended_ref, mixed_ref, full_ref = refs[:5]
    buffers, sems = refs[5:9], refs[9:13]
    count = items.shape[0]
    me, sibling, across, diagonal = tp_places()
    greet_all([{"tp": sibling}, {"tp": across}] + group_peers())
    gather = WeightGather((shard_ref,), full_ref, refs[13:])
    gather.begin()
    tp_size, rows, _ = gate_ref.shape
    local = rows // seq_count

    def mix(t, _):
        here = pl.ds(pl.multiple_of(t * local, local), local)
        for slot, (s, g) in enumerate(places[: seq_count * groups]):
            there = (t, pl.ds(s * local, local), pl.ds(g * width, width))
            value = items[slot % count, slot // count, here]
            attended_ref[there] = value
            mixed_ref[there] = (value.astype(F32) * gate_ref[there]).astype(BF16)
        return 0

    lax.fori_loop(0, tp_size, mix, 0)
    size = rows // SUM_CHUNKS

    def span(chunk):
        return pl.ds(pl.multiple_of(chunk * size, size), size)

    def partial(slot, chunk):
        return dot(mixed_ref[slot, span(chunk)], w_ref[...], NT)

    def finish(chunk, total):
        hidden = x_ref[span(chunk)].astype(F32) + total
        hidden_ref[span(chunk)] = hidden
        inverse = lax.rsqrt(jnp.mean(hidden * hidden, axis=1, keepdims=True) + epsilon)
        normed_ref[span(chunk)] = (hidden * inverse * gain_ref[...]).astype(BF16)

    def between(phase):
        if phase < 3:
            gather.advance(phase)
        else:
            for hop in range(3, gather.c_size):
                gather.advance(hop)

    scatter_loop(buffers, sems, partial, finish, between=between)
    gather.end()


def out_project(x, gate, full_out, gain, items, shard, layout, f_size, c_size, ident):
    seq_count, groups, width, places = layout
    rows, model_width = x.shape
    inner = groups * width
    tp_size = gate.shape[0]
    return pl.pallas_call(
        functools.partial(out_kernel, layout),
        grid=(1,),
        out_shape=[
            jax.ShapeDtypeStruct(x.shape, F32),
            jax.ShapeDtypeStruct(x.shape, BF16),
            jax.ShapeDtypeStruct(gate.shape, BF16),
            jax.ShapeDtypeStruct(gate.shape, BF16),
            jax.ShapeDtypeStruct((model_width, shard.shape[1]), BF16),
        ],
        in_specs=[
            whole(x.shape),
            whole(gate.shape),
            whole((model_width, inner), 0),
            whole(gain.shape),
            whole(items.shape),
            whole(shard.shape),
        ],
        out_specs=[
            whole(x.shape),
            whole(x.shape),
            whole(gate.shape),
            whole(gate.shape),
            pl.BlockSpec(memory_space=pl.ANY),
        ],
        scratch_shapes=scatter_buffers(rows, model_width)
        + SCATTER_SEMS
        + weight_sems(f_size, c_size, 1),
        compiler_params=remote_params(ident, 48),
        cost_estimate=pl.CostEstimate(
            flops=2 * gate.size * model_width, bytes_accessed=100 << 20, transcendentals=0
        ),
        name="out_project",
    )(x, gate, full_out, gain, items, shard)


def mlp_kernel(
    normed_ref, grad_hbm, gate_hbm, down_hbm, all_ref, inner_hbm, pair_hbm, table, inner_ref, pair_ref, *refs
):
    grad_ref, both_w, down_w, fetch_sem, out_sem = refs[:5]
    sems = refs[5:]
    fetch = Fetch([(gate_hbm, both_w), (grad_hbm, grad_ref), (down_hbm, down_w)], fetch_sem)
    me, sibling, across, diagonal = tp_places()
    greet((sibling, across))
    table[0] = normed_ref[...]
    rows, hidden = table.shape[1] // CHUNKS, down_w.shape[1]
    tile = min(hidden, 512)

    def writing(n, slot, chunk):
        here = (slot, pl.ds(pl.multiple_of(chunk * rows, rows), rows))
        source, target = ((inner_ref, inner_hbm), (pair_ref, pair_hbm), (table, all_ref))[n]
        return pltpu.make_async_copy(source.at[here], target.at[here], out_sem.at[n, slot, chunk])

    def compute(slot, chunk):
        spot = pl.ds(pl.multiple_of(chunk * rows, rows), rows)
        normed, grad = table[slot, spot], grad_ref[slot, spot]
        for start in range(0, hidden, tile):
            columns = pl.ds(start, tile)
            gate = dot(normed, both_w[:, columns], NN)
            up = dot(normed, both_w[:, pl.ds(hidden + start, tile)], NN)
            back = dot(grad, down_w[:, columns], NN)
            sig = 1.0 / (1.0 + jnp.exp(-gate))
            silu = gate * sig
            inner_ref[slot, spot, columns] = (silu * up).astype(BF16)
            pair_ref[slot, spot, columns] = (back * up * sig * (1.0 + gate * (1.0 - sig))).astype(BF16)
            pair_ref[slot, spot, pl.ds(hidden + start, tile)] = (back * silu).astype(BF16)
        for n in range(3):
            writing(n, slot, chunk).start()

    gather_loop(table, sems, compute, relative=True, ready=fetch.wait)
    for n in range(3):

        @pl.loop(0, 4 * CHUNKS)
        def _(step):
            writing(n, step // CHUNKS, lax.rem(step, CHUNKS)).wait()


def mlp(normed, grad_all, full_two, full_down, hidden, ident):
    tp_size, rows, model_width = grad_all.shape
    total = tp_size * rows
    place = pl.BlockSpec(memory_space=pl.ANY)
    inner, pair = (tp_size, rows, hidden), (tp_size, rows, 2 * hidden)
    dma = pltpu.SemaphoreType.DMA
    return pl.pallas_call(
        mlp_kernel,
        grid=(1,),
        out_shape=[
            jax.ShapeDtypeStruct(grad_all.shape, BF16),
            jax.ShapeDtypeStruct(inner, BF16),
            jax.ShapeDtypeStruct(pair, BF16),
        ],
        in_specs=[whole(normed.shape), place, place, place],
        out_specs=[place] * 3,
        scratch_shapes=[
            pltpu.VMEM(grad_all.shape, BF16),
            pltpu.VMEM(inner, BF16),
            pltpu.VMEM(pair, BF16),
            pltpu.VMEM(grad_all.shape, BF16),
            pltpu.VMEM((model_width, 2 * hidden), BF16),
            pltpu.VMEM((model_width, hidden), BF16),
            dma((3,)),
            dma((3, tp_size, CHUNKS)),
        ]
        + GATHER_SEMS,
        compiler_params=remote_params(ident, 56),
        cost_estimate=pl.CostEstimate(
            flops=6 * total * model_width * hidden, bytes_accessed=100 << 20, transcendentals=total * hidden
        ),
        name="mlp",
    )(normed, grad_all, full_two, full_down)


def mlp_back_kernel(
    pair_hbm, w_hbm, hidden_hbm, grad_hbm, gain_ref, sums_ref, out_ref, branch_ref, part_ref, sum_ref, *refs
):
    buffers, sems = refs[:4], refs[4:8]
    pair_ref, w_ref, hidden_ref, grad_ref, fetch_sem = refs[8:13]
    columns = pl.ds(0, w_ref.shape[1])
    fetch = Fetch(
        [
            (pair_hbm, pair_ref),
            (w_hbm.at[:, columns], w_ref),
            (hidden_hbm, hidden_ref),
            (grad_hbm, grad_ref),
        ],
        fetch_sem,
    )
    me, sibling, across, diagonal = tp_places()
    greet_all([{"tp": sibling}, {"tp": across}] + group_peers())
    weights = WeightSum(sums_ref, 0, sum_ref, refs[13:])
    weights.begin()
    fetch.wait()
    part_ref[...] = jnp.zeros_like(part_ref)
    size = hidden_ref.shape[0] // SUM_CHUNKS

    def span(chunk):
        return pl.ds(pl.multiple_of(chunk * size, size), size)

    def partial(slot, chunk):
        return dot(pair_ref[slot, span(chunk)], w_ref[...], NT)

    def finish(chunk, total):
        hidden = hidden_ref[span(chunk)]
        inverse = lax.rsqrt(jnp.mean(hidden * hidden, axis=1, keepdims=True) + epsilon)
        unit = hidden * inverse
        part_ref[...] += jnp.sum(total * unit, axis=0, keepdims=True)
        scaled = total * gain_ref[...]
        middle = jnp.mean(scaled * unit, axis=1, keepdims=True)
        grad = grad_ref[span(chunk)].astype(F32) + inverse * (scaled - unit * middle)
        out_ref[span(chunk)] = grad
        branch_ref[span(chunk)] = grad.astype(BF16)

    def between(phase):
        if phase < 3:
            weights.run_to(2 * phase - 2, 2 * phase)
        else:
            weights.run_to(4, weights.stages)

    scatter_loop(buffers, sems, partial, finish, relative=True, between=between)
    weights.end()


def mlp_back(pair, full_two, hidden_state, grad_out, gain, part, f_size, c_size, ident):
    tp_size, rows, wide = pair.shape
    model_width = hidden_state.shape[1]
    place = pl.BlockSpec(memory_space=pl.ANY)
    total = (part.shape[0] // (f_size * c_size), part.shape[1] // 2)
    return pl.pallas_call(
        mlp_back_kernel,
        grid=(1,),
        out_shape=[
            jax.ShapeDtypeStruct(hidden_state.shape, F32),
            jax.ShapeDtypeStruct(hidden_state.shape, BF16),
            jax.ShapeDtypeStruct(gain.shape, F32),
            jax.ShapeDtypeStruct(total, F32),
        ],
        in_specs=[
            place,
            place,
            place,
            place,
            whole(gain.shape),
            place,
        ],
        out_specs=[
            whole(hidden_state.shape),
            whole(hidden_state.shape),
            whole(gain.shape),
            whole(total),
        ],
        scratch_shapes=scatter_buffers(rows, model_width)
        + SCATTER_SEMS
        + [
            pltpu.VMEM(pair.shape, BF16),
            pltpu.VMEM((model_width, wide), BF16),
            pltpu.VMEM(hidden_state.shape, F32),
            pltpu.VMEM(grad_out.shape, BF16),
            pltpu.SemaphoreType.DMA((4,)),
        ]
        + sum_scratch(f_size, c_size, *total),
        compiler_params=remote_params(ident, 60),
        cost_estimate=pl.CostEstimate(
            flops=2 * pair.size * model_width, bytes_accessed=100 << 20, transcendentals=0
        ),
        name="mlp_back",
    )(pair, full_two, hidden_state, grad_out, gain, part)


def out_back_kernel(
    layout,
    branch_ref,
    w_ref,
    gate_ref,
    attended_ref,
    sums_ref,
    inner_hbm,
    grad_hbm,
    all_ref,
    logit_ref,
    items,
    sum_ref,
    part_hbm,
    *refs,
):
    seq_count, groups, width, places = layout
    table, grads, own_sem = refs[:3]
    sems = refs[3:9]
    inner_ref, grad_ref, part, fetch_sem, write_sem = refs[9:14]
    count = items.shape[0]
    me, sibling, across, diagonal = tp_places()
    greet_all([{"tp": sibling}, {"tp": across}] + group_peers())
    weights = WeightSum(sums_ref, sum_ref.shape[1], sum_ref, refs[14:])
    weights.begin()
    table[me] = branch_ref[...]
    tp_size, rows, _ = gate_ref.shape
    local, size = rows // seq_count, rows // CHUNKS
    model_width, hidden = part.shape
    tile = 2 * LANES
    tiles = model_width // tile
    fetches = []

    def begin_fetch():
        fetches.append(
            Fetch([(inner_hbm, inner_ref), (grad_hbm, grad_ref)], fetch_sem)
        )

    def compute(slot, chunk):
        spot = pl.ds(pl.multiple_of(chunk * size, size), size)
        mixed = dot(table[slot, spot], w_ref[...], NN)
        gate = gate_ref[slot, spot]
        scaled = mixed * gate
        grads[slot, spot] = scaled.astype(BF16)
        attended = attended_ref[slot, spot].astype(F32)
        logit_ref[slot, spot] = (scaled * attended * (1.0 - gate)).astype(BF16)

    def down_grad(n, _):
        columns = pl.ds(pl.multiple_of(n * tile, tile), tile)
        left = grad_ref[:, :, columns].reshape(tp_size * rows, tile)
        right = inner_ref[...].reshape(tp_size * rows, hidden)
        part[columns] = dot(left, right, TN).astype(BF16)
        return 0

    last = weights.stages
    middle = max(1, last - 4)

    def stage(n):
        weights.run(n)
        lax.fori_loop(n * tiles // last, (n + 1) * tiles // last, down_grad, 0)

    def between():
        fetches[0].wait()
        for n in range(middle):
            stage(n)

    gather_loop(table, sems, compute, between=between, ready=begin_fetch)
    copies = [
        pltpu.make_async_copy(table, all_ref, own_sem),
        pltpu.make_async_copy(part, part_hbm, write_sem),
    ]
    copies[0].start()

    def deal(t, _):
        here = pl.ds(pl.multiple_of(t * local, local), local)
        for slot, (s, g) in enumerate(places):
            piece = grads[t, pl.ds(s * local, local), pl.ds(g * width, width)]
            items[slot % count, slot // count, here] = piece
        return 0

    lax.fori_loop(0, tp_size, deal, 0)
    for n in range(middle, last):
        stage(n)
    for copy in copies[1:]:
        copy.start()
    for copy in copies:
        copy.wait()
    weights.end()


def out_back(
    branch, full_out, gate, attended, part, inner_act, grad_all, layout, item_count, f_size, ctx_size, ident
):
    seq_count, groups, width, places = layout
    rows, model_width = branch.shape
    tp_size, _, inner = gate.shape
    item = (item_count, ctx_size, tp_size * rows // seq_count, width)
    table = (tp_size, rows, model_width)
    down = (model_width, inner_act.shape[2])
    total = (part.shape[0] // (f_size * ctx_size), part.shape[1] // 2)
    place = pl.BlockSpec(memory_space=pl.ANY)
    dma = pltpu.SemaphoreType.DMA
    return pl.pallas_call(
        functools.partial(out_back_kernel, layout),
        grid=(1,),
        out_shape=[
            jax.ShapeDtypeStruct(table, BF16),
            jax.ShapeDtypeStruct(gate.shape, BF16),
            jax.ShapeDtypeStruct(item, BF16),
            jax.ShapeDtypeStruct(total, F32),
            jax.ShapeDtypeStruct(down, BF16),
        ],
        in_specs=[
            whole(branch.shape),
            whole((model_width, inner), 0),
            whole(gate.shape),
            whole(attended.shape),
            place,
            place,
            place,
        ],
        out_specs=[place, whole(gate.shape), whole(item), whole(total), place],
        scratch_shapes=[pltpu.VMEM(table, BF16), pltpu.VMEM(gate.shape, BF16), dma]
        + GATHER_SEMS
        + [
            pltpu.VMEM(inner_act.shape, BF16),
            pltpu.VMEM(table, BF16),
            pltpu.VMEM(down, BF16),
            dma((2,)),
            dma,
        ]
        + sum_scratch(f_size, ctx_size, *total),
        compiler_params=remote_params(ident, 60),
        cost_estimate=pl.CostEstimate(
            flops=2 * gate.size * model_width, bytes_accessed=100 << 20, transcendentals=0
        ),
        name="out_back",
    )(branch, full_out, gate, attended, part, inner_act, grad_all)


def assemble_kernel(layout, items, out_ref):
    seq_count, groups, width, places = layout
    count, local = items.shape[0], items.shape[3]
    inner = groups * width
    for slot, (s, g) in enumerate(places[: seq_count * groups]):
        for kind in range(3):
            columns = pl.ds(kind * inner + g * width, width)
            out_ref[0, pl.ds(s * local, local), columns] = items[slot % count, slot // count, kind]


def assemble(items, layout, tp_size):
    seq_count, groups, width, places = layout
    count, ctx_size, kinds, ctx_rows, _ = items.shape
    local = ctx_rows // tp_size
    shape = (tp_size, seq_count * local, kinds * groups * width)
    return pl.pallas_call(
        functools.partial(assemble_kernel, layout),
        grid=(tp_size,),
        out_shape=jax.ShapeDtypeStruct(shape, BF16),
        in_specs=[pl.BlockSpec((count, ctx_size, kinds, local, width), lambda t: (0, 0, 0, t, 0))],
        out_specs=pl.BlockSpec((1,) + shape[1:], lambda t: (t, 0, 0)),
        compiler_params=pltpu.CompilerParams(vmem_limit_bytes=32 << 20, dimension_semantics=("arbitrary",)),
        cost_estimate=pl.CostEstimate(flops=0, bytes_accessed=16 << 20, transcendentals=0),
        name="assemble",
    )(items)


def last_kernel(
    qkv_hbm,
    logit_hbm,
    forget_hbm,
    qkv_w_hbm,
    gate_w_hbm,
    x_hbm,
    grad_hbm,
    gain_ref,
    part_ref,
    extra_ref,
    out_ref,
    sum_ref,
    vector_ref,
    *refs,
):
    buffers, sems, (mine, near_in, group_in) = refs[:4], refs[4:8], refs[8:11]
    vector_sems = refs[11:15]
    qkv_ref, logit_ref, forget_ref, qkv_w, gate_w, x_ref, grad_ref, fetch_sem = refs[15:23]
    inner = gate_w.shape[1]
    fetch = Fetch(
        [
            (qkv_hbm, qkv_ref),
            (qkv_w_hbm, qkv_w),
            (logit_hbm, logit_ref),
            (forget_hbm, forget_ref),
            (gate_w_hbm.at[:, pl.ds(inner, inner)], gate_w),
            (x_hbm, x_ref),
            (grad_hbm, grad_ref),
        ],
        fetch_sem,
    )
    me, sibling, across, diagonal = tp_places()
    others = group_peers()
    greet_all([{"tp": sibling}, {"tp": across}, {"tp": diagonal}] + others)
    weights = WeightSum(part_ref, 0, sum_ref, refs[23:])
    weights.begin()
    fetch.wait()
    wide = qkv_ref.shape[2]
    mine[...] = extra_ref[...]
    size = x_ref.shape[0] // SUM_CHUNKS

    def span(chunk):
        return pl.ds(pl.multiple_of(chunk * size, size), size)

    def partial(slot, chunk):
        value = dot(qkv_ref[slot, span(chunk)], qkv_w[:, :wide], NT)
        value = value + dot(logit_ref[slot, span(chunk)], gate_w[...], NT)
        return value + dot(forget_ref[slot, span(chunk)], qkv_w[:, wide:], NT)

    def finish(chunk, total):
        x = x_ref[span(chunk)].astype(F32)
        inverse = lax.rsqrt(jnp.mean(x * x, axis=1, keepdims=True) + epsilon)
        unit = x * inverse
        mine[0:1] += jnp.sum(total * unit, axis=0, keepdims=True)
        scaled = total * gain_ref[...]
        middle = jnp.mean(scaled * unit, axis=1, keepdims=True)
        out_ref[span(chunk)] = (grad_ref[span(chunk)] + inverse * (scaled - unit * middle)).astype(BF16)

    stages = weights.stages
    late = max(4, stages - 4)

    def between(phase):
        if phase < 3:
            weights.run_to(2 * phase - 2, 2 * phase)
        else:
            weights.run_to(4, late)

    scatter_loop(buffers, sems, partial, finish, between=between)
    near_send, near_recv, group_send, group_recv = vector_sems
    copies = []
    for n, peer in enumerate((sibling, across, diagonal)):
        copies.append(sending(mine, near_in.at[n], near_send.at[n], near_recv.at[n], peer))
        copies[-1].start()
    weights.run_to(late, late + 2)
    for copy in copies:
        copy.wait()
    vector_ref[...] = mine[...] + near_in[0] + near_in[1] + near_in[2]
    mine[...] = vector_ref[...]
    copies = []
    for n, peer in enumerate(others):
        copies.append(moving(mine, group_in.at[n], group_send.at[n], group_recv.at[n], peer))
        copies[-1].start()
    weights.run_to(late + 2, stages)
    for n, copy in enumerate(copies):
        copy.wait()
        vector_ref[...] += group_in[n]
    weights.end()


def last(grad_qkv, grad_logit, grad_forget, full_one, full_out, x, grad_hidden, gain, part, extra, f_size, c_size, ident):
    rows, model_width = x.shape
    wide, inner = grad_qkv.shape[2], grad_logit.shape[2]
    shard, columns = part.shape[0] // (f_size * c_size), part.shape[1]
    dma = pltpu.SemaphoreType.DMA
    place = pl.BlockSpec(memory_space=pl.ANY)
    return pl.pallas_call(
        last_kernel,
        grid=(1,),
        out_shape=[
            jax.ShapeDtypeStruct(x.shape, BF16),
            jax.ShapeDtypeStruct((shard, columns), F32),
            jax.ShapeDtypeStruct(extra.shape, F32),
        ],
        in_specs=[
            place,
            place,
            place,
            place,
            place,
            place,
            place,
            whole(gain.shape),
            place,
            whole(extra.shape),
        ],
        out_specs=[whole(x.shape), whole((shard, columns)), whole(extra.shape)],
        scratch_shapes=scatter_buffers(rows, model_width)
        + SCATTER_SEMS
        + [
            pltpu.VMEM(extra.shape, F32),
            pltpu.VMEM((3,) + extra.shape, F32),
            pltpu.VMEM((f_size * c_size - 1,) + extra.shape, F32),
        ]
        + [dma((3,))] * 2
        + [dma((f_size * c_size - 1,))] * 2
        + [
            pltpu.VMEM(grad_qkv.shape, BF16),
            pltpu.VMEM(grad_logit.shape, BF16),
            pltpu.VMEM(grad_forget.shape, BF16),
            pltpu.VMEM(full_one.shape, BF16),
            pltpu.VMEM((model_width, inner), BF16),
            pltpu.VMEM(x.shape, BF16),
            pltpu.VMEM(x.shape, F32),
            dma((7,)),
        ]
        + sum_scratch(f_size, c_size, shard, columns),
        compiler_params=remote_params(ident, 60),
        cost_estimate=pl.CostEstimate(
            flops=8 * rows * model_width * (wide + inner + LANES), bytes_accessed=100 << 20, transcendentals=0
        ),
        name="last",
    )(grad_qkv, grad_logit, grad_forget, full_one, full_out, x, grad_hidden, gain, part, extra)


def per_device(
    layer_input,
    lengths,
    attn_gain,
    w_query,
    w_key,
    w_value,
    w_forget,
    forget_bias,
    w_gate_out,
    w_out,
    mlp_gain,
    w_gate,
    w_up,
    w_down,
    cotangent,
):
    local_rows, seq_count, model_width = layer_input.shape
    head_count = forget_bias.shape[0]
    inner_width = w_query.shape[1]
    hidden = w_gate.shape[1]
    head_size = inner_width // head_count
    tp_size = lax.axis_size("tp")
    ctx_size = lax.axis_size("ctx")
    shard_count = lax.axis_size("fsdp") * ctx_size
    ctx_rows = local_rows * tp_size
    seq_len = ctx_rows * ctx_size
    all_rows = seq_count * ctx_rows
    ctx_index = lax.axis_index("ctx")
    tp_index = lax.axis_index("tp")
    shard_index = lax.axis_index("fsdp") * ctx_size + ctx_index

    pair = LANES // head_size
    groups = head_count // pair
    width = pair * head_size
    item_count = pl.cdiv(seq_count * groups, ctx_size)
    used = seq_count * groups

    def place(slot):
        slot = slot % used
        return (slot // groups + slot % groups) % seq_count, slot % groups

    places = tuple(place(slot) for slot in range(ctx_size * item_count))
    layout = (seq_count, groups, width, places)

    fsdp_size = lax.axis_size("fsdp")
    wide_forget = jnp.pad(w_forget, ((0, 0), (0, LANES - head_count)))
    edge = 3 * inner_width
    input_rows = layer_input.transpose(1, 0, 2).reshape(seq_count * local_rows, model_width)
    shard_rows = model_width // shard_count
    own_gains = jnp.stack([attn_gain, mlp_gain]).astype(F32)
    own_gains = jnp.pad(own_gains, ((0, 6), (0, -shard_rows % LANES)))
    input_all, full_one, gains = startup(
        input_rows, own_gains, (w_query, w_key, w_value, wide_forget), fsdp_size, ctx_size, 1
    )
    gain_one = gains[:, 0, :shard_rows].reshape(1, model_width)
    gain_two = gains[:, 1, :shard_rows].reshape(1, model_width)

    def by_sequence(rows):
        return rows.transpose(1, 0, 2).reshape(seq_count * local_rows, model_width)

    def by_position(rows):
        return rows.reshape(seq_count, local_rows, model_width).transpose(1, 0, 2)

    local_pos = (ctx_index * tp_size + tp_index) * local_rows + jnp.arange(
        local_rows, dtype=jnp.int32
    )
    valid_rows = (local_pos[None, :] < lengths[:, None]).astype(F32)
    valid_rows = valid_rows.reshape(seq_count * local_rows, 1)
    ctx_pos = ctx_index * ctx_rows + jnp.arange(ctx_rows, dtype=jnp.int32)
    ctx_pos = ctx_pos.reshape(tp_size, 1, local_rows)
    ctx_valid = (ctx_pos < lengths[None, :, None]).astype(F32)

    grad_out = (valid_rows * by_sequence(cotangent).astype(F32)).astype(BF16)
    normed_one, forget_rows, items = project(
        input_all, gain_one, full_one, layout, item_count, ctx_size
    )
    normed_flat = normed_one.reshape(all_rows, model_width)
    forget_logit = forget_rows.reshape(all_rows, LANES)[:, :head_count].T
    forget_logit = forget_logit + forget_bias.astype(F32)[:, None]
    forget_logit = forget_logit.reshape(head_count, tp_size, seq_count, local_rows)
    log_forget = (ctx_valid[None] * jax.nn.log_sigmoid(forget_logit)).astype(BF16)

    cut = log_forget.astype(F32).reshape(groups, pair, tp_size, seq_count, local_rows)
    picked = jnp.stack([cut[g, :, :, s] for s, g in places])
    picked = picked.reshape(ctx_size, item_count, pair, ctx_rows).transpose(1, 0, 2, 3)
    picked = jnp.pad(picked, ((0, 0), (0, 0), (0, 8 - pair), (0, 0)))
    attended_items, qkv, full_two, full_out, grad_all, exact, lse, decay, out_gate = context(
        items,
        picked,
        (w_gate, w_up, w_out, w_gate_out),
        grad_out,
        normed_one,
        fsdp_size,
        head_size,
        7,
    )
    hidden_state, normed_two, attended, mixed, down_w = out_project(
        input_rows,
        out_gate,
        full_out,
        gain_two,
        attended_items,
        w_down,
        layout,
        fsdp_size,
        ctx_size,
        2,
    )
    normed_two_all, inner_act, grad_pair = mlp(normed_two, grad_all, full_two, down_w, hidden, 3)
    normed_two_flat = normed_two_all.reshape(all_rows, model_width)
    grad_pair_flat = grad_pair.reshape(all_rows, 2 * hidden)

    gate_up_part = dot(normed_two_flat, grad_pair_flat, TN).astype(BF16)
    grad_hidden, branch, mlp_gain_part, gate_sum = mlp_back(
        grad_pair, full_two, hidden_state, grad_out, gain_two, gate_up_part, fsdp_size, ctx_size, 4
    )
    branch_all, grad_gate_logit, grads, up_sum, down_part = out_back(
        branch,
        full_out,
        out_gate,
        attended,
        gate_up_part,
        inner_act,
        grad_all,
        layout,
        item_count,
        fsdp_size,
        ctx_size,
        5,
    )
    branch_flat = branch_all.reshape(all_rows, model_width)
    logit_flat = grad_gate_logit.reshape(all_rows, inner_width)

    out_part = jnp.concatenate(
        [
            dot(branch_flat, mixed.reshape(all_rows, inner_width), TN).astype(BF16),
            dot(normed_flat, logit_flat, TN).astype(BF16),
        ],
        axis=1,
    )
    grad_items, forget_items, down_sum, out_sum, feedforward = context_back(
        grads,
        qkv,
        exact,
        lse,
        decay,
        down_part,
        out_part,
        inner_act,
        down_w,
        fsdp_size,
        head_size,
        8,
    )
    output = (valid_rows * (hidden_state + feedforward.astype(F32))).astype(BF16)
    forget_back = forget_items[:, :, :pair].astype(BF16).transpose(1, 0, 2, 3)
    forget_back = forget_back.reshape(ctx_size * item_count, pair, tp_size, local_rows)
    slots = {place(slot): slot for slot in range(used)}
    forget_back = jnp.stack(
        [
            jnp.stack([forget_back[slots[s, g]] for s in range(seq_count)], axis=2)
            for g in range(groups)
        ]
    ).reshape(head_count, tp_size, seq_count, local_rows)
    grad_forget_logit = forget_back.astype(F32) * ctx_valid[None] * jax.nn.sigmoid(-forget_logit)
    grad_forget_logit = grad_forget_logit.astype(BF16).reshape(head_count, all_rows)
    bias_part = jnp.sum(grad_forget_logit.astype(F32), axis=1)
    grad_forget_rows = jnp.pad(grad_forget_logit, ((0, LANES - head_count), (0, 0))).T
    grad_qkv = assemble(grad_items, layout, tp_size)
    grad_qkvf = jnp.concatenate([grad_qkv.reshape(all_rows, edge), grad_forget_rows], axis=1)
    bias_full = lax.dynamic_update_slice(
        jnp.zeros((1, model_width), F32), bias_part[None], (0, tp_index * head_count)
    )
    extra = jnp.concatenate(
        [jnp.zeros_like(bias_full), mlp_gain_part, bias_full, jnp.zeros((5, model_width), F32)]
    )
    input_grad, qkv_sum, vectors = last(
        grad_qkv,
        grad_gate_logit,
        grad_forget_rows.reshape(tp_size, -1, LANES),
        full_one,
        full_out,
        input_rows,
        grad_hidden,
        gain_one,
        dot(normed_flat, grad_qkvf, TN).astype(BF16),
        extra,
        fsdp_size,
        ctx_size,
        6,
    )
    gain_one_sum, gain_two_sum, bias_sum = vectors[0], vectors[1], vectors[2]
    attn_gain_grad = lax.dynamic_slice_in_dim(gain_one_sum, shard_index * shard_rows, shard_rows, 0)
    mlp_gain_grad = lax.dynamic_slice_in_dim(gain_two_sum, shard_index * shard_rows, shard_rows, 0)
    forget_bias_grad = lax.dynamic_slice_in_dim(bias_sum, tp_index * head_count, head_count, 0)
    wide = inner_width
    return (
        by_position(output),
        by_position(input_grad),
        attn_gain_grad,
        qkv_sum[:, :wide],
        qkv_sum[:, wide : 2 * wide],
        qkv_sum[:, 2 * wide : 3 * wide],
        qkv_sum[:, 3 * wide : 3 * wide + head_count],
        forget_bias_grad,
        out_sum[:, wide:],
        out_sum[:, :wide],
        mlp_gain_grad,
        gate_sum,
        up_sum,
        down_sum,
    )


def solution(mesh):
    rows = P(("ctx", "tp"), "fsdp", None)
    matrix = P(("fsdp", "ctx"), "tp")
    vector = P(("fsdp", "ctx"))
    return jax.shard_map(
        per_device,
        mesh=mesh,
        in_specs=(
            rows,
            P("fsdp"),
            vector,
            matrix,
            matrix,
            matrix,
            matrix,
            P("tp"),
            matrix,
            matrix,
            vector,
            matrix,
            matrix,
            matrix,
            rows,
        ),
        out_specs=(
            rows,
            rows,
            vector,
            matrix,
            matrix,
            matrix,
            matrix,
            P("tp"),
            matrix,
            matrix,
            vector,
            matrix,
            matrix,
            matrix,
        ),
        check_vma=False,
    )
```
